128 devices in a mesh: lat: 16 (over x, y), var: 8 (over z, core).
Axes of the slice: x: 4, y: 4, z: 4, core: 2. Of those that a mesh axis runs over, the one named last changes fastest.
Arguments:
- patches: bfloat16 [96, 192, 1024], P('lat', 'var'), may hold values from -6 to 6
- norm_gain: float32 [1024], replicated, may hold values from 0.25 to 1.75
- input_proj: bfloat16 [1024, 3072], replicated, may hold values from -7 to 7
- output_proj: bfloat16 [1024, 1024], replicated, may hold values from -0.1875 to 0.1875
- level_scale: float32 [40, 1024], P('var'), may hold values from 0.1 to 1.9
- level_shift: float32 [40, 1024], P('var'), may hold values from -3 to 3
- head_weight: bfloat16 [40, 1024, 320], P('var', 'lat'), may hold values from -0.1875 to 0.1875
- targets: bfloat16 [40, 96, 192, 320], P('var', 'lat'), may hold values from -6 to 6
- level_counts: int32 [4], replicated, may hold values from 13 to 37
- tile_dataset: int32 [16, 8], P('lat'), may hold values from 0 to 3
- slot_level: int32 [40], P('var'), may hold values from 0 to 39, as said below
Outputs:
- latent: bfloat16 [96, 192, 1024], P('lat', 'var')
- grad_latent: bfloat16 [96, 192, 1024], P('lat', 'var')
- grad_head: float32 [40, 1024, 320], P('var', 'lat')
The draws below stay inside these ranges and needn't reach their ends.
Inputs may be any that keep to these rules, and one draw needn't show every extreme that they name: `slot_level`: for each j, slots j * 5 to (j + 1) * 5 - 1 hold the levels j * 5 to (j + 1) * 5 - 1 in some order.
All inputs are finite; a program needn't handle non-finite values.
Results may differ from the reference program's by a relative error of at most 0.012.
Values may be sent and summed in bfloat16 or wider, within the bound.
A program may use at most 128 MiB of HBM per device.

```python
import math
import jax
import jax.numpy as jnp
from jax import lax

D = 1024
HEADS = 16
WH = 6
WW = 12
BR = 6
BC = 24
OUT = 320
LEVELS = 37
LV_PAD = 40
DATASETS = 4
LPO = 5
NLAT_P = 96
NLON_P = 192
N_LAT = 16
N_VAR = 8


def draw_input_proj(key, part):
    base = jax.random.normal(key, (D, 3 * D), jnp.float32) / math.sqrt(D)
    base = jnp.clip(base, -6.0 / math.sqrt(D), 6.0 / math.sqrt(D))
    return base.astype(jnp.bfloat16)


def one_block(block_key):
    return jax.random.permutation(block_key, LPO).astype(jnp.int32)


def draw_slot_level(key, part):
    block_keys = jax.random.split(jax.random.fold_in(key, 23), N_VAR)
    orders = jax.vmap(one_block)(block_keys)
    offsets = jnp.arange(N_VAR, dtype=jnp.int32)[:, None] * LPO
    return (orders + offsets).reshape(LV_PAD)


def with_ends(array, key, smallest, high):
    dims = array.shape
    index_at = [jax.random.randint(jax.random.fold_in(key, axis), (), 0, dims[axis]) for axis in range(len(dims))]
    array = array.at[tuple(index_at)].set(smallest)
    longest = dims.index(max(dims))
    index_at[longest] = (index_at[longest] + 1) % dims[longest]
    return array.at[tuple(index_at)].set(high)


def shard_levels(stream_key, shape, pieces, smallest, top_value):
    level, own = 1.0, jax.random.fold_in(stream_key, 6)
    for axis_at, shards_of in pieces:
        steps = jnp.exp(jax.random.uniform(jax.random.fold_in(own, axis_at), (shards_of,), jnp.float32, smallest / len(pieces), top_value / len(pieces)))
        level = level * jnp.repeat(steps, shape[axis_at] // shards_of).reshape([-1 if axis == axis_at else 1 for axis in range(len(shape))])
    return level


def bell_draw(own_key, shape, scale, reach, cuts=(), held_as=jnp.bfloat16):
    level = shard_levels(own_key, shape, cuts, -0.22, 0.18) if cuts else 1.0
    array = jax.random.normal(own_key, shape, jnp.float32) * scale * level
    return jnp.minimum(jnp.maximum(array, -reach), reach).astype(held_as)


def setup_inputs(seed: int = 0) -> dict:
    key_of = jax.random.split(jax.random.key(seed), 12)
    patches = bell_draw(key_of[0], (NLAT_P, NLON_P, D), 1.0, 6.0, ((0, 16), (1, 8)))
    norm_gain = jnp.clip(1.0 + 0.15 * jax.random.normal(key_of[1], (D,), jnp.float32), 0.25, 1.75)
    input_proj = draw_input_proj(jax.random.fold_in(key_of[11], 71), 0)
    output_proj = bell_draw(key_of[3], (D, D), D ** -0.5, 0.1875)
    level_scale = jnp.clip(1.0 + 0.18 * jax.random.normal(key_of[4], (LV_PAD, D), jnp.float32), 0.1, 1.9)
    level_shift = bell_draw(key_of[5], (LV_PAD, D), 0.5, 3.0, ((0, 8),), jnp.float32)
    head_weight = bell_draw(key_of[6], (LV_PAD, D, OUT), D ** -0.5, 0.1875, ((0, 8), (1, 16)))
    targets = bell_draw(key_of[7], (LV_PAD, NLAT_P, NLON_P, OUT), 1.0, 6.0, ((0, 8), (1, 16)))
    level_counts = with_ends(jax.random.randint(key_of[8], (DATASETS,), 13, LEVELS + 1), jax.random.fold_in(key_of[8], 1), 13, LEVELS).astype(jnp.int32)
    tile_dataset = with_ends(jax.random.randint(key_of[9], (N_LAT, N_VAR), 0, DATASETS), jax.random.fold_in(key_of[9], 1), 0, DATASETS - 1).astype(jnp.int32)
    slot_level = draw_slot_level(jax.random.fold_in(key_of[11], 71), 0)
    return dict(patches=patches, norm_gain=norm_gain, input_proj=input_proj, output_proj=output_proj, level_scale=level_scale, level_shift=level_shift, head_weight=head_weight, targets=targets, level_counts=level_counts, tile_dataset=tile_dataset, slot_level=slot_level)


EPS = 1e-05

def layer_norm(values, gain):
    wide = values.astype(jnp.float32)
    average = lax.optimization_barrier(jnp.mean(wide, axis=-1, keepdims=True))
    centred = wide - average
    variance = lax.optimization_barrier(jnp.mean(centred * centred, axis=-1, keepdims=True))
    return (centred * lax.rsqrt(variance + EPS) * gain).astype(jnp.bfloat16)

def reference(patches, norm_gain, input_proj, output_proj, level_scale, level_shift, head_weight, targets, level_counts, tile_dataset, slot_level):
    nlat, nlon, width = patches.shape
    head_size = width // HEADS
    half_rows = WH // 2
    half_cols = WW // 2
    normed = layer_norm(patches, norm_gain)
    qkv = jnp.dot(normed.reshape(-1, width), input_proj, preferred_element_type=jnp.float32).astype(jnp.bfloat16)
    qkv = qkv.reshape(nlat, nlon, 3 * width)
    padded = jnp.pad(qkv, ((half_rows, WH - half_rows), (0, 0), (0, 0)))
    rolled = jnp.roll(padded, half_cols, axis=1)
    rows_pad = nlat + WH
    win_rows = rows_pad // WH
    win_cols = nlon // WW
    windows = rolled.reshape(win_rows, WH, win_cols, WW, 3, HEADS, head_size)
    windows = windows.transpose(0, 2, 1, 3, 4, 5, 6).reshape(win_rows * win_cols, WH * WW, 3, HEADS, head_size)
    query_win = windows[:, :, 0].astype(jnp.float32)
    key_win = windows[:, :, 1].astype(jnp.float32)
    value_win = windows[:, :, 2].astype(jnp.float32)
    row_ids = jnp.arange(rows_pad)
    row_valid = (row_ids >= half_rows) & (row_ids < half_rows + nlat)
    key_mask = jnp.broadcast_to(row_valid.reshape(win_rows, 1, WH, 1), (win_rows, win_cols, WH, WW)).reshape(win_rows * win_cols, WH * WW)
    scores = jnp.einsum('wqhd,wkhd->whqk', query_win, key_win) / math.sqrt(head_size)
    scores = jnp.where(key_mask[:, None, None, :], scores, -jnp.inf)
    peak = lax.optimization_barrier(jnp.max(scores, axis=-1, keepdims=True))
    weights = jnp.exp(scores - peak)
    probs = (weights / lax.optimization_barrier(jnp.sum(weights, axis=-1, keepdims=True))).astype(jnp.bfloat16)
    mixed = jnp.einsum('whqk,wkhd->wqhd', probs.astype(jnp.float32), value_win)
    mixed = mixed.reshape(win_rows, win_cols, WH, WW, width).transpose(0, 2, 1, 3, 4).reshape(rows_pad, nlon, width)
    mixed = jnp.roll(mixed, -half_cols, axis=1)[half_rows:half_rows + nlat]
    attn = mixed.astype(jnp.bfloat16)
    update = jnp.dot(attn.reshape(-1, width), output_proj, preferred_element_type=jnp.float32).reshape(nlat, nlon, width)
    latent = (patches.astype(jnp.float32) + update).astype(jnp.bfloat16)
    tile_levels = level_counts[tile_dataset]
    live = (slot_level[:, None, None] < tile_levels[None]).astype(jnp.float32)
    live_grid = jnp.repeat(jnp.repeat(live, BR, axis=1), BC, axis=2)
    latent_wide = latent.astype(jnp.float32)
    head_norm = 1.0 / math.sqrt(NLAT_P * NLON_P)

    def per_slot(carry, slot_inputs):
        scale, shift, weight, target, mask = slot_inputs
        rows = (latent_wide * scale + shift).astype(jnp.bfloat16).reshape(-1, width)
        predicted = jnp.dot(rows, weight, preferred_element_type=jnp.float32)
        errors = ((predicted - target.reshape(-1, OUT).astype(jnp.float32)) * mask.reshape(-1, 1)).astype(jnp.bfloat16)
        back_grad = jnp.dot(errors, weight.T, preferred_element_type=jnp.float32) * scale
        grad_slot = jnp.dot(rows.T, errors, preferred_element_type=jnp.float32) * head_norm
        return (carry + back_grad, grad_slot)
    start = jnp.zeros((nlat * nlon, width), jnp.float32)
    total, grad_head = lax.scan(per_slot, start, (level_scale, level_shift, head_weight, targets, live_grid))
    grad_latent = total.reshape(nlat, nlon, width).astype(jnp.bfloat16)
    return (latent, grad_latent, grad_head)
```

```python
import math

import jax
import jax.numpy as jnp
from jax import lax
from jax.sharding import PartitionSpec as P

HEADS = 16
WH = 6
WW = 12


EPS = 1e-05


def padded(array, sides, width, wrap):
    for axis, dim in sides:
        size, length = (lax.axis_size(axis), array.shape[dim])
        up = [(i, (i + 1) % size) for i in range(size if wrap else size - 1)]
        down = [(j, i) for i, j in up]
        last = lax.slice_in_dim(array, length - width, length, axis=dim)
        initial = lax.slice_in_dim(array, 0, width, axis=dim)
        before = lax.ppermute(last, axis, up)
        after = lax.ppermute(initial, axis, down)
        array = jnp.concatenate([before, array, after], axis=dim)
    return array


def layer_norm(values, gain):
    wide = values.astype(jnp.float32)
    average = jnp.mean(wide, axis=-1, keepdims=True)
    centred = wide - average
    variance = jnp.mean(centred * centred, axis=-1, keepdims=True)
    return (centred * lax.rsqrt(variance + EPS) * gain).astype(jnp.bfloat16)


def window_attention(query_ext, keyval, row_valid, heads):
    ext_rows, ext_cols, width = query_ext.shape
    head_size = width // heads
    win_rows = ext_rows // WH
    win_cols = ext_cols // WW

    def split(values, parts):
        shaped = values.reshape(win_rows, WH, win_cols, WW, parts, heads, head_size)
        return shaped.transpose(0, 2, 1, 3, 4, 5, 6).reshape(
            win_rows * win_cols, WH * WW, parts, heads, head_size
        )

    query_win = split(query_ext, 1)[:, :, 0]
    pairs = split(keyval, 2)
    key_win = pairs[:, :, 0]
    value_win = pairs[:, :, 1]
    key_mask = jnp.broadcast_to(
        row_valid.reshape(win_rows, 1, WH, 1), (win_rows, win_cols, WH, WW)
    ).reshape(win_rows * win_cols, WH * WW)
    scores = jnp.einsum(
        "wqhd,wkhd->whqk", query_win, key_win, preferred_element_type=jnp.float32
    ) / math.sqrt(head_size)
    scores = jnp.where(key_mask[:, None, None, :], scores, -jnp.inf)
    peak = jnp.max(scores, axis=-1, keepdims=True)
    weights = jnp.exp(scores - peak)
    probs = (weights / jnp.sum(weights, axis=-1, keepdims=True)).astype(jnp.bfloat16)
    mixed = jnp.einsum("whqk,wkhd->wqhd", probs, value_win, preferred_element_type=jnp.float32)
    return (
        mixed.reshape(win_rows, win_cols, WH, WW, width)
        .transpose(0, 2, 1, 3, 4)
        .reshape(ext_rows, ext_cols, width)
    )


def slot_terms(piece, target_rows, live_cols, level_scale, level_shift, heads_full):
    piece_wide = piece.astype(jnp.float32)
    rows = (
        piece_wide[None] * level_scale[:, None, None, :] + level_shift[:, None, None, :]
    ).astype(jnp.bfloat16)
    predicted = jnp.einsum("krnd,kdo->krno", rows, heads_full, preferred_element_type=jnp.float32)
    errors = ((predicted - target_rows.astype(jnp.float32)) * live_cols[:, None, :, None]).astype(
        jnp.bfloat16
    )
    back_grad = jnp.einsum("krno,kdo->krnd", errors, heads_full, preferred_element_type=jnp.float32)
    piece_grad = jnp.sum(back_grad * level_scale[:, None, None, :], axis=0)
    head_add = jnp.einsum("krnd,krno->dko", rows, errors, preferred_element_type=jnp.float32)
    return (piece_grad, head_add)


def local(
    patches,
    norm_gain,
    input_proj,
    output_proj,
    level_scale,
    level_shift,
    head_weight,
    targets,
    level_counts,
    tile_dataset,
    slot_level,
):
    band_rows, band_cols, width = patches.shape
    half_rows = WH // 2
    half_cols = WW // 2
    lat_count = lax.axis_size("lat")
    var_count = lax.axis_size("var")
    lat_place = lax.axis_index("lat")
    ext_rows = band_rows + WH
    ext_cols = band_cols + WW
    extended = padded(patches, (("lat", 0),), half_rows, False)
    extended = padded(extended, (("var", 1),), half_cols, True)
    normed_ext = layer_norm(extended, norm_gain)
    keyval = jnp.dot(
        normed_ext.reshape(-1, width), input_proj[:, width:], preferred_element_type=jnp.float32
    )
    keyval = keyval.astype(jnp.bfloat16).reshape(ext_rows, ext_cols, 2 * width)
    normed = normed_ext[half_rows : half_rows + band_rows, half_cols : half_cols + band_cols]
    queries = jnp.dot(
        normed.reshape(-1, width), input_proj[:, :width], preferred_element_type=jnp.float32
    )
    queries = queries.astype(jnp.bfloat16).reshape(band_rows, band_cols, width)
    query_ext = jnp.pad(queries, ((half_rows, WH - half_rows), (half_cols, WW - half_cols), (0, 0)))
    global_row = lat_place * band_rows - half_rows + jnp.arange(ext_rows, dtype=jnp.int32)
    row_valid = (global_row >= 0) & (global_row < lat_count * band_rows)
    mixed = window_attention(query_ext, keyval, row_valid, HEADS)
    attn = mixed[half_rows : half_rows + band_rows, half_cols : half_cols + band_cols].astype(
        jnp.bfloat16
    )
    update = jnp.dot(
        attn.reshape(-1, width), output_proj, preferred_element_type=jnp.float32
    ).reshape(band_rows, band_cols, width)
    latent = (patches.astype(jnp.float32) + update).astype(jnp.bfloat16)
    dataset_row = tile_dataset[0]
    dataset_ids = jnp.arange(level_counts.shape[0], dtype=jnp.int32)
    tile_levels = jnp.sum(
        jnp.where(dataset_row[:, None] == dataset_ids[None, :], level_counts[None, :], 0), axis=1
    )
    live_tiles = (slot_level[None, :] < tile_levels[:, None]).astype(jnp.float32)
    heads_full = lax.all_gather(head_weight, "lat", axis=1, tiled=True)
    tile_ids = jnp.arange(var_count, dtype=jnp.int32)
    piece = lax.all_gather(latent, "var", axis=1, tiled=True)
    piece_cols = piece.shape[1]
    column_tile = jnp.arange(piece_cols, dtype=jnp.int32) // band_cols
    onehot = (column_tile[:, None] == tile_ids[None, :]).astype(jnp.float32)
    column_live = jnp.dot(onehot, live_tiles)
    piece_grad, head_add = slot_terms(
        piece, targets, column_live.T, level_scale, level_shift, heads_full
    )
    latent_terms = piece_grad
    latent_terms, head_terms = (latent_terms, head_add)
    grad_latent = lax.psum_scatter(
        latent_terms.astype(jnp.bfloat16), "var", scatter_dimension=1, tiled=True
    )
    head_terms = head_terms * (1.0 / math.sqrt(lat_count * band_rows * var_count * band_cols))
    share_rows = width // lat_count
    mine = lax.psum_scatter(
        head_terms.astype(jnp.bfloat16), "lat", scatter_dimension=0, tiled=True
    ).astype(jnp.float32)
    grad_head = jnp.transpose(mine, (1, 0, 2))
    return (latent, grad_latent, grad_head)


def solution(mesh):
    in_specs = (
        P("lat", "var", None),
        P(),
        P(),
        P(),
        P("var", None),
        P("var", None),
        P("var", "lat", None),
        P("var", "lat", None, None),
        P(),
        P("lat", None),
        P("var"),
    )
    out_specs = (P("lat", "var", None), P("lat", "var", None), P("var", "lat", None))
    return jax.shard_map(local, mesh=mesh, in_specs=in_specs, out_specs=out_specs, check_vma=False)
```

```python
import math

import jax
import jax.numpy as jnp
from jax import lax
from jax.experimental import pallas as pl
from jax.experimental.pallas import tpu as pltpu
from jax.sharding import PartitionSpec as P

MESH_ID = pl.DeviceIdType.MESH


def _greet(axis, n, me):
    barrier = pltpu.get_barrier_semaphore()
    for k in range(1, n):
        pl.semaphore_signal(barrier, inc=1, device_id={axis: lax.rem(me + k, n)},
                            device_id_type=MESH_ID)
    pl.semaphore_wait(barrier, n - 1)


def peer_gather(block, axis, n, cid):
    def kernel(x_ref, out_ref, send_sem, recv_sem):
        me = lax.axis_index(axis)
        _greet(axis, n, me)
        sends = []
        for k in range(1, n):
            copy = pltpu.make_async_remote_copy(
                src_ref=x_ref, dst_ref=out_ref.at[me], send_sem=send_sem.at[k],
                recv_sem=recv_sem.at[me], device_id={axis: lax.rem(me + k, n)},
                device_id_type=MESH_ID)
            copy.start()
            sends.append(copy)
        out_ref[me] = x_ref[...]
        for k in range(1, n):
            src = lax.rem(me + n - k, n)
            pltpu.make_async_remote_copy(
                src_ref=x_ref, dst_ref=out_ref.at[src], send_sem=send_sem.at[k],
                recv_sem=recv_sem.at[src], device_id={axis: src},
                device_id_type=MESH_ID).wait_recv()
        for copy in sends:
            copy.wait_send()

    return pl.pallas_call(
        kernel,
        out_shape=jax.ShapeDtypeStruct((n,) + block.shape, block.dtype),
        in_specs=[pl.BlockSpec(memory_space=pltpu.VMEM)],
        out_specs=pl.BlockSpec(memory_space=pltpu.VMEM),
        scratch_shapes=[pltpu.SemaphoreType.DMA((n,)), pltpu.SemaphoreType.DMA((n,))],
        compiler_params=pltpu.CompilerParams(collective_id=cid, has_side_effects=True),
    )(block)


def peer_reduce_scatter(parts, axis, n, cid, out_dtype):
    def kernel(x_ref, out_ref, held, send_sem, recv_sem):
        me = lax.axis_index(axis)
        _greet(axis, n, me)
        sends = []
        for k in range(1, n):
            dst = lax.rem(me + k, n)
            copy = pltpu.make_async_remote_copy(
                src_ref=x_ref.at[dst], dst_ref=held.at[me], send_sem=send_sem.at[k],
                recv_sem=recv_sem.at[me], device_id={axis: dst},
                device_id_type=MESH_ID)
            copy.start()
            sends.append(copy)
        total = x_ref[me].astype(jnp.float32)
        for k in range(1, n):
            src = lax.rem(me + n - k, n)
            pltpu.make_async_remote_copy(
                src_ref=x_ref.at[src], dst_ref=held.at[src], send_sem=send_sem.at[k],
                recv_sem=recv_sem.at[src], device_id={axis: src},
                device_id_type=MESH_ID).wait_recv()
            total = total + held[src].astype(jnp.float32)
        out_ref[...] = total.astype(out_ref.dtype)
        for copy in sends:
            copy.wait_send()

    return pl.pallas_call(
        kernel,
        out_shape=jax.ShapeDtypeStruct(parts.shape[1:], out_dtype),
        in_specs=[pl.BlockSpec(memory_space=pltpu.VMEM)],
        out_specs=pl.BlockSpec(memory_space=pltpu.VMEM),
        scratch_shapes=[pltpu.VMEM(parts.shape, parts.dtype),
                        pltpu.SemaphoreType.DMA((n,)), pltpu.SemaphoreType.DMA((n,))],
        compiler_params=pltpu.CompilerParams(collective_id=cid, has_side_effects=True),
    )(parts)

HEADS = 16
WH = 6
WW = 12


EPS = 1e-05


def padded(array, sides, width, wrap):
    for axis, dim in sides:
        size, length = (lax.axis_size(axis), array.shape[dim])
        up = [(i, (i + 1) % size) for i in range(size if wrap else size - 1)]
        down = [(j, i) for i, j in up]
        last = lax.slice_in_dim(array, length - width, length, axis=dim)
        initial = lax.slice_in_dim(array, 0, width, axis=dim)
        before = lax.ppermute(last, axis, up)
        after = lax.ppermute(initial, axis, down)
        array = jnp.concatenate([before, array, after], axis=dim)
    return array


def layer_norm(values, gain):
    wide = values.astype(jnp.float32)
    average = jnp.mean(wide, axis=-1, keepdims=True)
    centred = wide - average
    variance = jnp.mean(centred * centred, axis=-1, keepdims=True)
    return (centred * lax.rsqrt(variance + EPS) * gain).astype(jnp.bfloat16)


def window_attention(query_ext, keyval, row_valid, heads):
    ext_rows, ext_cols, width = query_ext.shape
    head_size = width // heads
    win_rows = ext_rows // WH
    win_cols = ext_cols // WW

    def split(values, parts):
        shaped = values.reshape(win_rows, WH, win_cols, WW, parts, heads, head_size)
        return shaped.transpose(0, 2, 1, 3, 4, 5, 6).reshape(
            win_rows * win_cols, WH * WW, parts, heads, head_size
        )

    query_win = split(query_ext, 1)[:, :, 0]
    pairs = split(keyval, 2)
    key_win = pairs[:, :, 0]
    value_win = pairs[:, :, 1]
    key_mask = jnp.broadcast_to(
        row_valid.reshape(win_rows, 1, WH, 1), (win_rows, win_cols, WH, WW)
    ).reshape(win_rows * win_cols, WH * WW)
    scores = jnp.einsum(
        "wqhd,wkhd->whqk", query_win, key_win, preferred_element_type=jnp.float32
    ) / math.sqrt(head_size)
    scores = jnp.where(key_mask[:, None, None, :], scores, -jnp.inf)
    peak = jnp.max(scores, axis=-1, keepdims=True)
    weights = jnp.exp(scores - peak)
    probs = (weights / jnp.sum(weights, axis=-1, keepdims=True)).astype(jnp.bfloat16)
    mixed = jnp.einsum("whqk,wkhd->wqhd", probs, value_win, preferred_element_type=jnp.float32)
    return (
        mixed.reshape(win_rows, win_cols, WH, WW, width)
        .transpose(0, 2, 1, 3, 4)
        .reshape(ext_rows, ext_cols, width)
    )


def slot_terms(piece, target_rows, live_cols, level_scale, level_shift, heads_full):
    piece_wide = piece.astype(jnp.float32)
    rows = (
        piece_wide[None] * level_scale[:, None, None, :] + level_shift[:, None, None, :]
    ).astype(jnp.bfloat16)
    predicted = jnp.einsum("krnd,kdo->krno", rows, heads_full, preferred_element_type=jnp.float32)
    errors = ((predicted - target_rows.astype(jnp.float32)) * live_cols[:, None, :, None]).astype(
        jnp.bfloat16
    )
    back_grad = jnp.einsum("krno,kdo->krnd", errors, heads_full, preferred_element_type=jnp.float32)
    piece_grad = jnp.sum(back_grad * level_scale[:, None, None, :], axis=0)
    head_add = jnp.einsum("krnd,krno->dko", rows, errors, preferred_element_type=jnp.float32)
    return (piece_grad, head_add)


def local(
    patches,
    norm_gain,
    input_proj,
    output_proj,
    level_scale,
    level_shift,
    head_weight,
    targets,
    level_counts,
    tile_dataset,
    slot_level,
):
    band_rows, band_cols, width = patches.shape
    half_rows = WH // 2
    half_cols = WW // 2
    lat_count = lax.axis_size("lat")
    var_count = lax.axis_size("var")
    lat_place = lax.axis_index("lat")
    ext_rows = band_rows + WH
    ext_cols = band_cols + WW
    extended = padded(patches, (("lat", 0),), half_rows, False)
    extended = padded(extended, (("var", 1),), half_cols, True)
    normed_ext = layer_norm(extended, norm_gain)
    keyval = jnp.dot(
        normed_ext.reshape(-1, width), input_proj[:, width:], preferred_element_type=jnp.float32
    )
    keyval = keyval.astype(jnp.bfloat16).reshape(ext_rows, ext_cols, 2 * width)
    normed = normed_ext[half_rows : half_rows + band_rows, half_cols : half_cols + band_cols]
    queries = jnp.dot(
        normed.reshape(-1, width), input_proj[:, :width], preferred_element_type=jnp.float32
    )
    queries = queries.astype(jnp.bfloat16).reshape(band_rows, band_cols, width)
    query_ext = jnp.pad(queries, ((half_rows, WH - half_rows), (half_cols, WW - half_cols), (0, 0)))
    global_row = lat_place * band_rows - half_rows + jnp.arange(ext_rows, dtype=jnp.int32)
    row_valid = (global_row >= 0) & (global_row < lat_count * band_rows)
    mixed = window_attention(query_ext, keyval, row_valid, HEADS)
    attn = mixed[half_rows : half_rows + band_rows, half_cols : half_cols + band_cols].astype(
        jnp.bfloat16
    )
    update = jnp.dot(
        attn.reshape(-1, width), output_proj, preferred_element_type=jnp.float32
    ).reshape(band_rows, band_cols, width)
    latent = (patches.astype(jnp.float32) + update).astype(jnp.bfloat16)
    dataset_row = tile_dataset[0]
    dataset_ids = jnp.arange(level_counts.shape[0], dtype=jnp.int32)
    tile_levels = jnp.sum(
        jnp.where(dataset_row[:, None] == dataset_ids[None, :], level_counts[None, :], 0), axis=1
    )
    live_tiles = (slot_level[None, :] < tile_levels[:, None]).astype(jnp.float32)
    heads_full = lax.all_gather(head_weight, "lat", axis=1, tiled=True)
    tile_ids = jnp.arange(var_count, dtype=jnp.int32)
    tiles = peer_gather(latent.reshape(band_rows * band_cols, width), "var", var_count, 1)
    piece = (
        tiles.reshape(var_count, band_rows, band_cols, width)
        .transpose(1, 0, 2, 3)
        .reshape(band_rows, var_count * band_cols, width)
    )
    piece_cols = piece.shape[1]
    column_tile = jnp.arange(piece_cols, dtype=jnp.int32) // band_cols
    onehot = (column_tile[:, None] == tile_ids[None, :]).astype(jnp.float32)
    column_live = jnp.dot(onehot, live_tiles)
    piece_grad, head_add = slot_terms(
        piece, targets, column_live.T, level_scale, level_shift, heads_full
    )
    latent_terms = piece_grad
    latent_terms, head_terms = (latent_terms, head_add)
    latent_parts = (
        latent_terms.astype(jnp.bfloat16)
        .reshape(band_rows, var_count, band_cols, width)
        .transpose(1, 0, 2, 3)
        .reshape(var_count, band_rows * band_cols, width)
    )
    grad_latent = peer_reduce_scatter(
        latent_parts, "var", var_count, 2, jnp.bfloat16
    ).reshape(band_rows, band_cols, width)
    head_terms = head_terms * (1.0 / math.sqrt(lat_count * band_rows * var_count * band_cols))
    share_rows = width // lat_count
    slots, outs = head_terms.shape[1], head_terms.shape[2]
    head_parts = head_terms.astype(jnp.bfloat16).reshape(lat_count, share_rows * slots, outs)
    mine = peer_reduce_scatter(head_parts, "lat", lat_count, 3, jnp.float32)
    grad_head = jnp.transpose(mine.reshape(share_rows, slots, outs), (1, 0, 2))
    return (latent, grad_latent, grad_head)


def solution(mesh):
    in_specs = (
        P("lat", "var", None),
        P(),
        P(),
        P(),
        P("var", None),
        P("var", None),
        P("var", "lat", None),
        P("var", "lat", None, None),
        P(),
        P("lat", None),
        P("var"),
    )
    out_specs = (P("lat", "var", None), P("lat", "var", None), P("var", "lat", None))
    return jax.shard_map(local, mesh=mesh, in_specs=in_specs, out_specs=out_specs, check_vma=False)
```

```python
import math

import jax
import jax.numpy as jnp
from jax import lax
from jax.experimental import pallas as pl
from jax.experimental.pallas import tpu as pltpu
from jax.sharding import PartitionSpec as P

MESH_ID = pl.DeviceIdType.MESH


def _greet(axis, n, me):
    barrier = pltpu.get_barrier_semaphore()
    for k in range(1, n):
        pl.semaphore_signal(barrier, inc=1, device_id={axis: lax.rem(me + k, n)},
                            device_id_type=MESH_ID)
    pl.semaphore_wait(barrier, n - 1)


def peer_gather(block, axis, n, cid):
    def kernel(x_ref, out_ref, send_sem, recv_sem):
        me = lax.axis_index(axis)
        _greet(axis, n, me)
        sends = []
        for k in range(1, n):
            copy = pltpu.make_async_remote_copy(
                src_ref=x_ref, dst_ref=out_ref.at[me], send_sem=send_sem.at[k],
                recv_sem=recv_sem.at[me], device_id={axis: lax.rem(me + k, n)},
                device_id_type=MESH_ID)
            copy.start()
            sends.append(copy)
        out_ref[me] = x_ref[...]
        for k in range(1, n):
            src = lax.rem(me + n - k, n)
            pltpu.make_async_remote_copy(
                src_ref=x_ref, dst_ref=out_ref.at[src], send_sem=send_sem.at[k],
                recv_sem=recv_sem.at[src], device_id={axis: src},
                device_id_type=MESH_ID).wait_recv()
        for copy in sends:
            copy.wait_send()

    return pl.pallas_call(
        kernel,
        out_shape=jax.ShapeDtypeStruct((n,) + block.shape, block.dtype),
        in_specs=[pl.BlockSpec(memory_space=pltpu.VMEM)],
        out_specs=pl.BlockSpec(memory_space=pltpu.VMEM),
        scratch_shapes=[pltpu.SemaphoreType.DMA((n,)), pltpu.SemaphoreType.DMA((n,))],
        compiler_params=pltpu.CompilerParams(collective_id=cid, has_side_effects=True),
    )(block)


def peer_reduce_scatter(parts, axis, n, cid, out_dtype):
    def kernel(x_ref, out_ref, held, send_sem, recv_sem):
        me = lax.axis_index(axis)
        _greet(axis, n, me)
        sends = []
        for k in range(1, n):
            dst = lax.rem(me + k, n)
            copy = pltpu.make_async_remote_copy(
                src_ref=x_ref.at[dst], dst_ref=held.at[me], send_sem=send_sem.at[k],
                recv_sem=recv_sem.at[me], device_id={axis: dst},
                device_id_type=MESH_ID)
            copy.start()
            sends.append(copy)
        total = x_ref[me].astype(jnp.float32)
        for k in range(1, n):
            src = lax.rem(me + n - k, n)
            pltpu.make_async_remote_copy(
                src_ref=x_ref.at[src], dst_ref=held.at[src], send_sem=send_sem.at[k],
                recv_sem=recv_sem.at[src], device_id={axis: src},
                device_id_type=MESH_ID).wait_recv()
            total = total + held[src].astype(jnp.float32)
        out_ref[...] = total.astype(out_ref.dtype)
        for copy in sends:
            copy.wait_send()

    return pl.pallas_call(
        kernel,
        out_shape=jax.ShapeDtypeStruct(parts.shape[1:], out_dtype),
        in_specs=[pl.BlockSpec(memory_space=pltpu.VMEM)],
        out_specs=pl.BlockSpec(memory_space=pltpu.VMEM),
        scratch_shapes=[pltpu.VMEM(parts.shape, parts.dtype),
                        pltpu.SemaphoreType.DMA((n,)), pltpu.SemaphoreType.DMA((n,))],
        compiler_params=pltpu.CompilerParams(collective_id=cid, has_side_effects=True),
    )(parts)

HEADS = 16
WH = 6
WW = 12


EPS = 1e-05


def padded(array, sides, width, wrap):
    for axis, dim in sides:
        size, length = (lax.axis_size(axis), array.shape[dim])
        up = [(i, (i + 1) % size) for i in range(size if wrap else size - 1)]
        down = [(j, i) for i, j in up]
        last = lax.slice_in_dim(array, length - width, length, axis=dim)
        initial = lax.slice_in_dim(array, 0, width, axis=dim)
        before = lax.ppermute(last, axis, up)
        after = lax.ppermute(initial, axis, down)
        array = jnp.concatenate([before, array, after], axis=dim)
    return array


def layer_norm(values, gain):
    wide = values.astype(jnp.float32)
    average = jnp.mean(wide, axis=-1, keepdims=True)
    centred = wide - average
    variance = jnp.mean(centred * centred, axis=-1, keepdims=True)
    return (centred * lax.rsqrt(variance + EPS) * gain).astype(jnp.bfloat16)


def window_attention(query_ext, keyval, row_valid, heads):
    ext_rows, ext_cols, width = query_ext.shape
    head_size = width // heads
    win_rows = ext_rows // WH
    win_cols = ext_cols // WW

    def split(values, parts):
        shaped = values.reshape(win_rows, WH, win_cols, WW, parts, heads, head_size)
        return shaped.transpose(0, 2, 1, 3, 4, 5, 6).reshape(
            win_rows * win_cols, WH * WW, parts, heads, head_size
        )

    query_win = split(query_ext, 1)[:, :, 0]
    pairs = split(keyval, 2)
    key_win = pairs[:, :, 0]
    value_win = pairs[:, :, 1]
    key_mask = jnp.broadcast_to(
        row_valid.reshape(win_rows, 1, WH, 1), (win_rows, win_cols, WH, WW)
    ).reshape(win_rows * win_cols, WH * WW)
    scores = jnp.einsum(
        "wqhd,wkhd->whqk", query_win, key_win, preferred_element_type=jnp.float32
    ) / math.sqrt(head_size)
    scores = jnp.where(key_mask[:, None, None, :], scores, -jnp.inf)
    peak = jnp.max(scores, axis=-1, keepdims=True)
    weights = jnp.exp(scores - peak)
    probs = (weights / jnp.sum(weights, axis=-1, keepdims=True)).astype(jnp.bfloat16)
    mixed = jnp.einsum("whqk,wkhd->wqhd", probs, value_win, preferred_element_type=jnp.float32)
    return (
        mixed.reshape(win_rows, win_cols, WH, WW, width)
        .transpose(0, 2, 1, 3, 4)
        .reshape(ext_rows, ext_cols, width)
    )


def slot_terms(piece, target_rows, live_cols, level_scale, level_shift, heads_full):
    piece_wide = piece.astype(jnp.float32)
    rows = (
        piece_wide[None] * level_scale[:, None, None, :] + level_shift[:, None, None, :]
    ).astype(jnp.bfloat16)
    predicted = jnp.einsum("krnd,kdo->krno", rows, heads_full, preferred_element_type=jnp.float32)
    errors = ((predicted - target_rows.astype(jnp.float32)) * live_cols[:, None, :, None]).astype(
        jnp.bfloat16
    )
    back_grad = jnp.einsum("krno,kdo->krnd", errors, heads_full, preferred_element_type=jnp.float32)
    piece_grad = jnp.sum(back_grad * level_scale[:, None, None, :], axis=0)
    head_add = jnp.einsum("krnd,krno->dko", rows, errors, preferred_element_type=jnp.float32)
    return (piece_grad, head_add)


def local(
    patches,
    norm_gain,
    input_proj,
    output_proj,
    level_scale,
    level_shift,
    head_weight,
    targets,
    level_counts,
    tile_dataset,
    slot_level,
):
    band_rows, band_cols, width = patches.shape
    half_rows = WH // 2
    half_cols = WW // 2
    lat_count = lax.axis_size("lat")
    var_count = lax.axis_size("var")
    lat_place = lax.axis_index("lat")
    ext_rows = band_rows + WH
    ext_cols = band_cols + WW
    extended = padded(patches, (("lat", 0),), half_rows, False)
    extended = padded(extended, (("var", 1),), half_cols, True)
    normed_ext = layer_norm(extended, norm_gain)
    keyval = jnp.dot(
        normed_ext.reshape(-1, width), input_proj[:, width:], preferred_element_type=jnp.float32
    )
    keyval = keyval.astype(jnp.bfloat16).reshape(ext_rows, ext_cols, 2 * width)
    normed = normed_ext[half_rows : half_rows + band_rows, half_cols : half_cols + band_cols]
    queries = jnp.dot(
        normed.reshape(-1, width), input_proj[:, :width], preferred_element_type=jnp.float32
    )
    queries = queries.astype(jnp.bfloat16).reshape(band_rows, band_cols, width)
    query_ext = jnp.pad(queries, ((half_rows, WH - half_rows), (half_cols, WW - half_cols), (0, 0)))
    global_row = lat_place * band_rows - half_rows + jnp.arange(ext_rows, dtype=jnp.int32)
    row_valid = (global_row >= 0) & (global_row < lat_count * band_rows)
    mixed = window_attention(query_ext, keyval, row_valid, HEADS)
    attn = mixed[half_rows : half_rows + band_rows, half_cols : half_cols + band_cols].astype(
        jnp.bfloat16
    )
    update = jnp.dot(
        attn.reshape(-1, width), output_proj, preferred_element_type=jnp.float32
    ).reshape(band_rows, band_cols, width)
    latent = (patches.astype(jnp.float32) + update).astype(jnp.bfloat16)
    dataset_row = tile_dataset[0]
    dataset_ids = jnp.arange(level_counts.shape[0], dtype=jnp.int32)
    tile_levels = jnp.sum(
        jnp.where(dataset_row[:, None] == dataset_ids[None, :], level_counts[None, :], 0), axis=1
    )
    live_tiles = (slot_level[None, :] < tile_levels[:, None]).astype(jnp.float32)
    heads_full = lax.all_gather(head_weight, "lat", axis=1, tiled=True)
    tile_ids = jnp.arange(var_count, dtype=jnp.int32)
    tiles = peer_gather(latent.reshape(band_rows * band_cols, width), "var", var_count, 1)
    piece = (
        tiles.reshape(var_count, band_rows, band_cols, width)
        .transpose(1, 0, 2, 3)
        .reshape(band_rows, var_count * band_cols, width)
    )
    piece_cols = piece.shape[1]
    column_tile = jnp.arange(piece_cols, dtype=jnp.int32) // band_cols
    onehot = (column_tile[:, None] == tile_ids[None, :]).astype(jnp.float32)
    column_live = jnp.dot(onehot, live_tiles)
    piece_grad, head_add = slot_terms(
        piece, targets, column_live.T, level_scale, level_shift, heads_full
    )
    latent_terms = piece_grad
    latent_terms, head_terms = (latent_terms, head_add)
    latent_parts = (
        latent_terms.astype(jnp.bfloat16)
        .reshape(band_rows, var_count, band_cols, width)
        .transpose(1, 0, 2, 3)
        .reshape(var_count, band_rows * band_cols, width)
    )
    grad_latent = peer_reduce_scatter(
        latent_parts, "var", var_count, 2, jnp.bfloat16
    ).reshape(band_rows, band_cols, width)
    head_terms = head_terms * (1.0 / math.sqrt(lat_count * band_rows * var_count * band_cols))
    share_rows = width // lat_count
    mine = lax.psum_scatter(
        head_terms.astype(jnp.bfloat16), "lat", scatter_dimension=0, tiled=True
    ).astype(jnp.float32)
    grad_head = jnp.transpose(mine, (1, 0, 2))
    return (latent, grad_latent, grad_head)


def solution(mesh):
    in_specs = (
        P("lat", "var", None),
        P(),
        P(),
        P(),
        P("var", None),
        P("var", None),
        P("var", "lat", None),
        P("var", "lat", None, None),
        P(),
        P("lat", None),
        P("var"),
    )
    out_specs = (P("lat", "var", None), P("lat", "var", None), P("var", "lat", None))
    return jax.shard_map(local, mesh=mesh, in_specs=in_specs, out_specs=out_specs, check_vma=False)
```

```python
import math

import jax
import jax.numpy as jnp
from jax import lax
from jax.experimental import pallas as pl
from jax.experimental.pallas import tpu as pltpu
from jax.sharding import Mesh, PartitionSpec as P

MESH_ID = pl.DeviceIdType.MESH
LAT = ("lat_hi", "lat_lo")


def _greet(axis, n, me):
    barrier = pltpu.get_barrier_semaphore()
    for k in range(1, n):
        pl.semaphore_signal(barrier, inc=1, device_id={axis: lax.rem(me + k, n)},
                            device_id_type=MESH_ID)
    pl.semaphore_wait(barrier, n - 1)


def peer_gather(block, axis, n, cid):
    def kernel(x_ref, out_ref, send_sem, recv_sem):
        me = lax.axis_index(axis)
        _greet(axis, n, me)
        sends = []
        for k in range(1, n):
            copy = pltpu.make_async_remote_copy(
                src_ref=x_ref, dst_ref=out_ref.at[me], send_sem=send_sem.at[k],
                recv_sem=recv_sem.at[me], device_id={axis: lax.rem(me + k, n)},
                device_id_type=MESH_ID)
            copy.start()
            sends.append(copy)
        out_ref[me] = x_ref[...]
        for k in range(1, n):
            src = lax.rem(me + n - k, n)
            pltpu.make_async_remote_copy(
                src_ref=x_ref, dst_ref=out_ref.at[src], send_sem=send_sem.at[k],
                recv_sem=recv_sem.at[src], device_id={axis: src},
                device_id_type=MESH_ID).wait_recv()
        for copy in sends:
            copy.wait_send()

    return pl.pallas_call(
        kernel,
        out_shape=jax.ShapeDtypeStruct((n,) + block.shape, block.dtype),
        in_specs=[pl.BlockSpec(memory_space=pltpu.VMEM)],
        out_specs=pl.BlockSpec(memory_space=pltpu.VMEM),
        scratch_shapes=[pltpu.SemaphoreType.DMA((n,)), pltpu.SemaphoreType.DMA((n,))],
        compiler_params=pltpu.CompilerParams(collective_id=cid, has_side_effects=True),
    )(block)


def peer_reduce_scatter(parts, axis, n, cid, out_dtype):
    def kernel(x_ref, out_ref, held, send_sem, recv_sem):
        me = lax.axis_index(axis)
        _greet(axis, n, me)
        sends = []
        for k in range(1, n):
            dst = lax.rem(me + k, n)
            copy = pltpu.make_async_remote_copy(
                src_ref=x_ref.at[dst], dst_ref=held.at[me], send_sem=send_sem.at[k],
                recv_sem=recv_sem.at[me], device_id={axis: dst},
                device_id_type=MESH_ID)
            copy.start()
            sends.append(copy)
        total = x_ref[me].astype(jnp.float32)
        for k in range(1, n):
            src = lax.rem(me + n - k, n)
            pltpu.make_async_remote_copy(
                src_ref=x_ref.at[src], dst_ref=held.at[src], send_sem=send_sem.at[k],
                recv_sem=recv_sem.at[src], device_id={axis: src},
                device_id_type=MESH_ID).wait_recv()
            total = total + held[src].astype(jnp.float32)
        out_ref[...] = total.astype(out_ref.dtype)
        for copy in sends:
            copy.wait_send()

    return pl.pallas_call(
        kernel,
        out_shape=jax.ShapeDtypeStruct(parts.shape[1:], out_dtype),
        in_specs=[pl.BlockSpec(memory_space=pltpu.VMEM)],
        out_specs=pl.BlockSpec(memory_space=pltpu.VMEM),
        scratch_shapes=[pltpu.VMEM(parts.shape, parts.dtype),
                        pltpu.SemaphoreType.DMA((n,)), pltpu.SemaphoreType.DMA((n,))],
        compiler_params=pltpu.CompilerParams(collective_id=cid, has_side_effects=True),
    )(parts)

HEADS = 16
WH = 6
WW = 12


EPS = 1e-05


def padded(array, sides, width, wrap):
    for axis, dim in sides:
        size, length = (lax.axis_size(axis), array.shape[dim])
        up = [(i, (i + 1) % size) for i in range(size if wrap else size - 1)]
        down = [(j, i) for i, j in up]
        last = lax.slice_in_dim(array, length - width, length, axis=dim)
        initial = lax.slice_in_dim(array, 0, width, axis=dim)
        before = lax.ppermute(last, axis, up)
        after = lax.ppermute(initial, axis, down)
        array = jnp.concatenate([before, array, after], axis=dim)
    return array


def layer_norm(values, gain):
    wide = values.astype(jnp.float32)
    average = jnp.mean(wide, axis=-1, keepdims=True)
    centred = wide - average
    variance = jnp.mean(centred * centred, axis=-1, keepdims=True)
    return (centred * lax.rsqrt(variance + EPS) * gain).astype(jnp.bfloat16)


def window_attention(query_ext, keyval, row_valid, heads):
    ext_rows, ext_cols, width = query_ext.shape
    head_size = width // heads
    win_rows = ext_rows // WH
    win_cols = ext_cols // WW

    def split(values, parts):
        shaped = values.reshape(win_rows, WH, win_cols, WW, parts, heads, head_size)
        return shaped.transpose(0, 2, 1, 3, 4, 5, 6).reshape(
            win_rows * win_cols, WH * WW, parts, heads, head_size
        )

    query_win = split(query_ext, 1)[:, :, 0]
    pairs = split(keyval, 2)
    key_win = pairs[:, :, 0]
    value_win = pairs[:, :, 1]
    key_mask = jnp.broadcast_to(
        row_valid.reshape(win_rows, 1, WH, 1), (win_rows, win_cols, WH, WW)
    ).reshape(win_rows * win_cols, WH * WW)
    scores = jnp.einsum(
        "wqhd,wkhd->whqk", query_win, key_win, preferred_element_type=jnp.float32
    ) / math.sqrt(head_size)
    scores = jnp.where(key_mask[:, None, None, :], scores, -jnp.inf)
    peak = jnp.max(scores, axis=-1, keepdims=True)
    weights = jnp.exp(scores - peak)
    probs = (weights / jnp.sum(weights, axis=-1, keepdims=True)).astype(jnp.bfloat16)
    mixed = jnp.einsum("whqk,wkhd->wqhd", probs, value_win, preferred_element_type=jnp.float32)
    return (
        mixed.reshape(win_rows, win_cols, WH, WW, width)
        .transpose(0, 2, 1, 3, 4)
        .reshape(ext_rows, ext_cols, width)
    )


def slot_terms(piece, target_rows, live_cols, level_scale, level_shift, heads_full):
    piece_wide = piece.astype(jnp.float32)
    rows = (
        piece_wide[None] * level_scale[:, None, None, :] + level_shift[:, None, None, :]
    ).astype(jnp.bfloat16)
    predicted = jnp.einsum("krnd,kdo->krno", rows, heads_full, preferred_element_type=jnp.float32)
    errors = ((predicted - target_rows.astype(jnp.float32)) * live_cols[:, None, :, None]).astype(
        jnp.bfloat16
    )
    back_grad = jnp.einsum("krno,kdo->krnd", errors, heads_full, preferred_element_type=jnp.float32)
    piece_grad = jnp.sum(back_grad * level_scale[:, None, None, :], axis=0)
    head_add = jnp.einsum("krnd,krno->dko", rows, errors, preferred_element_type=jnp.float32)
    return (piece_grad, head_add)


def local(
    patches,
    norm_gain,
    input_proj,
    output_proj,
    level_scale,
    level_shift,
    head_weight,
    targets,
    level_counts,
    tile_dataset,
    slot_level,
):
    band_rows, band_cols, width = patches.shape
    half_rows = WH // 2
    half_cols = WW // 2
    lat_count = lax.axis_size(LAT)
    var_count = lax.axis_size("var")
    lat_place = lax.axis_index(LAT)
    ext_rows = band_rows + WH
    ext_cols = band_cols + WW
    extended = padded(patches, ((LAT, 0),), half_rows, False)
    extended = padded(extended, (("var", 1),), half_cols, True)
    normed_ext = layer_norm(extended, norm_gain)
    keyval = jnp.dot(
        normed_ext.reshape(-1, width), input_proj[:, width:], preferred_element_type=jnp.float32
    )
    keyval = keyval.astype(jnp.bfloat16).reshape(ext_rows, ext_cols, 2 * width)
    normed = normed_ext[half_rows : half_rows + band_rows, half_cols : half_cols + band_cols]
    queries = jnp.dot(
        normed.reshape(-1, width), input_proj[:, :width], preferred_element_type=jnp.float32
    )
    queries = queries.astype(jnp.bfloat16).reshape(band_rows, band_cols, width)
    query_ext = jnp.pad(queries, ((half_rows, WH - half_rows), (half_cols, WW - half_cols), (0, 0)))
    global_row = lat_place * band_rows - half_rows + jnp.arange(ext_rows, dtype=jnp.int32)
    row_valid = (global_row >= 0) & (global_row < lat_count * band_rows)
    mixed = window_attention(query_ext, keyval, row_valid, HEADS)
    attn = mixed[half_rows : half_rows + band_rows, half_cols : half_cols + band_cols].astype(
        jnp.bfloat16
    )
    update = jnp.dot(
        attn.reshape(-1, width), output_proj, preferred_element_type=jnp.float32
    ).reshape(band_rows, band_cols, width)
    latent = (patches.astype(jnp.float32) + update).astype(jnp.bfloat16)
    dataset_row = tile_dataset[0]
    dataset_ids = jnp.arange(level_counts.shape[0], dtype=jnp.int32)
    tile_levels = jnp.sum(
        jnp.where(dataset_row[:, None] == dataset_ids[None, :], level_counts[None, :], 0), axis=1
    )
    live_tiles = (slot_level[None, :] < tile_levels[:, None]).astype(jnp.float32)
    heads_full = lax.all_gather(head_weight, LAT, axis=1, tiled=True)
    tile_ids = jnp.arange(var_count, dtype=jnp.int32)
    tiles = peer_gather(latent.reshape(band_rows * band_cols, width), "var", var_count, 1)
    piece = (
        tiles.reshape(var_count, band_rows, band_cols, width)
        .transpose(1, 0, 2, 3)
        .reshape(band_rows, var_count * band_cols, width)
    )
    piece_cols = piece.shape[1]
    column_tile = jnp.arange(piece_cols, dtype=jnp.int32) // band_cols
    onehot = (column_tile[:, None] == tile_ids[None, :]).astype(jnp.float32)
    column_live = jnp.dot(onehot, live_tiles)
    piece_grad, head_add = slot_terms(
        piece, targets, column_live.T, level_scale, level_shift, heads_full
    )
    latent_terms = piece_grad
    latent_terms, head_terms = (latent_terms, head_add)
    latent_parts = (
        latent_terms.astype(jnp.bfloat16)
        .reshape(band_rows, var_count, band_cols, width)
        .transpose(1, 0, 2, 3)
        .reshape(var_count, band_rows * band_cols, width)
    )
    grad_latent = peer_reduce_scatter(
        latent_parts, "var", var_count, 2, jnp.bfloat16
    ).reshape(band_rows, band_cols, width)
    head_terms = head_terms * (1.0 / math.sqrt(lat_count * band_rows * var_count * band_cols))
    share_rows = width // lat_count
    outer, inner = lax.axis_size(LAT[0]), lax.axis_size(LAT[1])
    slots, outs = head_terms.shape[1], head_terms.shape[2]
    head_grid = (
        head_terms.astype(jnp.bfloat16)
        .reshape(outer, inner, share_rows * slots, outs)
        .transpose(1, 0, 2, 3)
        .reshape(inner * outer * share_rows * slots, outs)
    )
    head_grid = lax.psum_scatter(head_grid, LAT[1], scatter_dimension=0, tiled=True)
    head_grid = lax.psum_scatter(head_grid, LAT[0], scatter_dimension=0, tiled=True)
    mine = head_grid.reshape(share_rows, slots, outs).astype(jnp.float32)
    grad_head = jnp.transpose(mine, (1, 0, 2))
    return (latent, grad_latent, grad_head)


def solution(mesh):
    in_specs = (
        P(LAT, "var", None),
        P(),
        P(),
        P(),
        P("var", None),
        P("var", None),
        P("var", LAT, None),
        P("var", LAT, None, None),
        P(),
        P(LAT, None),
        P("var"),
    )
    out_specs = (P(LAT, "var", None), P(LAT, "var", None), P("var", LAT, None))
    lat_size = mesh.shape["lat"]
    inner = 4 if lat_size % 4 == 0 else 1
    grid = Mesh(
        mesh.devices.reshape(lat_size // inner, inner, mesh.shape["var"]), LAT + ("var",)
    )
    return jax.shard_map(local, mesh=grid, in_specs=in_specs, out_specs=out_specs, check_vma=False)
```

```python
import math

import jax
import jax.numpy as jnp
from jax import lax
from jax.experimental import pallas as pl
from jax.experimental.pallas import tpu as pltpu
from jax.sharding import PartitionSpec as P

MESH_ID = pl.DeviceIdType.MESH


def _greet(axis, n, me):
    barrier = pltpu.get_barrier_semaphore()
    for k in range(1, n):
        pl.semaphore_signal(barrier, inc=1, device_id={axis: lax.rem(me + k, n)},
                            device_id_type=MESH_ID)
    pl.semaphore_wait(barrier, n - 1)


def peer_gather(block, axis, n, cid):
    def kernel(x_ref, out_ref, send_sem, recv_sem):
        me = lax.axis_index(axis)
        _greet(axis, n, me)
        sends = []
        for k in range(1, n):
            copy = pltpu.make_async_remote_copy(
                src_ref=x_ref, dst_ref=out_ref.at[me], send_sem=send_sem.at[k],
                recv_sem=recv_sem.at[me], device_id={axis: lax.rem(me + k, n)},
                device_id_type=MESH_ID)
            copy.start()
            sends.append(copy)
        out_ref[me] = x_ref[...]
        for k in range(1, n):
            src = lax.rem(me + n - k, n)
            pltpu.make_async_remote_copy(
                src_ref=x_ref, dst_ref=out_ref.at[src], send_sem=send_sem.at[k],
                recv_sem=recv_sem.at[src], device_id={axis: src},
                device_id_type=MESH_ID).wait_recv()
        for copy in sends:
            copy.wait_send()

    return pl.pallas_call(
        kernel,
        out_shape=jax.ShapeDtypeStruct((n,) + block.shape, block.dtype),
        in_specs=[pl.BlockSpec(memory_space=pltpu.VMEM)],
        out_specs=pl.BlockSpec(memory_space=pltpu.VMEM),
        scratch_shapes=[pltpu.SemaphoreType.DMA((n,)), pltpu.SemaphoreType.DMA((n,))],
        compiler_params=pltpu.CompilerParams(collective_id=cid, has_side_effects=True),
    )(block)


def peer_reduce_scatter(parts, axis, n, cid, out_dtype):
    def kernel(x_ref, out_ref, held, send_sem, recv_sem):
        me = lax.axis_index(axis)
        _greet(axis, n, me)
        sends = []
        for k in range(1, n):
            dst = lax.rem(me + k, n)
            copy = pltpu.make_async_remote_copy(
                src_ref=x_ref.at[dst], dst_ref=held.at[me], send_sem=send_sem.at[k],
                recv_sem=recv_sem.at[me], device_id={axis: dst},
                device_id_type=MESH_ID)
            copy.start()
            sends.append(copy)
        total = x_ref[me].astype(jnp.float32)
        for k in range(1, n):
            src = lax.rem(me + n - k, n)
            pltpu.make_async_remote_copy(
                src_ref=x_ref.at[src], dst_ref=held.at[src], send_sem=send_sem.at[k],
                recv_sem=recv_sem.at[src], device_id={axis: src},
                device_id_type=MESH_ID).wait_recv()
            total = total + held[src].astype(jnp.float32)
        out_ref[...] = total.astype(out_ref.dtype)
        for copy in sends:
            copy.wait_send()

    return pl.pallas_call(
        kernel,
        out_shape=jax.ShapeDtypeStruct(parts.shape[1:], out_dtype),
        in_specs=[pl.BlockSpec(memory_space=pltpu.VMEM)],
        out_specs=pl.BlockSpec(memory_space=pltpu.VMEM),
        scratch_shapes=[pltpu.VMEM(parts.shape, parts.dtype),
                        pltpu.SemaphoreType.DMA((n,)), pltpu.SemaphoreType.DMA((n,))],
        compiler_params=pltpu.CompilerParams(collective_id=cid, has_side_effects=True),
    )(parts)


def masked_window_attention(queries, keyval, query_win, key_win, heads):
    nq, width = queries.shape
    head_size = width // heads
    scale = 1.0 / float(head_size) ** 0.5

    def kernel(q_ref, kv_ref, qw_ref, kw_ref, out_ref):
        mask = qw_ref[...] == kw_ref[...]
        for h in range(heads):
            cols = slice(h * head_size, (h + 1) * head_size)
            q = q_ref[:, cols]
            k = kv_ref[:, h * head_size:(h + 1) * head_size]
            v = kv_ref[:, width + h * head_size:width + (h + 1) * head_size]
            s = lax.dot_general(q, k, (((1,), (1,)), ((), ())),
                                preferred_element_type=jnp.float32) * scale
            s = jnp.where(mask, s, -jnp.inf)
            w = jnp.exp(s - jnp.max(s, axis=1, keepdims=True))
            p = (w / jnp.sum(w, axis=1, keepdims=True)).astype(jnp.bfloat16)
            out_ref[:, cols] = jnp.dot(p, v, preferred_element_type=jnp.float32).astype(out_ref.dtype)

    return pl.pallas_call(
        kernel,
        out_shape=jax.ShapeDtypeStruct((nq, width), jnp.bfloat16),
        in_specs=[pl.BlockSpec(memory_space=pltpu.VMEM)] * 4,
        out_specs=pl.BlockSpec(memory_space=pltpu.VMEM),
    )(queries, keyval, query_win, key_win)

HEADS = 16
WH = 6
WW = 12


EPS = 1e-05


def padded(array, sides, width, wrap):
    for axis, dim in sides:
        size, length = (lax.axis_size(axis), array.shape[dim])
        up = [(i, (i + 1) % size) for i in range(size if wrap else size - 1)]
        down = [(j, i) for i, j in up]
        last = lax.slice_in_dim(array, length - width, length, axis=dim)
        initial = lax.slice_in_dim(array, 0, width, axis=dim)
        before = lax.ppermute(last, axis, up)
        after = lax.ppermute(initial, axis, down)
        array = jnp.concatenate([before, array, after], axis=dim)
    return array


def layer_norm(values, gain):
    wide = values.astype(jnp.float32)
    average = jnp.mean(wide, axis=-1, keepdims=True)
    centred = wide - average
    variance = jnp.mean(centred * centred, axis=-1, keepdims=True)
    return (centred * lax.rsqrt(variance + EPS) * gain).astype(jnp.bfloat16)


def window_attention(query_ext, keyval, row_valid, heads):
    ext_rows, ext_cols, width = query_ext.shape
    head_size = width // heads
    win_rows = ext_rows // WH
    win_cols = ext_cols // WW

    def split(values, parts):
        shaped = values.reshape(win_rows, WH, win_cols, WW, parts, heads, head_size)
        return shaped.transpose(0, 2, 1, 3, 4, 5, 6).reshape(
            win_rows * win_cols, WH * WW, parts, heads, head_size
        )

    query_win = split(query_ext, 1)[:, :, 0]
    pairs = split(keyval, 2)
    key_win = pairs[:, :, 0]
    value_win = pairs[:, :, 1]
    key_mask = jnp.broadcast_to(
        row_valid.reshape(win_rows, 1, WH, 1), (win_rows, win_cols, WH, WW)
    ).reshape(win_rows * win_cols, WH * WW)
    scores = jnp.einsum(
        "wqhd,wkhd->whqk", query_win, key_win, preferred_element_type=jnp.float32
    ) / math.sqrt(head_size)
    scores = jnp.where(key_mask[:, None, None, :], scores, -jnp.inf)
    peak = jnp.max(scores, axis=-1, keepdims=True)
    weights = jnp.exp(scores - peak)
    probs = (weights / jnp.sum(weights, axis=-1, keepdims=True)).astype(jnp.bfloat16)
    mixed = jnp.einsum("whqk,wkhd->wqhd", probs, value_win, preferred_element_type=jnp.float32)
    return (
        mixed.reshape(win_rows, win_cols, WH, WW, width)
        .transpose(0, 2, 1, 3, 4)
        .reshape(ext_rows, ext_cols, width)
    )


def slot_terms(piece, target_rows, live_cols, level_scale, level_shift, heads_full):
    piece_wide = piece.astype(jnp.float32)
    rows = (
        piece_wide[None] * level_scale[:, None, None, :] + level_shift[:, None, None, :]
    ).astype(jnp.bfloat16)
    predicted = jnp.einsum("krnd,kdo->krno", rows, heads_full, preferred_element_type=jnp.float32)
    errors = ((predicted - target_rows.astype(jnp.float32)) * live_cols[:, None, :, None]).astype(
        jnp.bfloat16
    )
    back_grad = jnp.einsum("krno,kdo->krnd", errors, heads_full, preferred_element_type=jnp.float32)
    piece_grad = jnp.sum(back_grad * level_scale[:, None, None, :], axis=0)
    head_add = jnp.einsum("krnd,krno->dko", rows, errors, preferred_element_type=jnp.float32)
    return (piece_grad, head_add)


def local(
    patches,
    norm_gain,
    input_proj,
    output_proj,
    level_scale,
    level_shift,
    head_weight,
    targets,
    level_counts,
    tile_dataset,
    slot_level,
):
    band_rows, band_cols, width = patches.shape
    half_rows = WH // 2
    half_cols = WW // 2
    lat_count = lax.axis_size("lat")
    var_count = lax.axis_size("var")
    lat_place = lax.axis_index("lat")
    ext_rows = band_rows + WH
    ext_cols = band_cols + WW
    extended = padded(patches, (("lat", 0),), half_rows, False)
    extended = padded(extended, (("var", 1),), half_cols, True)
    normed_ext = layer_norm(extended, norm_gain)
    keyval = jnp.dot(
        normed_ext.reshape(-1, width), input_proj[:, width:], preferred_element_type=jnp.float32
    )
    keyval = keyval.astype(jnp.bfloat16).reshape(ext_rows, ext_cols, 2 * width)
    normed = normed_ext[half_rows : half_rows + band_rows, half_cols : half_cols + band_cols]
    queries = jnp.dot(
        normed.reshape(-1, width), input_proj[:, :width], preferred_element_type=jnp.float32
    )
    queries = queries.astype(jnp.bfloat16)
    global_row = lat_place * band_rows - half_rows + jnp.arange(ext_rows, dtype=jnp.int32)
    row_valid = (global_row >= 0) & (global_row < lat_count * band_rows)
    win_cols = ext_cols // WW
    ext_r = jnp.arange(ext_rows, dtype=jnp.int32)[:, None]
    ext_c = jnp.arange(ext_cols, dtype=jnp.int32)[None, :]
    key_win = jnp.where(row_valid[:, None], (ext_r // WH) * win_cols + ext_c // WW, -1)
    own_r = ext_r[half_rows : half_rows + band_rows]
    own_c = ext_c[:, half_cols : half_cols + band_cols]
    query_win = (own_r // WH) * win_cols + own_c // WW
    attn = masked_window_attention(
        queries,
        keyval.reshape(ext_rows * ext_cols, 2 * width),
        query_win.reshape(-1, 1),
        key_win.reshape(1, -1),
        HEADS,
    ).reshape(band_rows, band_cols, width)
    update = jnp.dot(
        attn.reshape(-1, width), output_proj, preferred_element_type=jnp.float32
    ).reshape(band_rows, band_cols, width)
    latent = (patches.astype(jnp.float32) + update).astype(jnp.bfloat16)
    dataset_row = tile_dataset[0]
    dataset_ids = jnp.arange(level_counts.shape[0], dtype=jnp.int32)
    tile_levels = jnp.sum(
        jnp.where(dataset_row[:, None] == dataset_ids[None, :], level_counts[None, :], 0), axis=1
    )
    live_tiles = (slot_level[None, :] < tile_levels[:, None]).astype(jnp.float32)
    heads_full = lax.all_gather(head_weight, "lat", axis=1, tiled=True)
    tile_ids = jnp.arange(var_count, dtype=jnp.int32)
    tiles = peer_gather(latent.reshape(band_rows * band_cols, width), "var", var_count, 1)
    piece = (
        tiles.reshape(var_count, band_rows, band_cols, width)
        .transpose(1, 0, 2, 3)
        .reshape(band_rows, var_count * band_cols, width)
    )
    piece_cols = piece.shape[1]
    column_tile = jnp.arange(piece_cols, dtype=jnp.int32) // band_cols
    onehot = (column_tile[:, None] == tile_ids[None, :]).astype(jnp.float32)
    column_live = jnp.dot(onehot, live_tiles)
    piece_grad, head_add = slot_terms(
        piece, targets, column_live.T, level_scale, level_shift, heads_full
    )
    latent_terms = piece_grad
    latent_terms, head_terms = (latent_terms, head_add)
    latent_parts = (
        latent_terms.astype(jnp.bfloat16)
        .reshape(band_rows, var_count, band_cols, width)
        .transpose(1, 0, 2, 3)
        .reshape(var_count, band_rows * band_cols, width)
    )
    grad_latent = peer_reduce_scatter(
        latent_parts, "var", var_count, 2, jnp.bfloat16
    ).reshape(band_rows, band_cols, width)
    head_terms = head_terms * (1.0 / math.sqrt(lat_count * band_rows * var_count * band_cols))
    share_rows = width // lat_count
    mine = lax.psum_scatter(
        head_terms.astype(jnp.bfloat16), "lat", scatter_dimension=0, tiled=True
    ).astype(jnp.float32)
    grad_head = jnp.transpose(mine, (1, 0, 2))
    return (latent, grad_latent, grad_head)


def solution(mesh):
    in_specs = (
        P("lat", "var", None),
        P(),
        P(),
        P(),
        P("var", None),
        P("var", None),
        P("var", "lat", None),
        P("var", "lat", None, None),
        P(),
        P("lat", None),
        P("var"),
    )
    out_specs = (P("lat", "var", None), P("lat", "var", None), P("var", "lat", None))
    return jax.shard_map(local, mesh=mesh, in_specs=in_specs, out_specs=out_specs, check_vma=False)
```

```python
import math

import jax
import jax.numpy as jnp
from jax import lax
from jax.experimental import pallas as pl
from jax.experimental.pallas import tpu as pltpu
from jax.sharding import PartitionSpec as P

MESH_ID = pl.DeviceIdType.MESH


def _greet(axis, n, me):
    barrier = pltpu.get_barrier_semaphore()
    for k in range(1, n):
        pl.semaphore_signal(barrier, inc=1, device_id={axis: lax.rem(me + k, n)},
                            device_id_type=MESH_ID)
    pl.semaphore_wait(barrier, n - 1)


def peer_gather(block, axis, n, cid):
    def kernel(x_ref, out_ref, send_sem, recv_sem):
        me = lax.axis_index(axis)
        _greet(axis, n, me)
        sends = []
        for k in range(1, n):
            copy = pltpu.make_async_remote_copy(
                src_ref=x_ref, dst_ref=out_ref.at[me], send_sem=send_sem.at[k],
                recv_sem=recv_sem.at[me], device_id={axis: lax.rem(me + k, n)},
                device_id_type=MESH_ID)
            copy.start()
            sends.append(copy)
        out_ref[me] = x_ref[...]
        for k in range(1, n):
            src = lax.rem(me + n - k, n)
            pltpu.make_async_remote_copy(
                src_ref=x_ref, dst_ref=out_ref.at[src], send_sem=send_sem.at[k],
                recv_sem=recv_sem.at[src], device_id={axis: src},
                device_id_type=MESH_ID).wait_recv()
        for copy in sends:
            copy.wait_send()

    return pl.pallas_call(
        kernel,
        out_shape=jax.ShapeDtypeStruct((n,) + block.shape, block.dtype),
        in_specs=[pl.BlockSpec(memory_space=pltpu.VMEM)],
        out_specs=pl.BlockSpec(memory_space=pltpu.VMEM),
        scratch_shapes=[pltpu.SemaphoreType.DMA((n,)), pltpu.SemaphoreType.DMA((n,))],
        compiler_params=pltpu.CompilerParams(collective_id=cid, has_side_effects=True),
    )(block)


def peer_reduce_scatter(parts, axis, n, cid, out_dtype):
    def kernel(x_ref, out_ref, held, send_sem, recv_sem):
        me = lax.axis_index(axis)
        _greet(axis, n, me)
        sends = []
        for k in range(1, n):
            dst = lax.rem(me + k, n)
            copy = pltpu.make_async_remote_copy(
                src_ref=x_ref.at[dst], dst_ref=held.at[me], send_sem=send_sem.at[k],
                recv_sem=recv_sem.at[me], device_id={axis: dst},
                device_id_type=MESH_ID)
            copy.start()
            sends.append(copy)
        total = x_ref[me].astype(jnp.float32)
        for k in range(1, n):
            src = lax.rem(me + n - k, n)
            pltpu.make_async_remote_copy(
                src_ref=x_ref.at[src], dst_ref=held.at[src], send_sem=send_sem.at[k],
                recv_sem=recv_sem.at[src], device_id={axis: src},
                device_id_type=MESH_ID).wait_recv()
            total = total + held[src].astype(jnp.float32)
        out_ref[...] = total.astype(out_ref.dtype)
        for copy in sends:
            copy.wait_send()

    return pl.pallas_call(
        kernel,
        out_shape=jax.ShapeDtypeStruct(parts.shape[1:], out_dtype),
        in_specs=[pl.BlockSpec(memory_space=pltpu.VMEM)],
        out_specs=pl.BlockSpec(memory_space=pltpu.VMEM),
        scratch_shapes=[pltpu.VMEM(parts.shape, parts.dtype),
                        pltpu.SemaphoreType.DMA((n,)), pltpu.SemaphoreType.DMA((n,))],
        compiler_params=pltpu.CompilerParams(collective_id=cid, has_side_effects=True),
    )(parts)


def masked_window_attention(queries, keyval, query_win, key_win, heads):
    nq, width = queries.shape
    head_size = width // heads
    scale = 1.0 / float(head_size) ** 0.5

    def kernel(q_ref, kv_ref, qw_ref, kw_ref, out_ref):
        mask = qw_ref[...] == kw_ref[...]
        for h in range(heads):
            cols = slice(h * head_size, (h + 1) * head_size)
            q = q_ref[:, cols]
            k = kv_ref[:, h * head_size:(h + 1) * head_size]
            v = kv_ref[:, width + h * head_size:width + (h + 1) * head_size]
            s = lax.dot_general(q, k, (((1,), (1,)), ((), ())),
                                preferred_element_type=jnp.float32) * scale
            s = jnp.where(mask, s, -jnp.inf)
            w = jnp.exp(s - jnp.max(s, axis=1, keepdims=True))
            p = (w / jnp.sum(w, axis=1, keepdims=True)).astype(jnp.bfloat16)
            out_ref[:, cols] = jnp.dot(p, v, preferred_element_type=jnp.float32).astype(out_ref.dtype)

    return pl.pallas_call(
        kernel,
        out_shape=jax.ShapeDtypeStruct((nq, width), jnp.bfloat16),
        in_specs=[pl.BlockSpec(memory_space=pltpu.VMEM)] * 4,
        out_specs=pl.BlockSpec(memory_space=pltpu.VMEM),
    )(queries, keyval, query_win, key_win)


def chip_pair_gather(block, axis, n, cid):
    nz = n // 2

    def kernel(x_ref, out_ref, send_sem, recv_sem):
        me = lax.axis_index(axis)
        partner = me + 1 - 2 * lax.rem(me, 2)
        peers = [lax.rem(me + 2 * k, n) for k in range(1, nz)]
        barrier = pltpu.get_barrier_semaphore()
        for dev in peers + [partner]:
            pl.semaphore_signal(barrier, inc=1, device_id={axis: dev}, device_id_type=MESH_ID)
        pl.semaphore_wait(barrier, nz)

        def send(src_ref, slot, dev, index):
            copy = pltpu.make_async_remote_copy(
                src_ref=src_ref, dst_ref=out_ref.at[slot], send_sem=send_sem.at[index],
                recv_sem=recv_sem.at[slot], device_id={axis: dev}, device_id_type=MESH_ID)
            copy.start()
            return copy

        def arrive(slot):
            pltpu.make_async_remote_copy(
                src_ref=x_ref, dst_ref=out_ref.at[slot], send_sem=send_sem.at[0],
                recv_sem=recv_sem.at[slot], device_id={axis: slot},
                device_id_type=MESH_ID).wait_recv()

        sends = [send(x_ref, me, dev, i) for i, dev in enumerate(peers)]
        sends.append(send(x_ref, me, partner, nz - 1))
        out_ref[me] = x_ref[...]
        for k in range(1, nz):
            src = lax.rem(me + n - 2 * k, n)
            arrive(src)
            sends.append(send(out_ref.at[src], src, partner, nz - 1 + k))
        for k in range(nz):
            arrive(lax.rem(partner + 2 * k, n))
        for copy in sends:
            copy.wait_send()

    return pl.pallas_call(
        kernel,
        out_shape=jax.ShapeDtypeStruct((n,) + block.shape, block.dtype),
        in_specs=[pl.BlockSpec(memory_space=pltpu.VMEM)],
        out_specs=pl.BlockSpec(memory_space=pltpu.VMEM),
        scratch_shapes=[pltpu.SemaphoreType.DMA((n,)), pltpu.SemaphoreType.DMA((n,))],
        compiler_params=pltpu.CompilerParams(collective_id=cid, has_side_effects=True),
    )(block)

HEADS = 16
WH = 6
WW = 12


EPS = 1e-05


def padded(array, sides, width, wrap):
    for axis, dim in sides:
        size, length = (lax.axis_size(axis), array.shape[dim])
        up = [(i, (i + 1) % size) for i in range(size if wrap else size - 1)]
        down = [(j, i) for i, j in up]
        last = lax.slice_in_dim(array, length - width, length, axis=dim)
        initial = lax.slice_in_dim(array, 0, width, axis=dim)
        before = lax.ppermute(last, axis, up)
        after = lax.ppermute(initial, axis, down)
        array = jnp.concatenate([before, array, after], axis=dim)
    return array


def layer_norm(values, gain):
    wide = values.astype(jnp.float32)
    average = jnp.mean(wide, axis=-1, keepdims=True)
    centred = wide - average
    variance = jnp.mean(centred * centred, axis=-1, keepdims=True)
    return (centred * lax.rsqrt(variance + EPS) * gain).astype(jnp.bfloat16)


def window_attention(query_ext, keyval, row_valid, heads):
    ext_rows, ext_cols, width = query_ext.shape
    head_size = width // heads
    win_rows = ext_rows // WH
    win_cols = ext_cols // WW

    def split(values, parts):
        shaped = values.reshape(win_rows, WH, win_cols, WW, parts, heads, head_size)
        return shaped.transpose(0, 2, 1, 3, 4, 5, 6).reshape(
            win_rows * win_cols, WH * WW, parts, heads, head_size
        )

    query_win = split(query_ext, 1)[:, :, 0]
    pairs = split(keyval, 2)
    key_win = pairs[:, :, 0]
    value_win = pairs[:, :, 1]
    key_mask = jnp.broadcast_to(
        row_valid.reshape(win_rows, 1, WH, 1), (win_rows, win_cols, WH, WW)
    ).reshape(win_rows * win_cols, WH * WW)
    scores = jnp.einsum(
        "wqhd,wkhd->whqk", query_win, key_win, preferred_element_type=jnp.float32
    ) / math.sqrt(head_size)
    scores = jnp.where(key_mask[:, None, None, :], scores, -jnp.inf)
    peak = jnp.max(scores, axis=-1, keepdims=True)
    weights = jnp.exp(scores - peak)
    probs = (weights / jnp.sum(weights, axis=-1, keepdims=True)).astype(jnp.bfloat16)
    mixed = jnp.einsum("whqk,wkhd->wqhd", probs, value_win, preferred_element_type=jnp.float32)
    return (
        mixed.reshape(win_rows, win_cols, WH, WW, width)
        .transpose(0, 2, 1, 3, 4)
        .reshape(ext_rows, ext_cols, width)
    )


def slot_terms(piece, target_rows, live_cols, level_scale, level_shift, heads_full):
    piece_wide = piece.astype(jnp.float32)
    rows = (
        piece_wide[None] * level_scale[:, None, None, :] + level_shift[:, None, None, :]
    ).astype(jnp.bfloat16)
    predicted = jnp.einsum("krnd,kdo->krno", rows, heads_full, preferred_element_type=jnp.float32)
    errors = ((predicted - target_rows.astype(jnp.float32)) * live_cols[:, None, :, None]).astype(
        jnp.bfloat16
    )
    back_grad = jnp.einsum("krno,kdo->krnd", errors, heads_full, preferred_element_type=jnp.float32)
    piece_grad = jnp.sum(back_grad * level_scale[:, None, None, :], axis=0)
    head_add = jnp.einsum("krnd,krno->dko", rows, errors, preferred_element_type=jnp.float32)
    return (piece_grad, head_add)


def local(
    patches,
    norm_gain,
    input_proj,
    output_proj,
    level_scale,
    level_shift,
    head_weight,
    targets,
    level_counts,
    tile_dataset,
    slot_level,
):
    band_rows, band_cols, width = patches.shape
    half_rows = WH // 2
    half_cols = WW // 2
    lat_count = lax.axis_size("lat")
    var_count = lax.axis_size("var")
    lat_place = lax.axis_index("lat")
    ext_rows = band_rows + WH
    ext_cols = band_cols + WW
    extended = padded(patches, (("lat", 0),), half_rows, False)
    extended = padded(extended, (("var", 1),), half_cols, True)
    normed_ext = layer_norm(extended, norm_gain)
    keyval = jnp.dot(
        normed_ext.reshape(-1, width), input_proj[:, width:], preferred_element_type=jnp.float32
    )
    keyval = keyval.astype(jnp.bfloat16).reshape(ext_rows, ext_cols, 2 * width)
    normed = normed_ext[half_rows : half_rows + band_rows, half_cols : half_cols + band_cols]
    queries = jnp.dot(
        normed.reshape(-1, width), input_proj[:, :width], preferred_element_type=jnp.float32
    )
    queries = queries.astype(jnp.bfloat16)
    global_row = lat_place * band_rows - half_rows + jnp.arange(ext_rows, dtype=jnp.int32)
    row_valid = (global_row >= 0) & (global_row < lat_count * band_rows)
    win_cols = ext_cols // WW
    ext_r = jnp.arange(ext_rows, dtype=jnp.int32)[:, None]
    ext_c = jnp.arange(ext_cols, dtype=jnp.int32)[None, :]
    key_win = jnp.where(row_valid[:, None], (ext_r // WH) * win_cols + ext_c // WW, -1)
    own_r = ext_r[half_rows : half_rows + band_rows]
    own_c = ext_c[:, half_cols : half_cols + band_cols]
    query_win = (own_r // WH) * win_cols + own_c // WW
    attn = masked_window_attention(
        queries,
        keyval.reshape(ext_rows * ext_cols, 2 * width),
        query_win.reshape(-1, 1),
        key_win.reshape(1, -1),
        HEADS,
    ).reshape(band_rows, band_cols, width)
    update = jnp.dot(
        attn.reshape(-1, width), output_proj, preferred_element_type=jnp.float32
    ).reshape(band_rows, band_cols, width)
    latent = (patches.astype(jnp.float32) + update).astype(jnp.bfloat16)
    dataset_row = tile_dataset[0]
    dataset_ids = jnp.arange(level_counts.shape[0], dtype=jnp.int32)
    tile_levels = jnp.sum(
        jnp.where(dataset_row[:, None] == dataset_ids[None, :], level_counts[None, :], 0), axis=1
    )
    live_tiles = (slot_level[None, :] < tile_levels[:, None]).astype(jnp.float32)
    heads_full = lax.all_gather(head_weight, "lat", axis=1, tiled=True)
    tile_ids = jnp.arange(var_count, dtype=jnp.int32)
    tiles = chip_pair_gather(latent.reshape(band_rows * band_cols, width), "var", var_count, 1)
    piece = (
        tiles.reshape(var_count, band_rows, band_cols, width)
        .transpose(1, 0, 2, 3)
        .reshape(band_rows, var_count * band_cols, width)
    )
    piece_cols = piece.shape[1]
    column_tile = jnp.arange(piece_cols, dtype=jnp.int32) // band_cols
    onehot = (column_tile[:, None] == tile_ids[None, :]).astype(jnp.float32)
    column_live = jnp.dot(onehot, live_tiles)
    piece_grad, head_add = slot_terms(
        piece, targets, column_live.T, level_scale, level_shift, heads_full
    )
    latent_terms = piece_grad
    latent_terms, head_terms = (latent_terms, head_add)
    latent_parts = (
        latent_terms.astype(jnp.bfloat16)
        .reshape(band_rows, var_count, band_cols, width)
        .transpose(1, 0, 2, 3)
        .reshape(var_count, band_rows * band_cols, width)
    )
    grad_latent = peer_reduce_scatter(
        latent_parts, "var", var_count, 2, jnp.bfloat16
    ).reshape(band_rows, band_cols, width)
    head_terms = head_terms * (1.0 / math.sqrt(lat_count * band_rows * var_count * band_cols))
    share_rows = width // lat_count
    mine = lax.psum_scatter(
        head_terms.astype(jnp.bfloat16), "lat", scatter_dimension=0, tiled=True
    ).astype(jnp.float32)
    grad_head = jnp.transpose(mine, (1, 0, 2))
    return (latent, grad_latent, grad_head)


def solution(mesh):
    in_specs = (
        P("lat", "var", None),
        P(),
        P(),
        P(),
        P("var", None),
        P("var", None),
        P("var", "lat", None),
        P("var", "lat", None, None),
        P(),
        P("lat", None),
        P("var"),
    )
    out_specs = (P("lat", "var", None), P("lat", "var", None), P("var", "lat", None))
    return jax.shard_map(local, mesh=mesh, in_specs=in_specs, out_specs=out_specs, check_vma=False)
```

```python
import math

import jax
import jax.numpy as jnp
from jax import lax
from jax.experimental import pallas as pl
from jax.experimental.pallas import tpu as pltpu
from jax.sharding import PartitionSpec as P

MESH_ID = pl.DeviceIdType.MESH


def _greet(axis, n, me):
    barrier = pltpu.get_barrier_semaphore()
    for k in range(1, n):
        pl.semaphore_signal(barrier, inc=1, device_id={axis: lax.rem(me + k, n)},
                            device_id_type=MESH_ID)
    pl.semaphore_wait(barrier, n - 1)


def peer_gather(block, axis, n, cid):
    def kernel(x_ref, out_ref, send_sem, recv_sem):
        me = lax.axis_index(axis)
        _greet(axis, n, me)
        sends = []
        for k in range(1, n):
            copy = pltpu.make_async_remote_copy(
                src_ref=x_ref, dst_ref=out_ref.at[me], send_sem=send_sem.at[k],
                recv_sem=recv_sem.at[me], device_id={axis: lax.rem(me + k, n)},
                device_id_type=MESH_ID)
            copy.start()
            sends.append(copy)
        out_ref[me] = x_ref[...]
        for k in range(1, n):
            src = lax.rem(me + n - k, n)
            pltpu.make_async_remote_copy(
                src_ref=x_ref, dst_ref=out_ref.at[src], send_sem=send_sem.at[k],
                recv_sem=recv_sem.at[src], device_id={axis: src},
                device_id_type=MESH_ID).wait_recv()
        for copy in sends:
            copy.wait_send()

    return pl.pallas_call(
        kernel,
        out_shape=jax.ShapeDtypeStruct((n,) + block.shape, block.dtype),
        in_specs=[pl.BlockSpec(memory_space=pltpu.VMEM)],
        out_specs=pl.BlockSpec(memory_space=pltpu.VMEM),
        scratch_shapes=[pltpu.SemaphoreType.DMA((n,)), pltpu.SemaphoreType.DMA((n,))],
        compiler_params=pltpu.CompilerParams(collective_id=cid, has_side_effects=True),
    )(block)


def peer_reduce_scatter(parts, axis, n, cid, out_dtype):
    def kernel(x_ref, out_ref, held, send_sem, recv_sem):
        me = lax.axis_index(axis)
        _greet(axis, n, me)
        sends = []
        for k in range(1, n):
            dst = lax.rem(me + k, n)
            copy = pltpu.make_async_remote_copy(
                src_ref=x_ref.at[dst], dst_ref=held.at[me], send_sem=send_sem.at[k],
                recv_sem=recv_sem.at[me], device_id={axis: dst},
                device_id_type=MESH_ID)
            copy.start()
            sends.append(copy)
        total = x_ref[me].astype(jnp.float32)
        for k in range(1, n):
            src = lax.rem(me + n - k, n)
            pltpu.make_async_remote_copy(
                src_ref=x_ref.at[src], dst_ref=held.at[src], send_sem=send_sem.at[k],
                recv_sem=recv_sem.at[src], device_id={axis: src},
                device_id_type=MESH_ID).wait_recv()
            total = total + held[src].astype(jnp.float32)
        out_ref[...] = total.astype(out_ref.dtype)
        for copy in sends:
            copy.wait_send()

    return pl.pallas_call(
        kernel,
        out_shape=jax.ShapeDtypeStruct(parts.shape[1:], out_dtype),
        in_specs=[pl.BlockSpec(memory_space=pltpu.VMEM)],
        out_specs=pl.BlockSpec(memory_space=pltpu.VMEM),
        scratch_shapes=[pltpu.VMEM(parts.shape, parts.dtype),
                        pltpu.SemaphoreType.DMA((n,)), pltpu.SemaphoreType.DMA((n,))],
        compiler_params=pltpu.CompilerParams(collective_id=cid, has_side_effects=True),
    )(parts)


def masked_window_attention(queries, keyval, query_win, key_win, heads):
    nq, width = queries.shape
    head_size = width // heads
    scale = 1.0 / float(head_size) ** 0.5

    def kernel(q_ref, kv_ref, qw_ref, kw_ref, out_ref):
        mask = qw_ref[...] == kw_ref[...]
        for h in range(heads):
            cols = slice(h * head_size, (h + 1) * head_size)
            q = q_ref[:, cols]
            k = kv_ref[:, h * head_size:(h + 1) * head_size]
            v = kv_ref[:, width + h * head_size:width + (h + 1) * head_size]
            s = lax.dot_general(q, k, (((1,), (1,)), ((), ())),
                                preferred_element_type=jnp.float32) * scale
            s = jnp.where(mask, s, -jnp.inf)
            w = jnp.exp(s - jnp.max(s, axis=1, keepdims=True))
            p = (w / jnp.sum(w, axis=1, keepdims=True)).astype(jnp.bfloat16)
            out_ref[:, cols] = jnp.dot(p, v, preferred_element_type=jnp.float32).astype(out_ref.dtype)

    return pl.pallas_call(
        kernel,
        out_shape=jax.ShapeDtypeStruct((nq, width), jnp.bfloat16),
        in_specs=[pl.BlockSpec(memory_space=pltpu.VMEM)] * 4,
        out_specs=pl.BlockSpec(memory_space=pltpu.VMEM),
    )(queries, keyval, query_win, key_win)


def chip_pair_gather(block, axis, n, cid):
    nz = n // 2

    def kernel(x_ref, out_ref, send_sem, recv_sem):
        me = lax.axis_index(axis)
        partner = me + 1 - 2 * lax.rem(me, 2)
        peers = [lax.rem(me + 2 * k, n) for k in range(1, nz)]
        barrier = pltpu.get_barrier_semaphore()
        for dev in peers + [partner]:
            pl.semaphore_signal(barrier, inc=1, device_id={axis: dev}, device_id_type=MESH_ID)
        pl.semaphore_wait(barrier, nz)

        def send(src_ref, slot, dev, index):
            copy = pltpu.make_async_remote_copy(
                src_ref=src_ref, dst_ref=out_ref.at[slot], send_sem=send_sem.at[index],
                recv_sem=recv_sem.at[slot], device_id={axis: dev}, device_id_type=MESH_ID)
            copy.start()
            return copy

        def arrive(slot):
            pltpu.make_async_remote_copy(
                src_ref=x_ref, dst_ref=out_ref.at[slot], send_sem=send_sem.at[0],
                recv_sem=recv_sem.at[slot], device_id={axis: slot},
                device_id_type=MESH_ID).wait_recv()

        sends = [send(x_ref, me, dev, i) for i, dev in enumerate(peers)]
        sends.append(send(x_ref, me, partner, nz - 1))
        out_ref[me] = x_ref[...]
        for k in range(1, nz):
            src = lax.rem(me + n - 2 * k, n)
            arrive(src)
            sends.append(send(out_ref.at[src], src, partner, nz - 1 + k))
        for k in range(nz):
            arrive(lax.rem(partner + 2 * k, n))
        for copy in sends:
            copy.wait_send()

    return pl.pallas_call(
        kernel,
        out_shape=jax.ShapeDtypeStruct((n,) + block.shape, block.dtype),
        in_specs=[pl.BlockSpec(memory_space=pltpu.VMEM)],
        out_specs=pl.BlockSpec(memory_space=pltpu.VMEM),
        scratch_shapes=[pltpu.SemaphoreType.DMA((n,)), pltpu.SemaphoreType.DMA((n,))],
        compiler_params=pltpu.CompilerParams(collective_id=cid, has_side_effects=True),
    )(block)

HEADS = 16
WH = 6
WW = 12


EPS = 1e-05


def padded(array, sides, width, wrap):
    for axis, dim in sides:
        size, length = (lax.axis_size(axis), array.shape[dim])
        up = [(i, (i + 1) % size) for i in range(size if wrap else size - 1)]
        down = [(j, i) for i, j in up]
        last = lax.slice_in_dim(array, length - width, length, axis=dim)
        initial = lax.slice_in_dim(array, 0, width, axis=dim)
        before = lax.ppermute(last, axis, up)
        after = lax.ppermute(initial, axis, down)
        array = jnp.concatenate([before, array, after], axis=dim)
    return array


def layer_norm(values, gain):
    wide = values.astype(jnp.float32)
    average = jnp.mean(wide, axis=-1, keepdims=True)
    centred = wide - average
    variance = jnp.mean(centred * centred, axis=-1, keepdims=True)
    return (centred * lax.rsqrt(variance + EPS) * gain).astype(jnp.bfloat16)


def window_attention(query_ext, keyval, row_valid, heads):
    ext_rows, ext_cols, width = query_ext.shape
    head_size = width // heads
    win_rows = ext_rows // WH
    win_cols = ext_cols // WW

    def split(values, parts):
        shaped = values.reshape(win_rows, WH, win_cols, WW, parts, heads, head_size)
        return shaped.transpose(0, 2, 1, 3, 4, 5, 6).reshape(
            win_rows * win_cols, WH * WW, parts, heads, head_size
        )

    query_win = split(query_ext, 1)[:, :, 0]
    pairs = split(keyval, 2)
    key_win = pairs[:, :, 0]
    value_win = pairs[:, :, 1]
    key_mask = jnp.broadcast_to(
        row_valid.reshape(win_rows, 1, WH, 1), (win_rows, win_cols, WH, WW)
    ).reshape(win_rows * win_cols, WH * WW)
    scores = jnp.einsum(
        "wqhd,wkhd->whqk", query_win, key_win, preferred_element_type=jnp.float32
    ) / math.sqrt(head_size)
    scores = jnp.where(key_mask[:, None, None, :], scores, -jnp.inf)
    peak = jnp.max(scores, axis=-1, keepdims=True)
    weights = jnp.exp(scores - peak)
    probs = (weights / jnp.sum(weights, axis=-1, keepdims=True)).astype(jnp.bfloat16)
    mixed = jnp.einsum("whqk,wkhd->wqhd", probs, value_win, preferred_element_type=jnp.float32)
    return (
        mixed.reshape(win_rows, win_cols, WH, WW, width)
        .transpose(0, 2, 1, 3, 4)
        .reshape(ext_rows, ext_cols, width)
    )


def slot_terms(piece, target_rows, live_cols, level_scale, level_shift, heads_full):
    piece_wide = piece.astype(jnp.float32)
    rows = (
        piece_wide[None] * level_scale[:, None, None, :] + level_shift[:, None, None, :]
    ).astype(jnp.bfloat16)
    predicted = jnp.einsum("krnd,kdo->krno", rows, heads_full, preferred_element_type=jnp.float32)
    errors = ((predicted - target_rows.astype(jnp.float32)) * live_cols[:, None, :, None]).astype(
        jnp.bfloat16
    )
    back_grad = jnp.einsum("krno,kdo->krnd", errors, heads_full, preferred_element_type=jnp.float32)
    piece_grad = jnp.sum(back_grad * level_scale[:, None, None, :], axis=0)
    head_add = jnp.einsum("krnd,krno->dko", rows, errors, preferred_element_type=jnp.float32)
    return (piece_grad, head_add)


def local(
    patches,
    norm_gain,
    input_proj,
    output_proj,
    level_scale,
    level_shift,
    head_weight,
    targets,
    level_counts,
    tile_dataset,
    slot_level,
):
    band_rows, band_cols, width = patches.shape
    half_rows = WH // 2
    half_cols = WW // 2
    lat_count = lax.axis_size("lat")
    var_count = lax.axis_size("var")
    lat_place = lax.axis_index("lat")
    ext_rows = band_rows + WH
    ext_cols = band_cols + WW
    extended = padded(patches, (("lat", 0),), half_rows, False)
    extended = padded(extended, (("var", 1),), half_cols, True)
    normed_ext = layer_norm(extended, norm_gain)
    keyval = jnp.dot(
        normed_ext.reshape(-1, width), input_proj[:, width:], preferred_element_type=jnp.float32
    )
    keyval = keyval.astype(jnp.bfloat16).reshape(ext_rows, ext_cols, 2 * width)
    normed = normed_ext[half_rows : half_rows + band_rows, half_cols : half_cols + band_cols]
    queries = jnp.dot(
        normed.reshape(-1, width), input_proj[:, :width], preferred_element_type=jnp.float32
    )
    queries = queries.astype(jnp.bfloat16)
    global_row = lat_place * band_rows - half_rows + jnp.arange(ext_rows, dtype=jnp.int32)
    row_valid = (global_row >= 0) & (global_row < lat_count * band_rows)
    win_cols = ext_cols // WW
    ext_r = jnp.arange(ext_rows, dtype=jnp.int32)[:, None]
    ext_c = jnp.arange(ext_cols, dtype=jnp.int32)[None, :]
    key_win = jnp.where(row_valid[:, None], (ext_r // WH) * win_cols + ext_c // WW, -1)
    own_r = ext_r[half_rows : half_rows + band_rows]
    own_c = ext_c[:, half_cols : half_cols + band_cols]
    query_win = (own_r // WH) * win_cols + own_c // WW
    attn = masked_window_attention(
        queries,
        keyval.reshape(ext_rows * ext_cols, 2 * width),
        query_win.reshape(-1, 1),
        key_win.reshape(1, -1),
        HEADS,
    ).reshape(band_rows, band_cols, width)
    update = jnp.dot(
        attn.reshape(-1, width), output_proj, preferred_element_type=jnp.float32
    ).reshape(band_rows, band_cols, width)
    latent = (patches.astype(jnp.float32) + update).astype(jnp.bfloat16)
    dataset_row = tile_dataset[0]
    dataset_ids = jnp.arange(level_counts.shape[0], dtype=jnp.int32)
    tile_levels = jnp.sum(
        jnp.where(dataset_row[:, None] == dataset_ids[None, :], level_counts[None, :], 0), axis=1
    )
    live_tiles = (slot_level[None, :] < tile_levels[:, None]).astype(jnp.float32)
    heads_full = lax.all_gather(head_weight, "lat", axis=1, tiled=True)
    tile_ids = jnp.arange(var_count, dtype=jnp.int32)
    tiles = chip_pair_gather(latent.reshape(band_rows * band_cols, width), "var", var_count, 1)
    piece = (
        tiles.reshape(var_count, band_rows, band_cols, width)
        .transpose(1, 0, 2, 3)
        .reshape(band_rows, var_count * band_cols, width)
    )
    piece_cols = piece.shape[1]
    column_tile = jnp.arange(piece_cols, dtype=jnp.int32) // band_cols
    onehot = (column_tile[:, None] == tile_ids[None, :]).astype(jnp.float32)
    column_live = jnp.dot(onehot, live_tiles)
    piece_grad, head_add = slot_terms(
        piece, targets, column_live.T, level_scale, level_shift, heads_full
    )
    latent_terms = piece_grad
    latent_terms, head_terms = (latent_terms, head_add)
    latent_parts = (
        latent_terms.astype(jnp.bfloat16)
        .reshape(band_rows, var_count, band_cols, width)
        .transpose(1, 0, 2, 3)
        .reshape(var_count, band_rows * band_cols, width)
    )
    grad_latent = peer_reduce_scatter(
        latent_parts, "var", var_count, 2, jnp.bfloat16
    ).reshape(band_rows, band_cols, width)
    head_terms = head_terms * (1.0 / math.sqrt(lat_count * band_rows * var_count * band_cols))
    share_rows = width // lat_count
    slots, outs = head_terms.shape[1], head_terms.shape[2]
    lanes = 128
    dense = head_terms.astype(jnp.bfloat16).reshape(width * slots * outs // lanes, lanes)
    mine = lax.psum_scatter(dense, "lat", scatter_dimension=0, tiled=True).astype(jnp.float32)
    grad_head = jnp.transpose(mine.reshape(share_rows, slots, outs), (1, 0, 2))
    return (latent, grad_latent, grad_head)


def solution(mesh):
    in_specs = (
        P("lat", "var", None),
        P(),
        P(),
        P(),
        P("var", None),
        P("var", None),
        P("var", "lat", None),
        P("var", "lat", None, None),
        P(),
        P("lat", None),
        P("var"),
    )
    out_specs = (P("lat", "var", None), P("lat", "var", None), P("var", "lat", None))
    return jax.shard_map(local, mesh=mesh, in_specs=in_specs, out_specs=out_specs, check_vma=False)
```

```python
import math

import jax
import jax.numpy as jnp
from jax import lax
from jax.experimental import pallas as pl
from jax.experimental.pallas import tpu as pltpu
from jax.sharding import Mesh, PartitionSpec as P

MESH_ID = pl.DeviceIdType.MESH
LAT = ("lat_hi", "lat_lo")


def _greet(axis, n, me):
    barrier = pltpu.get_barrier_semaphore()
    for k in range(1, n):
        pl.semaphore_signal(barrier, inc=1, device_id={axis: lax.rem(me + k, n)},
                            device_id_type=MESH_ID)
    pl.semaphore_wait(barrier, n - 1)


def peer_gather(block, axis, n, cid):
    def kernel(x_ref, out_ref, send_sem, recv_sem):
        me = lax.axis_index(axis)
        _greet(axis, n, me)
        sends = []
        for k in range(1, n):
            copy = pltpu.make_async_remote_copy(
                src_ref=x_ref, dst_ref=out_ref.at[me], send_sem=send_sem.at[k],
                recv_sem=recv_sem.at[me], device_id={axis: lax.rem(me + k, n)},
                device_id_type=MESH_ID)
            copy.start()
            sends.append(copy)
        out_ref[me] = x_ref[...]
        for k in range(1, n):
            src = lax.rem(me + n - k, n)
            pltpu.make_async_remote_copy(
                src_ref=x_ref, dst_ref=out_ref.at[src], send_sem=send_sem.at[k],
                recv_sem=recv_sem.at[src], device_id={axis: src},
                device_id_type=MESH_ID).wait_recv()
        for copy in sends:
            copy.wait_send()

    return pl.pallas_call(
        kernel,
        out_shape=jax.ShapeDtypeStruct((n,) + block.shape, block.dtype),
        in_specs=[pl.BlockSpec(memory_space=pltpu.VMEM)],
        out_specs=pl.BlockSpec(memory_space=pltpu.VMEM),
        scratch_shapes=[pltpu.SemaphoreType.DMA((n,)), pltpu.SemaphoreType.DMA((n,))],
        compiler_params=pltpu.CompilerParams(collective_id=cid, has_side_effects=True),
    )(block)


def peer_reduce_scatter(parts, axis, n, cid, out_dtype):
    def kernel(x_ref, out_ref, held, send_sem, recv_sem):
        me = lax.axis_index(axis)
        _greet(axis, n, me)
        sends = []
        for k in range(1, n):
            dst = lax.rem(me + k, n)
            copy = pltpu.make_async_remote_copy(
                src_ref=x_ref.at[dst], dst_ref=held.at[me], send_sem=send_sem.at[k],
                recv_sem=recv_sem.at[me], device_id={axis: dst},
                device_id_type=MESH_ID)
            copy.start()
            sends.append(copy)
        total = x_ref[me].astype(jnp.float32)
        for k in range(1, n):
            src = lax.rem(me + n - k, n)
            pltpu.make_async_remote_copy(
                src_ref=x_ref.at[src], dst_ref=held.at[src], send_sem=send_sem.at[k],
                recv_sem=recv_sem.at[src], device_id={axis: src},
                device_id_type=MESH_ID).wait_recv()
            total = total + held[src].astype(jnp.float32)
        out_ref[...] = total.astype(out_ref.dtype)
        for copy in sends:
            copy.wait_send()

    return pl.pallas_call(
        kernel,
        out_shape=jax.ShapeDtypeStruct(parts.shape[1:], out_dtype),
        in_specs=[pl.BlockSpec(memory_space=pltpu.VMEM)],
        out_specs=pl.BlockSpec(memory_space=pltpu.VMEM),
        scratch_shapes=[pltpu.VMEM(parts.shape, parts.dtype),
                        pltpu.SemaphoreType.DMA((n,)), pltpu.SemaphoreType.DMA((n,))],
        compiler_params=pltpu.CompilerParams(collective_id=cid, has_side_effects=True),
    )(parts)


def masked_window_attention(queries, keyval, query_win, key_win, heads):
    nq, width = queries.shape
    head_size = width // heads
    scale = 1.0 / float(head_size) ** 0.5

    def kernel(q_ref, kv_ref, qw_ref, kw_ref, out_ref):
        mask = qw_ref[...] == kw_ref[...]
        for h in range(heads):
            cols = slice(h * head_size, (h + 1) * head_size)
            q = q_ref[:, cols]
            k = kv_ref[:, h * head_size:(h + 1) * head_size]
            v = kv_ref[:, width + h * head_size:width + (h + 1) * head_size]
            s = lax.dot_general(q, k, (((1,), (1,)), ((), ())),
                                preferred_element_type=jnp.float32) * scale
            s = jnp.where(mask, s, -jnp.inf)
            w = jnp.exp(s - jnp.max(s, axis=1, keepdims=True))
            p = (w / jnp.sum(w, axis=1, keepdims=True)).astype(jnp.bfloat16)
            out_ref[:, cols] = jnp.dot(p, v, preferred_element_type=jnp.float32).astype(out_ref.dtype)

    return pl.pallas_call(
        kernel,
        out_shape=jax.ShapeDtypeStruct((nq, width), jnp.bfloat16),
        in_specs=[pl.BlockSpec(memory_space=pltpu.VMEM)] * 4,
        out_specs=pl.BlockSpec(memory_space=pltpu.VMEM),
    )(queries, keyval, query_win, key_win)


def chip_pair_gather(block, axis, n, cid):
    nz = n // 2

    def kernel(x_ref, out_ref, send_sem, recv_sem):
        me = lax.axis_index(axis)
        partner = me + 1 - 2 * lax.rem(me, 2)
        peers = [lax.rem(me + 2 * k, n) for k in range(1, nz)]
        barrier = pltpu.get_barrier_semaphore()
        for dev in peers + [partner]:
            pl.semaphore_signal(barrier, inc=1, device_id={axis: dev}, device_id_type=MESH_ID)
        pl.semaphore_wait(barrier, nz)

        def send(src_ref, slot, dev, index):
            copy = pltpu.make_async_remote_copy(
                src_ref=src_ref, dst_ref=out_ref.at[slot], send_sem=send_sem.at[index],
                recv_sem=recv_sem.at[slot], device_id={axis: dev}, device_id_type=MESH_ID)
            copy.start()
            return copy

        def arrive(slot):
            pltpu.make_async_remote_copy(
                src_ref=x_ref, dst_ref=out_ref.at[slot], send_sem=send_sem.at[0],
                recv_sem=recv_sem.at[slot], device_id={axis: slot},
                device_id_type=MESH_ID).wait_recv()

        sends = [send(x_ref, me, dev, i) for i, dev in enumerate(peers)]
        sends.append(send(x_ref, me, partner, nz - 1))
        out_ref[me] = x_ref[...]
        for k in range(1, nz):
            src = lax.rem(me + n - 2 * k, n)
            arrive(src)
            sends.append(send(out_ref.at[src], src, partner, nz - 1 + k))
        for k in range(nz):
            arrive(lax.rem(partner + 2 * k, n))
        for copy in sends:
            copy.wait_send()

    return pl.pallas_call(
        kernel,
        out_shape=jax.ShapeDtypeStruct((n,) + block.shape, block.dtype),
        in_specs=[pl.BlockSpec(memory_space=pltpu.VMEM)],
        out_specs=pl.BlockSpec(memory_space=pltpu.VMEM),
        scratch_shapes=[pltpu.SemaphoreType.DMA((n,)), pltpu.SemaphoreType.DMA((n,))],
        compiler_params=pltpu.CompilerParams(collective_id=cid, has_side_effects=True),
    )(block)


def grid_reduce_scatter(parts, outer, inner, cid):
    slots, n_hi, n_lo, rows, outs = parts.shape
    half = rows // 2

    def kernel(x_ref, out_ref, r1a, r1b, s1a, s1b, r2a, r2b, send_sem, recv_sem):
        hi = lax.axis_index(outer)
        lo = lax.axis_index(inner)
        barrier = pltpu.get_barrier_semaphore()
        for k in range(1, n_lo):
            pl.semaphore_signal(barrier, inc=1, device_id={inner: lax.rem(lo + k, n_lo)},
                                device_id_type=MESH_ID)
        for k in range(1, n_hi):
            pl.semaphore_signal(barrier, inc=1, device_id={outer: lax.rem(hi + k, n_hi)},
                                device_id_type=MESH_ID)
        pl.semaphore_wait(barrier, n_lo + n_hi - 2)

        def send(src_ref, dst_ref, axis, dev, group, k, slot):
            copy = pltpu.make_async_remote_copy(
                src_ref=src_ref, dst_ref=dst_ref, send_sem=send_sem.at[group, k],
                recv_sem=recv_sem.at[group, slot], device_id={axis: dev},
                device_id_type=MESH_ID)
            copy.start()
            return copy

        def arrive(dst_ref, group, slot):
            pltpu.make_async_remote_copy(
                src_ref=dst_ref, dst_ref=dst_ref, send_sem=send_sem.at[group, 0],
                recv_sem=recv_sem.at[group, slot], device_id={inner: lo},
                device_id_type=MESH_ID).wait_recv()

        sends = []
        for k in range(1, n_lo):
            dev = lax.rem(lo + k, n_lo)
            sends.append(send(x_ref.at[:, :, dev, pl.ds(0, half), :], r1a.at[lo], inner, dev, 0, k, lo))
        for k in range(1, n_hi):
            dev = lax.rem(hi + k, n_hi)
            sends.append(send(x_ref.at[:, dev, :, pl.ds(half, half), :], r1b.at[hi], outer, dev, 1, k, hi))

        sources_lo = [lax.rem(lo + n_lo - k, n_lo) for k in range(1, n_lo)]
        sources_hi = [lax.rem(hi + n_hi - k, n_hi) for k in range(1, n_hi)]
        for src in sources_lo:
            arrive(r1a.at[src], 0, src)
        for h in range(n_hi):
            total = x_ref[:, h, lo, pl.ds(0, half), :].astype(jnp.float32)
            for src in sources_lo:
                total = total + r1a[src, :, h].astype(jnp.float32)
            s1a[h] = total.astype(s1a.dtype)
        for k in range(1, n_hi):
            dev = lax.rem(hi + k, n_hi)
            sends.append(send(s1a.at[dev], r2a.at[hi], outer, dev, 2, k, hi))
        for src in sources_hi:
            arrive(r1b.at[src], 1, src)
        for l in range(n_lo):
            total = x_ref[:, hi, l, pl.ds(half, half), :].astype(jnp.float32)
            for src in sources_hi:
                total = total + r1b[src, :, l].astype(jnp.float32)
            s1b[l] = total.astype(s1b.dtype)
        for k in range(1, n_lo):
            dev = lax.rem(lo + k, n_lo)
            sends.append(send(s1b.at[dev], r2b.at[lo], inner, dev, 3, k, lo))

        total = s1a[hi].astype(jnp.float32)
        for src in sources_hi:
            arrive(r2a.at[src], 2, src)
            total = total + r2a[src].astype(jnp.float32)
        out_ref[:, pl.ds(0, half), :] = total
        total = s1b[lo].astype(jnp.float32)
        for src in sources_lo:
            arrive(r2b.at[src], 3, src)
            total = total + r2b[src].astype(jnp.float32)
        out_ref[:, pl.ds(half, half), :] = total
        for copy in sends:
            copy.wait_send()

    most = max(n_hi, n_lo)
    return pl.pallas_call(
        kernel,
        out_shape=jax.ShapeDtypeStruct((slots, rows, outs), jnp.float32),
        in_specs=[pl.BlockSpec(memory_space=pltpu.VMEM)],
        out_specs=pl.BlockSpec(memory_space=pltpu.VMEM),
        scratch_shapes=[
            pltpu.VMEM((n_lo, slots, n_hi, half, outs), parts.dtype),
            pltpu.VMEM((n_hi, slots, n_lo, half, outs), parts.dtype),
            pltpu.VMEM((n_hi, slots, half, outs), parts.dtype),
            pltpu.VMEM((n_lo, slots, half, outs), parts.dtype),
            pltpu.VMEM((n_hi, slots, half, outs), parts.dtype),
            pltpu.VMEM((n_lo, slots, half, outs), parts.dtype),
            pltpu.SemaphoreType.DMA((4, most)),
            pltpu.SemaphoreType.DMA((4, most)),
        ],
        compiler_params=pltpu.CompilerParams(collective_id=cid, has_side_effects=True),
    )(parts)

HEADS = 16
WH = 6
WW = 12


EPS = 1e-05


def padded(array, sides, width, wrap):
    for axis, dim in sides:
        size, length = (lax.axis_size(axis), array.shape[dim])
        up = [(i, (i + 1) % size) for i in range(size if wrap else size - 1)]
        down = [(j, i) for i, j in up]
        last = lax.slice_in_dim(array, length - width, length, axis=dim)
        initial = lax.slice_in_dim(array, 0, width, axis=dim)
        before = lax.ppermute(last, axis, up)
        after = lax.ppermute(initial, axis, down)
        array = jnp.concatenate([before, array, after], axis=dim)
    return array


def layer_norm(values, gain):
    wide = values.astype(jnp.float32)
    average = jnp.mean(wide, axis=-1, keepdims=True)
    centred = wide - average
    variance = jnp.mean(centred * centred, axis=-1, keepdims=True)
    return (centred * lax.rsqrt(variance + EPS) * gain).astype(jnp.bfloat16)


def window_attention(query_ext, keyval, row_valid, heads):
    ext_rows, ext_cols, width = query_ext.shape
    head_size = width // heads
    win_rows = ext_rows // WH
    win_cols = ext_cols // WW

    def split(values, parts):
        shaped = values.reshape(win_rows, WH, win_cols, WW, parts, heads, head_size)
        return shaped.transpose(0, 2, 1, 3, 4, 5, 6).reshape(
            win_rows * win_cols, WH * WW, parts, heads, head_size
        )

    query_win = split(query_ext, 1)[:, :, 0]
    pairs = split(keyval, 2)
    key_win = pairs[:, :, 0]
    value_win = pairs[:, :, 1]
    key_mask = jnp.broadcast_to(
        row_valid.reshape(win_rows, 1, WH, 1), (win_rows, win_cols, WH, WW)
    ).reshape(win_rows * win_cols, WH * WW)
    scores = jnp.einsum(
        "wqhd,wkhd->whqk", query_win, key_win, preferred_element_type=jnp.float32
    ) / math.sqrt(head_size)
    scores = jnp.where(key_mask[:, None, None, :], scores, -jnp.inf)
    peak = jnp.max(scores, axis=-1, keepdims=True)
    weights = jnp.exp(scores - peak)
    probs = (weights / jnp.sum(weights, axis=-1, keepdims=True)).astype(jnp.bfloat16)
    mixed = jnp.einsum("whqk,wkhd->wqhd", probs, value_win, preferred_element_type=jnp.float32)
    return (
        mixed.reshape(win_rows, win_cols, WH, WW, width)
        .transpose(0, 2, 1, 3, 4)
        .reshape(ext_rows, ext_cols, width)
    )


def slot_terms(piece, target_rows, live_cols, level_scale, level_shift, heads_full):
    piece_wide = piece.astype(jnp.float32)
    rows = (
        piece_wide[None] * level_scale[:, None, None, :] + level_shift[:, None, None, :]
    ).astype(jnp.bfloat16)
    predicted = jnp.einsum("krnd,kdo->krno", rows, heads_full, preferred_element_type=jnp.float32)
    errors = ((predicted - target_rows.astype(jnp.float32)) * live_cols[:, None, :, None]).astype(
        jnp.bfloat16
    )
    back_grad = jnp.einsum("krno,kdo->krnd", errors, heads_full, preferred_element_type=jnp.float32)
    piece_grad = jnp.sum(back_grad * level_scale[:, None, None, :], axis=0)
    head_add = jnp.einsum("krnd,krno->kdo", rows, errors, preferred_element_type=jnp.float32)
    return (piece_grad, head_add)


def local(
    patches,
    norm_gain,
    input_proj,
    output_proj,
    level_scale,
    level_shift,
    head_weight,
    targets,
    level_counts,
    tile_dataset,
    slot_level,
):
    band_rows, band_cols, width = patches.shape
    half_rows = WH // 2
    half_cols = WW // 2
    lat_count = lax.axis_size(LAT)
    var_count = lax.axis_size("var")
    lat_place = lax.axis_index(LAT)
    ext_rows = band_rows + WH
    ext_cols = band_cols + WW
    extended = padded(patches, ((LAT, 0),), half_rows, False)
    extended = padded(extended, (("var", 1),), half_cols, True)
    normed_ext = layer_norm(extended, norm_gain)
    keyval = jnp.dot(
        normed_ext.reshape(-1, width), input_proj[:, width:], preferred_element_type=jnp.float32
    )
    keyval = keyval.astype(jnp.bfloat16).reshape(ext_rows, ext_cols, 2 * width)
    normed = normed_ext[half_rows : half_rows + band_rows, half_cols : half_cols + band_cols]
    queries = jnp.dot(
        normed.reshape(-1, width), input_proj[:, :width], preferred_element_type=jnp.float32
    )
    queries = queries.astype(jnp.bfloat16)
    global_row = lat_place * band_rows - half_rows + jnp.arange(ext_rows, dtype=jnp.int32)
    row_valid = (global_row >= 0) & (global_row < lat_count * band_rows)
    win_cols = ext_cols // WW
    ext_r = jnp.arange(ext_rows, dtype=jnp.int32)[:, None]
    ext_c = jnp.arange(ext_cols, dtype=jnp.int32)[None, :]
    key_win = jnp.where(row_valid[:, None], (ext_r // WH) * win_cols + ext_c // WW, -1)
    own_r = ext_r[half_rows : half_rows + band_rows]
    own_c = ext_c[:, half_cols : half_cols + band_cols]
    query_win = (own_r // WH) * win_cols + own_c // WW
    attn = masked_window_attention(
        queries,
        keyval.reshape(ext_rows * ext_cols, 2 * width),
        query_win.reshape(-1, 1),
        key_win.reshape(1, -1),
        HEADS,
    ).reshape(band_rows, band_cols, width)
    update = jnp.dot(
        attn.reshape(-1, width), output_proj, preferred_element_type=jnp.float32
    ).reshape(band_rows, band_cols, width)
    latent = (patches.astype(jnp.float32) + update).astype(jnp.bfloat16)
    dataset_row = tile_dataset[0]
    dataset_ids = jnp.arange(level_counts.shape[0], dtype=jnp.int32)
    tile_levels = jnp.sum(
        jnp.where(dataset_row[:, None] == dataset_ids[None, :], level_counts[None, :], 0), axis=1
    )
    live_tiles = (slot_level[None, :] < tile_levels[:, None]).astype(jnp.float32)
    heads_full = lax.all_gather(head_weight, LAT, axis=1, tiled=True)
    tile_ids = jnp.arange(var_count, dtype=jnp.int32)
    tiles = chip_pair_gather(latent.reshape(band_rows * band_cols, width), "var", var_count, 1)
    piece = (
        tiles.reshape(var_count, band_rows, band_cols, width)
        .transpose(1, 0, 2, 3)
        .reshape(band_rows, var_count * band_cols, width)
    )
    piece_cols = piece.shape[1]
    column_tile = jnp.arange(piece_cols, dtype=jnp.int32) // band_cols
    onehot = (column_tile[:, None] == tile_ids[None, :]).astype(jnp.float32)
    column_live = jnp.dot(onehot, live_tiles)
    piece_grad, head_add = slot_terms(
        piece, targets, column_live.T, level_scale, level_shift, heads_full
    )
    latent_terms = piece_grad
    latent_terms, head_terms = (latent_terms, head_add)
    grad_latent = lax.psum_scatter(
        latent_terms.astype(jnp.bfloat16), "var", scatter_dimension=1, tiled=True
    )
    head_terms = head_terms * (1.0 / math.sqrt(lat_count * band_rows * var_count * band_cols))
    outer, inner = lax.axis_size(LAT[0]), lax.axis_size(LAT[1])
    slots, outs = head_terms.shape[0], head_terms.shape[2]
    share_rows = width // lat_count
    head_parts = head_terms.astype(jnp.bfloat16).reshape(slots, outer, inner, share_rows, outs)
    grad_head = grid_reduce_scatter(head_parts, LAT[0], LAT[1], 3)
    return (latent, grad_latent, grad_head)


def solution(mesh):
    in_specs = (
        P(LAT, "var", None),
        P(),
        P(),
        P(),
        P("var", None),
        P("var", None),
        P("var", LAT, None),
        P("var", LAT, None, None),
        P(),
        P(LAT, None),
        P("var"),
    )
    out_specs = (P(LAT, "var", None), P(LAT, "var", None), P("var", LAT, None))
    lat_size = mesh.shape["lat"]
    inner = 4 if lat_size % 4 == 0 else 1
    grid = Mesh(
        mesh.devices.reshape(lat_size // inner, inner, mesh.shape["var"]), LAT + ("var",)
    )
    return jax.shard_map(local, mesh=grid, in_specs=in_specs, out_specs=out_specs, check_vma=False)
```

```python
import math

import jax
import jax.numpy as jnp
from jax import lax
from jax.experimental import pallas as pl
from jax.experimental.pallas import tpu as pltpu
from jax.sharding import Mesh, PartitionSpec as P

MESH_ID = pl.DeviceIdType.MESH
LAT = ("lat_hi", "lat_lo")


def _greet(axis, n, me):
    barrier = pltpu.get_barrier_semaphore()
    for k in range(1, n):
        pl.semaphore_signal(barrier, inc=1, device_id={axis: lax.rem(me + k, n)},
                            device_id_type=MESH_ID)
    pl.semaphore_wait(barrier, n - 1)


def peer_gather(block, axis, n, cid):
    def kernel(x_ref, out_ref, send_sem, recv_sem):
        me = lax.axis_index(axis)
        _greet(axis, n, me)
        sends = []
        for k in range(1, n):
            copy = pltpu.make_async_remote_copy(
                src_ref=x_ref, dst_ref=out_ref.at[me], send_sem=send_sem.at[k],
                recv_sem=recv_sem.at[me], device_id={axis: lax.rem(me + k, n)},
                device_id_type=MESH_ID)
            copy.start()
            sends.append(copy)
        out_ref[me] = x_ref[...]
        for k in range(1, n):
            src = lax.rem(me + n - k, n)
            pltpu.make_async_remote_copy(
                src_ref=x_ref, dst_ref=out_ref.at[src], send_sem=send_sem.at[k],
                recv_sem=recv_sem.at[src], device_id={axis: src},
                device_id_type=MESH_ID).wait_recv()
        for copy in sends:
            copy.wait_send()

    return pl.pallas_call(
        kernel,
        out_shape=jax.ShapeDtypeStruct((n,) + block.shape, block.dtype),
        in_specs=[pl.BlockSpec(memory_space=pltpu.VMEM)],
        out_specs=pl.BlockSpec(memory_space=pltpu.VMEM),
        scratch_shapes=[pltpu.SemaphoreType.DMA((n,)), pltpu.SemaphoreType.DMA((n,))],
        compiler_params=pltpu.CompilerParams(collective_id=cid, has_side_effects=True),
    )(block)


def peer_reduce_scatter(parts, axis, n, cid, out_dtype):
    def kernel(x_ref, out_ref, held, send_sem, recv_sem):
        me = lax.axis_index(axis)
        _greet(axis, n, me)
        sends = []
        for k in range(1, n):
            dst = lax.rem(me + k, n)
            copy = pltpu.make_async_remote_copy(
                src_ref=x_ref.at[dst], dst_ref=held.at[me], send_sem=send_sem.at[k],
                recv_sem=recv_sem.at[me], device_id={axis: dst},
                device_id_type=MESH_ID)
            copy.start()
            sends.append(copy)
        total = x_ref[me].astype(jnp.float32)
        for k in range(1, n):
            src = lax.rem(me + n - k, n)
            pltpu.make_async_remote_copy(
                src_ref=x_ref.at[src], dst_ref=held.at[src], send_sem=send_sem.at[k],
                recv_sem=recv_sem.at[src], device_id={axis: src},
                device_id_type=MESH_ID).wait_recv()
            total = total + held[src].astype(jnp.float32)
        out_ref[...] = total.astype(out_ref.dtype)
        for copy in sends:
            copy.wait_send()

    return pl.pallas_call(
        kernel,
        out_shape=jax.ShapeDtypeStruct(parts.shape[1:], out_dtype),
        in_specs=[pl.BlockSpec(memory_space=pltpu.VMEM)],
        out_specs=pl.BlockSpec(memory_space=pltpu.VMEM),
        scratch_shapes=[pltpu.VMEM(parts.shape, parts.dtype),
                        pltpu.SemaphoreType.DMA((n,)), pltpu.SemaphoreType.DMA((n,))],
        compiler_params=pltpu.CompilerParams(collective_id=cid, has_side_effects=True),
    )(parts)


def masked_window_attention(queries, keyval, query_win, key_win, heads):
    nq, width = queries.shape
    head_size = width // heads
    scale = 1.0 / float(head_size) ** 0.5

    def kernel(q_ref, kv_ref, qw_ref, kw_ref, out_ref):
        mask = qw_ref[...] == kw_ref[...]
        for h in range(heads):
            cols = slice(h * head_size, (h + 1) * head_size)
            q = q_ref[:, cols]
            k = kv_ref[:, h * head_size:(h + 1) * head_size]
            v = kv_ref[:, width + h * head_size:width + (h + 1) * head_size]
            s = lax.dot_general(q, k, (((1,), (1,)), ((), ())),
                                preferred_element_type=jnp.float32) * scale
            s = jnp.where(mask, s, -jnp.inf)
            w = jnp.exp(s - jnp.max(s, axis=1, keepdims=True))
            p = (w / jnp.sum(w, axis=1, keepdims=True)).astype(jnp.bfloat16)
            out_ref[:, cols] = jnp.dot(p, v, preferred_element_type=jnp.float32).astype(out_ref.dtype)

    return pl.pallas_call(
        kernel,
        out_shape=jax.ShapeDtypeStruct((nq, width), jnp.bfloat16),
        in_specs=[pl.BlockSpec(memory_space=pltpu.VMEM)] * 4,
        out_specs=pl.BlockSpec(memory_space=pltpu.VMEM),
    )(queries, keyval, query_win, key_win)


def chip_pair_gather(block, axis, n, cid):
    nz = n // 2

    def kernel(x_ref, out_ref, send_sem, recv_sem):
        me = lax.axis_index(axis)
        partner = me + 1 - 2 * lax.rem(me, 2)
        peers = [lax.rem(me + 2 * k, n) for k in range(1, nz)]
        barrier = pltpu.get_barrier_semaphore()
        for dev in peers + [partner]:
            pl.semaphore_signal(barrier, inc=1, device_id={axis: dev}, device_id_type=MESH_ID)
        pl.semaphore_wait(barrier, nz)

        def send(src_ref, slot, dev, index):
            copy = pltpu.make_async_remote_copy(
                src_ref=src_ref, dst_ref=out_ref.at[slot], send_sem=send_sem.at[index],
                recv_sem=recv_sem.at[slot], device_id={axis: dev}, device_id_type=MESH_ID)
            copy.start()
            return copy

        def arrive(slot):
            pltpu.make_async_remote_copy(
                src_ref=x_ref, dst_ref=out_ref.at[slot], send_sem=send_sem.at[0],
                recv_sem=recv_sem.at[slot], device_id={axis: slot},
                device_id_type=MESH_ID).wait_recv()

        sends = [send(x_ref, me, dev, i) for i, dev in enumerate(peers)]
        sends.append(send(x_ref, me, partner, nz - 1))
        out_ref[me] = x_ref[...]
        for k in range(1, nz):
            src = lax.rem(me + n - 2 * k, n)
            arrive(src)
            sends.append(send(out_ref.at[src], src, partner, nz - 1 + k))
        for k in range(nz):
            arrive(lax.rem(partner + 2 * k, n))
        for copy in sends:
            copy.wait_send()

    return pl.pallas_call(
        kernel,
        out_shape=jax.ShapeDtypeStruct((n,) + block.shape, block.dtype),
        in_specs=[pl.BlockSpec(memory_space=pltpu.VMEM)],
        out_specs=pl.BlockSpec(memory_space=pltpu.VMEM),
        scratch_shapes=[pltpu.SemaphoreType.DMA((n,)), pltpu.SemaphoreType.DMA((n,))],
        compiler_params=pltpu.CompilerParams(collective_id=cid, has_side_effects=True),
    )(block)


def grid_reduce_scatter(parts, outer, inner, cid):
    slots, n_hi, n_lo, rows, outs = parts.shape
    half = rows // 2

    def kernel(x_ref, out_ref, r1a, r1b, s1a, s1b, r2a, r2b, send_sem, recv_sem):
        hi = lax.axis_index(outer)
        lo = lax.axis_index(inner)
        barrier = pltpu.get_barrier_semaphore()
        for k in range(1, n_lo):
            pl.semaphore_signal(barrier, inc=1, device_id={inner: lax.rem(lo + k, n_lo)},
                                device_id_type=MESH_ID)
        for k in range(1, n_hi):
            pl.semaphore_signal(barrier, inc=1, device_id={outer: lax.rem(hi + k, n_hi)},
                                device_id_type=MESH_ID)
        pl.semaphore_wait(barrier, n_lo + n_hi - 2)

        def send(src_ref, dst_ref, axis, dev, group, k, slot):
            copy = pltpu.make_async_remote_copy(
                src_ref=src_ref, dst_ref=dst_ref, send_sem=send_sem.at[group, k],
                recv_sem=recv_sem.at[group, slot], device_id={axis: dev},
                device_id_type=MESH_ID)
            copy.start()
            return copy

        def arrive(dst_ref, group, slot):
            pltpu.make_async_remote_copy(
                src_ref=dst_ref, dst_ref=dst_ref, send_sem=send_sem.at[group, 0],
                recv_sem=recv_sem.at[group, slot], device_id={inner: lo},
                device_id_type=MESH_ID).wait_recv()

        sends = []
        for k in range(1, n_lo):
            dev = lax.rem(lo + k, n_lo)
            sends.append(send(x_ref.at[:, :, dev, pl.ds(0, half), :], r1a.at[lo], inner, dev, 0, k, lo))
        for k in range(1, n_hi):
            dev = lax.rem(hi + k, n_hi)
            sends.append(send(x_ref.at[:, dev, :, pl.ds(half, half), :], r1b.at[hi], outer, dev, 1, k, hi))

        sources_lo = [lax.rem(lo + n_lo - k, n_lo) for k in range(1, n_lo)]
        sources_hi = [lax.rem(hi + n_hi - k, n_hi) for k in range(1, n_hi)]
        for src in sources_lo:
            arrive(r1a.at[src], 0, src)
        for h in range(n_hi):
            total = x_ref[:, h, lo, pl.ds(0, half), :].astype(jnp.float32)
            for src in sources_lo:
                total = total + r1a[src, :, h].astype(jnp.float32)
            s1a[h] = total.astype(s1a.dtype)
        for k in range(1, n_hi):
            dev = lax.rem(hi + k, n_hi)
            sends.append(send(s1a.at[dev], r2a.at[hi], outer, dev, 2, k, hi))
        for src in sources_hi:
            arrive(r1b.at[src], 1, src)
        for l in range(n_lo):
            total = x_ref[:, hi, l, pl.ds(half, half), :].astype(jnp.float32)
            for src in sources_hi:
                total = total + r1b[src, :, l].astype(jnp.float32)
            s1b[l] = total.astype(s1b.dtype)
        for k in range(1, n_lo):
            dev = lax.rem(lo + k, n_lo)
            sends.append(send(s1b.at[dev], r2b.at[lo], inner, dev, 3, k, lo))

        total = s1a[hi].astype(jnp.float32)
        for src in sources_hi:
            arrive(r2a.at[src], 2, src)
            total = total + r2a[src].astype(jnp.float32)
        out_ref[:, pl.ds(0, half), :] = total
        total = s1b[lo].astype(jnp.float32)
        for src in sources_lo:
            arrive(r2b.at[src], 3, src)
            total = total + r2b[src].astype(jnp.float32)
        out_ref[:, pl.ds(half, half), :] = total
        for copy in sends:
            copy.wait_send()

    most = max(n_hi, n_lo)
    return pl.pallas_call(
        kernel,
        out_shape=jax.ShapeDtypeStruct((slots, rows, outs), jnp.float32),
        in_specs=[pl.BlockSpec(memory_space=pltpu.VMEM)],
        out_specs=pl.BlockSpec(memory_space=pltpu.VMEM),
        scratch_shapes=[
            pltpu.VMEM((n_lo, slots, n_hi, half, outs), parts.dtype),
            pltpu.VMEM((n_hi, slots, n_lo, half, outs), parts.dtype),
            pltpu.VMEM((n_hi, slots, half, outs), parts.dtype),
            pltpu.VMEM((n_lo, slots, half, outs), parts.dtype),
            pltpu.VMEM((n_hi, slots, half, outs), parts.dtype),
            pltpu.VMEM((n_lo, slots, half, outs), parts.dtype),
            pltpu.SemaphoreType.DMA((4, most)),
            pltpu.SemaphoreType.DMA((4, most)),
        ],
        compiler_params=pltpu.CompilerParams(collective_id=cid, has_side_effects=True),
    )(parts)

HEADS = 16
WH = 6
WW = 12


EPS = 1e-05


def padded(array, sides, width, wrap):
    for axis, dim in sides:
        size, length = (lax.axis_size(axis), array.shape[dim])
        up = [(i, (i + 1) % size) for i in range(size if wrap else size - 1)]
        down = [(j, i) for i, j in up]
        last = lax.slice_in_dim(array, length - width, length, axis=dim)
        initial = lax.slice_in_dim(array, 0, width, axis=dim)
        before = lax.ppermute(last, axis, up)
        after = lax.ppermute(initial, axis, down)
        array = jnp.concatenate([before, array, after], axis=dim)
    return array


def layer_norm(values, gain):
    wide = values.astype(jnp.float32)
    average = jnp.mean(wide, axis=-1, keepdims=True)
    centred = wide - average
    variance = jnp.mean(centred * centred, axis=-1, keepdims=True)
    return (centred * lax.rsqrt(variance + EPS) * gain).astype(jnp.bfloat16)


def window_attention(query_ext, keyval, row_valid, heads):
    ext_rows, ext_cols, width = query_ext.shape
    head_size = width // heads
    win_rows = ext_rows // WH
    win_cols = ext_cols // WW

    def split(values, parts):
        shaped = values.reshape(win_rows, WH, win_cols, WW, parts, heads, head_size)
        return shaped.transpose(0, 2, 1, 3, 4, 5, 6).reshape(
            win_rows * win_cols, WH * WW, parts, heads, head_size
        )

    query_win = split(query_ext, 1)[:, :, 0]
    pairs = split(keyval, 2)
    key_win = pairs[:, :, 0]
    value_win = pairs[:, :, 1]
    key_mask = jnp.broadcast_to(
        row_valid.reshape(win_rows, 1, WH, 1), (win_rows, win_cols, WH, WW)
    ).reshape(win_rows * win_cols, WH * WW)
    scores = jnp.einsum(
        "wqhd,wkhd->whqk", query_win, key_win, preferred_element_type=jnp.float32
    ) / math.sqrt(head_size)
    scores = jnp.where(key_mask[:, None, None, :], scores, -jnp.inf)
    peak = jnp.max(scores, axis=-1, keepdims=True)
    weights = jnp.exp(scores - peak)
    probs = (weights / jnp.sum(weights, axis=-1, keepdims=True)).astype(jnp.bfloat16)
    mixed = jnp.einsum("whqk,wkhd->wqhd", probs, value_win, preferred_element_type=jnp.float32)
    return (
        mixed.reshape(win_rows, win_cols, WH, WW, width)
        .transpose(0, 2, 1, 3, 4)
        .reshape(ext_rows, ext_cols, width)
    )


def slot_terms(tiles, target_rows, live, level_scale, level_shift, heads_full):
    n_tiles, per_tile, _ = tiles.shape
    slots, band_rows, _, outs = target_rows.shape
    targets_t = (
        target_rows.reshape(slots, band_rows, n_tiles, per_tile // band_rows, outs)
        .transpose(0, 2, 1, 3, 4)
        .reshape(slots, n_tiles, per_tile, outs)
    )
    rows = (
        tiles.astype(jnp.float32)[None] * level_scale[:, None, None, :]
        + level_shift[:, None, None, :]
    ).astype(jnp.bfloat16)
    predicted = jnp.einsum("ktnd,kdo->ktno", rows, heads_full, preferred_element_type=jnp.float32)
    errors = ((predicted - targets_t.astype(jnp.float32)) * live[:, :, None, None]).astype(
        jnp.bfloat16
    )
    back_grad = jnp.einsum("ktno,kdo->ktnd", errors, heads_full, preferred_element_type=jnp.float32)
    piece_grad = jnp.sum(back_grad * level_scale[:, None, None, :], axis=0)
    head_add = jnp.einsum("ktnd,ktno->kdo", rows, errors, preferred_element_type=jnp.float32)
    return (piece_grad, head_add)


def local(
    patches,
    norm_gain,
    input_proj,
    output_proj,
    level_scale,
    level_shift,
    head_weight,
    targets,
    level_counts,
    tile_dataset,
    slot_level,
):
    band_rows, band_cols, width = patches.shape
    half_rows = WH // 2
    half_cols = WW // 2
    lat_count = lax.axis_size(LAT)
    var_count = lax.axis_size("var")
    lat_place = lax.axis_index(LAT)
    ext_rows = band_rows + WH
    ext_cols = band_cols + WW
    extended = padded(patches, ((LAT, 0),), half_rows, False)
    extended = padded(extended, (("var", 1),), half_cols, True)
    normed_ext = layer_norm(extended, norm_gain)
    keyval = jnp.dot(
        normed_ext.reshape(-1, width), input_proj[:, width:], preferred_element_type=jnp.float32
    )
    keyval = keyval.astype(jnp.bfloat16).reshape(ext_rows, ext_cols, 2 * width)
    normed = normed_ext[half_rows : half_rows + band_rows, half_cols : half_cols + band_cols]
    queries = jnp.dot(
        normed.reshape(-1, width), input_proj[:, :width], preferred_element_type=jnp.float32
    )
    queries = queries.astype(jnp.bfloat16)
    global_row = lat_place * band_rows - half_rows + jnp.arange(ext_rows, dtype=jnp.int32)
    row_valid = (global_row >= 0) & (global_row < lat_count * band_rows)
    win_cols = ext_cols // WW
    ext_r = jnp.arange(ext_rows, dtype=jnp.int32)[:, None]
    ext_c = jnp.arange(ext_cols, dtype=jnp.int32)[None, :]
    key_win = jnp.where(row_valid[:, None], (ext_r // WH) * win_cols + ext_c // WW, -1)
    own_r = ext_r[half_rows : half_rows + band_rows]
    own_c = ext_c[:, half_cols : half_cols + band_cols]
    query_win = (own_r // WH) * win_cols + own_c // WW
    attn = masked_window_attention(
        queries,
        keyval.reshape(ext_rows * ext_cols, 2 * width),
        query_win.reshape(-1, 1),
        key_win.reshape(1, -1),
        HEADS,
    ).reshape(band_rows, band_cols, width)
    update = jnp.dot(
        attn.reshape(-1, width), output_proj, preferred_element_type=jnp.float32
    ).reshape(band_rows, band_cols, width)
    latent = (patches.astype(jnp.float32) + update).astype(jnp.bfloat16)
    dataset_row = tile_dataset[0]
    dataset_ids = jnp.arange(level_counts.shape[0], dtype=jnp.int32)
    tile_levels = jnp.sum(
        jnp.where(dataset_row[:, None] == dataset_ids[None, :], level_counts[None, :], 0), axis=1
    )
    live_tiles = (slot_level[None, :] < tile_levels[:, None]).astype(jnp.float32)
    heads_full = lax.all_gather(head_weight, LAT, axis=1, tiled=True)
    tiles = chip_pair_gather(latent.reshape(band_rows * band_cols, width), "var", var_count, 1)
    piece_grad, head_add = slot_terms(
        tiles, targets, live_tiles.T, level_scale, level_shift, heads_full
    )
    grad_latent = lax.psum_scatter(
        piece_grad.astype(jnp.bfloat16), "var", scatter_dimension=0, tiled=True
    ).reshape(band_rows, band_cols, width)
    head_terms = head_add
    head_terms = head_terms * (1.0 / math.sqrt(lat_count * band_rows * var_count * band_cols))
    outer, inner = lax.axis_size(LAT[0]), lax.axis_size(LAT[1])
    slots, outs = head_terms.shape[0], head_terms.shape[2]
    share_rows = width // lat_count
    head_parts = head_terms.astype(jnp.bfloat16).reshape(slots, outer, inner, share_rows, outs)
    grad_head = grid_reduce_scatter(head_parts, LAT[0], LAT[1], 3)
    return (latent, grad_latent, grad_head)


def solution(mesh):
    in_specs = (
        P(LAT, "var", None),
        P(),
        P(),
        P(),
        P("var", None),
        P("var", None),
        P("var", LAT, None),
        P("var", LAT, None, None),
        P(),
        P(LAT, None),
        P("var"),
    )
    out_specs = (P(LAT, "var", None), P(LAT, "var", None), P("var", LAT, None))
    lat_size = mesh.shape["lat"]
    inner = 4 if lat_size % 4 == 0 else 1
    grid = Mesh(
        mesh.devices.reshape(lat_size // inner, inner, mesh.shape["var"]), LAT + ("var",)
    )
    return jax.shard_map(local, mesh=grid, in_specs=in_specs, out_specs=out_specs, check_vma=False)
```

```python
import math

import jax
import jax.numpy as jnp
from jax import lax
from jax.experimental import pallas as pl
from jax.experimental.pallas import tpu as pltpu
from jax.sharding import Mesh, PartitionSpec as P

MESH_ID = pl.DeviceIdType.MESH
LAT = ("lat_hi", "lat_lo")


def _greet(axis, n, me):
    barrier = pltpu.get_barrier_semaphore()
    for k in range(1, n):
        pl.semaphore_signal(barrier, inc=1, device_id={axis: lax.rem(me + k, n)},
                            device_id_type=MESH_ID)
    pl.semaphore_wait(barrier, n - 1)


def peer_gather(block, axis, n, cid):
    def kernel(x_ref, out_ref, send_sem, recv_sem):
        me = lax.axis_index(axis)
        _greet(axis, n, me)
        sends = []
        for k in range(1, n):
            copy = pltpu.make_async_remote_copy(
                src_ref=x_ref, dst_ref=out_ref.at[me], send_sem=send_sem.at[k],
                recv_sem=recv_sem.at[me], device_id={axis: lax.rem(me + k, n)},
                device_id_type=MESH_ID)
            copy.start()
            sends.append(copy)
        out_ref[me] = x_ref[...]
        for k in range(1, n):
            src = lax.rem(me + n - k, n)
            pltpu.make_async_remote_copy(
                src_ref=x_ref, dst_ref=out_ref.at[src], send_sem=send_sem.at[k],
                recv_sem=recv_sem.at[src], device_id={axis: src},
                device_id_type=MESH_ID).wait_recv()
        for copy in sends:
            copy.wait_send()

    return pl.pallas_call(
        kernel,
        out_shape=jax.ShapeDtypeStruct((n,) + block.shape, block.dtype),
        in_specs=[pl.BlockSpec(memory_space=pltpu.VMEM)],
        out_specs=pl.BlockSpec(memory_space=pltpu.VMEM),
        scratch_shapes=[pltpu.SemaphoreType.DMA((n,)), pltpu.SemaphoreType.DMA((n,))],
        compiler_params=pltpu.CompilerParams(collective_id=cid, has_side_effects=True),
    )(block)


def peer_reduce_scatter(parts, axis, n, cid, out_dtype):
    def kernel(x_ref, out_ref, held, send_sem, recv_sem):
        me = lax.axis_index(axis)
        _greet(axis, n, me)
        sends = []
        for k in range(1, n):
            dst = lax.rem(me + k, n)
            copy = pltpu.make_async_remote_copy(
                src_ref=x_ref.at[dst], dst_ref=held.at[me], send_sem=send_sem.at[k],
                recv_sem=recv_sem.at[me], device_id={axis: dst},
                device_id_type=MESH_ID)
            copy.start()
            sends.append(copy)
        total = x_ref[me].astype(jnp.float32)
        for k in range(1, n):
            src = lax.rem(me + n - k, n)
            pltpu.make_async_remote_copy(
                src_ref=x_ref.at[src], dst_ref=held.at[src], send_sem=send_sem.at[k],
                recv_sem=recv_sem.at[src], device_id={axis: src},
                device_id_type=MESH_ID).wait_recv()
            total = total + held[src].astype(jnp.float32)
        out_ref[...] = total.astype(out_ref.dtype)
        for copy in sends:
            copy.wait_send()

    return pl.pallas_call(
        kernel,
        out_shape=jax.ShapeDtypeStruct(parts.shape[1:], out_dtype),
        in_specs=[pl.BlockSpec(memory_space=pltpu.VMEM)],
        out_specs=pl.BlockSpec(memory_space=pltpu.VMEM),
        scratch_shapes=[pltpu.VMEM(parts.shape, parts.dtype),
                        pltpu.SemaphoreType.DMA((n,)), pltpu.SemaphoreType.DMA((n,))],
        compiler_params=pltpu.CompilerParams(collective_id=cid, has_side_effects=True),
    )(parts)


def masked_window_attention(queries, keyval, query_win, key_win, heads):
    nq, width = queries.shape
    head_size = width // heads
    scale = 1.0 / float(head_size) ** 0.5

    def kernel(q_ref, kv_ref, qw_ref, kw_ref, out_ref):
        mask = qw_ref[...] == kw_ref[...]
        for h in range(heads):
            cols = slice(h * head_size, (h + 1) * head_size)
            q = q_ref[:, cols]
            k = kv_ref[:, h * head_size:(h + 1) * head_size]
            v = kv_ref[:, width + h * head_size:width + (h + 1) * head_size]
            s = lax.dot_general(q, k, (((1,), (1,)), ((), ())),
                                preferred_element_type=jnp.float32) * scale
            s = jnp.where(mask, s, -jnp.inf)
            w = jnp.exp(s - jnp.max(s, axis=1, keepdims=True))
            p = (w / jnp.sum(w, axis=1, keepdims=True)).astype(jnp.bfloat16)
            out_ref[:, cols] = jnp.dot(p, v, preferred_element_type=jnp.float32).astype(out_ref.dtype)

    return pl.pallas_call(
        kernel,
        out_shape=jax.ShapeDtypeStruct((nq, width), jnp.bfloat16),
        in_specs=[pl.BlockSpec(memory_space=pltpu.VMEM)] * 4,
        out_specs=pl.BlockSpec(memory_space=pltpu.VMEM),
    )(queries, keyval, query_win, key_win)


def chip_pair_gather(block, axis, n, cid):
    nz = n // 2

    def kernel(x_ref, out_ref, send_sem, recv_sem):
        me = lax.axis_index(axis)
        partner = me + 1 - 2 * lax.rem(me, 2)
        peers = [lax.rem(me + 2 * k, n) for k in range(1, nz)]
        barrier = pltpu.get_barrier_semaphore()
        for dev in peers + [partner]:
            pl.semaphore_signal(barrier, inc=1, device_id={axis: dev}, device_id_type=MESH_ID)
        pl.semaphore_wait(barrier, nz)

        def send(src_ref, slot, dev, index):
            copy = pltpu.make_async_remote_copy(
                src_ref=src_ref, dst_ref=out_ref.at[slot], send_sem=send_sem.at[index],
                recv_sem=recv_sem.at[slot], device_id={axis: dev}, device_id_type=MESH_ID)
            copy.start()
            return copy

        def arrive(slot):
            pltpu.make_async_remote_copy(
                src_ref=x_ref, dst_ref=out_ref.at[slot], send_sem=send_sem.at[0],
                recv_sem=recv_sem.at[slot], device_id={axis: slot},
                device_id_type=MESH_ID).wait_recv()

        sends = [send(x_ref, me, dev, i) for i, dev in enumerate(peers)]
        sends.append(send(x_ref, me, partner, nz - 1))
        out_ref[me] = x_ref[...]
        for k in range(1, nz):
            src = lax.rem(me + n - 2 * k, n)
            arrive(src)
            sends.append(send(out_ref.at[src], src, partner, nz - 1 + k))
        for k in range(nz):
            arrive(lax.rem(partner + 2 * k, n))
        for copy in sends:
            copy.wait_send()

    return pl.pallas_call(
        kernel,
        out_shape=jax.ShapeDtypeStruct((n,) + block.shape, block.dtype),
        in_specs=[pl.BlockSpec(memory_space=pltpu.VMEM)],
        out_specs=pl.BlockSpec(memory_space=pltpu.VMEM),
        scratch_shapes=[pltpu.SemaphoreType.DMA((n,)), pltpu.SemaphoreType.DMA((n,))],
        compiler_params=pltpu.CompilerParams(collective_id=cid, has_side_effects=True),
    )(block)


def grid_reduce_scatter(parts, outer, inner, cid):
    slots, n_hi, n_lo, rows, outs = parts.shape
    half = rows // 2

    def kernel(x_ref, out_ref, r1a, r1b, s1a, s1b, r2a, r2b, send_sem, recv_sem):
        hi = lax.axis_index(outer)
        lo = lax.axis_index(inner)
        barrier = pltpu.get_barrier_semaphore()
        for k in range(1, n_lo):
            pl.semaphore_signal(barrier, inc=1, device_id={inner: lax.rem(lo + k, n_lo)},
                                device_id_type=MESH_ID)
        for k in range(1, n_hi):
            pl.semaphore_signal(barrier, inc=1, device_id={outer: lax.rem(hi + k, n_hi)},
                                device_id_type=MESH_ID)
        pl.semaphore_wait(barrier, n_lo + n_hi - 2)

        def send(src_ref, dst_ref, axis, dev, group, k, slot):
            copy = pltpu.make_async_remote_copy(
                src_ref=src_ref, dst_ref=dst_ref, send_sem=send_sem.at[group, k],
                recv_sem=recv_sem.at[group, slot], device_id={axis: dev},
                device_id_type=MESH_ID)
            copy.start()
            return copy

        def arrive(dst_ref, group, slot):
            pltpu.make_async_remote_copy(
                src_ref=dst_ref, dst_ref=dst_ref, send_sem=send_sem.at[group, 0],
                recv_sem=recv_sem.at[group, slot], device_id={inner: lo},
                device_id_type=MESH_ID).wait_recv()

        sends = []
        for k in range(1, n_lo):
            dev = lax.rem(lo + k, n_lo)
            sends.append(send(x_ref.at[:, :, dev, pl.ds(0, half), :], r1a.at[lo], inner, dev, 0, k, lo))
        for k in range(1, n_hi):
            dev = lax.rem(hi + k, n_hi)
            sends.append(send(x_ref.at[:, dev, :, pl.ds(half, half), :], r1b.at[hi], outer, dev, 1, k, hi))

        sources_lo = [lax.rem(lo + n_lo - k, n_lo) for k in range(1, n_lo)]
        sources_hi = [lax.rem(hi + n_hi - k, n_hi) for k in range(1, n_hi)]
        for src in sources_lo:
            arrive(r1a.at[src], 0, src)
        for h in range(n_hi):
            total = x_ref[:, h, lo, pl.ds(0, half), :].astype(jnp.float32)
            for src in sources_lo:
                total = total + r1a[src, :, h].astype(jnp.float32)
            s1a[h] = total.astype(s1a.dtype)
        for k in range(1, n_hi):
            dev = lax.rem(hi + k, n_hi)
            sends.append(send(s1a.at[dev], r2a.at[hi], outer, dev, 2, k, hi))
        for src in sources_hi:
            arrive(r1b.at[src], 1, src)
        for l in range(n_lo):
            total = x_ref[:, hi, l, pl.ds(half, half), :].astype(jnp.float32)
            for src in sources_hi:
                total = total + r1b[src, :, l].astype(jnp.float32)
            s1b[l] = total.astype(s1b.dtype)
        for k in range(1, n_lo):
            dev = lax.rem(lo + k, n_lo)
            sends.append(send(s1b.at[dev], r2b.at[lo], inner, dev, 3, k, lo))

        total = s1a[hi].astype(jnp.float32)
        for src in sources_hi:
            arrive(r2a.at[src], 2, src)
            total = total + r2a[src].astype(jnp.float32)
        out_ref[:, pl.ds(0, half), :] = total
        total = s1b[lo].astype(jnp.float32)
        for src in sources_lo:
            arrive(r2b.at[src], 3, src)
            total = total + r2b[src].astype(jnp.float32)
        out_ref[:, pl.ds(half, half), :] = total
        for copy in sends:
            copy.wait_send()

    most = max(n_hi, n_lo)
    return pl.pallas_call(
        kernel,
        out_shape=jax.ShapeDtypeStruct((slots, rows, outs), jnp.float32),
        in_specs=[pl.BlockSpec(memory_space=pltpu.VMEM)],
        out_specs=pl.BlockSpec(memory_space=pltpu.VMEM),
        scratch_shapes=[
            pltpu.VMEM((n_lo, slots, n_hi, half, outs), parts.dtype),
            pltpu.VMEM((n_hi, slots, n_lo, half, outs), parts.dtype),
            pltpu.VMEM((n_hi, slots, half, outs), parts.dtype),
            pltpu.VMEM((n_lo, slots, half, outs), parts.dtype),
            pltpu.VMEM((n_hi, slots, half, outs), parts.dtype),
            pltpu.VMEM((n_lo, slots, half, outs), parts.dtype),
            pltpu.SemaphoreType.DMA((4, most)),
            pltpu.SemaphoreType.DMA((4, most)),
        ],
        compiler_params=pltpu.CompilerParams(collective_id=cid, has_side_effects=True),
    )(parts)

HEADS = 16
WH = 6
WW = 12


EPS = 1e-05


def padded(array, sides, width, wrap):
    for axis, dim in sides:
        size, length = (lax.axis_size(axis), array.shape[dim])
        up = [(i, (i + 1) % size) for i in range(size if wrap else size - 1)]
        down = [(j, i) for i, j in up]
        last = lax.slice_in_dim(array, length - width, length, axis=dim)
        initial = lax.slice_in_dim(array, 0, width, axis=dim)
        before = lax.ppermute(last, axis, up)
        after = lax.ppermute(initial, axis, down)
        array = jnp.concatenate([before, array, after], axis=dim)
    return array


def layer_norm(values, gain):
    wide = values.astype(jnp.float32)
    average = jnp.mean(wide, axis=-1, keepdims=True)
    centred = wide - average
    variance = jnp.mean(centred * centred, axis=-1, keepdims=True)
    return (centred * lax.rsqrt(variance + EPS) * gain).astype(jnp.bfloat16)


def window_attention(query_ext, keyval, row_valid, heads):
    ext_rows, ext_cols, width = query_ext.shape
    head_size = width // heads
    win_rows = ext_rows // WH
    win_cols = ext_cols // WW

    def split(values, parts):
        shaped = values.reshape(win_rows, WH, win_cols, WW, parts, heads, head_size)
        return shaped.transpose(0, 2, 1, 3, 4, 5, 6).reshape(
            win_rows * win_cols, WH * WW, parts, heads, head_size
        )

    query_win = split(query_ext, 1)[:, :, 0]
    pairs = split(keyval, 2)
    key_win = pairs[:, :, 0]
    value_win = pairs[:, :, 1]
    key_mask = jnp.broadcast_to(
        row_valid.reshape(win_rows, 1, WH, 1), (win_rows, win_cols, WH, WW)
    ).reshape(win_rows * win_cols, WH * WW)
    scores = jnp.einsum(
        "wqhd,wkhd->whqk", query_win, key_win, preferred_element_type=jnp.float32
    ) / math.sqrt(head_size)
    scores = jnp.where(key_mask[:, None, None, :], scores, -jnp.inf)
    peak = jnp.max(scores, axis=-1, keepdims=True)
    weights = jnp.exp(scores - peak)
    probs = (weights / jnp.sum(weights, axis=-1, keepdims=True)).astype(jnp.bfloat16)
    mixed = jnp.einsum("whqk,wkhd->wqhd", probs, value_win, preferred_element_type=jnp.float32)
    return (
        mixed.reshape(win_rows, win_cols, WH, WW, width)
        .transpose(0, 2, 1, 3, 4)
        .reshape(ext_rows, ext_cols, width)
    )


def slot_terms(piece, target_rows, live_cols, level_scale, level_shift, heads_full):
    piece_wide = piece.astype(jnp.float32)
    rows = (
        piece_wide[None] * level_scale[:, None, None, :] + level_shift[:, None, None, :]
    ).astype(jnp.bfloat16)
    predicted = jnp.einsum("krnd,kdo->krno", rows, heads_full, preferred_element_type=jnp.float32)
    errors = ((predicted - target_rows.astype(jnp.float32)) * live_cols[:, None, :, None]).astype(
        jnp.bfloat16
    )
    back_grad = jnp.einsum("krno,kdo->krnd", errors, heads_full, preferred_element_type=jnp.float32)
    piece_grad = jnp.sum(back_grad * level_scale[:, None, None, :], axis=0)
    head_add = jnp.einsum("krnd,krno->kdo", rows, errors, preferred_element_type=jnp.float32)
    return (piece_grad, head_add)


def local(
    patches,
    norm_gain,
    input_proj,
    output_proj,
    level_scale,
    level_shift,
    head_weight,
    targets,
    level_counts,
    tile_dataset,
    slot_level,
):
    band_rows, band_cols, width = patches.shape
    half_rows = WH // 2
    half_cols = WW // 2
    lat_count = lax.axis_size(LAT)
    var_count = lax.axis_size("var")
    lat_place = lax.axis_index(LAT)
    ext_rows = band_rows + WH
    ext_cols = band_cols + WW
    own_normed = layer_norm(patches, norm_gain).reshape(-1, width)
    queries = jnp.dot(own_normed, input_proj[:, :width], preferred_element_type=jnp.float32)
    queries = queries.astype(jnp.bfloat16)
    own_keyval = jnp.dot(own_normed, input_proj[:, width:], preferred_element_type=jnp.float32)
    extended = padded(patches, ((LAT, 0),), half_rows, False)
    extended = padded(extended, (("var", 1),), half_cols, True)

    def ring(grid):
        top, bottom = grid[:half_rows], grid[half_rows + band_rows :]
        middle = grid[half_rows : half_rows + band_rows]
        left, right = middle[:, :half_cols], middle[:, half_cols + band_cols :]
        return jnp.concatenate(
            [part.reshape((-1,) + grid.shape[2:]) for part in (top, bottom, left, right)]
        )

    halo_normed = layer_norm(ring(extended), norm_gain)
    halo_keyval = jnp.dot(halo_normed, input_proj[:, width:], preferred_element_type=jnp.float32)
    keyval = jnp.concatenate([own_keyval, halo_keyval]).astype(jnp.bfloat16)
    global_row = lat_place * band_rows - half_rows + jnp.arange(ext_rows, dtype=jnp.int32)
    row_valid = (global_row >= 0) & (global_row < lat_count * band_rows)
    win_cols = ext_cols // WW
    ext_r = jnp.arange(ext_rows, dtype=jnp.int32)[:, None]
    ext_c = jnp.arange(ext_cols, dtype=jnp.int32)[None, :]
    key_grid = jnp.where(row_valid[:, None], (ext_r // WH) * win_cols + ext_c // WW, -1)
    query_win = key_grid[half_rows : half_rows + band_rows, half_cols : half_cols + band_cols]
    key_win = jnp.concatenate([query_win.reshape(-1), ring(key_grid)])
    attn = masked_window_attention(
        queries,
        keyval,
        query_win.reshape(-1, 1),
        key_win.reshape(1, -1),
        HEADS,
    ).reshape(band_rows, band_cols, width)
    update = jnp.dot(
        attn.reshape(-1, width), output_proj, preferred_element_type=jnp.float32
    ).reshape(band_rows, band_cols, width)
    latent = (patches.astype(jnp.float32) + update).astype(jnp.bfloat16)
    dataset_row = tile_dataset[0]
    dataset_ids = jnp.arange(level_counts.shape[0], dtype=jnp.int32)
    tile_levels = jnp.sum(
        jnp.where(dataset_row[:, None] == dataset_ids[None, :], level_counts[None, :], 0), axis=1
    )
    live_tiles = (slot_level[None, :] < tile_levels[:, None]).astype(jnp.float32)
    heads_full = lax.all_gather(head_weight, LAT, axis=1, tiled=True)
    tile_ids = jnp.arange(var_count, dtype=jnp.int32)
    tiles = chip_pair_gather(latent.reshape(band_rows * band_cols, width), "var", var_count, 1)
    piece = (
        tiles.reshape(var_count, band_rows, band_cols, width)
        .transpose(1, 0, 2, 3)
        .reshape(band_rows, var_count * band_cols, width)
    )
    piece_cols = piece.shape[1]
    column_tile = jnp.arange(piece_cols, dtype=jnp.int32) // band_cols
    onehot = (column_tile[:, None] == tile_ids[None, :]).astype(jnp.float32)
    column_live = jnp.dot(onehot, live_tiles)
    piece_grad, head_add = slot_terms(
        piece, targets, column_live.T, level_scale, level_shift, heads_full
    )
    latent_terms = piece_grad
    latent_terms, head_terms = (latent_terms, head_add)
    grad_latent = lax.psum_scatter(
        latent_terms.astype(jnp.bfloat16), "var", scatter_dimension=1, tiled=True
    )
    head_terms = head_terms * (1.0 / math.sqrt(lat_count * band_rows * var_count * band_cols))
    outer, inner = lax.axis_size(LAT[0]), lax.axis_size(LAT[1])
    slots, outs = head_terms.shape[0], head_terms.shape[2]
    share_rows = width // lat_count
    head_parts = head_terms.astype(jnp.bfloat16).reshape(slots, outer, inner, share_rows, outs)
    grad_head = grid_reduce_scatter(head_parts, LAT[0], LAT[1], 3)
    return (latent, grad_latent, grad_head)


def solution(mesh):
    in_specs = (
        P(LAT, "var", None),
        P(),
        P(),
        P(),
        P("var", None),
        P("var", None),
        P("var", LAT, None),
        P("var", LAT, None, None),
        P(),
        P(LAT, None),
        P("var"),
    )
    out_specs = (P(LAT, "var", None), P(LAT, "var", None), P("var", LAT, None))
    lat_size = mesh.shape["lat"]
    inner = 4 if lat_size % 4 == 0 else 1
    grid = Mesh(
        mesh.devices.reshape(lat_size // inner, inner, mesh.shape["var"]), LAT + ("var",)
    )
    return jax.shard_map(local, mesh=grid, in_specs=in_specs, out_specs=out_specs, check_vma=False)
```

```python
import math

import jax
import jax.numpy as jnp
from jax import lax
from jax.experimental import pallas as pl
from jax.experimental.pallas import tpu as pltpu
from jax.sharding import Mesh, PartitionSpec as P

MESH_ID = pl.DeviceIdType.MESH
LAT = ("lat_hi", "lat_lo")


def _greet(axis, n, me):
    barrier = pltpu.get_barrier_semaphore()
    for k in range(1, n):
        pl.semaphore_signal(barrier, inc=1, device_id={axis: lax.rem(me + k, n)},
                            device_id_type=MESH_ID)
    pl.semaphore_wait(barrier, n - 1)


def peer_gather(block, axis, n, cid):
    def kernel(x_ref, out_ref, send_sem, recv_sem):
        me = lax.axis_index(axis)
        _greet(axis, n, me)
        sends = []
        for k in range(1, n):
            copy = pltpu.make_async_remote_copy(
                src_ref=x_ref, dst_ref=out_ref.at[me], send_sem=send_sem.at[k],
                recv_sem=recv_sem.at[me], device_id={axis: lax.rem(me + k, n)},
                device_id_type=MESH_ID)
            copy.start()
            sends.append(copy)
        out_ref[me] = x_ref[...]
        for k in range(1, n):
            src = lax.rem(me + n - k, n)
            pltpu.make_async_remote_copy(
                src_ref=x_ref, dst_ref=out_ref.at[src], send_sem=send_sem.at[k],
                recv_sem=recv_sem.at[src], device_id={axis: src},
                device_id_type=MESH_ID).wait_recv()
        for copy in sends:
            copy.wait_send()

    return pl.pallas_call(
        kernel,
        out_shape=jax.ShapeDtypeStruct((n,) + block.shape, block.dtype),
        in_specs=[pl.BlockSpec(memory_space=pltpu.VMEM)],
        out_specs=pl.BlockSpec(memory_space=pltpu.VMEM),
        scratch_shapes=[pltpu.SemaphoreType.DMA((n,)), pltpu.SemaphoreType.DMA((n,))],
        compiler_params=pltpu.CompilerParams(collective_id=cid, has_side_effects=True),
    )(block)


def peer_reduce_scatter(parts, axis, n, cid, out_dtype):
    def kernel(x_ref, out_ref, held, send_sem, recv_sem):
        me = lax.axis_index(axis)
        _greet(axis, n, me)
        sends = []
        for k in range(1, n):
            dst = lax.rem(me + k, n)
            copy = pltpu.make_async_remote_copy(
                src_ref=x_ref.at[dst], dst_ref=held.at[me], send_sem=send_sem.at[k],
                recv_sem=recv_sem.at[me], device_id={axis: dst},
                device_id_type=MESH_ID)
            copy.start()
            sends.append(copy)
        total = x_ref[me].astype(jnp.float32)
        for k in range(1, n):
            src = lax.rem(me + n - k, n)
            pltpu.make_async_remote_copy(
                src_ref=x_ref.at[src], dst_ref=held.at[src], send_sem=send_sem.at[k],
                recv_sem=recv_sem.at[src], device_id={axis: src},
                device_id_type=MESH_ID).wait_recv()
            total = total + held[src].astype(jnp.float32)
        out_ref[...] = total.astype(out_ref.dtype)
        for copy in sends:
            copy.wait_send()

    return pl.pallas_call(
        kernel,
        out_shape=jax.ShapeDtypeStruct(parts.shape[1:], out_dtype),
        in_specs=[pl.BlockSpec(memory_space=pltpu.VMEM)],
        out_specs=pl.BlockSpec(memory_space=pltpu.VMEM),
        scratch_shapes=[pltpu.VMEM(parts.shape, parts.dtype),
                        pltpu.SemaphoreType.DMA((n,)), pltpu.SemaphoreType.DMA((n,))],
        compiler_params=pltpu.CompilerParams(collective_id=cid, has_side_effects=True),
    )(parts)


def masked_window_attention(queries, keyval, query_win, key_win, heads):
    nq, width = queries.shape
    head_size = width // heads
    scale = 1.0 / float(head_size) ** 0.5

    def kernel(q_ref, kv_ref, qw_ref, kw_ref, out_ref):
        mask = qw_ref[...] == kw_ref[...]
        for h in range(heads):
            cols = slice(h * head_size, (h + 1) * head_size)
            q = q_ref[:, cols]
            k = kv_ref[:, h * head_size:(h + 1) * head_size]
            v = kv_ref[:, width + h * head_size:width + (h + 1) * head_size]
            s = lax.dot_general(q, k, (((1,), (1,)), ((), ())),
                                preferred_element_type=jnp.float32) * scale
            s = jnp.where(mask, s, -jnp.inf)
            w = jnp.exp(s - jnp.max(s, axis=1, keepdims=True))
            p = (w / jnp.sum(w, axis=1, keepdims=True)).astype(jnp.bfloat16)
            out_ref[:, cols] = jnp.dot(p, v, preferred_element_type=jnp.float32).astype(out_ref.dtype)

    return pl.pallas_call(
        kernel,
        out_shape=jax.ShapeDtypeStruct((nq, width), jnp.bfloat16),
        in_specs=[pl.BlockSpec(memory_space=pltpu.VMEM)] * 4,
        out_specs=pl.BlockSpec(memory_space=pltpu.VMEM),
    )(queries, keyval, query_win, key_win)


def chip_pair_gather(block, axis, n, cid):
    nz = n // 2

    def kernel(x_ref, out_ref, send_sem, recv_sem):
        me = lax.axis_index(axis)
        partner = me + 1 - 2 * lax.rem(me, 2)
        peers = [lax.rem(me + 2 * k, n) for k in range(1, nz)]
        barrier = pltpu.get_barrier_semaphore()
        for dev in peers + [partner]:
            pl.semaphore_signal(barrier, inc=1, device_id={axis: dev}, device_id_type=MESH_ID)
        pl.semaphore_wait(barrier, nz)

        def send(src_ref, slot, dev, index):
            copy = pltpu.make_async_remote_copy(
                src_ref=src_ref, dst_ref=out_ref.at[slot], send_sem=send_sem.at[index],
                recv_sem=recv_sem.at[slot], device_id={axis: dev}, device_id_type=MESH_ID)
            copy.start()
            return copy

        def arrive(slot):
            pltpu.make_async_remote_copy(
                src_ref=x_ref, dst_ref=out_ref.at[slot], send_sem=send_sem.at[0],
                recv_sem=recv_sem.at[slot], device_id={axis: slot},
                device_id_type=MESH_ID).wait_recv()

        sends = [send(x_ref, me, dev, i) for i, dev in enumerate(peers)]
        sends.append(send(x_ref, me, partner, nz - 1))
        out_ref[me] = x_ref[...]
        for k in range(1, nz):
            src = lax.rem(me + n - 2 * k, n)
            arrive(src)
            sends.append(send(out_ref.at[src], src, partner, nz - 1 + k))
        for k in range(nz):
            arrive(lax.rem(partner + 2 * k, n))
        for copy in sends:
            copy.wait_send()

    return pl.pallas_call(
        kernel,
        out_shape=jax.ShapeDtypeStruct((n,) + block.shape, block.dtype),
        in_specs=[pl.BlockSpec(memory_space=pltpu.VMEM)],
        out_specs=pl.BlockSpec(memory_space=pltpu.VMEM),
        scratch_shapes=[pltpu.SemaphoreType.DMA((n,)), pltpu.SemaphoreType.DMA((n,))],
        compiler_params=pltpu.CompilerParams(collective_id=cid, has_side_effects=True),
    )(block)


def grid_reduce_scatter(parts, outer, inner, cid):
    slots, n_hi, n_lo, rows, outs = parts.shape
    half = rows // 2

    def kernel(x_ref, out_ref, r1a, r1b, s1a, s1b, r2a, r2b, send_sem, recv_sem):
        hi = lax.axis_index(outer)
        lo = lax.axis_index(inner)
        barrier = pltpu.get_barrier_semaphore()
        for k in range(1, n_lo):
            pl.semaphore_signal(barrier, inc=1, device_id={inner: lax.rem(lo + k, n_lo)},
                                device_id_type=MESH_ID)
        for k in range(1, n_hi):
            pl.semaphore_signal(barrier, inc=1, device_id={outer: lax.rem(hi + k, n_hi)},
                                device_id_type=MESH_ID)
        pl.semaphore_wait(barrier, n_lo + n_hi - 2)

        def send(src_ref, dst_ref, axis, dev, group, k, slot):
            copy = pltpu.make_async_remote_copy(
                src_ref=src_ref, dst_ref=dst_ref, send_sem=send_sem.at[group, k],
                recv_sem=recv_sem.at[group, slot], device_id={axis: dev},
                device_id_type=MESH_ID)
            copy.start()
            return copy

        def arrive(dst_ref, group, slot):
            pltpu.make_async_remote_copy(
                src_ref=dst_ref, dst_ref=dst_ref, send_sem=send_sem.at[group, 0],
                recv_sem=recv_sem.at[group, slot], device_id={inner: lo},
                device_id_type=MESH_ID).wait_recv()

        sends = []
        for k in range(1, n_lo):
            dev = lax.rem(lo + k, n_lo)
            sends.append(send(x_ref.at[:, :, dev, pl.ds(0, half), :], r1a.at[lo], inner, dev, 0, k, lo))
        for k in range(1, n_hi):
            dev = lax.rem(hi + k, n_hi)
            sends.append(send(x_ref.at[:, dev, :, pl.ds(half, half), :], r1b.at[hi], outer, dev, 1, k, hi))

        sources_lo = [lax.rem(lo + n_lo - k, n_lo) for k in range(1, n_lo)]
        sources_hi = [lax.rem(hi + n_hi - k, n_hi) for k in range(1, n_hi)]
        for src in sources_lo:
            arrive(r1a.at[src], 0, src)
        for h in range(n_hi):
            total = x_ref[:, h, lo, pl.ds(0, half), :].astype(jnp.float32)
            for src in sources_lo:
                total = total + r1a[src, :, h].astype(jnp.float32)
            s1a[h] = total.astype(s1a.dtype)
        for k in range(1, n_hi):
            dev = lax.rem(hi + k, n_hi)
            sends.append(send(s1a.at[dev], r2a.at[hi], outer, dev, 2, k, hi))
        for src in sources_hi:
            arrive(r1b.at[src], 1, src)
        for l in range(n_lo):
            total = x_ref[:, hi, l, pl.ds(half, half), :].astype(jnp.float32)
            for src in sources_hi:
                total = total + r1b[src, :, l].astype(jnp.float32)
            s1b[l] = total.astype(s1b.dtype)
        for k in range(1, n_lo):
            dev = lax.rem(lo + k, n_lo)
            sends.append(send(s1b.at[dev], r2b.at[lo], inner, dev, 3, k, lo))

        total = s1a[hi].astype(jnp.float32)
        for src in sources_hi:
            arrive(r2a.at[src], 2, src)
            total = total + r2a[src].astype(jnp.float32)
        out_ref[:, pl.ds(0, half), :] = total
        total = s1b[lo].astype(jnp.float32)
        for src in sources_lo:
            arrive(r2b.at[src], 3, src)
            total = total + r2b[src].astype(jnp.float32)
        out_ref[:, pl.ds(half, half), :] = total
        for copy in sends:
            copy.wait_send()

    most = max(n_hi, n_lo)
    return pl.pallas_call(
        kernel,
        out_shape=jax.ShapeDtypeStruct((slots, rows, outs), jnp.float32),
        in_specs=[pl.BlockSpec(memory_space=pltpu.VMEM)],
        out_specs=pl.BlockSpec(memory_space=pltpu.VMEM),
        scratch_shapes=[
            pltpu.VMEM((n_lo, slots, n_hi, half, outs), parts.dtype),
            pltpu.VMEM((n_hi, slots, n_lo, half, outs), parts.dtype),
            pltpu.VMEM((n_hi, slots, half, outs), parts.dtype),
            pltpu.VMEM((n_lo, slots, half, outs), parts.dtype),
            pltpu.VMEM((n_hi, slots, half, outs), parts.dtype),
            pltpu.VMEM((n_lo, slots, half, outs), parts.dtype),
            pltpu.SemaphoreType.DMA((4, most)),
            pltpu.SemaphoreType.DMA((4, most)),
        ],
        compiler_params=pltpu.CompilerParams(collective_id=cid, has_side_effects=True),
    )(parts)

HEADS = 16
WH = 6
WW = 12


EPS = 1e-05


def padded(array, sides, width, wrap):
    for axis, dim in sides:
        size, length = (lax.axis_size(axis), array.shape[dim])
        up = [(i, (i + 1) % size) for i in range(size if wrap else size - 1)]
        down = [(j, i) for i, j in up]
        last = lax.slice_in_dim(array, length - width, length, axis=dim)
        initial = lax.slice_in_dim(array, 0, width, axis=dim)
        before = lax.ppermute(last, axis, up)
        after = lax.ppermute(initial, axis, down)
        array = jnp.concatenate([before, array, after], axis=dim)
    return array


def layer_norm(values, gain):
    wide = values.astype(jnp.float32)
    average = jnp.mean(wide, axis=-1, keepdims=True)
    centred = wide - average
    variance = jnp.mean(centred * centred, axis=-1, keepdims=True)
    return (centred * lax.rsqrt(variance + EPS) * gain).astype(jnp.bfloat16)


def window_attention(query_ext, keyval, row_valid, heads):
    ext_rows, ext_cols, width = query_ext.shape
    head_size = width // heads
    win_rows = ext_rows // WH
    win_cols = ext_cols // WW

    def split(values, parts):
        shaped = values.reshape(win_rows, WH, win_cols, WW, parts, heads, head_size)
        return shaped.transpose(0, 2, 1, 3, 4, 5, 6).reshape(
            win_rows * win_cols, WH * WW, parts, heads, head_size
        )

    query_win = split(query_ext, 1)[:, :, 0]
    pairs = split(keyval, 2)
    key_win = pairs[:, :, 0]
    value_win = pairs[:, :, 1]
    key_mask = jnp.broadcast_to(
        row_valid.reshape(win_rows, 1, WH, 1), (win_rows, win_cols, WH, WW)
    ).reshape(win_rows * win_cols, WH * WW)
    scores = jnp.einsum(
        "wqhd,wkhd->whqk", query_win, key_win, preferred_element_type=jnp.float32
    ) / math.sqrt(head_size)
    scores = jnp.where(key_mask[:, None, None, :], scores, -jnp.inf)
    peak = jnp.max(scores, axis=-1, keepdims=True)
    weights = jnp.exp(scores - peak)
    probs = (weights / jnp.sum(weights, axis=-1, keepdims=True)).astype(jnp.bfloat16)
    mixed = jnp.einsum("whqk,wkhd->wqhd", probs, value_win, preferred_element_type=jnp.float32)
    return (
        mixed.reshape(win_rows, win_cols, WH, WW, width)
        .transpose(0, 2, 1, 3, 4)
        .reshape(ext_rows, ext_cols, width)
    )


def slot_terms(piece, target_rows, live_cols, level_scale, level_shift, heads_full):
    piece_wide = piece.astype(jnp.float32)
    rows = (
        piece_wide[None] * level_scale[:, None, None, :] + level_shift[:, None, None, :]
    ).astype(jnp.bfloat16)
    predicted = jnp.einsum("krnd,kdo->krno", rows, heads_full, preferred_element_type=jnp.float32)
    errors = ((predicted - target_rows.astype(jnp.float32)) * live_cols[:, None, :, None]).astype(
        jnp.bfloat16
    )
    back_grad = jnp.einsum("krno,kdo->krnd", errors, heads_full, preferred_element_type=jnp.float32)
    piece_grad = jnp.sum(back_grad * level_scale[:, None, None, :], axis=0)
    head_add = jnp.einsum("krnd,krno->kdo", rows, errors, preferred_element_type=jnp.float32)
    return (piece_grad, head_add)


def local(
    patches,
    norm_gain,
    input_proj,
    output_proj,
    level_scale,
    level_shift,
    head_weight,
    targets,
    level_counts,
    tile_dataset,
    slot_level,
):
    band_rows, band_cols, width = patches.shape
    half_rows = WH // 2
    half_cols = WW // 2
    lat_count = lax.axis_size(LAT)
    var_count = lax.axis_size("var")
    lat_place = lax.axis_index(LAT)
    ext_rows = band_rows + WH
    ext_cols = band_cols + WW
    own_normed = layer_norm(patches, norm_gain).reshape(-1, width)
    queries = jnp.dot(own_normed, input_proj[:, :width], preferred_element_type=jnp.float32)
    queries = queries.astype(jnp.bfloat16)
    own_keyval = jnp.dot(own_normed, input_proj[:, width:], preferred_element_type=jnp.float32)
    every = LAT + ("var",)

    def shifted(piece, rows_from, cols_from):
        pairs = []
        for lat in range(lat_count):
            for var in range(var_count):
                source = lat + rows_from
                if 0 <= source < lat_count:
                    pairs.append((source * var_count + (var + cols_from) % var_count, lat * var_count + var))
        return lax.ppermute(piece, every, pairs)

    low, high = patches[band_rows - half_rows :], patches[:half_rows]
    top = jnp.concatenate(
        [shifted(low[:, band_cols - half_cols :], -1, -1), shifted(low, -1, 0),
         shifted(low[:, :half_cols], -1, 1)], axis=1)
    bottom = jnp.concatenate(
        [shifted(high[:, band_cols - half_cols :], 1, -1), shifted(high, 1, 0),
         shifted(high[:, :half_cols], 1, 1)], axis=1)
    left = shifted(patches[:, band_cols - half_cols :], 0, -1)
    right = shifted(patches[:, :half_cols], 0, 1)
    halo = jnp.concatenate(
        [part.reshape(-1, width) for part in (top, bottom, left, right)]
    )

    def ring(grid):
        top, bottom = grid[:half_rows], grid[half_rows + band_rows :]
        middle = grid[half_rows : half_rows + band_rows]
        left, right = middle[:, :half_cols], middle[:, half_cols + band_cols :]
        return jnp.concatenate(
            [part.reshape((-1,) + grid.shape[2:]) for part in (top, bottom, left, right)]
        )

    halo_normed = layer_norm(halo, norm_gain)
    halo_keyval = jnp.dot(halo_normed, input_proj[:, width:], preferred_element_type=jnp.float32)
    keyval = jnp.concatenate([own_keyval, halo_keyval]).astype(jnp.bfloat16)
    global_row = lat_place * band_rows - half_rows + jnp.arange(ext_rows, dtype=jnp.int32)
    row_valid = (global_row >= 0) & (global_row < lat_count * band_rows)
    win_cols = ext_cols // WW
    ext_r = jnp.arange(ext_rows, dtype=jnp.int32)[:, None]
    ext_c = jnp.arange(ext_cols, dtype=jnp.int32)[None, :]
    key_grid = jnp.where(row_valid[:, None], (ext_r // WH) * win_cols + ext_c // WW, -1)
    query_win = key_grid[half_rows : half_rows + band_rows, half_cols : half_cols + band_cols]
    key_win = jnp.concatenate([query_win.reshape(-1), ring(key_grid)])
    attn = masked_window_attention(
        queries,
        keyval,
        query_win.reshape(-1, 1),
        key_win.reshape(1, -1),
        HEADS,
    ).reshape(band_rows, band_cols, width)
    update = jnp.dot(
        attn.reshape(-1, width), output_proj, preferred_element_type=jnp.float32
    ).reshape(band_rows, band_cols, width)
    latent = (patches.astype(jnp.float32) + update).astype(jnp.bfloat16)
    dataset_row = tile_dataset[0]
    dataset_ids = jnp.arange(level_counts.shape[0], dtype=jnp.int32)
    tile_levels = jnp.sum(
        jnp.where(dataset_row[:, None] == dataset_ids[None, :], level_counts[None, :], 0), axis=1
    )
    live_tiles = (slot_level[None, :] < tile_levels[:, None]).astype(jnp.float32)
    heads_full = lax.all_gather(head_weight, LAT, axis=1, tiled=True)
    tile_ids = jnp.arange(var_count, dtype=jnp.int32)
    tiles = chip_pair_gather(latent.reshape(band_rows * band_cols, width), "var", var_count, 1)
    piece = (
        tiles.reshape(var_count, band_rows, band_cols, width)
        .transpose(1, 0, 2, 3)
        .reshape(band_rows, var_count * band_cols, width)
    )
    piece_cols = piece.shape[1]
    column_tile = jnp.arange(piece_cols, dtype=jnp.int32) // band_cols
    onehot = (column_tile[:, None] == tile_ids[None, :]).astype(jnp.float32)
    column_live = jnp.dot(onehot, live_tiles)
    piece_grad, head_add = slot_terms(
        piece, targets, column_live.T, level_scale, level_shift, heads_full
    )
    latent_terms = piece_grad
    latent_terms, head_terms = (latent_terms, head_add)
    grad_latent = lax.psum_scatter(
        latent_terms.astype(jnp.bfloat16), "var", scatter_dimension=1, tiled=True
    )
    head_terms = head_terms * (1.0 / math.sqrt(lat_count * band_rows * var_count * band_cols))
    outer, inner = lax.axis_size(LAT[0]), lax.axis_size(LAT[1])
    slots, outs = head_terms.shape[0], head_terms.shape[2]
    share_rows = width // lat_count
    head_parts = head_terms.astype(jnp.bfloat16).reshape(slots, outer, inner, share_rows, outs)
    grad_head = grid_reduce_scatter(head_parts, LAT[0], LAT[1], 3)
    return (latent, grad_latent, grad_head)


def solution(mesh):
    in_specs = (
        P(LAT, "var", None),
        P(),
        P(),
        P(),
        P("var", None),
        P("var", None),
        P("var", LAT, None),
        P("var", LAT, None, None),
        P(),
        P(LAT, None),
        P("var"),
    )
    out_specs = (P(LAT, "var", None), P(LAT, "var", None), P("var", LAT, None))
    lat_size = mesh.shape["lat"]
    inner = 4 if lat_size % 4 == 0 else 1
    grid = Mesh(
        mesh.devices.reshape(lat_size // inner, inner, mesh.shape["var"]), LAT + ("var",)
    )
    return jax.shard_map(local, mesh=grid, in_specs=in_specs, out_specs=out_specs, check_vma=False)
```

```python
import math

import jax
import jax.numpy as jnp
from jax import lax
from jax.experimental import pallas as pl
from jax.experimental.pallas import tpu as pltpu
from jax.sharding import Mesh, PartitionSpec as P

MESH_ID = pl.DeviceIdType.MESH
LAT = ("lat_hi", "lat_lo")


def _greet(axis, n, me):
    barrier = pltpu.get_barrier_semaphore()
    for k in range(1, n):
        pl.semaphore_signal(barrier, inc=1, device_id={axis: lax.rem(me + k, n)},
                            device_id_type=MESH_ID)
    pl.semaphore_wait(barrier, n - 1)


def peer_gather(block, axis, n, cid):
    def kernel(x_ref, out_ref, send_sem, recv_sem):
        me = lax.axis_index(axis)
        _greet(axis, n, me)
        sends = []
        for k in range(1, n):
            copy = pltpu.make_async_remote_copy(
                src_ref=x_ref, dst_ref=out_ref.at[me], send_sem=send_sem.at[k],
                recv_sem=recv_sem.at[me], device_id={axis: lax.rem(me + k, n)},
                device_id_type=MESH_ID)
            copy.start()
            sends.append(copy)
        out_ref[me] = x_ref[...]
        for k in range(1, n):
            src = lax.rem(me + n - k, n)
            pltpu.make_async_remote_copy(
                src_ref=x_ref, dst_ref=out_ref.at[src], send_sem=send_sem.at[k],
                recv_sem=recv_sem.at[src], device_id={axis: src},
                device_id_type=MESH_ID).wait_recv()
        for copy in sends:
            copy.wait_send()

    return pl.pallas_call(
        kernel,
        out_shape=jax.ShapeDtypeStruct((n,) + block.shape, block.dtype),
        in_specs=[pl.BlockSpec(memory_space=pltpu.VMEM)],
        out_specs=pl.BlockSpec(memory_space=pltpu.VMEM),
        scratch_shapes=[pltpu.SemaphoreType.DMA((n,)), pltpu.SemaphoreType.DMA((n,))],
        compiler_params=pltpu.CompilerParams(collective_id=cid, has_side_effects=True),
    )(block)


def peer_reduce_scatter(parts, axis, n, cid, out_dtype):
    def kernel(x_ref, out_ref, held, send_sem, recv_sem):
        me = lax.axis_index(axis)
        _greet(axis, n, me)
        sends = []
        for k in range(1, n):
            dst = lax.rem(me + k, n)
            copy = pltpu.make_async_remote_copy(
                src_ref=x_ref.at[dst], dst_ref=held.at[me], send_sem=send_sem.at[k],
                recv_sem=recv_sem.at[me], device_id={axis: dst},
                device_id_type=MESH_ID)
            copy.start()
            sends.append(copy)
        total = x_ref[me].astype(jnp.float32)
        for k in range(1, n):
            src = lax.rem(me + n - k, n)
            pltpu.make_async_remote_copy(
                src_ref=x_ref.at[src], dst_ref=held.at[src], send_sem=send_sem.at[k],
                recv_sem=recv_sem.at[src], device_id={axis: src},
                device_id_type=MESH_ID).wait_recv()
            total = total + held[src].astype(jnp.float32)
        out_ref[...] = total.astype(out_ref.dtype)
        for copy in sends:
            copy.wait_send()

    return pl.pallas_call(
        kernel,
        out_shape=jax.ShapeDtypeStruct(parts.shape[1:], out_dtype),
        in_specs=[pl.BlockSpec(memory_space=pltpu.VMEM)],
        out_specs=pl.BlockSpec(memory_space=pltpu.VMEM),
        scratch_shapes=[pltpu.VMEM(parts.shape, parts.dtype),
                        pltpu.SemaphoreType.DMA((n,)), pltpu.SemaphoreType.DMA((n,))],
        compiler_params=pltpu.CompilerParams(collective_id=cid, has_side_effects=True),
    )(parts)


def masked_window_attention(queries, keyval, query_win, key_win, heads):
    nq, width = queries.shape
    head_size = width // heads
    scale = 1.0 / float(head_size) ** 0.5

    def kernel(q_ref, kv_ref, qw_ref, kw_ref, out_ref):
        mask = qw_ref[...] == kw_ref[...]
        for h in range(heads):
            cols = slice(h * head_size, (h + 1) * head_size)
            q = q_ref[:, cols]
            k = kv_ref[:, h * head_size:(h + 1) * head_size]
            v = kv_ref[:, width + h * head_size:width + (h + 1) * head_size]
            s = lax.dot_general(q, k, (((1,), (1,)), ((), ())),
                                preferred_element_type=jnp.float32) * scale
            s = jnp.where(mask, s, -jnp.inf)
            w = jnp.exp(s - jnp.max(s, axis=1, keepdims=True))
            p = (w / jnp.sum(w, axis=1, keepdims=True)).astype(jnp.bfloat16)
            out_ref[:, cols] = jnp.dot(p, v, preferred_element_type=jnp.float32).astype(out_ref.dtype)

    return pl.pallas_call(
        kernel,
        out_shape=jax.ShapeDtypeStruct((nq, width), jnp.bfloat16),
        in_specs=[pl.BlockSpec(memory_space=pltpu.VMEM)] * 4,
        out_specs=pl.BlockSpec(memory_space=pltpu.VMEM),
    )(queries, keyval, query_win, key_win)


def chip_pair_gather(block, axis, n, cid):
    nz = n // 2

    def kernel(x_ref, out_ref, send_sem, recv_sem):
        me = lax.axis_index(axis)
        partner = me + 1 - 2 * lax.rem(me, 2)
        peers = [lax.rem(me + 2 * k, n) for k in range(1, nz)]
        barrier = pltpu.get_barrier_semaphore()
        for dev in peers + [partner]:
            pl.semaphore_signal(barrier, inc=1, device_id={axis: dev}, device_id_type=MESH_ID)
        pl.semaphore_wait(barrier, nz)

        def send(src_ref, slot, dev, index):
            copy = pltpu.make_async_remote_copy(
                src_ref=src_ref, dst_ref=out_ref.at[slot], send_sem=send_sem.at[index],
                recv_sem=recv_sem.at[slot], device_id={axis: dev}, device_id_type=MESH_ID)
            copy.start()
            return copy

        def arrive(slot):
            pltpu.make_async_remote_copy(
                src_ref=x_ref, dst_ref=out_ref.at[slot], send_sem=send_sem.at[0],
                recv_sem=recv_sem.at[slot], device_id={axis: slot},
                device_id_type=MESH_ID).wait_recv()

        sends = [send(x_ref, me, dev, i) for i, dev in enumerate(peers)]
        sends.append(send(x_ref, me, partner, nz - 1))
        out_ref[me] = x_ref[...]
        for k in range(1, nz):
            src = lax.rem(me + n - 2 * k, n)
            arrive(src)
            sends.append(send(out_ref.at[src], src, partner, nz - 1 + k))
        for k in range(nz):
            arrive(lax.rem(partner + 2 * k, n))
        for copy in sends:
            copy.wait_send()

    return pl.pallas_call(
        kernel,
        out_shape=jax.ShapeDtypeStruct((n,) + block.shape, block.dtype),
        in_specs=[pl.BlockSpec(memory_space=pltpu.VMEM)],
        out_specs=pl.BlockSpec(memory_space=pltpu.VMEM),
        scratch_shapes=[pltpu.SemaphoreType.DMA((n,)), pltpu.SemaphoreType.DMA((n,))],
        compiler_params=pltpu.CompilerParams(collective_id=cid, has_side_effects=True),
    )(block)


def grid_reduce_scatter(parts, outer, inner, cid):
    slots, n_hi, n_lo, rows, outs = parts.shape
    half = rows // 2

    def kernel(x_ref, out_ref, r1a, r1b, s1a, s1b, r2a, r2b, send_sem, recv_sem):
        hi = lax.axis_index(outer)
        lo = lax.axis_index(inner)
        barrier = pltpu.get_barrier_semaphore()
        for k in range(1, n_lo):
            pl.semaphore_signal(barrier, inc=1, device_id={inner: lax.rem(lo + k, n_lo)},
                                device_id_type=MESH_ID)
        for k in range(1, n_hi):
            pl.semaphore_signal(barrier, inc=1, device_id={outer: lax.rem(hi + k, n_hi)},
                                device_id_type=MESH_ID)
        pl.semaphore_wait(barrier, n_lo + n_hi - 2)

        def send(src_ref, dst_ref, axis, dev, group, k, slot):
            copy = pltpu.make_async_remote_copy(
                src_ref=src_ref, dst_ref=dst_ref, send_sem=send_sem.at[group, k],
                recv_sem=recv_sem.at[group, slot], device_id={axis: dev},
                device_id_type=MESH_ID)
            copy.start()
            return copy

        def arrive(dst_ref, group, slot):
            pltpu.make_async_remote_copy(
                src_ref=dst_ref, dst_ref=dst_ref, send_sem=send_sem.at[group, 0],
                recv_sem=recv_sem.at[group, slot], device_id={inner: lo},
                device_id_type=MESH_ID).wait_recv()

        sends = []
        for k in range(1, n_lo):
            dev = lax.rem(lo + k, n_lo)
            sends.append(send(x_ref.at[:, :, dev, pl.ds(0, half), :], r1a.at[lo], inner, dev, 0, k, lo))
        for k in range(1, n_hi):
            dev = lax.rem(hi + k, n_hi)
            sends.append(send(x_ref.at[:, dev, :, pl.ds(half, half), :], r1b.at[hi], outer, dev, 1, k, hi))

        sources_lo = [lax.rem(lo + n_lo - k, n_lo) for k in range(1, n_lo)]
        sources_hi = [lax.rem(hi + n_hi - k, n_hi) for k in range(1, n_hi)]
        for src in sources_lo:
            arrive(r1a.at[src], 0, src)
        for h in range(n_hi):
            total = x_ref[:, h, lo, pl.ds(0, half), :].astype(jnp.float32)
            for src in sources_lo:
                total = total + r1a[src, :, h].astype(jnp.float32)
            s1a[h] = total.astype(s1a.dtype)
        for k in range(1, n_hi):
            dev = lax.rem(hi + k, n_hi)
            sends.append(send(s1a.at[dev], r2a.at[hi], outer, dev, 2, k, hi))
        for src in sources_hi:
            arrive(r1b.at[src], 1, src)
        for l in range(n_lo):
            total = x_ref[:, hi, l, pl.ds(half, half), :].astype(jnp.float32)
            for src in sources_hi:
                total = total + r1b[src, :, l].astype(jnp.float32)
            s1b[l] = total.astype(s1b.dtype)
        for k in range(1, n_lo):
            dev = lax.rem(lo + k, n_lo)
            sends.append(send(s1b.at[dev], r2b.at[lo], inner, dev, 3, k, lo))

        total = s1a[hi].astype(jnp.float32)
        for src in sources_hi:
            arrive(r2a.at[src], 2, src)
            total = total + r2a[src].astype(jnp.float32)
        out_ref[:, pl.ds(0, half), :] = total
        total = s1b[lo].astype(jnp.float32)
        for src in sources_lo:
            arrive(r2b.at[src], 3, src)
            total = total + r2b[src].astype(jnp.float32)
        out_ref[:, pl.ds(half, half), :] = total
        for copy in sends:
            copy.wait_send()

    most = max(n_hi, n_lo)
    return pl.pallas_call(
        kernel,
        out_shape=jax.ShapeDtypeStruct((slots, rows, outs), jnp.float32),
        in_specs=[pl.BlockSpec(memory_space=pltpu.VMEM)],
        out_specs=pl.BlockSpec(memory_space=pltpu.VMEM),
        scratch_shapes=[
            pltpu.VMEM((n_lo, slots, n_hi, half, outs), parts.dtype),
            pltpu.VMEM((n_hi, slots, n_lo, half, outs), parts.dtype),
            pltpu.VMEM((n_hi, slots, half, outs), parts.dtype),
            pltpu.VMEM((n_lo, slots, half, outs), parts.dtype),
            pltpu.VMEM((n_hi, slots, half, outs), parts.dtype),
            pltpu.VMEM((n_lo, slots, half, outs), parts.dtype),
            pltpu.SemaphoreType.DMA((4, most)),
            pltpu.SemaphoreType.DMA((4, most)),
        ],
        compiler_params=pltpu.CompilerParams(collective_id=cid, has_side_effects=True),
    )(parts)


def chip_ring_gather(block, axis, n, cid):
    rows = block.shape[0]
    cut = rows // 32 * 16

    def kernel(x_ref, out_ref, send_sem, recv_sem):
        me = lax.axis_index(axis)
        partner = me + 1 - 2 * lax.rem(me, 2)
        up, down, far = lax.rem(me + 2, n), lax.rem(me + n - 2, n), lax.rem(me + 4, n)
        barrier = pltpu.get_barrier_semaphore()
        for dev in (up, down, partner):
            pl.semaphore_signal(barrier, inc=1, device_id={axis: dev}, device_id_type=MESH_ID)
        pl.semaphore_wait(barrier, 3)
        head, tail = pl.ds(0, cut), pl.ds(cut, rows - cut)

        def send(src_ref, slot, part, dev, index, sem_col):
            copy = pltpu.make_async_remote_copy(
                src_ref=src_ref, dst_ref=out_ref.at[slot, part], send_sem=send_sem.at[index],
                recv_sem=recv_sem.at[slot, sem_col], device_id={axis: dev},
                device_id_type=MESH_ID)
            copy.start()
            return copy

        def arrive(slot, part, sem_col):
            pltpu.make_async_remote_copy(
                src_ref=out_ref.at[slot, part], dst_ref=out_ref.at[slot, part],
                send_sem=send_sem.at[0], recv_sem=recv_sem.at[slot, sem_col],
                device_id={axis: slot}, device_id_type=MESH_ID).wait_recv()

        whole = pl.ds(0, rows)
        sends = [send(x_ref, me, whole, up, 0, 0), send(x_ref, me, whole, down, 1, 0),
                 send(x_ref, me, whole, partner, 2, 0)]
        out_ref[me] = x_ref[...]
        arrive(down, whole, 0)
        sends.append(send(out_ref.at[down, head], down, head, up, 3, 0))
        sends.append(send(out_ref.at[down], down, whole, partner, 4, 0))
        arrive(up, whole, 0)
        sends.append(send(out_ref.at[up, tail], up, tail, down, 5, 1))
        sends.append(send(out_ref.at[up], up, whole, partner, 6, 0))
        arrive(far, head, 0)
        arrive(far, tail, 1)
        sends.append(send(out_ref.at[far], far, whole, partner, 7, 0))
        for k in range(4):
            arrive(lax.rem(partner + 2 * k, n), whole, 0)
        for copy in sends:
            copy.wait_send()

    return pl.pallas_call(
        kernel,
        out_shape=jax.ShapeDtypeStruct((n,) + block.shape, block.dtype),
        in_specs=[pl.BlockSpec(memory_space=pltpu.VMEM)],
        out_specs=pl.BlockSpec(memory_space=pltpu.VMEM),
        scratch_shapes=[pltpu.SemaphoreType.DMA((8,)), pltpu.SemaphoreType.DMA((n, 2))],
        compiler_params=pltpu.CompilerParams(collective_id=cid, has_side_effects=True),
    )(block)

HEADS = 16
WH = 6
WW = 12


EPS = 1e-05


def padded(array, sides, width, wrap):
    for axis, dim in sides:
        size, length = (lax.axis_size(axis), array.shape[dim])
        up = [(i, (i + 1) % size) for i in range(size if wrap else size - 1)]
        down = [(j, i) for i, j in up]
        last = lax.slice_in_dim(array, length - width, length, axis=dim)
        initial = lax.slice_in_dim(array, 0, width, axis=dim)
        before = lax.ppermute(last, axis, up)
        after = lax.ppermute(initial, axis, down)
        array = jnp.concatenate([before, array, after], axis=dim)
    return array


def layer_norm(values, gain):
    wide = values.astype(jnp.float32)
    average = jnp.mean(wide, axis=-1, keepdims=True)
    centred = wide - average
    variance = jnp.mean(centred * centred, axis=-1, keepdims=True)
    return (centred * lax.rsqrt(variance + EPS) * gain).astype(jnp.bfloat16)


def window_attention(query_ext, keyval, row_valid, heads):
    ext_rows, ext_cols, width = query_ext.shape
    head_size = width // heads
    win_rows = ext_rows // WH
    win_cols = ext_cols // WW

    def split(values, parts):
        shaped = values.reshape(win_rows, WH, win_cols, WW, parts, heads, head_size)
        return shaped.transpose(0, 2, 1, 3, 4, 5, 6).reshape(
            win_rows * win_cols, WH * WW, parts, heads, head_size
        )

    query_win = split(query_ext, 1)[:, :, 0]
    pairs = split(keyval, 2)
    key_win = pairs[:, :, 0]
    value_win = pairs[:, :, 1]
    key_mask = jnp.broadcast_to(
        row_valid.reshape(win_rows, 1, WH, 1), (win_rows, win_cols, WH, WW)
    ).reshape(win_rows * win_cols, WH * WW)
    scores = jnp.einsum(
        "wqhd,wkhd->whqk", query_win, key_win, preferred_element_type=jnp.float32
    ) / math.sqrt(head_size)
    scores = jnp.where(key_mask[:, None, None, :], scores, -jnp.inf)
    peak = jnp.max(scores, axis=-1, keepdims=True)
    weights = jnp.exp(scores - peak)
    probs = (weights / jnp.sum(weights, axis=-1, keepdims=True)).astype(jnp.bfloat16)
    mixed = jnp.einsum("whqk,wkhd->wqhd", probs, value_win, preferred_element_type=jnp.float32)
    return (
        mixed.reshape(win_rows, win_cols, WH, WW, width)
        .transpose(0, 2, 1, 3, 4)
        .reshape(ext_rows, ext_cols, width)
    )


def slot_terms(piece, target_rows, live_cols, level_scale, level_shift, heads_full):
    piece_wide = piece.astype(jnp.float32)
    rows = (
        piece_wide[None] * level_scale[:, None, None, :] + level_shift[:, None, None, :]
    ).astype(jnp.bfloat16)
    predicted = jnp.einsum("krnd,kdo->krno", rows, heads_full, preferred_element_type=jnp.float32)
    errors = ((predicted - target_rows.astype(jnp.float32)) * live_cols[:, None, :, None]).astype(
        jnp.bfloat16
    )
    back_grad = jnp.einsum("krno,kdo->krnd", errors, heads_full, preferred_element_type=jnp.float32)
    piece_grad = jnp.sum(back_grad * level_scale[:, None, None, :], axis=0)
    head_add = jnp.einsum("krnd,krno->kdo", rows, errors, preferred_element_type=jnp.float32)
    return (piece_grad, head_add)


def local(
    patches,
    norm_gain,
    input_proj,
    output_proj,
    level_scale,
    level_shift,
    head_weight,
    targets,
    level_counts,
    tile_dataset,
    slot_level,
):
    band_rows, band_cols, width = patches.shape
    half_rows = WH // 2
    half_cols = WW // 2
    lat_count = lax.axis_size(LAT)
    var_count = lax.axis_size("var")
    lat_place = lax.axis_index(LAT)
    ext_rows = band_rows + WH
    ext_cols = band_cols + WW
    extended = padded(patches, ((LAT, 0),), half_rows, False)
    extended = padded(extended, (("var", 1),), half_cols, True)
    normed_ext = layer_norm(extended, norm_gain)
    keyval = jnp.dot(
        normed_ext.reshape(-1, width), input_proj[:, width:], preferred_element_type=jnp.float32
    )
    keyval = keyval.astype(jnp.bfloat16).reshape(ext_rows, ext_cols, 2 * width)
    normed = normed_ext[half_rows : half_rows + band_rows, half_cols : half_cols + band_cols]
    queries = jnp.dot(
        normed.reshape(-1, width), input_proj[:, :width], preferred_element_type=jnp.float32
    )
    queries = queries.astype(jnp.bfloat16)
    global_row = lat_place * band_rows - half_rows + jnp.arange(ext_rows, dtype=jnp.int32)
    row_valid = (global_row >= 0) & (global_row < lat_count * band_rows)
    win_cols = ext_cols // WW
    ext_r = jnp.arange(ext_rows, dtype=jnp.int32)[:, None]
    ext_c = jnp.arange(ext_cols, dtype=jnp.int32)[None, :]
    key_win = jnp.where(row_valid[:, None], (ext_r // WH) * win_cols + ext_c // WW, -1)
    own_r = ext_r[half_rows : half_rows + band_rows]
    own_c = ext_c[:, half_cols : half_cols + band_cols]
    query_win = (own_r // WH) * win_cols + own_c // WW
    attn = masked_window_attention(
        queries,
        keyval.reshape(ext_rows * ext_cols, 2 * width),
        query_win.reshape(-1, 1),
        key_win.reshape(1, -1),
        HEADS,
    ).reshape(band_rows, band_cols, width)
    update = jnp.dot(
        attn.reshape(-1, width), output_proj, preferred_element_type=jnp.float32
    ).reshape(band_rows, band_cols, width)
    latent = (patches.astype(jnp.float32) + update).astype(jnp.bfloat16)
    dataset_row = tile_dataset[0]
    dataset_ids = jnp.arange(level_counts.shape[0], dtype=jnp.int32)
    tile_levels = jnp.sum(
        jnp.where(dataset_row[:, None] == dataset_ids[None, :], level_counts[None, :], 0), axis=1
    )
    live_tiles = (slot_level[None, :] < tile_levels[:, None]).astype(jnp.float32)
    heads_full = lax.all_gather(head_weight, LAT, axis=1, tiled=True)
    tile_ids = jnp.arange(var_count, dtype=jnp.int32)
    gather = chip_ring_gather if var_count == 8 else chip_pair_gather
    tiles = gather(latent.reshape(band_rows * band_cols, width), "var", var_count, 1)
    piece = (
        tiles.reshape(var_count, band_rows, band_cols, width)
        .transpose(1, 0, 2, 3)
        .reshape(band_rows, var_count * band_cols, width)
    )
    piece_cols = piece.shape[1]
    column_tile = jnp.arange(piece_cols, dtype=jnp.int32) // band_cols
    onehot = (column_tile[:, None] == tile_ids[None, :]).astype(jnp.float32)
    column_live = jnp.dot(onehot, live_tiles)
    piece_grad, head_add = slot_terms(
        piece, targets, column_live.T, level_scale, level_shift, heads_full
    )
    latent_terms = piece_grad
    latent_terms, head_terms = (latent_terms, head_add)
    grad_latent = lax.psum_scatter(
        latent_terms.astype(jnp.bfloat16), "var", scatter_dimension=1, tiled=True
    )
    head_terms = head_terms * (1.0 / math.sqrt(lat_count * band_rows * var_count * band_cols))
    outer, inner = lax.axis_size(LAT[0]), lax.axis_size(LAT[1])
    slots, outs = head_terms.shape[0], head_terms.shape[2]
    share_rows = width // lat_count
    head_parts = head_terms.astype(jnp.bfloat16).reshape(slots, outer, inner, share_rows, outs)
    grad_head = grid_reduce_scatter(head_parts, LAT[0], LAT[1], 3)
    return (latent, grad_latent, grad_head)


def solution(mesh):
    in_specs = (
        P(LAT, "var", None),
        P(),
        P(),
        P(),
        P("var", None),
        P("var", None),
        P("var", LAT, None),
        P("var", LAT, None, None),
        P(),
        P(LAT, None),
        P("var"),
    )
    out_specs = (P(LAT, "var", None), P(LAT, "var", None), P("var", LAT, None))
    lat_size = mesh.shape["lat"]
    inner = 4 if lat_size % 4 == 0 else 1
    grid = Mesh(
        mesh.devices.reshape(lat_size // inner, inner, mesh.shape["var"]), LAT + ("var",)
    )
    return jax.shard_map(local, mesh=grid, in_specs=in_specs, out_specs=out_specs, check_vma=False)
```

```python
import math

import jax
import jax.numpy as jnp
from jax import lax
from jax.experimental import pallas as pl
from jax.experimental.pallas import tpu as pltpu
from jax.sharding import Mesh, PartitionSpec as P

MESH_ID = pl.DeviceIdType.MESH
LAT = ("lat_hi", "lat_lo")


def _greet(axis, n, me):
    barrier = pltpu.get_barrier_semaphore()
    for k in range(1, n):
        pl.semaphore_signal(barrier, inc=1, device_id={axis: lax.rem(me + k, n)},
                            device_id_type=MESH_ID)
    pl.semaphore_wait(barrier, n - 1)


def peer_gather(block, axis, n, cid):
    def kernel(x_ref, out_ref, send_sem, recv_sem):
        me = lax.axis_index(axis)
        _greet(axis, n, me)
        sends = []
        for k in range(1, n):
            copy = pltpu.make_async_remote_copy(
                src_ref=x_ref, dst_ref=out_ref.at[me], send_sem=send_sem.at[k],
                recv_sem=recv_sem.at[me], device_id={axis: lax.rem(me + k, n)},
                device_id_type=MESH_ID)
            copy.start()
            sends.append(copy)
        out_ref[me] = x_ref[...]
        for k in range(1, n):
            src = lax.rem(me + n - k, n)
            pltpu.make_async_remote_copy(
                src_ref=x_ref, dst_ref=out_ref.at[src], send_sem=send_sem.at[k],
                recv_sem=recv_sem.at[src], device_id={axis: src},
                device_id_type=MESH_ID).wait_recv()
        for copy in sends:
            copy.wait_send()

    return pl.pallas_call(
        kernel,
        out_shape=jax.ShapeDtypeStruct((n,) + block.shape, block.dtype),
        in_specs=[pl.BlockSpec(memory_space=pltpu.VMEM)],
        out_specs=pl.BlockSpec(memory_space=pltpu.VMEM),
        scratch_shapes=[pltpu.SemaphoreType.DMA((n,)), pltpu.SemaphoreType.DMA((n,))],
        compiler_params=pltpu.CompilerParams(collective_id=cid, has_side_effects=True),
    )(block)


def peer_reduce_scatter(parts, axis, n, cid, out_dtype):
    def kernel(x_ref, out_ref, held, send_sem, recv_sem):
        me = lax.axis_index(axis)
        _greet(axis, n, me)
        sends = []
        for k in range(1, n):
            dst = lax.rem(me + k, n)
            copy = pltpu.make_async_remote_copy(
                src_ref=x_ref.at[dst], dst_ref=held.at[me], send_sem=send_sem.at[k],
                recv_sem=recv_sem.at[me], device_id={axis: dst},
                device_id_type=MESH_ID)
            copy.start()
            sends.append(copy)
        total = x_ref[me].astype(jnp.float32)
        for k in range(1, n):
            src = lax.rem(me + n - k, n)
            pltpu.make_async_remote_copy(
                src_ref=x_ref.at[src], dst_ref=held.at[src], send_sem=send_sem.at[k],
                recv_sem=recv_sem.at[src], device_id={axis: src},
                device_id_type=MESH_ID).wait_recv()
            total = total + held[src].astype(jnp.float32)
        out_ref[...] = total.astype(out_ref.dtype)
        for copy in sends:
            copy.wait_send()

    return pl.pallas_call(
        kernel,
        out_shape=jax.ShapeDtypeStruct(parts.shape[1:], out_dtype),
        in_specs=[pl.BlockSpec(memory_space=pltpu.VMEM)],
        out_specs=pl.BlockSpec(memory_space=pltpu.VMEM),
        scratch_shapes=[pltpu.VMEM(parts.shape, parts.dtype),
                        pltpu.SemaphoreType.DMA((n,)), pltpu.SemaphoreType.DMA((n,))],
        compiler_params=pltpu.CompilerParams(collective_id=cid, has_side_effects=True),
    )(parts)


def masked_window_attention(queries, keyval, query_win, key_win, heads):
    nq, width = queries.shape
    head_size = width // heads
    scale = 1.0 / float(head_size) ** 0.5

    def kernel(q_ref, kv_ref, qw_ref, kw_ref, out_ref):
        mask = qw_ref[...] == kw_ref[...]
        for h in range(heads):
            cols = slice(h * head_size, (h + 1) * head_size)
            q = q_ref[:, cols]
            k = kv_ref[:, h * head_size:(h + 1) * head_size]
            v = kv_ref[:, width + h * head_size:width + (h + 1) * head_size]
            s = lax.dot_general(q, k, (((1,), (1,)), ((), ())),
                                preferred_element_type=jnp.float32) * scale
            s = jnp.where(mask, s, -jnp.inf)
            w = jnp.exp(s - jnp.max(s, axis=1, keepdims=True))
            p = (w / jnp.sum(w, axis=1, keepdims=True)).astype(jnp.bfloat16)
            out_ref[:, cols] = jnp.dot(p, v, preferred_element_type=jnp.float32).astype(out_ref.dtype)

    return pl.pallas_call(
        kernel,
        out_shape=jax.ShapeDtypeStruct((nq, width), jnp.bfloat16),
        in_specs=[pl.BlockSpec(memory_space=pltpu.VMEM)] * 4,
        out_specs=pl.BlockSpec(memory_space=pltpu.VMEM),
    )(queries, keyval, query_win, key_win)


def chip_pair_gather(block, axis, n, cid):
    nz = n // 2

    def kernel(x_ref, out_ref, send_sem, recv_sem):
        me = lax.axis_index(axis)
        partner = me + 1 - 2 * lax.rem(me, 2)
        peers = [lax.rem(me + 2 * k, n) for k in range(1, nz)]
        barrier = pltpu.get_barrier_semaphore()
        for dev in peers + [partner]:
            pl.semaphore_signal(barrier, inc=1, device_id={axis: dev}, device_id_type=MESH_ID)
        pl.semaphore_wait(barrier, nz)

        def send(src_ref, slot, dev, index):
            copy = pltpu.make_async_remote_copy(
                src_ref=src_ref, dst_ref=out_ref.at[slot], send_sem=send_sem.at[index],
                recv_sem=recv_sem.at[slot], device_id={axis: dev}, device_id_type=MESH_ID)
            copy.start()
            return copy

        def arrive(slot):
            pltpu.make_async_remote_copy(
                src_ref=x_ref, dst_ref=out_ref.at[slot], send_sem=send_sem.at[0],
                recv_sem=recv_sem.at[slot], device_id={axis: slot},
                device_id_type=MESH_ID).wait_recv()

        sends = [send(x_ref, me, dev, i) for i, dev in enumerate(peers)]
        sends.append(send(x_ref, me, partner, nz - 1))
        out_ref[me] = x_ref[...]
        for k in range(1, nz):
            src = lax.rem(me + n - 2 * k, n)
            arrive(src)
            sends.append(send(out_ref.at[src], src, partner, nz - 1 + k))
        for k in range(nz):
            arrive(lax.rem(partner + 2 * k, n))
        for copy in sends:
            copy.wait_send()

    return pl.pallas_call(
        kernel,
        out_shape=jax.ShapeDtypeStruct((n,) + block.shape, block.dtype),
        in_specs=[pl.BlockSpec(memory_space=pltpu.VMEM)],
        out_specs=pl.BlockSpec(memory_space=pltpu.VMEM),
        scratch_shapes=[pltpu.SemaphoreType.DMA((n,)), pltpu.SemaphoreType.DMA((n,))],
        compiler_params=pltpu.CompilerParams(collective_id=cid, has_side_effects=True),
    )(block)


def grid_reduce_scatter(parts, outer, inner, cid):
    slots, n_hi, n_lo, rows, outs = parts.shape
    half = rows // 2

    def kernel(x_ref, out_ref, r1a, r1b, s1a, s1b, r2a, r2b, send_sem, recv_sem):
        hi = lax.axis_index(outer)
        lo = lax.axis_index(inner)
        barrier = pltpu.get_barrier_semaphore()
        for k in range(1, n_lo):
            pl.semaphore_signal(barrier, inc=1, device_id={inner: lax.rem(lo + k, n_lo)},
                                device_id_type=MESH_ID)
        for k in range(1, n_hi):
            pl.semaphore_signal(barrier, inc=1, device_id={outer: lax.rem(hi + k, n_hi)},
                                device_id_type=MESH_ID)
        pl.semaphore_wait(barrier, n_lo + n_hi - 2)

        def send(src_ref, dst_ref, axis, dev, group, k, slot):
            copy = pltpu.make_async_remote_copy(
                src_ref=src_ref, dst_ref=dst_ref, send_sem=send_sem.at[group, k],
                recv_sem=recv_sem.at[group, slot], device_id={axis: dev},
                device_id_type=MESH_ID)
            copy.start()
            return copy

        def arrive(dst_ref, group, slot):
            pltpu.make_async_remote_copy(
                src_ref=dst_ref, dst_ref=dst_ref, send_sem=send_sem.at[group, 0],
                recv_sem=recv_sem.at[group, slot], device_id={inner: lo},
                device_id_type=MESH_ID).wait_recv()

        sends = []
        for k in range(1, n_lo):
            dev = lax.rem(lo + k, n_lo)
            sends.append(send(x_ref.at[:, :, dev, pl.ds(0, half), :], r1a.at[lo], inner, dev, 0, k, lo))
        for k in range(1, n_hi):
            dev = lax.rem(hi + k, n_hi)
            sends.append(send(x_ref.at[:, dev, :, pl.ds(half, half), :], r1b.at[hi], outer, dev, 1, k, hi))

        sources_lo = [lax.rem(lo + n_lo - k, n_lo) for k in range(1, n_lo)]
        sources_hi = [lax.rem(hi + n_hi - k, n_hi) for k in range(1, n_hi)]
        for src in sources_lo:
            arrive(r1a.at[src], 0, src)
        for h in range(n_hi):
            total = x_ref[:, h, lo, pl.ds(0, half), :].astype(jnp.float32)
            for src in sources_lo:
                total = total + r1a[src, :, h].astype(jnp.float32)
            s1a[h] = total.astype(s1a.dtype)
        for k in range(1, n_hi):
            dev = lax.rem(hi + k, n_hi)
            sends.append(send(s1a.at[dev], r2a.at[hi], outer, dev, 2, k, hi))
        for src in sources_hi:
            arrive(r1b.at[src], 1, src)
        for l in range(n_lo):
            total = x_ref[:, hi, l, pl.ds(half, half), :].astype(jnp.float32)
            for src in sources_hi:
                total = total + r1b[src, :, l].astype(jnp.float32)
            s1b[l] = total.astype(s1b.dtype)
        for k in range(1, n_lo):
            dev = lax.rem(lo + k, n_lo)
            sends.append(send(s1b.at[dev], r2b.at[lo], inner, dev, 3, k, lo))

        total = s1a[hi].astype(jnp.float32)
        for src in sources_hi:
            arrive(r2a.at[src], 2, src)
            total = total + r2a[src].astype(jnp.float32)
        out_ref[:, pl.ds(0, half), :] = total
        total = s1b[lo].astype(jnp.float32)
        for src in sources_lo:
            arrive(r2b.at[src], 3, src)
            total = total + r2b[src].astype(jnp.float32)
        out_ref[:, pl.ds(half, half), :] = total
        for copy in sends:
            copy.wait_send()

    most = max(n_hi, n_lo)
    return pl.pallas_call(
        kernel,
        out_shape=jax.ShapeDtypeStruct((slots, rows, outs), jnp.float32),
        in_specs=[pl.BlockSpec(memory_space=pltpu.VMEM)],
        out_specs=pl.BlockSpec(memory_space=pltpu.VMEM),
        scratch_shapes=[
            pltpu.VMEM((n_lo, slots, n_hi, half, outs), parts.dtype),
            pltpu.VMEM((n_hi, slots, n_lo, half, outs), parts.dtype),
            pltpu.VMEM((n_hi, slots, half, outs), parts.dtype),
            pltpu.VMEM((n_lo, slots, half, outs), parts.dtype),
            pltpu.VMEM((n_hi, slots, half, outs), parts.dtype),
            pltpu.VMEM((n_lo, slots, half, outs), parts.dtype),
            pltpu.SemaphoreType.DMA((4, most)),
            pltpu.SemaphoreType.DMA((4, most)),
        ],
        compiler_params=pltpu.CompilerParams(collective_id=cid, has_side_effects=True),
    )(parts)


def chip_ring_gather(block, axis, n, cid):
    rows = block.shape[0]
    cut = rows // 32 * 16

    def kernel(x_ref, out_ref, send_sem, recv_sem):
        me = lax.axis_index(axis)
        partner = me + 1 - 2 * lax.rem(me, 2)
        up, down, far = lax.rem(me + 2, n), lax.rem(me + n - 2, n), lax.rem(me + 4, n)
        barrier = pltpu.get_barrier_semaphore()
        for dev in (up, down, partner):
            pl.semaphore_signal(barrier, inc=1, device_id={axis: dev}, device_id_type=MESH_ID)
        pl.semaphore_wait(barrier, 3)
        head, tail = pl.ds(0, cut), pl.ds(cut, rows - cut)

        def send(src_ref, slot, part, dev, index, sem_col):
            copy = pltpu.make_async_remote_copy(
                src_ref=src_ref, dst_ref=out_ref.at[slot, part], send_sem=send_sem.at[index],
                recv_sem=recv_sem.at[slot, sem_col], device_id={axis: dev},
                device_id_type=MESH_ID)
            copy.start()
            return copy

        def arrive(slot, part, sem_col):
            pltpu.make_async_remote_copy(
                src_ref=out_ref.at[slot, part], dst_ref=out_ref.at[slot, part],
                send_sem=send_sem.at[0], recv_sem=recv_sem.at[slot, sem_col],
                device_id={axis: slot}, device_id_type=MESH_ID).wait_recv()

        whole = pl.ds(0, rows)
        sends = [send(x_ref, me, whole, up, 0, 0), send(x_ref, me, whole, down, 1, 0),
                 send(x_ref, me, whole, partner, 2, 0)]
        out_ref[me] = x_ref[...]
        arrive(down, whole, 0)
        sends.append(send(out_ref.at[down, head], down, head, up, 3, 0))
        sends.append(send(out_ref.at[down], down, whole, partner, 4, 0))
        arrive(up, whole, 0)
        sends.append(send(out_ref.at[up, tail], up, tail, down, 5, 1))
        sends.append(send(out_ref.at[up], up, whole, partner, 6, 0))
        arrive(far, head, 0)
        arrive(far, tail, 1)
        sends.append(send(out_ref.at[far], far, whole, partner, 7, 0))
        for k in range(4):
            arrive(lax.rem(partner + 2 * k, n), whole, 0)
        for copy in sends:
            copy.wait_send()

    return pl.pallas_call(
        kernel,
        out_shape=jax.ShapeDtypeStruct((n,) + block.shape, block.dtype),
        in_specs=[pl.BlockSpec(memory_space=pltpu.VMEM)],
        out_specs=pl.BlockSpec(memory_space=pltpu.VMEM),
        scratch_shapes=[pltpu.SemaphoreType.DMA((8,)), pltpu.SemaphoreType.DMA((n, 2))],
        compiler_params=pltpu.CompilerParams(collective_id=cid, has_side_effects=True),
    )(block)


def grid_ring_reduce_scatter(parts, outer, inner, cid):
    slots, n_hi, n_lo, rows, outs = parts.shape
    half = rows // 2
    quarter = half // 2
    ring = 4

    def kernel(x_ref, out_ref, r1a, r1b, s1a, s1b, r2a, r2b, ta, tb, send_sem, recv_sem):
        hi = lax.axis_index(outer)
        lo = lax.axis_index(inner)
        barrier = pltpu.get_barrier_semaphore()
        for k in range(1, ring):
            pl.semaphore_signal(barrier, inc=1, device_id={inner: lax.rem(lo + k, ring)},
                                device_id_type=MESH_ID)
            pl.semaphore_signal(barrier, inc=1, device_id={outer: lax.rem(hi + k, ring)},
                                device_id_type=MESH_ID)
        pl.semaphore_wait(barrier, 2 * ring - 2)
        sends = []

        def send(src_ref, dst_ref, axis, dev, sem):
            copy = pltpu.make_async_remote_copy(
                src_ref=src_ref, dst_ref=dst_ref, send_sem=send_sem.at[len(sends)],
                recv_sem=recv_sem.at[sem], device_id={axis: dev}, device_id_type=MESH_ID)
            copy.start()
            sends.append(copy)

        def arrive(dst_ref, sem):
            pltpu.make_async_remote_copy(
                src_ref=dst_ref, dst_ref=dst_ref, send_sem=send_sem.at[0],
                recv_sem=recv_sem.at[sem], device_id={inner: lo},
                device_id_type=MESH_ID).wait_recv()

        def first_stage(axis, pos, piece, recv, transit, group):
            up, down, far = lax.rem(pos + 1, ring), lax.rem(pos + 3, ring), lax.rem(pos + 2, ring)
            send(piece(up, 0, half), recv.at[pos], axis, up, (group, pos, 0))
            send(piece(down, 0, half), recv.at[pos], axis, down, (group, pos, 0))
            send(piece(far, 0, quarter), transit.at[0], axis, up, (group + 4, 0, 0))
            send(piece(far, quarter, quarter), transit.at[1], axis, down, (group + 4, 1, 0))
            arrive(transit.at[0], (group + 4, 0, 0))
            send(transit.at[0], recv.at[down, :, :, pl.ds(0, quarter)], axis, up, (group, down, 0))
            arrive(transit.at[1], (group + 4, 1, 0))
            send(transit.at[1], recv.at[up, :, :, pl.ds(quarter, quarter)], axis, down, (group, up, 1))
            return up, down, far

        ends_a = first_stage(inner, lo, lambda d, s, z: x_ref.at[:, :, d, pl.ds(s, z), :], r1a, ta, 0)
        ends_b = first_stage(outer, hi, lambda d, s, z: x_ref.at[:, d, :, pl.ds(half + s, z), :], r1b, tb, 1)

        def settle(recv, ends, group):
            up, down, far = ends
            arrive(recv.at[up], (group, up, 0))
            arrive(recv.at[down], (group, down, 0))
            arrive(recv.at[far, :, :, pl.ds(0, quarter)], (group, far, 0))
            arrive(recv.at[far, :, :, pl.ds(quarter, quarter)], (group, far, 1))
            return ends

        sources_lo = settle(r1a, ends_a, 0)
        for h in range(n_hi):
            total = x_ref[:, h, lo, pl.ds(0, half), :].astype(jnp.float32)
            for src in sources_lo:
                total = total + r1a[src, :, h].astype(jnp.float32)
            s1a[h] = total.astype(s1a.dtype)
        for k in range(1, ring):
            dev = lax.rem(hi + k, ring)
            send(s1a.at[dev], r2a.at[hi], outer, dev, (2, hi, 0))
        sources_hi = settle(r1b, ends_b, 1)
        for l in range(n_lo):
            total = x_ref[:, hi, l, pl.ds(half, half), :].astype(jnp.float32)
            for src in sources_hi:
                total = total + r1b[src, :, l].astype(jnp.float32)
            s1b[l] = total.astype(s1b.dtype)
        for k in range(1, ring):
            dev = lax.rem(lo + k, ring)
            send(s1b.at[dev], r2b.at[lo], inner, dev, (3, lo, 0))

        total = s1a[hi].astype(jnp.float32)
        for k in range(1, ring):
            src = lax.rem(hi + ring - k, ring)
            arrive(r2a.at[src], (2, src, 0))
            total = total + r2a[src].astype(jnp.float32)
        out_ref[:, pl.ds(0, half), :] = total
        total = s1b[lo].astype(jnp.float32)
        for k in range(1, ring):
            src = lax.rem(lo + ring - k, ring)
            arrive(r2b.at[src], (3, src, 0))
            total = total + r2b[src].astype(jnp.float32)
        out_ref[:, pl.ds(half, half), :] = total
        for copy in sends:
            copy.wait_send()

    return pl.pallas_call(
        kernel,
        out_shape=jax.ShapeDtypeStruct((slots, rows, outs), jnp.float32),
        in_specs=[pl.BlockSpec(memory_space=pltpu.VMEM)],
        out_specs=pl.BlockSpec(memory_space=pltpu.VMEM),
        scratch_shapes=[
            pltpu.VMEM((ring, slots, n_hi, half, outs), parts.dtype),
            pltpu.VMEM((ring, slots, n_lo, half, outs), parts.dtype),
            pltpu.VMEM((n_hi, slots, half, outs), parts.dtype),
            pltpu.VMEM((n_lo, slots, half, outs), parts.dtype),
            pltpu.VMEM((ring, slots, half, outs), parts.dtype),
            pltpu.VMEM((ring, slots, half, outs), parts.dtype),
            pltpu.VMEM((2, slots, n_hi, quarter, outs), parts.dtype),
            pltpu.VMEM((2, slots, n_lo, quarter, outs), parts.dtype),
            pltpu.SemaphoreType.DMA((24,)),
            pltpu.SemaphoreType.DMA((6, ring, 2)),
        ],
        compiler_params=pltpu.CompilerParams(collective_id=cid, has_side_effects=True),
    )(parts)

HEADS = 16
WH = 6
WW = 12


EPS = 1e-05


def padded(array, sides, width, wrap):
    for axis, dim in sides:
        size, length = (lax.axis_size(axis), array.shape[dim])
        up = [(i, (i + 1) % size) for i in range(size if wrap else size - 1)]
        down = [(j, i) for i, j in up]
        last = lax.slice_in_dim(array, length - width, length, axis=dim)
        initial = lax.slice_in_dim(array, 0, width, axis=dim)
        before = lax.ppermute(last, axis, up)
        after = lax.ppermute(initial, axis, down)
        array = jnp.concatenate([before, array, after], axis=dim)
    return array


def layer_norm(values, gain):
    wide = values.astype(jnp.float32)
    average = jnp.mean(wide, axis=-1, keepdims=True)
    centred = wide - average
    variance = jnp.mean(centred * centred, axis=-1, keepdims=True)
    return (centred * lax.rsqrt(variance + EPS) * gain).astype(jnp.bfloat16)


def window_attention(query_ext, keyval, row_valid, heads):
    ext_rows, ext_cols, width = query_ext.shape
    head_size = width // heads
    win_rows = ext_rows // WH
    win_cols = ext_cols // WW

    def split(values, parts):
        shaped = values.reshape(win_rows, WH, win_cols, WW, parts, heads, head_size)
        return shaped.transpose(0, 2, 1, 3, 4, 5, 6).reshape(
            win_rows * win_cols, WH * WW, parts, heads, head_size
        )

    query_win = split(query_ext, 1)[:, :, 0]
    pairs = split(keyval, 2)
    key_win = pairs[:, :, 0]
    value_win = pairs[:, :, 1]
    key_mask = jnp.broadcast_to(
        row_valid.reshape(win_rows, 1, WH, 1), (win_rows, win_cols, WH, WW)
    ).reshape(win_rows * win_cols, WH * WW)
    scores = jnp.einsum(
        "wqhd,wkhd->whqk", query_win, key_win, preferred_element_type=jnp.float32
    ) / math.sqrt(head_size)
    scores = jnp.where(key_mask[:, None, None, :], scores, -jnp.inf)
    peak = jnp.max(scores, axis=-1, keepdims=True)
    weights = jnp.exp(scores - peak)
    probs = (weights / jnp.sum(weights, axis=-1, keepdims=True)).astype(jnp.bfloat16)
    mixed = jnp.einsum("whqk,wkhd->wqhd", probs, value_win, preferred_element_type=jnp.float32)
    return (
        mixed.reshape(win_rows, win_cols, WH, WW, width)
        .transpose(0, 2, 1, 3, 4)
        .reshape(ext_rows, ext_cols, width)
    )


def slot_terms(piece, target_rows, live_cols, level_scale, level_shift, heads_full):
    piece_wide = piece.astype(jnp.float32)
    rows = (
        piece_wide[None] * level_scale[:, None, None, :] + level_shift[:, None, None, :]
    ).astype(jnp.bfloat16)
    predicted = jnp.einsum("krnd,kdo->krno", rows, heads_full, preferred_element_type=jnp.float32)
    errors = ((predicted - target_rows.astype(jnp.float32)) * live_cols[:, None, :, None]).astype(
        jnp.bfloat16
    )
    back_grad = jnp.einsum("krno,kdo->krnd", errors, heads_full, preferred_element_type=jnp.float32)
    piece_grad = jnp.sum(back_grad * level_scale[:, None, None, :], axis=0)
    head_add = jnp.einsum("krnd,krno->kdo", rows, errors, preferred_element_type=jnp.float32)
    return (piece_grad, head_add)


def local(
    patches,
    norm_gain,
    input_proj,
    output_proj,
    level_scale,
    level_shift,
    head_weight,
    targets,
    level_counts,
    tile_dataset,
    slot_level,
):
    band_rows, band_cols, width = patches.shape
    half_rows = WH // 2
    half_cols = WW // 2
    lat_count = lax.axis_size(LAT)
    var_count = lax.axis_size("var")
    lat_place = lax.axis_index(LAT)
    ext_rows = band_rows + WH
    ext_cols = band_cols + WW
    extended = padded(patches, ((LAT, 0),), half_rows, False)
    extended = padded(extended, (("var", 1),), half_cols, True)
    normed_ext = layer_norm(extended, norm_gain)
    keyval = jnp.dot(
        normed_ext.reshape(-1, width), input_proj[:, width:], preferred_element_type=jnp.float32
    )
    keyval = keyval.astype(jnp.bfloat16).reshape(ext_rows, ext_cols, 2 * width)
    normed = normed_ext[half_rows : half_rows + band_rows, half_cols : half_cols + band_cols]
    queries = jnp.dot(
        normed.reshape(-1, width), input_proj[:, :width], preferred_element_type=jnp.float32
    )
    queries = queries.astype(jnp.bfloat16)
    global_row = lat_place * band_rows - half_rows + jnp.arange(ext_rows, dtype=jnp.int32)
    row_valid = (global_row >= 0) & (global_row < lat_count * band_rows)
    win_cols = ext_cols // WW
    ext_r = jnp.arange(ext_rows, dtype=jnp.int32)[:, None]
    ext_c = jnp.arange(ext_cols, dtype=jnp.int32)[None, :]
    key_win = jnp.where(row_valid[:, None], (ext_r // WH) * win_cols + ext_c // WW, -1)
    own_r = ext_r[half_rows : half_rows + band_rows]
    own_c = ext_c[:, half_cols : half_cols + band_cols]
    query_win = (own_r // WH) * win_cols + own_c // WW
    attn = masked_window_attention(
        queries,
        keyval.reshape(ext_rows * ext_cols, 2 * width),
        query_win.reshape(-1, 1),
        key_win.reshape(1, -1),
        HEADS,
    ).reshape(band_rows, band_cols, width)
    update = jnp.dot(
        attn.reshape(-1, width), output_proj, preferred_element_type=jnp.float32
    ).reshape(band_rows, band_cols, width)
    latent = (patches.astype(jnp.float32) + update).astype(jnp.bfloat16)
    dataset_row = tile_dataset[0]
    dataset_ids = jnp.arange(level_counts.shape[0], dtype=jnp.int32)
    tile_levels = jnp.sum(
        jnp.where(dataset_row[:, None] == dataset_ids[None, :], level_counts[None, :], 0), axis=1
    )
    live_tiles = (slot_level[None, :] < tile_levels[:, None]).astype(jnp.float32)
    heads_full = lax.all_gather(head_weight, LAT, axis=1, tiled=True)
    tile_ids = jnp.arange(var_count, dtype=jnp.int32)
    gather = chip_ring_gather if var_count == 8 else chip_pair_gather
    tiles = gather(latent.reshape(band_rows * band_cols, width), "var", var_count, 1)
    piece = (
        tiles.reshape(var_count, band_rows, band_cols, width)
        .transpose(1, 0, 2, 3)
        .reshape(band_rows, var_count * band_cols, width)
    )
    piece_cols = piece.shape[1]
    column_tile = jnp.arange(piece_cols, dtype=jnp.int32) // band_cols
    onehot = (column_tile[:, None] == tile_ids[None, :]).astype(jnp.float32)
    column_live = jnp.dot(onehot, live_tiles)
    piece_grad, head_add = slot_terms(
        piece, targets, column_live.T, level_scale, level_shift, heads_full
    )
    latent_terms = piece_grad
    latent_terms, head_terms = (latent_terms, head_add)
    grad_latent = lax.psum_scatter(
        latent_terms.astype(jnp.bfloat16), "var", scatter_dimension=1, tiled=True
    )
    head_terms = head_terms * (1.0 / math.sqrt(lat_count * band_rows * var_count * band_cols))
    outer, inner = lax.axis_size(LAT[0]), lax.axis_size(LAT[1])
    slots, outs = head_terms.shape[0], head_terms.shape[2]
    share_rows = width // lat_count
    head_parts = head_terms.astype(jnp.bfloat16).reshape(slots, outer, inner, share_rows, outs)
    reduce = grid_ring_reduce_scatter if outer == inner == 4 else grid_reduce_scatter
    grad_head = reduce(head_parts, LAT[0], LAT[1], 3)
    return (latent, grad_latent, grad_head)


def solution(mesh):
    in_specs = (
        P(LAT, "var", None),
        P(),
        P(),
        P(),
        P("var", None),
        P("var", None),
        P("var", LAT, None),
        P("var", LAT, None, None),
        P(),
        P(LAT, None),
        P("var"),
    )
    out_specs = (P(LAT, "var", None), P(LAT, "var", None), P("var", LAT, None))
    lat_size = mesh.shape["lat"]
    inner = 4 if lat_size % 4 == 0 else 1
    grid = Mesh(
        mesh.devices.reshape(lat_size // inner, inner, mesh.shape["var"]), LAT + ("var",)
    )
    return jax.shard_map(local, mesh=grid, in_specs=in_specs, out_specs=out_specs, check_vma=False)
```

```python
import math

import jax
import jax.numpy as jnp
from jax import lax
from jax.experimental import pallas as pl
from jax.experimental.pallas import tpu as pltpu
from jax.sharding import Mesh, PartitionSpec as P

MESH_ID = pl.DeviceIdType.MESH
LAT = ("lat_hi", "lat_lo")


def _greet(axis, n, me):
    barrier = pltpu.get_barrier_semaphore()
    for k in range(1, n):
        pl.semaphore_signal(barrier, inc=1, device_id={axis: lax.rem(me + k, n)},
                            device_id_type=MESH_ID)
    pl.semaphore_wait(barrier, n - 1)


def peer_gather(block, axis, n, cid):
    def kernel(x_ref, out_ref, send_sem, recv_sem):
        me = lax.axis_index(axis)
        _greet(axis, n, me)
        sends = []
        for k in range(1, n):
            copy = pltpu.make_async_remote_copy(
                src_ref=x_ref, dst_ref=out_ref.at[me], send_sem=send_sem.at[k],
                recv_sem=recv_sem.at[me], device_id={axis: lax.rem(me + k, n)},
                device_id_type=MESH_ID)
            copy.start()
            sends.append(copy)
        out_ref[me] = x_ref[...]
        for k in range(1, n):
            src = lax.rem(me + n - k, n)
            pltpu.make_async_remote_copy(
                src_ref=x_ref, dst_ref=out_ref.at[src], send_sem=send_sem.at[k],
                recv_sem=recv_sem.at[src], device_id={axis: src},
                device_id_type=MESH_ID).wait_recv()
        for copy in sends:
            copy.wait_send()

    return pl.pallas_call(
        kernel,
        out_shape=jax.ShapeDtypeStruct((n,) + block.shape, block.dtype),
        in_specs=[pl.BlockSpec(memory_space=pltpu.VMEM)],
        out_specs=pl.BlockSpec(memory_space=pltpu.VMEM),
        scratch_shapes=[pltpu.SemaphoreType.DMA((n,)), pltpu.SemaphoreType.DMA((n,))],
        compiler_params=pltpu.CompilerParams(collective_id=cid, has_side_effects=True),
    )(block)


def peer_reduce_scatter(parts, axis, n, cid, out_dtype):
    def kernel(x_ref, out_ref, held, send_sem, recv_sem):
        me = lax.axis_index(axis)
        _greet(axis, n, me)
        sends = []
        for k in range(1, n):
            dst = lax.rem(me + k, n)
            copy = pltpu.make_async_remote_copy(
                src_ref=x_ref.at[dst], dst_ref=held.at[me], send_sem=send_sem.at[k],
                recv_sem=recv_sem.at[me], device_id={axis: dst},
                device_id_type=MESH_ID)
            copy.start()
            sends.append(copy)
        total = x_ref[me].astype(jnp.float32)
        for k in range(1, n):
            src = lax.rem(me + n - k, n)
            pltpu.make_async_remote_copy(
                src_ref=x_ref.at[src], dst_ref=held.at[src], send_sem=send_sem.at[k],
                recv_sem=recv_sem.at[src], device_id={axis: src},
                device_id_type=MESH_ID).wait_recv()
            total = total + held[src].astype(jnp.float32)
        out_ref[...] = total.astype(out_ref.dtype)
        for copy in sends:
            copy.wait_send()

    return pl.pallas_call(
        kernel,
        out_shape=jax.ShapeDtypeStruct(parts.shape[1:], out_dtype),
        in_specs=[pl.BlockSpec(memory_space=pltpu.VMEM)],
        out_specs=pl.BlockSpec(memory_space=pltpu.VMEM),
        scratch_shapes=[pltpu.VMEM(parts.shape, parts.dtype),
                        pltpu.SemaphoreType.DMA((n,)), pltpu.SemaphoreType.DMA((n,))],
        compiler_params=pltpu.CompilerParams(collective_id=cid, has_side_effects=True),
    )(parts)


def masked_window_attention(queries, keyval, query_win, key_win, heads):
    nq, width = queries.shape
    head_size = width // heads
    scale = 1.0 / float(head_size) ** 0.5

    def kernel(q_ref, kv_ref, qw_ref, kw_ref, out_ref):
        mask = qw_ref[...] == kw_ref[...]
        for h in range(heads):
            cols = slice(h * head_size, (h + 1) * head_size)
            q = q_ref[:, cols]
            k = kv_ref[:, h * head_size:(h + 1) * head_size]
            v = kv_ref[:, width + h * head_size:width + (h + 1) * head_size]
            s = lax.dot_general(q, k, (((1,), (1,)), ((), ())),
                                preferred_element_type=jnp.float32) * scale
            s = jnp.where(mask, s, -jnp.inf)
            w = jnp.exp(s - jnp.max(s, axis=1, keepdims=True))
            p = (w / jnp.sum(w, axis=1, keepdims=True)).astype(jnp.bfloat16)
            out_ref[:, cols] = jnp.dot(p, v, preferred_element_type=jnp.float32).astype(out_ref.dtype)

    return pl.pallas_call(
        kernel,
        out_shape=jax.ShapeDtypeStruct((nq, width), jnp.bfloat16),
        in_specs=[pl.BlockSpec(memory_space=pltpu.VMEM)] * 4,
        out_specs=pl.BlockSpec(memory_space=pltpu.VMEM),
    )(queries, keyval, query_win, key_win)


def chip_pair_gather(block, axis, n, cid):
    nz = n // 2

    def kernel(x_ref, out_ref, send_sem, recv_sem):
        me = lax.axis_index(axis)
        partner = me + 1 - 2 * lax.rem(me, 2)
        peers = [lax.rem(me + 2 * k, n) for k in range(1, nz)]
        barrier = pltpu.get_barrier_semaphore()
        for dev in peers + [partner]:
            pl.semaphore_signal(barrier, inc=1, device_id={axis: dev}, device_id_type=MESH_ID)
        pl.semaphore_wait(barrier, nz)

        def send(src_ref, slot, dev, index):
            copy = pltpu.make_async_remote_copy(
                src_ref=src_ref, dst_ref=out_ref.at[slot], send_sem=send_sem.at[index],
                recv_sem=recv_sem.at[slot], device_id={axis: dev}, device_id_type=MESH_ID)
            copy.start()
            return copy

        def arrive(slot):
            pltpu.make_async_remote_copy(
                src_ref=x_ref, dst_ref=out_ref.at[slot], send_sem=send_sem.at[0],
                recv_sem=recv_sem.at[slot], device_id={axis: slot},
                device_id_type=MESH_ID).wait_recv()

        sends = [send(x_ref, me, dev, i) for i, dev in enumerate(peers)]
        sends.append(send(x_ref, me, partner, nz - 1))
        out_ref[me] = x_ref[...]
        for k in range(1, nz):
            src = lax.rem(me + n - 2 * k, n)
            arrive(src)
            sends.append(send(out_ref.at[src], src, partner, nz - 1 + k))
        for k in range(nz):
            arrive(lax.rem(partner + 2 * k, n))
        for copy in sends:
            copy.wait_send()

    return pl.pallas_call(
        kernel,
        out_shape=jax.ShapeDtypeStruct((n,) + block.shape, block.dtype),
        in_specs=[pl.BlockSpec(memory_space=pltpu.VMEM)],
        out_specs=pl.BlockSpec(memory_space=pltpu.VMEM),
        scratch_shapes=[pltpu.SemaphoreType.DMA((n,)), pltpu.SemaphoreType.DMA((n,))],
        compiler_params=pltpu.CompilerParams(collective_id=cid, has_side_effects=True),
    )(block)


def grid_reduce_scatter(parts, outer, inner, cid):
    slots, n_hi, n_lo, rows, outs = parts.shape
    half = rows // 2

    def kernel(x_ref, out_ref, r1a, r1b, s1a, s1b, r2a, r2b, send_sem, recv_sem):
        hi = lax.axis_index(outer)
        lo = lax.axis_index(inner)
        barrier = pltpu.get_barrier_semaphore()
        for k in range(1, n_lo):
            pl.semaphore_signal(barrier, inc=1, device_id={inner: lax.rem(lo + k, n_lo)},
                                device_id_type=MESH_ID)
        for k in range(1, n_hi):
            pl.semaphore_signal(barrier, inc=1, device_id={outer: lax.rem(hi + k, n_hi)},
                                device_id_type=MESH_ID)
        pl.semaphore_wait(barrier, n_lo + n_hi - 2)

        def send(src_ref, dst_ref, axis, dev, group, k, slot):
            copy = pltpu.make_async_remote_copy(
                src_ref=src_ref, dst_ref=dst_ref, send_sem=send_sem.at[group, k],
                recv_sem=recv_sem.at[group, slot], device_id={axis: dev},
                device_id_type=MESH_ID)
            copy.start()
            return copy

        def arrive(dst_ref, group, slot):
            pltpu.make_async_remote_copy(
                src_ref=dst_ref, dst_ref=dst_ref, send_sem=send_sem.at[group, 0],
                recv_sem=recv_sem.at[group, slot], device_id={inner: lo},
                device_id_type=MESH_ID).wait_recv()

        sends = []
        for k in range(1, n_lo):
            dev = lax.rem(lo + k, n_lo)
            sends.append(send(x_ref.at[:, :, dev, pl.ds(0, half), :], r1a.at[lo], inner, dev, 0, k, lo))
        for k in range(1, n_hi):
            dev = lax.rem(hi + k, n_hi)
            sends.append(send(x_ref.at[:, dev, :, pl.ds(half, half), :], r1b.at[hi], outer, dev, 1, k, hi))

        sources_lo = [lax.rem(lo + n_lo - k, n_lo) for k in range(1, n_lo)]
        sources_hi = [lax.rem(hi + n_hi - k, n_hi) for k in range(1, n_hi)]
        for src in sources_lo:
            arrive(r1a.at[src], 0, src)
        for h in range(n_hi):
            total = x_ref[:, h, lo, pl.ds(0, half), :].astype(jnp.float32)
            for src in sources_lo:
                total = total + r1a[src, :, h].astype(jnp.float32)
            s1a[h] = total.astype(s1a.dtype)
        for k in range(1, n_hi):
            dev = lax.rem(hi + k, n_hi)
            sends.append(send(s1a.at[dev], r2a.at[hi], outer, dev, 2, k, hi))
        for src in sources_hi:
            arrive(r1b.at[src], 1, src)
        for l in range(n_lo):
            total = x_ref[:, hi, l, pl.ds(half, half), :].astype(jnp.float32)
            for src in sources_hi:
                total = total + r1b[src, :, l].astype(jnp.float32)
            s1b[l] = total.astype(s1b.dtype)
        for k in range(1, n_lo):
            dev = lax.rem(lo + k, n_lo)
            sends.append(send(s1b.at[dev], r2b.at[lo], inner, dev, 3, k, lo))

        total = s1a[hi].astype(jnp.float32)
        for src in sources_hi:
            arrive(r2a.at[src], 2, src)
            total = total + r2a[src].astype(jnp.float32)
        out_ref[:, pl.ds(0, half), :] = total
        total = s1b[lo].astype(jnp.float32)
        for src in sources_lo:
            arrive(r2b.at[src], 3, src)
            total = total + r2b[src].astype(jnp.float32)
        out_ref[:, pl.ds(half, half), :] = total
        for copy in sends:
            copy.wait_send()

    most = max(n_hi, n_lo)
    return pl.pallas_call(
        kernel,
        out_shape=jax.ShapeDtypeStruct((slots, rows, outs), jnp.float32),
        in_specs=[pl.BlockSpec(memory_space=pltpu.VMEM)],
        out_specs=pl.BlockSpec(memory_space=pltpu.VMEM),
        scratch_shapes=[
            pltpu.VMEM((n_lo, slots, n_hi, half, outs), parts.dtype),
            pltpu.VMEM((n_hi, slots, n_lo, half, outs), parts.dtype),
            pltpu.VMEM((n_hi, slots, half, outs), parts.dtype),
            pltpu.VMEM((n_lo, slots, half, outs), parts.dtype),
            pltpu.VMEM((n_hi, slots, half, outs), parts.dtype),
            pltpu.VMEM((n_lo, slots, half, outs), parts.dtype),
            pltpu.SemaphoreType.DMA((4, most)),
            pltpu.SemaphoreType.DMA((4, most)),
        ],
        compiler_params=pltpu.CompilerParams(collective_id=cid, has_side_effects=True),
    )(parts)


def chip_ring_gather(block, axis, n, cid):
    rows = block.shape[0]
    cut = rows // 32 * 16

    def kernel(x_ref, out_ref, send_sem, recv_sem):
        me = lax.axis_index(axis)
        partner = me + 1 - 2 * lax.rem(me, 2)
        up, down, far = lax.rem(me + 2, n), lax.rem(me + n - 2, n), lax.rem(me + 4, n)
        barrier = pltpu.get_barrier_semaphore()
        for dev in (up, down, partner):
            pl.semaphore_signal(barrier, inc=1, device_id={axis: dev}, device_id_type=MESH_ID)
        pl.semaphore_wait(barrier, 3)
        head, tail = pl.ds(0, cut), pl.ds(cut, rows - cut)

        def send(src_ref, slot, part, dev, index, sem_col):
            copy = pltpu.make_async_remote_copy(
                src_ref=src_ref, dst_ref=out_ref.at[slot, part], send_sem=send_sem.at[index],
                recv_sem=recv_sem.at[slot, sem_col], device_id={axis: dev},
                device_id_type=MESH_ID)
            copy.start()
            return copy

        def arrive(slot, part, sem_col):
            pltpu.make_async_remote_copy(
                src_ref=out_ref.at[slot, part], dst_ref=out_ref.at[slot, part],
                send_sem=send_sem.at[0], recv_sem=recv_sem.at[slot, sem_col],
                device_id={axis: slot}, device_id_type=MESH_ID).wait_recv()

        whole = pl.ds(0, rows)
        sends = [send(x_ref, me, whole, up, 0, 0), send(x_ref, me, whole, down, 1, 0),
                 send(x_ref, me, whole, partner, 2, 0)]
        out_ref[me] = x_ref[...]
        arrive(down, whole, 0)
        sends.append(send(out_ref.at[down, head], down, head, up, 3, 0))
        sends.append(send(out_ref.at[down], down, whole, partner, 4, 0))
        arrive(up, whole, 0)
        sends.append(send(out_ref.at[up, tail], up, tail, down, 5, 1))
        sends.append(send(out_ref.at[up], up, whole, partner, 6, 0))
        arrive(far, head, 0)
        arrive(far, tail, 1)
        sends.append(send(out_ref.at[far], far, whole, partner, 7, 0))
        for k in range(4):
            arrive(lax.rem(partner + 2 * k, n), whole, 0)
        for copy in sends:
            copy.wait_send()

    return pl.pallas_call(
        kernel,
        out_shape=jax.ShapeDtypeStruct((n,) + block.shape, block.dtype),
        in_specs=[pl.BlockSpec(memory_space=pltpu.VMEM)],
        out_specs=pl.BlockSpec(memory_space=pltpu.VMEM),
        scratch_shapes=[pltpu.SemaphoreType.DMA((8,)), pltpu.SemaphoreType.DMA((n, 2))],
        compiler_params=pltpu.CompilerParams(collective_id=cid, has_side_effects=True),
    )(block)


def grid_ring_reduce_scatter(parts, outer, inner, cid):
    slots, n_hi, n_lo, rows, outs = parts.shape
    half = rows // 2
    quarter = half // 2
    ring = 4

    def kernel(x_ref, out_ref, r1a, r1b, s1a, s1b, r2a, r2b, ta, tb, send_sem, recv_sem):
        hi = lax.axis_index(outer)
        lo = lax.axis_index(inner)
        barrier = pltpu.get_barrier_semaphore()
        for k in range(1, ring):
            pl.semaphore_signal(barrier, inc=1, device_id={inner: lax.rem(lo + k, ring)},
                                device_id_type=MESH_ID)
            pl.semaphore_signal(barrier, inc=1, device_id={outer: lax.rem(hi + k, ring)},
                                device_id_type=MESH_ID)
        pl.semaphore_wait(barrier, 2 * ring - 2)
        sends = []

        def send(src_ref, dst_ref, axis, dev, sem):
            copy = pltpu.make_async_remote_copy(
                src_ref=src_ref, dst_ref=dst_ref, send_sem=send_sem.at[len(sends)],
                recv_sem=recv_sem.at[sem], device_id={axis: dev}, device_id_type=MESH_ID)
            copy.start()
            sends.append(copy)

        def arrive(dst_ref, sem):
            pltpu.make_async_remote_copy(
                src_ref=dst_ref, dst_ref=dst_ref, send_sem=send_sem.at[0],
                recv_sem=recv_sem.at[sem], device_id={inner: lo},
                device_id_type=MESH_ID).wait_recv()

        def launch(axis, pos, piece, recv, transit, group):
            up, down, far = lax.rem(pos + 1, ring), lax.rem(pos + 3, ring), lax.rem(pos + 2, ring)
            send(piece(far, 0, quarter), transit.at[0], axis, up, (group + 4, 0, 0))
            send(piece(far, quarter, quarter), transit.at[1], axis, down, (group + 4, 1, 0))
            send(piece(up, 0, half), recv.at[pos], axis, up, (group, pos, 0))
            send(piece(down, 0, half), recv.at[pos], axis, down, (group, pos, 0))
            return up, down, far

        def relay(axis, ends, recv, transit, group):
            up, down, far = ends
            arrive(transit.at[0], (group + 4, 0, 0))
            send(transit.at[0], recv.at[down, :, :, pl.ds(0, quarter)], axis, up, (group, down, 0))
            arrive(transit.at[1], (group + 4, 1, 0))
            send(transit.at[1], recv.at[up, :, :, pl.ds(quarter, quarter)], axis, down, (group, up, 1))

        ends_a = launch(inner, lo, lambda d, s, z: x_ref.at[:, :, d, pl.ds(s, z), :], r1a, ta, 0)
        ends_b = launch(outer, hi, lambda d, s, z: x_ref.at[:, d, :, pl.ds(half + s, z), :], r1b, tb, 1)
        relay(inner, ends_a, r1a, ta, 0)
        relay(outer, ends_b, r1b, tb, 1)

        def settle(recv, ends, group):
            up, down, far = ends
            arrive(recv.at[up], (group, up, 0))
            arrive(recv.at[down], (group, down, 0))
            arrive(recv.at[far, :, :, pl.ds(0, quarter)], (group, far, 0))
            arrive(recv.at[far, :, :, pl.ds(quarter, quarter)], (group, far, 1))
            return ends

        sources_lo = settle(r1a, ends_a, 0)
        for h in range(n_hi):
            total = x_ref[:, h, lo, pl.ds(0, half), :].astype(jnp.float32)
            for src in sources_lo:
                total = total + r1a[src, :, h].astype(jnp.float32)
            s1a[h] = total.astype(s1a.dtype)
        for k in range(1, ring):
            dev = lax.rem(hi + k, ring)
            send(s1a.at[dev], r2a.at[hi], outer, dev, (2, hi, 0))
        sources_hi = settle(r1b, ends_b, 1)
        for l in range(n_lo):
            total = x_ref[:, hi, l, pl.ds(half, half), :].astype(jnp.float32)
            for src in sources_hi:
                total = total + r1b[src, :, l].astype(jnp.float32)
            s1b[l] = total.astype(s1b.dtype)
        for k in range(1, ring):
            dev = lax.rem(lo + k, ring)
            send(s1b.at[dev], r2b.at[lo], inner, dev, (3, lo, 0))

        total = s1a[hi].astype(jnp.float32)
        for k in range(1, ring):
            src = lax.rem(hi + ring - k, ring)
            arrive(r2a.at[src], (2, src, 0))
            total = total + r2a[src].astype(jnp.float32)
        out_ref[:, pl.ds(0, half), :] = total
        total = s1b[lo].astype(jnp.float32)
        for k in range(1, ring):
            src = lax.rem(lo + ring - k, ring)
            arrive(r2b.at[src], (3, src, 0))
            total = total + r2b[src].astype(jnp.float32)
        out_ref[:, pl.ds(half, half), :] = total
        for copy in sends:
            copy.wait_send()

    return pl.pallas_call(
        kernel,
        out_shape=jax.ShapeDtypeStruct((slots, rows, outs), jnp.float32),
        in_specs=[pl.BlockSpec(memory_space=pltpu.VMEM)],
        out_specs=pl.BlockSpec(memory_space=pltpu.VMEM),
        scratch_shapes=[
            pltpu.VMEM((ring, slots, n_hi, half, outs), parts.dtype),
            pltpu.VMEM((ring, slots, n_lo, half, outs), parts.dtype),
            pltpu.VMEM((n_hi, slots, half, outs), parts.dtype),
            pltpu.VMEM((n_lo, slots, half, outs), parts.dtype),
            pltpu.VMEM((ring, slots, half, outs), parts.dtype),
            pltpu.VMEM((ring, slots, half, outs), parts.dtype),
            pltpu.VMEM((2, slots, n_hi, quarter, outs), parts.dtype),
            pltpu.VMEM((2, slots, n_lo, quarter, outs), parts.dtype),
            pltpu.SemaphoreType.DMA((24,)),
            pltpu.SemaphoreType.DMA((6, ring, 2)),
        ],
        compiler_params=pltpu.CompilerParams(collective_id=cid, has_side_effects=True),
    )(parts)

HEADS = 16
WH = 6
WW = 12


EPS = 1e-05


def padded(array, sides, width, wrap):
    for axis, dim in sides:
        size, length = (lax.axis_size(axis), array.shape[dim])
        up = [(i, (i + 1) % size) for i in range(size if wrap else size - 1)]
        down = [(j, i) for i, j in up]
        last = lax.slice_in_dim(array, length - width, length, axis=dim)
        initial = lax.slice_in_dim(array, 0, width, axis=dim)
        before = lax.ppermute(last, axis, up)
        after = lax.ppermute(initial, axis, down)
        array = jnp.concatenate([before, array, after], axis=dim)
    return array


def layer_norm(values, gain):
    wide = values.astype(jnp.float32)
    average = jnp.mean(wide, axis=-1, keepdims=True)
    centred = wide - average
    variance = jnp.mean(centred * centred, axis=-1, keepdims=True)
    return (centred * lax.rsqrt(variance + EPS) * gain).astype(jnp.bfloat16)


def window_attention(query_ext, keyval, row_valid, heads):
    ext_rows, ext_cols, width = query_ext.shape
    head_size = width // heads
    win_rows = ext_rows // WH
    win_cols = ext_cols // WW

    def split(values, parts):
        shaped = values.reshape(win_rows, WH, win_cols, WW, parts, heads, head_size)
        return shaped.transpose(0, 2, 1, 3, 4, 5, 6).reshape(
            win_rows * win_cols, WH * WW, parts, heads, head_size
        )

    query_win = split(query_ext, 1)[:, :, 0]
    pairs = split(keyval, 2)
    key_win = pairs[:, :, 0]
    value_win = pairs[:, :, 1]
    key_mask = jnp.broadcast_to(
        row_valid.reshape(win_rows, 1, WH, 1), (win_rows, win_cols, WH, WW)
    ).reshape(win_rows * win_cols, WH * WW)
    scores = jnp.einsum(
        "wqhd,wkhd->whqk", query_win, key_win, preferred_element_type=jnp.float32
    ) / math.sqrt(head_size)
    scores = jnp.where(key_mask[:, None, None, :], scores, -jnp.inf)
    peak = jnp.max(scores, axis=-1, keepdims=True)
    weights = jnp.exp(scores - peak)
    probs = (weights / jnp.sum(weights, axis=-1, keepdims=True)).astype(jnp.bfloat16)
    mixed = jnp.einsum("whqk,wkhd->wqhd", probs, value_win, preferred_element_type=jnp.float32)
    return (
        mixed.reshape(win_rows, win_cols, WH, WW, width)
        .transpose(0, 2, 1, 3, 4)
        .reshape(ext_rows, ext_cols, width)
    )


def slot_terms(piece, target_rows, live_cols, level_scale, level_shift, heads_full):
    piece_wide = piece.astype(jnp.float32)
    rows = (
        piece_wide[None] * level_scale[:, None, None, :] + level_shift[:, None, None, :]
    ).astype(jnp.bfloat16)
    predicted = jnp.einsum("krnd,kdo->krno", rows, heads_full, preferred_element_type=jnp.float32)
    errors = ((predicted - target_rows.astype(jnp.float32)) * live_cols[:, None, :, None]).astype(
        jnp.bfloat16
    )
    back_grad = jnp.einsum("krno,kdo->krnd", errors, heads_full, preferred_element_type=jnp.float32)
    piece_grad = jnp.sum(back_grad * level_scale[:, None, None, :], axis=0)
    head_add = jnp.einsum("krnd,krno->kdo", rows, errors, preferred_element_type=jnp.float32)
    return (piece_grad, head_add)


def local(
    patches,
    norm_gain,
    input_proj,
    output_proj,
    level_scale,
    level_shift,
    head_weight,
    targets,
    level_counts,
    tile_dataset,
    slot_level,
):
    band_rows, band_cols, width = patches.shape
    half_rows = WH // 2
    half_cols = WW // 2
    lat_count = lax.axis_size(LAT)
    var_count = lax.axis_size("var")
    lat_place = lax.axis_index(LAT)
    ext_rows = band_rows + WH
    ext_cols = band_cols + WW
    extended = padded(patches, ((LAT, 0),), half_rows, False)
    extended = padded(extended, (("var", 1),), half_cols, True)
    normed_ext = layer_norm(extended, norm_gain)
    keyval = jnp.dot(
        normed_ext.reshape(-1, width), input_proj[:, width:], preferred_element_type=jnp.float32
    )
    keyval = keyval.astype(jnp.bfloat16).reshape(ext_rows, ext_cols, 2 * width)
    normed = normed_ext[half_rows : half_rows + band_rows, half_cols : half_cols + band_cols]
    queries = jnp.dot(
        normed.reshape(-1, width), input_proj[:, :width], preferred_element_type=jnp.float32
    )
    queries = queries.astype(jnp.bfloat16)
    global_row = lat_place * band_rows - half_rows + jnp.arange(ext_rows, dtype=jnp.int32)
    row_valid = (global_row >= 0) & (global_row < lat_count * band_rows)
    win_cols = ext_cols // WW
    ext_r = jnp.arange(ext_rows, dtype=jnp.int32)[:, None]
    ext_c = jnp.arange(ext_cols, dtype=jnp.int32)[None, :]
    key_win = jnp.where(row_valid[:, None], (ext_r // WH) * win_cols + ext_c // WW, -1)
    own_r = ext_r[half_rows : half_rows + band_rows]
    own_c = ext_c[:, half_cols : half_cols + band_cols]
    query_win = (own_r // WH) * win_cols + own_c // WW
    attn = masked_window_attention(
        queries,
        keyval.reshape(ext_rows * ext_cols, 2 * width),
        query_win.reshape(-1, 1),
        key_win.reshape(1, -1),
        HEADS,
    ).reshape(band_rows, band_cols, width)
    update = jnp.dot(
        attn.reshape(-1, width), output_proj, preferred_element_type=jnp.float32
    ).reshape(band_rows, band_cols, width)
    latent = (patches.astype(jnp.float32) + update).astype(jnp.bfloat16)
    dataset_row = tile_dataset[0]
    dataset_ids = jnp.arange(level_counts.shape[0], dtype=jnp.int32)
    tile_levels = jnp.sum(
        jnp.where(dataset_row[:, None] == dataset_ids[None, :], level_counts[None, :], 0), axis=1
    )
    live_tiles = (slot_level[None, :] < tile_levels[:, None]).astype(jnp.float32)
    heads_full = lax.all_gather(head_weight, LAT, axis=1, tiled=True)
    tile_ids = jnp.arange(var_count, dtype=jnp.int32)
    gather = chip_ring_gather if var_count == 8 else chip_pair_gather
    tiles = gather(latent.reshape(band_rows * band_cols, width), "var", var_count, 1)
    piece = (
        tiles.reshape(var_count, band_rows, band_cols, width)
        .transpose(1, 0, 2, 3)
        .reshape(band_rows, var_count * band_cols, width)
    )
    piece_cols = piece.shape[1]
    column_tile = jnp.arange(piece_cols, dtype=jnp.int32) // band_cols
    onehot = (column_tile[:, None] == tile_ids[None, :]).astype(jnp.float32)
    column_live = jnp.dot(onehot, live_tiles)
    piece_grad, head_add = slot_terms(
        piece, targets, column_live.T, level_scale, level_shift, heads_full
    )
    latent_terms = piece_grad
    latent_terms, head_terms = (latent_terms, head_add)
    grad_latent = lax.psum_scatter(
        latent_terms.astype(jnp.bfloat16), "var", scatter_dimension=1, tiled=True
    )
    head_terms = head_terms * (1.0 / math.sqrt(lat_count * band_rows * var_count * band_cols))
    outer, inner = lax.axis_size(LAT[0]), lax.axis_size(LAT[1])
    slots, outs = head_terms.shape[0], head_terms.shape[2]
    share_rows = width // lat_count
    head_parts = head_terms.astype(jnp.bfloat16).reshape(slots, outer, inner, share_rows, outs)
    reduce = grid_ring_reduce_scatter if outer == inner == 4 else grid_reduce_scatter
    grad_head = reduce(head_parts, LAT[0], LAT[1], 3)
    return (latent, grad_latent, grad_head)


def solution(mesh):
    in_specs = (
        P(LAT, "var", None),
        P(),
        P(),
        P(),
        P("var", None),
        P("var", None),
        P("var", LAT, None),
        P("var", LAT, None, None),
        P(),
        P(LAT, None),
        P("var"),
    )
    out_specs = (P(LAT, "var", None), P(LAT, "var", None), P("var", LAT, None))
    lat_size = mesh.shape["lat"]
    inner = 4 if lat_size % 4 == 0 else 1
    grid = Mesh(
        mesh.devices.reshape(lat_size // inner, inner, mesh.shape["var"]), LAT + ("var",)
    )
    return jax.shard_map(local, mesh=grid, in_specs=in_specs, out_specs=out_specs, check_vma=False)
```

```python
import math

import jax
import jax.numpy as jnp
from jax import lax
from jax.experimental import pallas as pl
from jax.experimental.pallas import tpu as pltpu
from jax.sharding import Mesh, PartitionSpec as P

MESH_ID = pl.DeviceIdType.MESH
LAT = ("lat_hi", "lat_lo")


def _greet(axis, n, me):
    barrier = pltpu.get_barrier_semaphore()
    for k in range(1, n):
        pl.semaphore_signal(barrier, inc=1, device_id={axis: lax.rem(me + k, n)},
                            device_id_type=MESH_ID)
    pl.semaphore_wait(barrier, n - 1)


def peer_gather(block, axis, n, cid):
    def kernel(x_ref, out_ref, send_sem, recv_sem):
        me = lax.axis_index(axis)
        _greet(axis, n, me)
        sends = []
        for k in range(1, n):
            copy = pltpu.make_async_remote_copy(
                src_ref=x_ref, dst_ref=out_ref.at[me], send_sem=send_sem.at[k],
                recv_sem=recv_sem.at[me], device_id={axis: lax.rem(me + k, n)},
                device_id_type=MESH_ID)
            copy.start()
            sends.append(copy)
        out_ref[me] = x_ref[...]
        for k in range(1, n):
            src = lax.rem(me + n - k, n)
            pltpu.make_async_remote_copy(
                src_ref=x_ref, dst_ref=out_ref.at[src], send_sem=send_sem.at[k],
                recv_sem=recv_sem.at[src], device_id={axis: src},
                device_id_type=MESH_ID).wait_recv()
        for copy in sends:
            copy.wait_send()

    return pl.pallas_call(
        kernel,
        out_shape=jax.ShapeDtypeStruct((n,) + block.shape, block.dtype),
        in_specs=[pl.BlockSpec(memory_space=pltpu.VMEM)],
        out_specs=pl.BlockSpec(memory_space=pltpu.VMEM),
        scratch_shapes=[pltpu.SemaphoreType.DMA((n,)), pltpu.SemaphoreType.DMA((n,))],
        compiler_params=pltpu.CompilerParams(collective_id=cid, has_side_effects=True),
    )(block)


def peer_reduce_scatter(parts, axis, n, cid, out_dtype):
    def kernel(x_ref, out_ref, held, send_sem, recv_sem):
        me = lax.axis_index(axis)
        _greet(axis, n, me)
        sends = []
        for k in range(1, n):
            dst = lax.rem(me + k, n)
            copy = pltpu.make_async_remote_copy(
                src_ref=x_ref.at[dst], dst_ref=held.at[me], send_sem=send_sem.at[k],
                recv_sem=recv_sem.at[me], device_id={axis: dst},
                device_id_type=MESH_ID)
            copy.start()
            sends.append(copy)
        total = x_ref[me].astype(jnp.float32)
        for k in range(1, n):
            src = lax.rem(me + n - k, n)
            pltpu.make_async_remote_copy(
                src_ref=x_ref.at[src], dst_ref=held.at[src], send_sem=send_sem.at[k],
                recv_sem=recv_sem.at[src], device_id={axis: src},
                device_id_type=MESH_ID).wait_recv()
            total = total + held[src].astype(jnp.float32)
        out_ref[...] = total.astype(out_ref.dtype)
        for copy in sends:
            copy.wait_send()

    return pl.pallas_call(
        kernel,
        out_shape=jax.ShapeDtypeStruct(parts.shape[1:], out_dtype),
        in_specs=[pl.BlockSpec(memory_space=pltpu.VMEM)],
        out_specs=pl.BlockSpec(memory_space=pltpu.VMEM),
        scratch_shapes=[pltpu.VMEM(parts.shape, parts.dtype),
                        pltpu.SemaphoreType.DMA((n,)), pltpu.SemaphoreType.DMA((n,))],
        compiler_params=pltpu.CompilerParams(collective_id=cid, has_side_effects=True),
    )(parts)


def masked_window_attention(queries, keyval, query_win, key_win, heads):
    nq, width = queries.shape
    head_size = width // heads
    scale = 1.0 / float(head_size) ** 0.5

    def kernel(q_ref, kv_ref, qw_ref, kw_ref, out_ref):
        mask = qw_ref[...] == kw_ref[...]
        for h in range(heads):
            cols = slice(h * head_size, (h + 1) * head_size)
            q = q_ref[:, cols]
            k = kv_ref[:, h * head_size:(h + 1) * head_size]
            v = kv_ref[:, width + h * head_size:width + (h + 1) * head_size]
            s = lax.dot_general(q, k, (((1,), (1,)), ((), ())),
                                preferred_element_type=jnp.float32) * scale
            s = jnp.where(mask, s, -jnp.inf)
            w = jnp.exp(s - jnp.max(s, axis=1, keepdims=True))
            p = (w / jnp.sum(w, axis=1, keepdims=True)).astype(jnp.bfloat16)
            out_ref[:, cols] = jnp.dot(p, v, preferred_element_type=jnp.float32).astype(out_ref.dtype)

    return pl.pallas_call(
        kernel,
        out_shape=jax.ShapeDtypeStruct((nq, width), jnp.bfloat16),
        in_specs=[pl.BlockSpec(memory_space=pltpu.VMEM)] * 4,
        out_specs=pl.BlockSpec(memory_space=pltpu.VMEM),
    )(queries, keyval, query_win, key_win)


def chip_pair_gather(block, axis, n, cid):
    nz = n // 2

    def kernel(x_ref, out_ref, send_sem, recv_sem):
        me = lax.axis_index(axis)
        partner = me + 1 - 2 * lax.rem(me, 2)
        peers = [lax.rem(me + 2 * k, n) for k in range(1, nz)]
        barrier = pltpu.get_barrier_semaphore()
        for dev in peers + [partner]:
            pl.semaphore_signal(barrier, inc=1, device_id={axis: dev}, device_id_type=MESH_ID)
        pl.semaphore_wait(barrier, nz)

        def send(src_ref, slot, dev, index):
            copy = pltpu.make_async_remote_copy(
                src_ref=src_ref, dst_ref=out_ref.at[slot], send_sem=send_sem.at[index],
                recv_sem=recv_sem.at[slot], device_id={axis: dev}, device_id_type=MESH_ID)
            copy.start()
            return copy

        def arrive(slot):
            pltpu.make_async_remote_copy(
                src_ref=x_ref, dst_ref=out_ref.at[slot], send_sem=send_sem.at[0],
                recv_sem=recv_sem.at[slot], device_id={axis: slot},
                device_id_type=MESH_ID).wait_recv()

        sends = [send(x_ref, me, dev, i) for i, dev in enumerate(peers)]
        sends.append(send(x_ref, me, partner, nz - 1))
        out_ref[me] = x_ref[...]
        for k in range(1, nz):
            src = lax.rem(me + n - 2 * k, n)
            arrive(src)
            sends.append(send(out_ref.at[src], src, partner, nz - 1 + k))
        for k in range(nz):
            arrive(lax.rem(partner + 2 * k, n))
        for copy in sends:
            copy.wait_send()

    return pl.pallas_call(
        kernel,
        out_shape=jax.ShapeDtypeStruct((n,) + block.shape, block.dtype),
        in_specs=[pl.BlockSpec(memory_space=pltpu.VMEM)],
        out_specs=pl.BlockSpec(memory_space=pltpu.VMEM),
        scratch_shapes=[pltpu.SemaphoreType.DMA((n,)), pltpu.SemaphoreType.DMA((n,))],
        compiler_params=pltpu.CompilerParams(collective_id=cid, has_side_effects=True),
    )(block)


def grid_reduce_scatter(parts, outer, inner, cid):
    slots, n_hi, n_lo, rows, outs = parts.shape
    half = rows // 2

    def kernel(x_ref, out_ref, r1a, r1b, s1a, s1b, r2a, r2b, send_sem, recv_sem):
        hi = lax.axis_index(outer)
        lo = lax.axis_index(inner)
        barrier = pltpu.get_barrier_semaphore()
        for k in range(1, n_lo):
            pl.semaphore_signal(barrier, inc=1, device_id={inner: lax.rem(lo + k, n_lo)},
                                device_id_type=MESH_ID)
        for k in range(1, n_hi):
            pl.semaphore_signal(barrier, inc=1, device_id={outer: lax.rem(hi + k, n_hi)},
                                device_id_type=MESH_ID)
        pl.semaphore_wait(barrier, n_lo + n_hi - 2)

        def send(src_ref, dst_ref, axis, dev, group, k, slot):
            copy = pltpu.make_async_remote_copy(
                src_ref=src_ref, dst_ref=dst_ref, send_sem=send_sem.at[group, k],
                recv_sem=recv_sem.at[group, slot], device_id={axis: dev},
                device_id_type=MESH_ID)
            copy.start()
            return copy

        def arrive(dst_ref, group, slot):
            pltpu.make_async_remote_copy(
                src_ref=dst_ref, dst_ref=dst_ref, send_sem=send_sem.at[group, 0],
                recv_sem=recv_sem.at[group, slot], device_id={inner: lo},
                device_id_type=MESH_ID).wait_recv()

        sends = []
        for k in range(1, n_lo):
            dev = lax.rem(lo + k, n_lo)
            sends.append(send(x_ref.at[:, :, dev, pl.ds(0, half), :], r1a.at[lo], inner, dev, 0, k, lo))
        for k in range(1, n_hi):
            dev = lax.rem(hi + k, n_hi)
            sends.append(send(x_ref.at[:, dev, :, pl.ds(half, half), :], r1b.at[hi], outer, dev, 1, k, hi))

        sources_lo = [lax.rem(lo + n_lo - k, n_lo) for k in range(1, n_lo)]
        sources_hi = [lax.rem(hi + n_hi - k, n_hi) for k in range(1, n_hi)]
        for src in sources_lo:
            arrive(r1a.at[src], 0, src)
        for h in range(n_hi):
            total = x_ref[:, h, lo, pl.ds(0, half), :].astype(jnp.float32)
            for src in sources_lo:
                total = total + r1a[src, :, h].astype(jnp.float32)
            s1a[h] = total.astype(s1a.dtype)
        for k in range(1, n_hi):
            dev = lax.rem(hi + k, n_hi)
            sends.append(send(s1a.at[dev], r2a.at[hi], outer, dev, 2, k, hi))
        for src in sources_hi:
            arrive(r1b.at[src], 1, src)
        for l in range(n_lo):
            total = x_ref[:, hi, l, pl.ds(half, half), :].astype(jnp.float32)
            for src in sources_hi:
                total = total + r1b[src, :, l].astype(jnp.float32)
            s1b[l] = total.astype(s1b.dtype)
        for k in range(1, n_lo):
            dev = lax.rem(lo + k, n_lo)
            sends.append(send(s1b.at[dev], r2b.at[lo], inner, dev, 3, k, lo))

        total = s1a[hi].astype(jnp.float32)
        for src in sources_hi:
            arrive(r2a.at[src], 2, src)
            total = total + r2a[src].astype(jnp.float32)
        out_ref[:, pl.ds(0, half), :] = total
        total = s1b[lo].astype(jnp.float32)
        for src in sources_lo:
            arrive(r2b.at[src], 3, src)
            total = total + r2b[src].astype(jnp.float32)
        out_ref[:, pl.ds(half, half), :] = total
        for copy in sends:
            copy.wait_send()

    most = max(n_hi, n_lo)
    return pl.pallas_call(
        kernel,
        out_shape=jax.ShapeDtypeStruct((slots, rows, outs), jnp.float32),
        in_specs=[pl.BlockSpec(memory_space=pltpu.VMEM)],
        out_specs=pl.BlockSpec(memory_space=pltpu.VMEM),
        scratch_shapes=[
            pltpu.VMEM((n_lo, slots, n_hi, half, outs), parts.dtype),
            pltpu.VMEM((n_hi, slots, n_lo, half, outs), parts.dtype),
            pltpu.VMEM((n_hi, slots, half, outs), parts.dtype),
            pltpu.VMEM((n_lo, slots, half, outs), parts.dtype),
            pltpu.VMEM((n_hi, slots, half, outs), parts.dtype),
            pltpu.VMEM((n_lo, slots, half, outs), parts.dtype),
            pltpu.SemaphoreType.DMA((4, most)),
            pltpu.SemaphoreType.DMA((4, most)),
        ],
        compiler_params=pltpu.CompilerParams(collective_id=cid, has_side_effects=True),
    )(parts)


def chip_ring_gather(block, axis, n, cid):
    rows = block.shape[0]
    cut = rows // 32 * 16

    def kernel(x_ref, out_ref, send_sem, recv_sem):
        me = lax.axis_index(axis)
        partner = me + 1 - 2 * lax.rem(me, 2)
        up, down, far = lax.rem(me + 2, n), lax.rem(me + n - 2, n), lax.rem(me + 4, n)
        barrier = pltpu.get_barrier_semaphore()
        for dev in (up, down, partner):
            pl.semaphore_signal(barrier, inc=1, device_id={axis: dev}, device_id_type=MESH_ID)
        pl.semaphore_wait(barrier, 3)
        head, tail = pl.ds(0, cut), pl.ds(cut, rows - cut)

        def send(src_ref, slot, part, dev, index, sem_col):
            copy = pltpu.make_async_remote_copy(
                src_ref=src_ref, dst_ref=out_ref.at[slot, part], send_sem=send_sem.at[index],
                recv_sem=recv_sem.at[slot, sem_col], device_id={axis: dev},
                device_id_type=MESH_ID)
            copy.start()
            return copy

        def arrive(slot, part, sem_col):
            pltpu.make_async_remote_copy(
                src_ref=out_ref.at[slot, part], dst_ref=out_ref.at[slot, part],
                send_sem=send_sem.at[0], recv_sem=recv_sem.at[slot, sem_col],
                device_id={axis: slot}, device_id_type=MESH_ID).wait_recv()

        whole = pl.ds(0, rows)
        sends = [send(x_ref, me, whole, up, 0, 0), send(x_ref, me, whole, down, 1, 0),
                 send(x_ref, me, whole, partner, 2, 0)]
        out_ref[me] = x_ref[...]
        arrive(down, whole, 0)
        sends.append(send(out_ref.at[down, head], down, head, up, 3, 0))
        sends.append(send(out_ref.at[down], down, whole, partner, 4, 0))
        arrive(up, whole, 0)
        sends.append(send(out_ref.at[up, tail], up, tail, down, 5, 1))
        sends.append(send(out_ref.at[up], up, whole, partner, 6, 0))
        arrive(far, head, 0)
        arrive(far, tail, 1)
        sends.append(send(out_ref.at[far], far, whole, partner, 7, 0))
        for k in range(4):
            arrive(lax.rem(partner + 2 * k, n), whole, 0)
        for copy in sends:
            copy.wait_send()

    return pl.pallas_call(
        kernel,
        out_shape=jax.ShapeDtypeStruct((n,) + block.shape, block.dtype),
        in_specs=[pl.BlockSpec(memory_space=pltpu.VMEM)],
        out_specs=pl.BlockSpec(memory_space=pltpu.VMEM),
        scratch_shapes=[pltpu.SemaphoreType.DMA((8,)), pltpu.SemaphoreType.DMA((n, 2))],
        compiler_params=pltpu.CompilerParams(collective_id=cid, has_side_effects=True),
    )(block)

HEADS = 16
WH = 6
WW = 12


EPS = 1e-05


def padded(array, sides, width, wrap):
    for axis, dim in sides:
        size, length = (lax.axis_size(axis), array.shape[dim])
        up = [(i, (i + 1) % size) for i in range(size if wrap else size - 1)]
        down = [(j, i) for i, j in up]
        last = lax.slice_in_dim(array, length - width, length, axis=dim)
        initial = lax.slice_in_dim(array, 0, width, axis=dim)
        before = lax.ppermute(last, axis, up)
        after = lax.ppermute(initial, axis, down)
        array = jnp.concatenate([before, array, after], axis=dim)
    return array


def layer_norm(values, gain):
    wide = values.astype(jnp.float32)
    average = jnp.mean(wide, axis=-1, keepdims=True)
    centred = wide - average
    variance = jnp.mean(centred * centred, axis=-1, keepdims=True)
    return (centred * lax.rsqrt(variance + EPS) * gain).astype(jnp.bfloat16)


def window_attention(query_ext, keyval, row_valid, heads):
    ext_rows, ext_cols, width = query_ext.shape
    head_size = width // heads
    win_rows = ext_rows // WH
    win_cols = ext_cols // WW

    def split(values, parts):
        shaped = values.reshape(win_rows, WH, win_cols, WW, parts, heads, head_size)
        return shaped.transpose(0, 2, 1, 3, 4, 5, 6).reshape(
            win_rows * win_cols, WH * WW, parts, heads, head_size
        )

    query_win = split(query_ext, 1)[:, :, 0]
    pairs = split(keyval, 2)
    key_win = pairs[:, :, 0]
    value_win = pairs[:, :, 1]
    key_mask = jnp.broadcast_to(
        row_valid.reshape(win_rows, 1, WH, 1), (win_rows, win_cols, WH, WW)
    ).reshape(win_rows * win_cols, WH * WW)
    scores = jnp.einsum(
        "wqhd,wkhd->whqk", query_win, key_win, preferred_element_type=jnp.float32
    ) / math.sqrt(head_size)
    scores = jnp.where(key_mask[:, None, None, :], scores, -jnp.inf)
    peak = jnp.max(scores, axis=-1, keepdims=True)
    weights = jnp.exp(scores - peak)
    probs = (weights / jnp.sum(weights, axis=-1, keepdims=True)).astype(jnp.bfloat16)
    mixed = jnp.einsum("whqk,wkhd->wqhd", probs, value_win, preferred_element_type=jnp.float32)
    return (
        mixed.reshape(win_rows, win_cols, WH, WW, width)
        .transpose(0, 2, 1, 3, 4)
        .reshape(ext_rows, ext_cols, width)
    )


def slot_terms(piece, target_rows, live_cols, level_scale, level_shift, heads_full):
    piece_wide = piece.astype(jnp.float32)
    rows = (
        piece_wide[None] * level_scale[:, None, None, :] + level_shift[:, None, None, :]
    ).astype(jnp.bfloat16)
    predicted = jnp.einsum("krnd,kdo->krno", rows, heads_full, preferred_element_type=jnp.float32)
    errors = ((predicted - target_rows.astype(jnp.float32)) * live_cols[:, None, :, None]).astype(
        jnp.bfloat16
    )
    back_grad = jnp.einsum("krno,kdo->krnd", errors, heads_full, preferred_element_type=jnp.float32)
    piece_grad = jnp.sum(back_grad * level_scale[:, None, None, :], axis=0)
    head_add = jnp.einsum("krnd,krno->kdo", rows, errors, preferred_element_type=jnp.float32)
    return (piece_grad, head_add)


def local(
    patches,
    norm_gain,
    input_proj,
    output_proj,
    level_scale,
    level_shift,
    head_weight,
    targets,
    level_counts,
    tile_dataset,
    slot_level,
):
    band_rows, band_cols, width = patches.shape
    half_rows = WH // 2
    half_cols = WW // 2
    lat_count = lax.axis_size(LAT)
    var_count = lax.axis_size("var")
    lat_place = lax.axis_index(LAT)
    ext_rows = band_rows + WH
    ext_cols = band_cols + WW
    extended = padded(patches, ((LAT, 0),), half_rows, False)
    extended, own = lax.optimization_barrier((extended, patches))
    own_normed = layer_norm(own, norm_gain).reshape(-1, width)
    queries = jnp.dot(own_normed, input_proj[:, :width], preferred_element_type=jnp.float32)
    queries = queries.astype(jnp.bfloat16)
    own_keyval = jnp.dot(own_normed, input_proj[:, width:], preferred_element_type=jnp.float32)
    extended = padded(extended, (("var", 1),), half_cols, True)

    def ring(grid):
        top, bottom = grid[:half_rows], grid[half_rows + band_rows :]
        middle = grid[half_rows : half_rows + band_rows]
        left, right = middle[:, :half_cols], middle[:, half_cols + band_cols :]
        return jnp.concatenate(
            [part.reshape((-1,) + grid.shape[2:]) for part in (top, bottom, left, right)]
        )

    halo_normed = layer_norm(ring(extended), norm_gain)
    halo_keyval = jnp.dot(halo_normed, input_proj[:, width:], preferred_element_type=jnp.float32)
    keyval = jnp.concatenate([own_keyval, halo_keyval]).astype(jnp.bfloat16)
    global_row = lat_place * band_rows - half_rows + jnp.arange(ext_rows, dtype=jnp.int32)
    row_valid = (global_row >= 0) & (global_row < lat_count * band_rows)
    win_cols = ext_cols // WW
    ext_r = jnp.arange(ext_rows, dtype=jnp.int32)[:, None]
    ext_c = jnp.arange(ext_cols, dtype=jnp.int32)[None, :]
    key_grid = jnp.where(row_valid[:, None], (ext_r // WH) * win_cols + ext_c // WW, -1)
    query_win = key_grid[half_rows : half_rows + band_rows, half_cols : half_cols + band_cols]
    key_win = jnp.concatenate([query_win.reshape(-1), ring(key_grid)])
    attn = masked_window_attention(
        queries,
        keyval,
        query_win.reshape(-1, 1),
        key_win.reshape(1, -1),
        HEADS,
    ).reshape(band_rows, band_cols, width)
    update = jnp.dot(
        attn.reshape(-1, width), output_proj, preferred_element_type=jnp.float32
    ).reshape(band_rows, band_cols, width)
    latent = (patches.astype(jnp.float32) + update).astype(jnp.bfloat16)
    dataset_row = tile_dataset[0]
    dataset_ids = jnp.arange(level_counts.shape[0], dtype=jnp.int32)
    tile_levels = jnp.sum(
        jnp.where(dataset_row[:, None] == dataset_ids[None, :], level_counts[None, :], 0), axis=1
    )
    live_tiles = (slot_level[None, :] < tile_levels[:, None]).astype(jnp.float32)
    heads_full = lax.all_gather(head_weight, LAT, axis=1, tiled=True)
    tile_ids = jnp.arange(var_count, dtype=jnp.int32)
    gather = chip_ring_gather if var_count == 8 else chip_pair_gather
    tiles = gather(latent.reshape(band_rows * band_cols, width), "var", var_count, 1)
    piece = (
        tiles.reshape(var_count, band_rows, band_cols, width)
        .transpose(1, 0, 2, 3)
        .reshape(band_rows, var_count * band_cols, width)
    )
    piece_cols = piece.shape[1]
    column_tile = jnp.arange(piece_cols, dtype=jnp.int32) // band_cols
    onehot = (column_tile[:, None] == tile_ids[None, :]).astype(jnp.float32)
    column_live = jnp.dot(onehot, live_tiles)
    piece_grad, head_add = slot_terms(
        piece, targets, column_live.T, level_scale, level_shift, heads_full
    )
    latent_terms = piece_grad
    latent_terms, head_terms = (latent_terms, head_add)
    grad_latent = lax.psum_scatter(
        latent_terms.astype(jnp.bfloat16), "var", scatter_dimension=1, tiled=True
    )
    head_terms = head_terms * (1.0 / math.sqrt(lat_count * band_rows * var_count * band_cols))
    outer, inner = lax.axis_size(LAT[0]), lax.axis_size(LAT[1])
    slots, outs = head_terms.shape[0], head_terms.shape[2]
    share_rows = width // lat_count
    head_parts = head_terms.astype(jnp.bfloat16).reshape(slots, outer, inner, share_rows, outs)
    grad_head = grid_reduce_scatter(head_parts, LAT[0], LAT[1], 3)
    return (latent, grad_latent, grad_head)


def solution(mesh):
    in_specs = (
        P(LAT, "var", None),
        P(),
        P(),
        P(),
        P("var", None),
        P("var", None),
        P("var", LAT, None),
        P("var", LAT, None, None),
        P(),
        P(LAT, None),
        P("var"),
    )
    out_specs = (P(LAT, "var", None), P(LAT, "var", None), P("var", LAT, None))
    lat_size = mesh.shape["lat"]
    inner = 4 if lat_size % 4 == 0 else 1
    grid = Mesh(
        mesh.devices.reshape(lat_size // inner, inner, mesh.shape["var"]), LAT + ("var",)
    )
    return jax.shard_map(local, mesh=grid, in_specs=in_specs, out_specs=out_specs, check_vma=False)
```

```python
import math

import jax
import jax.numpy as jnp
from jax import lax
from jax.experimental import pallas as pl
from jax.experimental.pallas import tpu as pltpu
from jax.sharding import Mesh, PartitionSpec as P

MESH_ID = pl.DeviceIdType.MESH
LAT = ("lat_hi", "lat_lo")


def _greet(axis, n, me):
    barrier = pltpu.get_barrier_semaphore()
    for k in range(1, n):
        pl.semaphore_signal(barrier, inc=1, device_id={axis: lax.rem(me + k, n)},
                            device_id_type=MESH_ID)
    pl.semaphore_wait(barrier, n - 1)


def peer_gather(block, axis, n, cid):
    def kernel(x_ref, out_ref, send_sem, recv_sem):
        me = lax.axis_index(axis)
        _greet(axis, n, me)
        sends = []
        for k in range(1, n):
            copy = pltpu.make_async_remote_copy(
                src_ref=x_ref, dst_ref=out_ref.at[me], send_sem=send_sem.at[k],
                recv_sem=recv_sem.at[me], device_id={axis: lax.rem(me + k, n)},
                device_id_type=MESH_ID)
            copy.start()
            sends.append(copy)
        out_ref[me] = x_ref[...]
        for k in range(1, n):
            src = lax.rem(me + n - k, n)
            pltpu.make_async_remote_copy(
                src_ref=x_ref, dst_ref=out_ref.at[src], send_sem=send_sem.at[k],
                recv_sem=recv_sem.at[src], device_id={axis: src},
                device_id_type=MESH_ID).wait_recv()
        for copy in sends:
            copy.wait_send()

    return pl.pallas_call(
        kernel,
        out_shape=jax.ShapeDtypeStruct((n,) + block.shape, block.dtype),
        in_specs=[pl.BlockSpec(memory_space=pltpu.VMEM)],
        out_specs=pl.BlockSpec(memory_space=pltpu.VMEM),
        scratch_shapes=[pltpu.SemaphoreType.DMA((n,)), pltpu.SemaphoreType.DMA((n,))],
        compiler_params=pltpu.CompilerParams(collective_id=cid, has_side_effects=True),
    )(block)


def peer_reduce_scatter(parts, axis, n, cid, out_dtype):
    def kernel(x_ref, out_ref, held, send_sem, recv_sem):
        me = lax.axis_index(axis)
        _greet(axis, n, me)
        sends = []
        for k in range(1, n):
            dst = lax.rem(me + k, n)
            copy = pltpu.make_async_remote_copy(
                src_ref=x_ref.at[dst], dst_ref=held.at[me], send_sem=send_sem.at[k],
                recv_sem=recv_sem.at[me], device_id={axis: dst},
                device_id_type=MESH_ID)
            copy.start()
            sends.append(copy)
        total = x_ref[me].astype(jnp.float32)
        for k in range(1, n):
            src = lax.rem(me + n - k, n)
            pltpu.make_async_remote_copy(
                src_ref=x_ref.at[src], dst_ref=held.at[src], send_sem=send_sem.at[k],
                recv_sem=recv_sem.at[src], device_id={axis: src},
                device_id_type=MESH_ID).wait_recv()
            total = total + held[src].astype(jnp.float32)
        out_ref[...] = total.astype(out_ref.dtype)
        for copy in sends:
            copy.wait_send()

    return pl.pallas_call(
        kernel,
        out_shape=jax.ShapeDtypeStruct(parts.shape[1:], out_dtype),
        in_specs=[pl.BlockSpec(memory_space=pltpu.VMEM)],
        out_specs=pl.BlockSpec(memory_space=pltpu.VMEM),
        scratch_shapes=[pltpu.VMEM(parts.shape, parts.dtype),
                        pltpu.SemaphoreType.DMA((n,)), pltpu.SemaphoreType.DMA((n,))],
        compiler_params=pltpu.CompilerParams(collective_id=cid, has_side_effects=True),
    )(parts)


def masked_window_attention(queries, keyval, query_win, key_win, heads):
    nq, width = queries.shape
    head_size = width // heads
    scale = 1.0 / float(head_size) ** 0.5

    def kernel(q_ref, kv_ref, qw_ref, kw_ref, out_ref):
        mask = qw_ref[...] == kw_ref[...]
        for h in range(heads):
            cols = slice(h * head_size, (h + 1) * head_size)
            q = q_ref[:, cols]
            k = kv_ref[:, h * head_size:(h + 1) * head_size]
            v = kv_ref[:, width + h * head_size:width + (h + 1) * head_size]
            s = lax.dot_general(q, k, (((1,), (1,)), ((), ())),
                                preferred_element_type=jnp.float32) * scale
            s = jnp.where(mask, s, -jnp.inf)
            w = jnp.exp(s - jnp.max(s, axis=1, keepdims=True))
            p = (w / jnp.sum(w, axis=1, keepdims=True)).astype(jnp.bfloat16)
            out_ref[:, cols] = jnp.dot(p, v, preferred_element_type=jnp.float32).astype(out_ref.dtype)

    return pl.pallas_call(
        kernel,
        out_shape=jax.ShapeDtypeStruct((nq, width), jnp.bfloat16),
        in_specs=[pl.BlockSpec(memory_space=pltpu.VMEM)] * 4,
        out_specs=pl.BlockSpec(memory_space=pltpu.VMEM),
    )(queries, keyval, query_win, key_win)


def chip_pair_gather(block, axis, n, cid):
    nz = n // 2

    def kernel(x_ref, out_ref, send_sem, recv_sem):
        me = lax.axis_index(axis)
        partner = me + 1 - 2 * lax.rem(me, 2)
        peers = [lax.rem(me + 2 * k, n) for k in range(1, nz)]
        barrier = pltpu.get_barrier_semaphore()
        for dev in peers + [partner]:
            pl.semaphore_signal(barrier, inc=1, device_id={axis: dev}, device_id_type=MESH_ID)
        pl.semaphore_wait(barrier, nz)

        def send(src_ref, slot, dev, index):
            copy = pltpu.make_async_remote_copy(
                src_ref=src_ref, dst_ref=out_ref.at[slot], send_sem=send_sem.at[index],
                recv_sem=recv_sem.at[slot], device_id={axis: dev}, device_id_type=MESH_ID)
            copy.start()
            return copy

        def arrive(slot):
            pltpu.make_async_remote_copy(
                src_ref=x_ref, dst_ref=out_ref.at[slot], send_sem=send_sem.at[0],
                recv_sem=recv_sem.at[slot], device_id={axis: slot},
                device_id_type=MESH_ID).wait_recv()

        sends = [send(x_ref, me, dev, i) for i, dev in enumerate(peers)]
        sends.append(send(x_ref, me, partner, nz - 1))
        out_ref[me] = x_ref[...]
        for k in range(1, nz):
            src = lax.rem(me + n - 2 * k, n)
            arrive(src)
            sends.append(send(out_ref.at[src], src, partner, nz - 1 + k))
        for k in range(nz):
            arrive(lax.rem(partner + 2 * k, n))
        for copy in sends:
            copy.wait_send()

    return pl.pallas_call(
        kernel,
        out_shape=jax.ShapeDtypeStruct((n,) + block.shape, block.dtype),
        in_specs=[pl.BlockSpec(memory_space=pltpu.VMEM)],
        out_specs=pl.BlockSpec(memory_space=pltpu.VMEM),
        scratch_shapes=[pltpu.SemaphoreType.DMA((n,)), pltpu.SemaphoreType.DMA((n,))],
        compiler_params=pltpu.CompilerParams(collective_id=cid, has_side_effects=True),
    )(block)


def grid_reduce_scatter(parts, outer, inner, cid):
    slots, n_hi, n_lo, rows, outs = parts.shape
    half = rows // 2

    def kernel(x_ref, out_ref, r1a, r1b, s1a, s1b, r2a, r2b, send_sem, recv_sem):
        hi = lax.axis_index(outer)
        lo = lax.axis_index(inner)
        barrier = pltpu.get_barrier_semaphore()
        for k in range(1, n_lo):
            pl.semaphore_signal(barrier, inc=1, device_id={inner: lax.rem(lo + k, n_lo)},
                                device_id_type=MESH_ID)
        for k in range(1, n_hi):
            pl.semaphore_signal(barrier, inc=1, device_id={outer: lax.rem(hi + k, n_hi)},
                                device_id_type=MESH_ID)
        pl.semaphore_wait(barrier, n_lo + n_hi - 2)

        def send(src_ref, dst_ref, axis, dev, group, k, slot):
            copy = pltpu.make_async_remote_copy(
                src_ref=src_ref, dst_ref=dst_ref, send_sem=send_sem.at[group, k],
                recv_sem=recv_sem.at[group, slot], device_id={axis: dev},
                device_id_type=MESH_ID)
            copy.start()
            return copy

        def arrive(dst_ref, group, slot):
            pltpu.make_async_remote_copy(
                src_ref=dst_ref, dst_ref=dst_ref, send_sem=send_sem.at[group, 0],
                recv_sem=recv_sem.at[group, slot], device_id={inner: lo},
                device_id_type=MESH_ID).wait_recv()

        sends = []
        for k in range(1, n_lo):
            dev = lax.rem(lo + k, n_lo)
            sends.append(send(x_ref.at[:, :, dev, pl.ds(0, half), :], r1a.at[lo], inner, dev, 0, k, lo))
        for k in range(1, n_hi):
            dev = lax.rem(hi + k, n_hi)
            sends.append(send(x_ref.at[:, dev, :, pl.ds(half, half), :], r1b.at[hi], outer, dev, 1, k, hi))

        sources_lo = [lax.rem(lo + n_lo - k, n_lo) for k in range(1, n_lo)]
        sources_hi = [lax.rem(hi + n_hi - k, n_hi) for k in range(1, n_hi)]
        for src in sources_lo:
            arrive(r1a.at[src], 0, src)
        for h in range(n_hi):
            total = x_ref[:, h, lo, pl.ds(0, half), :].astype(jnp.float32)
            for src in sources_lo:
                total = total + r1a[src, :, h].astype(jnp.float32)
            s1a[h] = total.astype(s1a.dtype)
        for k in range(1, n_hi):
            dev = lax.rem(hi + k, n_hi)
            sends.append(send(s1a.at[dev], r2a.at[hi], outer, dev, 2, k, hi))
        for src in sources_hi:
            arrive(r1b.at[src], 1, src)
        for l in range(n_lo):
            total = x_ref[:, hi, l, pl.ds(half, half), :].astype(jnp.float32)
            for src in sources_hi:
                total = total + r1b[src, :, l].astype(jnp.float32)
            s1b[l] = total.astype(s1b.dtype)
        for k in range(1, n_lo):
            dev = lax.rem(lo + k, n_lo)
            sends.append(send(s1b.at[dev], r2b.at[lo], inner, dev, 3, k, lo))

        total = s1a[hi].astype(jnp.float32)
        for src in sources_hi:
            arrive(r2a.at[src], 2, src)
            total = total + r2a[src].astype(jnp.float32)
        out_ref[:, pl.ds(0, half), :] = total
        total = s1b[lo].astype(jnp.float32)
        for src in sources_lo:
            arrive(r2b.at[src], 3, src)
            total = total + r2b[src].astype(jnp.float32)
        out_ref[:, pl.ds(half, half), :] = total
        for copy in sends:
            copy.wait_send()

    most = max(n_hi, n_lo)
    return pl.pallas_call(
        kernel,
        out_shape=jax.ShapeDtypeStruct((slots, rows, outs), jnp.float32),
        in_specs=[pl.BlockSpec(memory_space=pltpu.VMEM)],
        out_specs=pl.BlockSpec(memory_space=pltpu.VMEM),
        scratch_shapes=[
            pltpu.VMEM((n_lo, slots, n_hi, half, outs), parts.dtype),
            pltpu.VMEM((n_hi, slots, n_lo, half, outs), parts.dtype),
            pltpu.VMEM((n_hi, slots, half, outs), parts.dtype),
            pltpu.VMEM((n_lo, slots, half, outs), parts.dtype),
            pltpu.VMEM((n_hi, slots, half, outs), parts.dtype),
            pltpu.VMEM((n_lo, slots, half, outs), parts.dtype),
            pltpu.SemaphoreType.DMA((4, most)),
            pltpu.SemaphoreType.DMA((4, most)),
        ],
        compiler_params=pltpu.CompilerParams(collective_id=cid, has_side_effects=True),
    )(parts)


def chip_ring_gather(block, axis, n, cid):
    rows = block.shape[0]
    cut = rows // 32 * 16

    def kernel(x_ref, out_ref, send_sem, recv_sem):
        me = lax.axis_index(axis)
        partner = me + 1 - 2 * lax.rem(me, 2)
        up, down, far = lax.rem(me + 2, n), lax.rem(me + n - 2, n), lax.rem(me + 4, n)
        barrier = pltpu.get_barrier_semaphore()
        for dev in (up, down, partner):
            pl.semaphore_signal(barrier, inc=1, device_id={axis: dev}, device_id_type=MESH_ID)
        pl.semaphore_wait(barrier, 3)
        head, tail = pl.ds(0, cut), pl.ds(cut, rows - cut)

        def send(src_ref, slot, part, dev, index, sem_col):
            copy = pltpu.make_async_remote_copy(
                src_ref=src_ref, dst_ref=out_ref.at[slot, part], send_sem=send_sem.at[index],
                recv_sem=recv_sem.at[slot, sem_col], device_id={axis: dev},
                device_id_type=MESH_ID)
            copy.start()
            return copy

        def arrive(slot, part, sem_col):
            pltpu.make_async_remote_copy(
                src_ref=out_ref.at[slot, part], dst_ref=out_ref.at[slot, part],
                send_sem=send_sem.at[0], recv_sem=recv_sem.at[slot, sem_col],
                device_id={axis: slot}, device_id_type=MESH_ID).wait_recv()

        whole = pl.ds(0, rows)
        sends = [send(x_ref, me, whole, up, 0, 0), send(x_ref, me, whole, down, 1, 0),
                 send(x_ref, me, whole, partner, 2, 0)]
        out_ref[me] = x_ref[...]
        arrive(down, whole, 0)
        sends.append(send(out_ref.at[down, head], down, head, up, 3, 0))
        sends.append(send(out_ref.at[down], down, whole, partner, 4, 0))
        arrive(up, whole, 0)
        sends.append(send(out_ref.at[up, tail], up, tail, down, 5, 1))
        sends.append(send(out_ref.at[up], up, whole, partner, 6, 0))
        arrive(far, head, 0)
        arrive(far, tail, 1)
        sends.append(send(out_ref.at[far], far, whole, partner, 7, 0))
        for k in range(4):
            arrive(lax.rem(partner + 2 * k, n), whole, 0)
        for copy in sends:
            copy.wait_send()

    return pl.pallas_call(
        kernel,
        out_shape=jax.ShapeDtypeStruct((n,) + block.shape, block.dtype),
        in_specs=[pl.BlockSpec(memory_space=pltpu.VMEM)],
        out_specs=pl.BlockSpec(memory_space=pltpu.VMEM),
        scratch_shapes=[pltpu.SemaphoreType.DMA((8,)), pltpu.SemaphoreType.DMA((n, 2))],
        compiler_params=pltpu.CompilerParams(collective_id=cid, has_side_effects=True),
    )(block)

HEADS = 16
WH = 6
WW = 12


EPS = 1e-05


def padded(array, sides, width, wrap):
    for axis, dim in sides:
        size, length = (lax.axis_size(axis), array.shape[dim])
        up = [(i, (i + 1) % size) for i in range(size if wrap else size - 1)]
        down = [(j, i) for i, j in up]
        last = lax.slice_in_dim(array, length - width, length, axis=dim)
        initial = lax.slice_in_dim(array, 0, width, axis=dim)
        before = lax.ppermute(last, axis, up)
        after = lax.ppermute(initial, axis, down)
        array = jnp.concatenate([before, array, after], axis=dim)
    return array


def layer_norm(values, gain):
    wide = values.astype(jnp.float32)
    average = jnp.mean(wide, axis=-1, keepdims=True)
    centred = wide - average
    variance = jnp.mean(centred * centred, axis=-1, keepdims=True)
    return (centred * lax.rsqrt(variance + EPS) * gain).astype(jnp.bfloat16)


def window_attention(query_ext, keyval, row_valid, heads):
    ext_rows, ext_cols, width = query_ext.shape
    head_size = width // heads
    win_rows = ext_rows // WH
    win_cols = ext_cols // WW

    def split(values, parts):
        shaped = values.reshape(win_rows, WH, win_cols, WW, parts, heads, head_size)
        return shaped.transpose(0, 2, 1, 3, 4, 5, 6).reshape(
            win_rows * win_cols, WH * WW, parts, heads, head_size
        )

    query_win = split(query_ext, 1)[:, :, 0]
    pairs = split(keyval, 2)
    key_win = pairs[:, :, 0]
    value_win = pairs[:, :, 1]
    key_mask = jnp.broadcast_to(
        row_valid.reshape(win_rows, 1, WH, 1), (win_rows, win_cols, WH, WW)
    ).reshape(win_rows * win_cols, WH * WW)
    scores = jnp.einsum(
        "wqhd,wkhd->whqk", query_win, key_win, preferred_element_type=jnp.float32
    ) / math.sqrt(head_size)
    scores = jnp.where(key_mask[:, None, None, :], scores, -jnp.inf)
    peak = jnp.max(scores, axis=-1, keepdims=True)
    weights = jnp.exp(scores - peak)
    probs = (weights / jnp.sum(weights, axis=-1, keepdims=True)).astype(jnp.bfloat16)
    mixed = jnp.einsum("whqk,wkhd->wqhd", probs, value_win, preferred_element_type=jnp.float32)
    return (
        mixed.reshape(win_rows, win_cols, WH, WW, width)
        .transpose(0, 2, 1, 3, 4)
        .reshape(ext_rows, ext_cols, width)
    )


def slot_terms(piece, target_rows, live_cols, level_scale, level_shift, heads_full):
    piece_wide = piece.astype(jnp.float32)
    rows = (
        piece_wide[None] * level_scale[:, None, None, :] + level_shift[:, None, None, :]
    ).astype(jnp.bfloat16)
    predicted = jnp.einsum("krnd,kdo->krno", rows, heads_full, preferred_element_type=jnp.float32)
    errors = ((predicted - target_rows.astype(jnp.float32)) * live_cols[:, None, :, None]).astype(
        jnp.bfloat16
    )
    back_grad = jnp.einsum("krno,kdo->krnd", errors, heads_full, preferred_element_type=jnp.float32)
    piece_grad = jnp.sum(back_grad * level_scale[:, None, None, :], axis=0)
    head_add = jnp.einsum("krnd,krno->kdo", rows, errors, preferred_element_type=jnp.float32)
    return (piece_grad, head_add)


def local(
    patches,
    norm_gain,
    input_proj,
    output_proj,
    level_scale,
    level_shift,
    head_weight,
    targets,
    level_counts,
    tile_dataset,
    slot_level,
):
    band_rows, band_cols, width = patches.shape
    half_rows = WH // 2
    half_cols = WW // 2
    lat_count = lax.axis_size(LAT)
    var_count = lax.axis_size("var")
    lat_place = lax.axis_index(LAT)
    ext_rows = band_rows + WH
    ext_cols = band_cols + WW
    extended = padded(patches, ((LAT, 0),), half_rows, False)
    extended, own = lax.optimization_barrier((extended, patches))
    own_normed = layer_norm(own, norm_gain).reshape(-1, width)
    queries = jnp.dot(own_normed, input_proj[:, :width], preferred_element_type=jnp.float32)
    queries = queries.astype(jnp.bfloat16)
    own_keyval = jnp.dot(own_normed, input_proj[:, width:], preferred_element_type=jnp.float32)
    extended = padded(extended, (("var", 1),), half_cols, True)

    def ring(grid):
        top, bottom = grid[:half_rows], grid[half_rows + band_rows :]
        middle = grid[half_rows : half_rows + band_rows]
        left, right = middle[:, :half_cols], middle[:, half_cols + band_cols :]
        return jnp.concatenate(
            [part.reshape((-1,) + grid.shape[2:]) for part in (top, bottom, left, right)]
        )

    halo_normed = layer_norm(ring(extended), norm_gain)
    halo_keyval = jnp.dot(halo_normed, input_proj[:, width:], preferred_element_type=jnp.float32)
    keyval = jnp.concatenate([own_keyval, halo_keyval]).astype(jnp.bfloat16)
    global_row = lat_place * band_rows - half_rows + jnp.arange(ext_rows, dtype=jnp.int32)
    row_valid = (global_row >= 0) & (global_row < lat_count * band_rows)
    win_cols = ext_cols // WW
    ext_r = jnp.arange(ext_rows, dtype=jnp.int32)[:, None]
    ext_c = jnp.arange(ext_cols, dtype=jnp.int32)[None, :]
    key_grid = jnp.where(row_valid[:, None], (ext_r // WH) * win_cols + ext_c // WW, -1)
    query_win = key_grid[half_rows : half_rows + band_rows, half_cols : half_cols + band_cols]
    key_win = jnp.concatenate([query_win.reshape(-1), ring(key_grid)])
    attn = masked_window_attention(
        queries,
        keyval,
        query_win.reshape(-1, 1),
        key_win.reshape(1, -1),
        HEADS,
    ).reshape(band_rows, band_cols, width)
    update = jnp.dot(
        attn.reshape(-1, width), output_proj, preferred_element_type=jnp.float32
    ).reshape(band_rows, band_cols, width)
    latent = (patches.astype(jnp.float32) + update).astype(jnp.bfloat16)
    dataset_row = tile_dataset[0]
    dataset_ids = jnp.arange(level_counts.shape[0], dtype=jnp.int32)
    tile_levels = jnp.sum(
        jnp.where(dataset_row[:, None] == dataset_ids[None, :], level_counts[None, :], 0), axis=1
    )
    live_tiles = (slot_level[None, :] < tile_levels[:, None]).astype(jnp.float32)
    heads_full = lax.all_gather(head_weight, LAT, axis=1, tiled=True)
    tile_ids = jnp.arange(var_count, dtype=jnp.int32)
    gather = chip_ring_gather if var_count == 8 else chip_pair_gather
    tiles = gather(latent.reshape(band_rows * band_cols, width), "var", var_count, 1)
    piece = (
        tiles.reshape(var_count, band_rows, band_cols, width)
        .transpose(1, 0, 2, 3)
        .reshape(band_rows, var_count * band_cols, width)
    )
    piece_cols = piece.shape[1]
    column_tile = jnp.arange(piece_cols, dtype=jnp.int32) // band_cols
    onehot = (column_tile[:, None] == tile_ids[None, :]).astype(jnp.float32)
    column_live = jnp.dot(onehot, live_tiles)
    piece_grad, head_add = slot_terms(
        piece, targets, column_live.T, level_scale, level_shift, heads_full
    )
    latent_terms = piece_grad
    latent_terms, head_terms = (latent_terms, head_add)
    latent_parts = (
        latent_terms.astype(jnp.bfloat16)
        .reshape(band_rows, var_count, band_cols, width)
        .transpose(1, 0, 2, 3)
    )
    grad_latent = lax.psum_scatter(latent_parts, "var", scatter_dimension=0, tiled=True)
    grad_latent = grad_latent.reshape(band_rows, band_cols, width)
    head_terms = head_terms * (1.0 / math.sqrt(lat_count * band_rows * var_count * band_cols))
    outer, inner = lax.axis_size(LAT[0]), lax.axis_size(LAT[1])
    slots, outs = head_terms.shape[0], head_terms.shape[2]
    share_rows = width // lat_count
    head_parts = head_terms.astype(jnp.bfloat16).reshape(slots, outer, inner, share_rows, outs)
    grad_head = grid_reduce_scatter(head_parts, LAT[0], LAT[1], 3)
    return (latent, grad_latent, grad_head)


def solution(mesh):
    in_specs = (
        P(LAT, "var", None),
        P(),
        P(),
        P(),
        P("var", None),
        P("var", None),
        P("var", LAT, None),
        P("var", LAT, None, None),
        P(),
        P(LAT, None),
        P("var"),
    )
    out_specs = (P(LAT, "var", None), P(LAT, "var", None), P("var", LAT, None))
    lat_size = mesh.shape["lat"]
    inner = 4 if lat_size % 4 == 0 else 1
    grid = Mesh(
        mesh.devices.reshape(lat_size // inner, inner, mesh.shape["var"]), LAT + ("var",)
    )
    return jax.shard_map(local, mesh=grid, in_specs=in_specs, out_specs=out_specs, check_vma=False)
```

```python
import math

import jax
import jax.numpy as jnp
from jax import lax
from jax.experimental import pallas as pl
from jax.experimental.pallas import tpu as pltpu
from jax.sharding import Mesh, PartitionSpec as P

MESH_ID = pl.DeviceIdType.MESH
LAT = ("lat_hi", "lat_lo")


def _greet(axis, n, me):
    barrier = pltpu.get_barrier_semaphore()
    for k in range(1, n):
        pl.semaphore_signal(barrier, inc=1, device_id={axis: lax.rem(me + k, n)},
                            device_id_type=MESH_ID)
    pl.semaphore_wait(barrier, n - 1)


def peer_gather(block, axis, n, cid):
    def kernel(x_ref, out_ref, send_sem, recv_sem):
        me = lax.axis_index(axis)
        _greet(axis, n, me)
        sends = []
        for k in range(1, n):
            copy = pltpu.make_async_remote_copy(
                src_ref=x_ref, dst_ref=out_ref.at[me], send_sem=send_sem.at[k],
                recv_sem=recv_sem.at[me], device_id={axis: lax.rem(me + k, n)},
                device_id_type=MESH_ID)
            copy.start()
            sends.append(copy)
        out_ref[me] = x_ref[...]
        for k in range(1, n):
            src = lax.rem(me + n - k, n)
            pltpu.make_async_remote_copy(
                src_ref=x_ref, dst_ref=out_ref.at[src], send_sem=send_sem.at[k],
                recv_sem=recv_sem.at[src], device_id={axis: src},
                device_id_type=MESH_ID).wait_recv()
        for copy in sends:
            copy.wait_send()

    return pl.pallas_call(
        kernel,
        out_shape=jax.ShapeDtypeStruct((n,) + block.shape, block.dtype),
        in_specs=[pl.BlockSpec(memory_space=pltpu.VMEM)],
        out_specs=pl.BlockSpec(memory_space=pltpu.VMEM),
        scratch_shapes=[pltpu.SemaphoreType.DMA((n,)), pltpu.SemaphoreType.DMA((n,))],
        compiler_params=pltpu.CompilerParams(collective_id=cid, has_side_effects=True),
    )(block)


def peer_reduce_scatter(parts, axis, n, cid, out_dtype):
    def kernel(x_ref, out_ref, held, send_sem, recv_sem):
        me = lax.axis_index(axis)
        _greet(axis, n, me)
        sends = []
        for k in range(1, n):
            dst = lax.rem(me + k, n)
            copy = pltpu.make_async_remote_copy(
                src_ref=x_ref.at[dst], dst_ref=held.at[me], send_sem=send_sem.at[k],
                recv_sem=recv_sem.at[me], device_id={axis: dst},
                device_id_type=MESH_ID)
            copy.start()
            sends.append(copy)
        total = x_ref[me].astype(jnp.float32)
        for k in range(1, n):
            src = lax.rem(me + n - k, n)
            pltpu.make_async_remote_copy(
                src_ref=x_ref.at[src], dst_ref=held.at[src], send_sem=send_sem.at[k],
                recv_sem=recv_sem.at[src], device_id={axis: src},
                device_id_type=MESH_ID).wait_recv()
            total = total + held[src].astype(jnp.float32)
        out_ref[...] = total.astype(out_ref.dtype)
        for copy in sends:
            copy.wait_send()

    return pl.pallas_call(
        kernel,
        out_shape=jax.ShapeDtypeStruct(parts.shape[1:], out_dtype),
        in_specs=[pl.BlockSpec(memory_space=pltpu.VMEM)],
        out_specs=pl.BlockSpec(memory_space=pltpu.VMEM),
        scratch_shapes=[pltpu.VMEM(parts.shape, parts.dtype),
                        pltpu.SemaphoreType.DMA((n,)), pltpu.SemaphoreType.DMA((n,))],
        compiler_params=pltpu.CompilerParams(collective_id=cid, has_side_effects=True),
    )(parts)


def masked_window_attention(queries, keyval, query_win, key_win, heads):
    nq, width = queries.shape
    head_size = width // heads
    scale = 1.0 / float(head_size) ** 0.5

    def kernel(q_ref, kv_ref, qw_ref, kw_ref, out_ref):
        mask = qw_ref[...] == kw_ref[...]
        for h in range(heads):
            cols = slice(h * head_size, (h + 1) * head_size)
            q = q_ref[:, cols]
            k = kv_ref[:, h * head_size:(h + 1) * head_size]
            v = kv_ref[:, width + h * head_size:width + (h + 1) * head_size]
            s = lax.dot_general(q, k, (((1,), (1,)), ((), ())),
                                preferred_element_type=jnp.float32) * scale
            s = jnp.where(mask, s, -jnp.inf)
            w = jnp.exp(s - jnp.max(s, axis=1, keepdims=True))
            p = (w / jnp.sum(w, axis=1, keepdims=True)).astype(jnp.bfloat16)
            out_ref[:, cols] = jnp.dot(p, v, preferred_element_type=jnp.float32).astype(out_ref.dtype)

    return pl.pallas_call(
        kernel,
        out_shape=jax.ShapeDtypeStruct((nq, width), jnp.bfloat16),
        in_specs=[pl.BlockSpec(memory_space=pltpu.VMEM)] * 4,
        out_specs=pl.BlockSpec(memory_space=pltpu.VMEM),
    )(queries, keyval, query_win, key_win)


def chip_pair_gather(block, axis, n, cid):
    nz = n // 2

    def kernel(x_ref, out_ref, send_sem, recv_sem):
        me = lax.axis_index(axis)
        partner = me + 1 - 2 * lax.rem(me, 2)
        peers = [lax.rem(me + 2 * k, n) for k in range(1, nz)]
        barrier = pltpu.get_barrier_semaphore()
        for dev in peers + [partner]:
            pl.semaphore_signal(barrier, inc=1, device_id={axis: dev}, device_id_type=MESH_ID)
        pl.semaphore_wait(barrier, nz)

        def send(src_ref, slot, dev, index):
            copy = pltpu.make_async_remote_copy(
                src_ref=src_ref, dst_ref=out_ref.at[slot], send_sem=send_sem.at[index],
                recv_sem=recv_sem.at[slot], device_id={axis: dev}, device_id_type=MESH_ID)
            copy.start()
            return copy

        def arrive(slot):
            pltpu.make_async_remote_copy(
                src_ref=x_ref, dst_ref=out_ref.at[slot], send_sem=send_sem.at[0],
                recv_sem=recv_sem.at[slot], device_id={axis: slot},
                device_id_type=MESH_ID).wait_recv()

        sends = [send(x_ref, me, dev, i) for i, dev in enumerate(peers)]
        sends.append(send(x_ref, me, partner, nz - 1))
        out_ref[me] = x_ref[...]
        for k in range(1, nz):
            src = lax.rem(me + n - 2 * k, n)
            arrive(src)
            sends.append(send(out_ref.at[src], src, partner, nz - 1 + k))
        for k in range(nz):
            arrive(lax.rem(partner + 2 * k, n))
        for copy in sends:
            copy.wait_send()

    return pl.pallas_call(
        kernel,
        out_shape=jax.ShapeDtypeStruct((n,) + block.shape, block.dtype),
        in_specs=[pl.BlockSpec(memory_space=pltpu.VMEM)],
        out_specs=pl.BlockSpec(memory_space=pltpu.VMEM),
        scratch_shapes=[pltpu.SemaphoreType.DMA((n,)), pltpu.SemaphoreType.DMA((n,))],
        compiler_params=pltpu.CompilerParams(collective_id=cid, has_side_effects=True),
    )(block)


def grid_reduce_scatter(parts, outer, inner, cid):
    slots, n_hi, n_lo, rows, outs = parts.shape
    half = rows // 2

    def kernel(x_ref, out_ref, r1a, r1b, s1a, s1b, r2a, r2b, send_sem, recv_sem):
        hi = lax.axis_index(outer)
        lo = lax.axis_index(inner)
        barrier = pltpu.get_barrier_semaphore()
        for k in range(1, n_lo):
            pl.semaphore_signal(barrier, inc=1, device_id={inner: lax.rem(lo + k, n_lo)},
                                device_id_type=MESH_ID)
        for k in range(1, n_hi):
            pl.semaphore_signal(barrier, inc=1, device_id={outer: lax.rem(hi + k, n_hi)},
                                device_id_type=MESH_ID)
        pl.semaphore_wait(barrier, n_lo + n_hi - 2)

        def send(src_ref, dst_ref, axis, dev, group, k, slot):
            copy = pltpu.make_async_remote_copy(
                src_ref=src_ref, dst_ref=dst_ref, send_sem=send_sem.at[group, k],
                recv_sem=recv_sem.at[group, slot], device_id={axis: dev},
                device_id_type=MESH_ID)
            copy.start()
            return copy

        def arrive(dst_ref, group, slot):
            pltpu.make_async_remote_copy(
                src_ref=dst_ref, dst_ref=dst_ref, send_sem=send_sem.at[group, 0],
                recv_sem=recv_sem.at[group, slot], device_id={inner: lo},
                device_id_type=MESH_ID).wait_recv()

        sends = []
        for k in range(1, n_lo):
            dev = lax.rem(lo + k, n_lo)
            sends.append(send(x_ref.at[:, :, dev, pl.ds(0, half), :], r1a.at[lo], inner, dev, 0, k, lo))
        for k in range(1, n_hi):
            dev = lax.rem(hi + k, n_hi)
            sends.append(send(x_ref.at[:, dev, :, pl.ds(half, half), :], r1b.at[hi], outer, dev, 1, k, hi))

        sources_lo = [lax.rem(lo + n_lo - k, n_lo) for k in range(1, n_lo)]
        sources_hi = [lax.rem(hi + n_hi - k, n_hi) for k in range(1, n_hi)]
        for src in sources_lo:
            arrive(r1a.at[src], 0, src)
        for h in range(n_hi):
            total = x_ref[:, h, lo, pl.ds(0, half), :].astype(jnp.float32)
            for src in sources_lo:
                total = total + r1a[src, :, h].astype(jnp.float32)
            s1a[h] = total.astype(s1a.dtype)
        for k in range(1, n_hi):
            dev = lax.rem(hi + k, n_hi)
            sends.append(send(s1a.at[dev], r2a.at[hi], outer, dev, 2, k, hi))
        for src in sources_hi:
            arrive(r1b.at[src], 1, src)
        for l in range(n_lo):
            total = x_ref[:, hi, l, pl.ds(half, half), :].astype(jnp.float32)
            for src in sources_hi:
                total = total + r1b[src, :, l].astype(jnp.float32)
            s1b[l] = total.astype(s1b.dtype)
        for k in range(1, n_lo):
            dev = lax.rem(lo + k, n_lo)
            sends.append(send(s1b.at[dev], r2b.at[lo], inner, dev, 3, k, lo))

        total = s1a[hi].astype(jnp.float32)
        for src in sources_hi:
            arrive(r2a.at[src], 2, src)
            total = total + r2a[src].astype(jnp.float32)
        out_ref[:, pl.ds(0, half), :] = total
        total = s1b[lo].astype(jnp.float32)
        for src in sources_lo:
            arrive(r2b.at[src], 3, src)
            total = total + r2b[src].astype(jnp.float32)
        out_ref[:, pl.ds(half, half), :] = total
        for copy in sends:
            copy.wait_send()

    most = max(n_hi, n_lo)
    return pl.pallas_call(
        kernel,
        out_shape=jax.ShapeDtypeStruct((slots, rows, outs), jnp.float32),
        in_specs=[pl.BlockSpec(memory_space=pltpu.VMEM)],
        out_specs=pl.BlockSpec(memory_space=pltpu.VMEM),
        scratch_shapes=[
            pltpu.VMEM((n_lo, slots, n_hi, half, outs), parts.dtype),
            pltpu.VMEM((n_hi, slots, n_lo, half, outs), parts.dtype),
            pltpu.VMEM((n_hi, slots, half, outs), parts.dtype),
            pltpu.VMEM((n_lo, slots, half, outs), parts.dtype),
            pltpu.VMEM((n_hi, slots, half, outs), parts.dtype),
            pltpu.VMEM((n_lo, slots, half, outs), parts.dtype),
            pltpu.SemaphoreType.DMA((4, most)),
            pltpu.SemaphoreType.DMA((4, most)),
        ],
        compiler_params=pltpu.CompilerParams(collective_id=cid, has_side_effects=True),
    )(parts)


def chip_ring_gather(block, axis, n, cid):
    rows = block.shape[0]
    cut = rows // 32 * 16

    def kernel(x_ref, out_ref, send_sem, recv_sem):
        me = lax.axis_index(axis)
        partner = me + 1 - 2 * lax.rem(me, 2)
        up, down, far = lax.rem(me + 2, n), lax.rem(me + n - 2, n), lax.rem(me + 4, n)
        barrier = pltpu.get_barrier_semaphore()
        for dev in (up, down, partner):
            pl.semaphore_signal(barrier, inc=1, device_id={axis: dev}, device_id_type=MESH_ID)
        pl.semaphore_wait(barrier, 3)
        head, tail = pl.ds(0, cut), pl.ds(cut, rows - cut)

        def send(src_ref, slot, part, dev, index, sem_col):
            copy = pltpu.make_async_remote_copy(
                src_ref=src_ref, dst_ref=out_ref.at[slot, part], send_sem=send_sem.at[index],
                recv_sem=recv_sem.at[slot, sem_col], device_id={axis: dev},
                device_id_type=MESH_ID)
            copy.start()
            return copy

        def arrive(slot, part, sem_col):
            pltpu.make_async_remote_copy(
                src_ref=out_ref.at[slot, part], dst_ref=out_ref.at[slot, part],
                send_sem=send_sem.at[0], recv_sem=recv_sem.at[slot, sem_col],
                device_id={axis: slot}, device_id_type=MESH_ID).wait_recv()

        whole = pl.ds(0, rows)
        sends = [send(x_ref, me, whole, up, 0, 0), send(x_ref, me, whole, down, 1, 0),
                 send(x_ref, me, whole, partner, 2, 0)]
        out_ref[me] = x_ref[...]
        arrive(down, whole, 0)
        sends.append(send(out_ref.at[down, head], down, head, up, 3, 0))
        sends.append(send(out_ref.at[down], down, whole, partner, 4, 0))
        arrive(up, whole, 0)
        sends.append(send(out_ref.at[up, tail], up, tail, down, 5, 1))
        sends.append(send(out_ref.at[up], up, whole, partner, 6, 0))
        arrive(far, head, 0)
        arrive(far, tail, 1)
        sends.append(send(out_ref.at[far], far, whole, partner, 7, 0))
        for k in range(4):
            arrive(lax.rem(partner + 2 * k, n), whole, 0)
        for copy in sends:
            copy.wait_send()

    return pl.pallas_call(
        kernel,
        out_shape=jax.ShapeDtypeStruct((n,) + block.shape, block.dtype),
        in_specs=[pl.BlockSpec(memory_space=pltpu.VMEM)],
        out_specs=pl.BlockSpec(memory_space=pltpu.VMEM),
        scratch_shapes=[pltpu.SemaphoreType.DMA((8,)), pltpu.SemaphoreType.DMA((n, 2))],
        compiler_params=pltpu.CompilerParams(collective_id=cid, has_side_effects=True),
    )(block)

HEADS = 16
WH = 6
WW = 12


EPS = 1e-05


def padded(array, sides, width, wrap):
    for axis, dim in sides:
        size, length = (lax.axis_size(axis), array.shape[dim])
        up = [(i, (i + 1) % size) for i in range(size if wrap else size - 1)]
        down = [(j, i) for i, j in up]
        last = lax.slice_in_dim(array, length - width, length, axis=dim)
        initial = lax.slice_in_dim(array, 0, width, axis=dim)
        before = lax.ppermute(last, axis, up)
        after = lax.ppermute(initial, axis, down)
        array = jnp.concatenate([before, array, after], axis=dim)
    return array


def layer_norm(values, gain):
    wide = values.astype(jnp.float32)
    average = jnp.mean(wide, axis=-1, keepdims=True)
    centred = wide - average
    variance = jnp.mean(centred * centred, axis=-1, keepdims=True)
    return (centred * lax.rsqrt(variance + EPS) * gain).astype(jnp.bfloat16)


def window_attention(query_ext, keyval, row_valid, heads):
    ext_rows, ext_cols, width = query_ext.shape
    head_size = width // heads
    win_rows = ext_rows // WH
    win_cols = ext_cols // WW

    def split(values, parts):
        shaped = values.reshape(win_rows, WH, win_cols, WW, parts, heads, head_size)
        return shaped.transpose(0, 2, 1, 3, 4, 5, 6).reshape(
            win_rows * win_cols, WH * WW, parts, heads, head_size
        )

    query_win = split(query_ext, 1)[:, :, 0]
    pairs = split(keyval, 2)
    key_win = pairs[:, :, 0]
    value_win = pairs[:, :, 1]
    key_mask = jnp.broadcast_to(
        row_valid.reshape(win_rows, 1, WH, 1), (win_rows, win_cols, WH, WW)
    ).reshape(win_rows * win_cols, WH * WW)
    scores = jnp.einsum(
        "wqhd,wkhd->whqk", query_win, key_win, preferred_element_type=jnp.float32
    ) / math.sqrt(head_size)
    scores = jnp.where(key_mask[:, None, None, :], scores, -jnp.inf)
    peak = jnp.max(scores, axis=-1, keepdims=True)
    weights = jnp.exp(scores - peak)
    probs = (weights / jnp.sum(weights, axis=-1, keepdims=True)).astype(jnp.bfloat16)
    mixed = jnp.einsum("whqk,wkhd->wqhd", probs, value_win, preferred_element_type=jnp.float32)
    return (
        mixed.reshape(win_rows, win_cols, WH, WW, width)
        .transpose(0, 2, 1, 3, 4)
        .reshape(ext_rows, ext_cols, width)
    )


def slot_terms(piece, target_rows, live_cols, level_scale, level_shift, heads_full):
    piece_wide = piece.astype(jnp.float32)
    rows = (
        piece_wide[None] * level_scale[:, None, None, :] + level_shift[:, None, None, :]
    ).astype(jnp.bfloat16)
    predicted = jnp.einsum("krnd,kdo->krno", rows, heads_full, preferred_element_type=jnp.float32)
    errors = ((predicted - target_rows.astype(jnp.float32)) * live_cols[:, None, :, None]).astype(
        jnp.bfloat16
    )
    back_grad = jnp.einsum("krno,kdo->krnd", errors, heads_full, preferred_element_type=jnp.float32)
    piece_grad = jnp.sum(back_grad * level_scale[:, None, None, :], axis=0)
    head_add = jnp.einsum("krnd,krno->kdo", rows, errors, preferred_element_type=jnp.float32)
    return (piece_grad, head_add)


def local(
    patches,
    norm_gain,
    input_proj,
    output_proj,
    level_scale,
    level_shift,
    head_weight,
    targets,
    level_counts,
    tile_dataset,
    slot_level,
):
    band_rows, band_cols, width = patches.shape
    half_rows = WH // 2
    half_cols = WW // 2
    lat_count = lax.axis_size(LAT)
    var_count = lax.axis_size("var")
    lat_place = lax.axis_index(LAT)
    ext_rows = band_rows + WH
    ext_cols = band_cols + WW
    own_normed = layer_norm(patches, norm_gain).reshape(-1, width)
    extended = padded(patches, ((LAT, 0),), half_rows, False)
    extended, own_normed = lax.optimization_barrier((extended, own_normed))
    queries = jnp.dot(own_normed, input_proj[:, :width], preferred_element_type=jnp.float32)
    queries = queries.astype(jnp.bfloat16)
    own_keyval = jnp.dot(own_normed, input_proj[:, width:], preferred_element_type=jnp.float32)
    extended = padded(extended, (("var", 1),), half_cols, True)

    def ring(grid):
        top, bottom = grid[:half_rows], grid[half_rows + band_rows :]
        middle = grid[half_rows : half_rows + band_rows]
        left, right = middle[:, :half_cols], middle[:, half_cols + band_cols :]
        return jnp.concatenate(
            [part.reshape((-1,) + grid.shape[2:]) for part in (top, bottom, left, right)]
        )

    halo_normed = layer_norm(ring(extended), norm_gain)
    halo_keyval = jnp.dot(halo_normed, input_proj[:, width:], preferred_element_type=jnp.float32)
    keyval = jnp.concatenate([own_keyval, halo_keyval]).astype(jnp.bfloat16)
    global_row = lat_place * band_rows - half_rows + jnp.arange(ext_rows, dtype=jnp.int32)
    row_valid = (global_row >= 0) & (global_row < lat_count * band_rows)
    win_cols = ext_cols // WW
    ext_r = jnp.arange(ext_rows, dtype=jnp.int32)[:, None]
    ext_c = jnp.arange(ext_cols, dtype=jnp.int32)[None, :]
    key_grid = jnp.where(row_valid[:, None], (ext_r // WH) * win_cols + ext_c // WW, -1)
    query_win = key_grid[half_rows : half_rows + band_rows, half_cols : half_cols + band_cols]
    key_win = jnp.concatenate([query_win.reshape(-1), ring(key_grid)])
    attn = masked_window_attention(
        queries,
        keyval,
        query_win.reshape(-1, 1),
        key_win.reshape(1, -1),
        HEADS,
    ).reshape(band_rows, band_cols, width)
    update = jnp.dot(
        attn.reshape(-1, width), output_proj, preferred_element_type=jnp.float32
    ).reshape(band_rows, band_cols, width)
    latent = (patches.astype(jnp.float32) + update).astype(jnp.bfloat16)
    dataset_row = tile_dataset[0]
    dataset_ids = jnp.arange(level_counts.shape[0], dtype=jnp.int32)
    tile_levels = jnp.sum(
        jnp.where(dataset_row[:, None] == dataset_ids[None, :], level_counts[None, :], 0), axis=1
    )
    live_tiles = (slot_level[None, :] < tile_levels[:, None]).astype(jnp.float32)
    heads_full = lax.all_gather(head_weight, LAT, axis=1, tiled=True)
    tile_ids = jnp.arange(var_count, dtype=jnp.int32)
    gather = chip_ring_gather if var_count == 8 else chip_pair_gather
    tiles = gather(latent.reshape(band_rows * band_cols, width), "var", var_count, 1)
    piece = (
        tiles.reshape(var_count, band_rows, band_cols, width)
        .transpose(1, 0, 2, 3)
        .reshape(band_rows, var_count * band_cols, width)
    )
    piece_cols = piece.shape[1]
    column_tile = jnp.arange(piece_cols, dtype=jnp.int32) // band_cols
    onehot = (column_tile[:, None] == tile_ids[None, :]).astype(jnp.float32)
    column_live = jnp.dot(onehot, live_tiles)
    piece_grad, head_add = slot_terms(
        piece, targets, column_live.T, level_scale, level_shift, heads_full
    )
    latent_terms = piece_grad
    latent_terms, head_terms = (latent_terms, head_add)
    grad_latent = lax.psum_scatter(
        latent_terms.astype(jnp.bfloat16), "var", scatter_dimension=1, tiled=True
    )
    head_terms = head_terms * (1.0 / math.sqrt(lat_count * band_rows * var_count * band_cols))
    outer, inner = lax.axis_size(LAT[0]), lax.axis_size(LAT[1])
    slots, outs = head_terms.shape[0], head_terms.shape[2]
    share_rows = width // lat_count
    head_parts = head_terms.astype(jnp.bfloat16).reshape(slots, outer, inner, share_rows, outs)
    grad_head = grid_reduce_scatter(head_parts, LAT[0], LAT[1], 3)
    return (latent, grad_latent, grad_head)


def solution(mesh):
    in_specs = (
        P(LAT, "var", None),
        P(),
        P(),
        P(),
        P("var", None),
        P("var", None),
        P("var", LAT, None),
        P("var", LAT, None, None),
        P(),
        P(LAT, None),
        P("var"),
    )
    out_specs = (P(LAT, "var", None), P(LAT, "var", None), P("var", LAT, None))
    lat_size = mesh.shape["lat"]
    inner = 4 if lat_size % 4 == 0 else 1
    grid = Mesh(
        mesh.devices.reshape(lat_size // inner, inner, mesh.shape["var"]), LAT + ("var",)
    )
    return jax.shard_map(local, mesh=grid, in_specs=in_specs, out_specs=out_specs, check_vma=False)
```

```python
import math

import jax
import jax.numpy as jnp
from jax import lax
from jax.experimental import pallas as pl
from jax.experimental.pallas import tpu as pltpu
from jax.sharding import Mesh, PartitionSpec as P

MESH_ID = pl.DeviceIdType.MESH
LAT = ("lat_hi", "lat_lo")


def _greet(axis, n, me):
    barrier = pltpu.get_barrier_semaphore()
    for k in range(1, n):
        pl.semaphore_signal(barrier, inc=1, device_id={axis: lax.rem(me + k, n)},
                            device_id_type=MESH_ID)
    pl.semaphore_wait(barrier, n - 1)


def peer_gather(block, axis, n, cid):
    def kernel(x_ref, out_ref, send_sem, recv_sem):
        me = lax.axis_index(axis)
        _greet(axis, n, me)
        sends = []
        for k in range(1, n):
            copy = pltpu.make_async_remote_copy(
                src_ref=x_ref, dst_ref=out_ref.at[me], send_sem=send_sem.at[k],
                recv_sem=recv_sem.at[me], device_id={axis: lax.rem(me + k, n)},
                device_id_type=MESH_ID)
            copy.start()
            sends.append(copy)
        out_ref[me] = x_ref[...]
        for k in range(1, n):
            src = lax.rem(me + n - k, n)
            pltpu.make_async_remote_copy(
                src_ref=x_ref, dst_ref=out_ref.at[src], send_sem=send_sem.at[k],
                recv_sem=recv_sem.at[src], device_id={axis: src},
                device_id_type=MESH_ID).wait_recv()
        for copy in sends:
            copy.wait_send()

    return pl.pallas_call(
        kernel,
        out_shape=jax.ShapeDtypeStruct((n,) + block.shape, block.dtype),
        in_specs=[pl.BlockSpec(memory_space=pltpu.VMEM)],
        out_specs=pl.BlockSpec(memory_space=pltpu.VMEM),
        scratch_shapes=[pltpu.SemaphoreType.DMA((n,)), pltpu.SemaphoreType.DMA((n,))],
        compiler_params=pltpu.CompilerParams(collective_id=cid, has_side_effects=True),
    )(block)


def peer_reduce_scatter(parts, axis, n, cid, out_dtype):
    def kernel(x_ref, out_ref, held, send_sem, recv_sem):
        me = lax.axis_index(axis)
        _greet(axis, n, me)
        sends = []
        for k in range(1, n):
            dst = lax.rem(me + k, n)
            copy = pltpu.make_async_remote_copy(
                src_ref=x_ref.at[dst], dst_ref=held.at[me], send_sem=send_sem.at[k],
                recv_sem=recv_sem.at[me], device_id={axis: dst},
                device_id_type=MESH_ID)
            copy.start()
            sends.append(copy)
        total = x_ref[me].astype(jnp.float32)
        for k in range(1, n):
            src = lax.rem(me + n - k, n)
            pltpu.make_async_remote_copy(
                src_ref=x_ref.at[src], dst_ref=held.at[src], send_sem=send_sem.at[k],
                recv_sem=recv_sem.at[src], device_id={axis: src},
                device_id_type=MESH_ID).wait_recv()
            total = total + held[src].astype(jnp.float32)
        out_ref[...] = total.astype(out_ref.dtype)
        for copy in sends:
            copy.wait_send()

    return pl.pallas_call(
        kernel,
        out_shape=jax.ShapeDtypeStruct(parts.shape[1:], out_dtype),
        in_specs=[pl.BlockSpec(memory_space=pltpu.VMEM)],
        out_specs=pl.BlockSpec(memory_space=pltpu.VMEM),
        scratch_shapes=[pltpu.VMEM(parts.shape, parts.dtype),
                        pltpu.SemaphoreType.DMA((n,)), pltpu.SemaphoreType.DMA((n,))],
        compiler_params=pltpu.CompilerParams(collective_id=cid, has_side_effects=True),
    )(parts)


def masked_window_attention(queries, keyval, query_win, key_win, heads, patches, output_proj):
    nq, width = queries.shape
    head_size = width // heads
    scale = 1.0 / float(head_size) ** 0.5

    def kernel(q_ref, kv_ref, qw_ref, kw_ref, p_ref, w_ref, out_ref, attn_ref):
        mask = qw_ref[...] == kw_ref[...]
        for h in range(heads):
            cols = slice(h * head_size, (h + 1) * head_size)
            q = q_ref[:, cols]
            k = kv_ref[:, h * head_size:(h + 1) * head_size]
            v = kv_ref[:, width + h * head_size:width + (h + 1) * head_size]
            s = lax.dot_general(q, k, (((1,), (1,)), ((), ())),
                                preferred_element_type=jnp.float32) * scale
            s = jnp.where(mask, s, -jnp.inf)
            w = jnp.exp(s - jnp.max(s, axis=1, keepdims=True))
            p = (w / jnp.sum(w, axis=1, keepdims=True)).astype(jnp.bfloat16)
            attn_ref[:, cols] = jnp.dot(p, v, preferred_element_type=jnp.float32).astype(attn_ref.dtype)
        update = jnp.dot(attn_ref[...], w_ref[...], preferred_element_type=jnp.float32)
        out_ref[...] = (p_ref[...].astype(jnp.float32) + update).astype(out_ref.dtype)

    return pl.pallas_call(
        kernel,
        out_shape=jax.ShapeDtypeStruct((nq, width), patches.dtype),
        in_specs=[pl.BlockSpec(memory_space=pltpu.VMEM)] * 6,
        out_specs=pl.BlockSpec(memory_space=pltpu.VMEM),
        scratch_shapes=[pltpu.VMEM((nq, width), jnp.bfloat16)],
    )(queries, keyval, query_win, key_win, patches, output_proj)


def chip_pair_gather(block, axis, n, cid):
    nz = n // 2

    def kernel(x_ref, out_ref, send_sem, recv_sem):
        me = lax.axis_index(axis)
        partner = me + 1 - 2 * lax.rem(me, 2)
        peers = [lax.rem(me + 2 * k, n) for k in range(1, nz)]
        barrier = pltpu.get_barrier_semaphore()
        for dev in peers + [partner]:
            pl.semaphore_signal(barrier, inc=1, device_id={axis: dev}, device_id_type=MESH_ID)
        pl.semaphore_wait(barrier, nz)

        def send(src_ref, slot, dev, index):
            copy = pltpu.make_async_remote_copy(
                src_ref=src_ref, dst_ref=out_ref.at[slot], send_sem=send_sem.at[index],
                recv_sem=recv_sem.at[slot], device_id={axis: dev}, device_id_type=MESH_ID)
            copy.start()
            return copy

        def arrive(slot):
            pltpu.make_async_remote_copy(
                src_ref=x_ref, dst_ref=out_ref.at[slot], send_sem=send_sem.at[0],
                recv_sem=recv_sem.at[slot], device_id={axis: slot},
                device_id_type=MESH_ID).wait_recv()

        sends = [send(x_ref, me, dev, i) for i, dev in enumerate(peers)]
        sends.append(send(x_ref, me, partner, nz - 1))
        out_ref[me] = x_ref[...]
        for k in range(1, nz):
            src = lax.rem(me + n - 2 * k, n)
            arrive(src)
            sends.append(send(out_ref.at[src], src, partner, nz - 1 + k))
        for k in range(nz):
            arrive(lax.rem(partner + 2 * k, n))
        for copy in sends:
            copy.wait_send()

    return pl.pallas_call(
        kernel,
        out_shape=jax.ShapeDtypeStruct((n,) + block.shape, block.dtype),
        in_specs=[pl.BlockSpec(memory_space=pltpu.VMEM)],
        out_specs=pl.BlockSpec(memory_space=pltpu.VMEM),
        scratch_shapes=[pltpu.SemaphoreType.DMA((n,)), pltpu.SemaphoreType.DMA((n,))],
        compiler_params=pltpu.CompilerParams(collective_id=cid, has_side_effects=True),
    )(block)


def grid_reduce_scatter(parts, outer, inner, cid):
    slots, n_hi, n_lo, rows, outs = parts.shape
    half = rows // 2

    def kernel(x_ref, out_ref, r1a, r1b, s1a, s1b, r2a, r2b, send_sem, recv_sem):
        hi = lax.axis_index(outer)
        lo = lax.axis_index(inner)
        barrier = pltpu.get_barrier_semaphore()
        for k in range(1, n_lo):
            pl.semaphore_signal(barrier, inc=1, device_id={inner: lax.rem(lo + k, n_lo)},
                                device_id_type=MESH_ID)
        for k in range(1, n_hi):
            pl.semaphore_signal(barrier, inc=1, device_id={outer: lax.rem(hi + k, n_hi)},
                                device_id_type=MESH_ID)
        pl.semaphore_wait(barrier, n_lo + n_hi - 2)

        def send(src_ref, dst_ref, axis, dev, group, k, slot):
            copy = pltpu.make_async_remote_copy(
                src_ref=src_ref, dst_ref=dst_ref, send_sem=send_sem.at[group, k],
                recv_sem=recv_sem.at[group, slot], device_id={axis: dev},
                device_id_type=MESH_ID)
            copy.start()
            return copy

        def arrive(dst_ref, group, slot):
            pltpu.make_async_remote_copy(
                src_ref=dst_ref, dst_ref=dst_ref, send_sem=send_sem.at[group, 0],
                recv_sem=recv_sem.at[group, slot], device_id={inner: lo},
                device_id_type=MESH_ID).wait_recv()

        sends = []
        for k in range(1, n_lo):
            dev = lax.rem(lo + k, n_lo)
            sends.append(send(x_ref.at[:, :, dev, pl.ds(0, half), :], r1a.at[lo], inner, dev, 0, k, lo))
        for k in range(1, n_hi):
            dev = lax.rem(hi + k, n_hi)
            sends.append(send(x_ref.at[:, dev, :, pl.ds(half, half), :], r1b.at[hi], outer, dev, 1, k, hi))

        sources_lo = [lax.rem(lo + n_lo - k, n_lo) for k in range(1, n_lo)]
        sources_hi = [lax.rem(hi + n_hi - k, n_hi) for k in range(1, n_hi)]
        for src in sources_lo:
            arrive(r1a.at[src], 0, src)
        for h in range(n_hi):
            total = x_ref[:, h, lo, pl.ds(0, half), :].astype(jnp.float32)
            for src in sources_lo:
                total = total + r1a[src, :, h].astype(jnp.float32)
            s1a[h] = total.astype(s1a.dtype)
        for k in range(1, n_hi):
            dev = lax.rem(hi + k, n_hi)
            sends.append(send(s1a.at[dev], r2a.at[hi], outer, dev, 2, k, hi))
        for src in sources_hi:
            arrive(r1b.at[src], 1, src)
        for l in range(n_lo):
            total = x_ref[:, hi, l, pl.ds(half, half), :].astype(jnp.float32)
            for src in sources_hi:
                total = total + r1b[src, :, l].astype(jnp.float32)
            s1b[l] = total.astype(s1b.dtype)
        for k in range(1, n_lo):
            dev = lax.rem(lo + k, n_lo)
            sends.append(send(s1b.at[dev], r2b.at[lo], inner, dev, 3, k, lo))

        total = s1a[hi].astype(jnp.float32)
        for src in sources_hi:
            arrive(r2a.at[src], 2, src)
            total = total + r2a[src].astype(jnp.float32)
        out_ref[:, pl.ds(0, half), :] = total
        total = s1b[lo].astype(jnp.float32)
        for src in sources_lo:
            arrive(r2b.at[src], 3, src)
            total = total + r2b[src].astype(jnp.float32)
        out_ref[:, pl.ds(half, half), :] = total
        for copy in sends:
            copy.wait_send()

    most = max(n_hi, n_lo)
    return pl.pallas_call(
        kernel,
        out_shape=jax.ShapeDtypeStruct((slots, rows, outs), jnp.float32),
        in_specs=[pl.BlockSpec(memory_space=pltpu.VMEM)],
        out_specs=pl.BlockSpec(memory_space=pltpu.VMEM),
        scratch_shapes=[
            pltpu.VMEM((n_lo, slots, n_hi, half, outs), parts.dtype),
            pltpu.VMEM((n_hi, slots, n_lo, half, outs), parts.dtype),
            pltpu.VMEM((n_hi, slots, half, outs), parts.dtype),
            pltpu.VMEM((n_lo, slots, half, outs), parts.dtype),
            pltpu.VMEM((n_hi, slots, half, outs), parts.dtype),
            pltpu.VMEM((n_lo, slots, half, outs), parts.dtype),
            pltpu.SemaphoreType.DMA((4, most)),
            pltpu.SemaphoreType.DMA((4, most)),
        ],
        compiler_params=pltpu.CompilerParams(collective_id=cid, has_side_effects=True),
    )(parts)


def chip_ring_gather(block, axis, n, cid):
    rows = block.shape[0]
    cut = rows // 32 * 16

    def kernel(x_ref, out_ref, send_sem, recv_sem):
        me = lax.axis_index(axis)
        partner = me + 1 - 2 * lax.rem(me, 2)
        up, down, far = lax.rem(me + 2, n), lax.rem(me + n - 2, n), lax.rem(me + 4, n)
        barrier = pltpu.get_barrier_semaphore()
        for dev in (up, down, partner):
            pl.semaphore_signal(barrier, inc=1, device_id={axis: dev}, device_id_type=MESH_ID)
        pl.semaphore_wait(barrier, 3)
        head, tail = pl.ds(0, cut), pl.ds(cut, rows - cut)

        def send(src_ref, slot, part, dev, index, sem_col):
            copy = pltpu.make_async_remote_copy(
                src_ref=src_ref, dst_ref=out_ref.at[slot, part], send_sem=send_sem.at[index],
                recv_sem=recv_sem.at[slot, sem_col], device_id={axis: dev},
                device_id_type=MESH_ID)
            copy.start()
            return copy

        def arrive(slot, part, sem_col):
            pltpu.make_async_remote_copy(
                src_ref=out_ref.at[slot, part], dst_ref=out_ref.at[slot, part],
                send_sem=send_sem.at[0], recv_sem=recv_sem.at[slot, sem_col],
                device_id={axis: slot}, device_id_type=MESH_ID).wait_recv()

        whole = pl.ds(0, rows)
        sends = [send(x_ref, me, whole, up, 0, 0), send(x_ref, me, whole, down, 1, 0),
                 send(x_ref, me, whole, partner, 2, 0)]
        out_ref[me] = x_ref[...]
        arrive(down, whole, 0)
        sends.append(send(out_ref.at[down, head], down, head, up, 3, 0))
        sends.append(send(out_ref.at[down], down, whole, partner, 4, 0))
        arrive(up, whole, 0)
        sends.append(send(out_ref.at[up, tail], up, tail, down, 5, 1))
        sends.append(send(out_ref.at[up], up, whole, partner, 6, 0))
        arrive(far, head, 0)
        arrive(far, tail, 1)
        sends.append(send(out_ref.at[far], far, whole, partner, 7, 0))
        for k in range(4):
            arrive(lax.rem(partner + 2 * k, n), whole, 0)
        for copy in sends:
            copy.wait_send()

    return pl.pallas_call(
        kernel,
        out_shape=jax.ShapeDtypeStruct((n,) + block.shape, block.dtype),
        in_specs=[pl.BlockSpec(memory_space=pltpu.VMEM)],
        out_specs=pl.BlockSpec(memory_space=pltpu.VMEM),
        scratch_shapes=[pltpu.SemaphoreType.DMA((8,)), pltpu.SemaphoreType.DMA((n, 2))],
        compiler_params=pltpu.CompilerParams(collective_id=cid, has_side_effects=True),
    )(block)

HEADS = 16
WH = 6
WW = 12


EPS = 1e-05


def padded(array, sides, width, wrap):
    for axis, dim in sides:
        size, length = (lax.axis_size(axis), array.shape[dim])
        up = [(i, (i + 1) % size) for i in range(size if wrap else size - 1)]
        down = [(j, i) for i, j in up]
        last = lax.slice_in_dim(array, length - width, length, axis=dim)
        initial = lax.slice_in_dim(array, 0, width, axis=dim)
        before = lax.ppermute(last, axis, up)
        after = lax.ppermute(initial, axis, down)
        array = jnp.concatenate([before, array, after], axis=dim)
    return array


def layer_norm(values, gain):
    wide = values.astype(jnp.float32)
    average = jnp.mean(wide, axis=-1, keepdims=True)
    centred = wide - average
    variance = jnp.mean(centred * centred, axis=-1, keepdims=True)
    return (centred * lax.rsqrt(variance + EPS) * gain).astype(jnp.bfloat16)


def window_attention(query_ext, keyval, row_valid, heads):
    ext_rows, ext_cols, width = query_ext.shape
    head_size = width // heads
    win_rows = ext_rows // WH
    win_cols = ext_cols // WW

    def split(values, parts):
        shaped = values.reshape(win_rows, WH, win_cols, WW, parts, heads, head_size)
        return shaped.transpose(0, 2, 1, 3, 4, 5, 6).reshape(
            win_rows * win_cols, WH * WW, parts, heads, head_size
        )

    query_win = split(query_ext, 1)[:, :, 0]
    pairs = split(keyval, 2)
    key_win = pairs[:, :, 0]
    value_win = pairs[:, :, 1]
    key_mask = jnp.broadcast_to(
        row_valid.reshape(win_rows, 1, WH, 1), (win_rows, win_cols, WH, WW)
    ).reshape(win_rows * win_cols, WH * WW)
    scores = jnp.einsum(
        "wqhd,wkhd->whqk", query_win, key_win, preferred_element_type=jnp.float32
    ) / math.sqrt(head_size)
    scores = jnp.where(key_mask[:, None, None, :], scores, -jnp.inf)
    peak = jnp.max(scores, axis=-1, keepdims=True)
    weights = jnp.exp(scores - peak)
    probs = (weights / jnp.sum(weights, axis=-1, keepdims=True)).astype(jnp.bfloat16)
    mixed = jnp.einsum("whqk,wkhd->wqhd", probs, value_win, preferred_element_type=jnp.float32)
    return (
        mixed.reshape(win_rows, win_cols, WH, WW, width)
        .transpose(0, 2, 1, 3, 4)
        .reshape(ext_rows, ext_cols, width)
    )


def slot_terms(piece, target_rows, live_cols, level_scale, level_shift, heads_full):
    piece_wide = piece.astype(jnp.float32)
    rows = (
        piece_wide[None] * level_scale[:, None, None, :] + level_shift[:, None, None, :]
    ).astype(jnp.bfloat16)
    predicted = jnp.einsum("krnd,kdo->krno", rows, heads_full, preferred_element_type=jnp.float32)
    errors = ((predicted - target_rows.astype(jnp.float32)) * live_cols[:, None, :, None]).astype(
        jnp.bfloat16
    )
    back_grad = jnp.einsum("krno,kdo->krnd", errors, heads_full, preferred_element_type=jnp.float32)
    piece_grad = jnp.sum(back_grad * level_scale[:, None, None, :], axis=0)
    head_add = jnp.einsum("krnd,krno->kdo", rows, errors, preferred_element_type=jnp.float32)
    return (piece_grad, head_add)


def local(
    patches,
    norm_gain,
    input_proj,
    output_proj,
    level_scale,
    level_shift,
    head_weight,
    targets,
    level_counts,
    tile_dataset,
    slot_level,
):
    band_rows, band_cols, width = patches.shape
    half_rows = WH // 2
    half_cols = WW // 2
    lat_count = lax.axis_size(LAT)
    var_count = lax.axis_size("var")
    lat_place = lax.axis_index(LAT)
    ext_rows = band_rows + WH
    ext_cols = band_cols + WW
    own_normed = layer_norm(patches, norm_gain).reshape(-1, width)
    extended = padded(patches, ((LAT, 0),), half_rows, False)
    extended, own_normed = lax.optimization_barrier((extended, own_normed))
    queries = jnp.dot(own_normed, input_proj[:, :width], preferred_element_type=jnp.float32)
    queries = queries.astype(jnp.bfloat16)
    own_keyval = jnp.dot(own_normed, input_proj[:, width:], preferred_element_type=jnp.float32)
    extended = padded(extended, (("var", 1),), half_cols, True)

    def ring(grid):
        top, bottom = grid[:half_rows], grid[half_rows + band_rows :]
        middle = grid[half_rows : half_rows + band_rows]
        left, right = middle[:, :half_cols], middle[:, half_cols + band_cols :]
        return jnp.concatenate(
            [part.reshape((-1,) + grid.shape[2:]) for part in (top, bottom, left, right)]
        )

    halo_normed = layer_norm(ring(extended), norm_gain)
    halo_keyval = jnp.dot(halo_normed, input_proj[:, width:], preferred_element_type=jnp.float32)
    keyval = jnp.concatenate([own_keyval, halo_keyval]).astype(jnp.bfloat16)
    global_row = lat_place * band_rows - half_rows + jnp.arange(ext_rows, dtype=jnp.int32)
    row_valid = (global_row >= 0) & (global_row < lat_count * band_rows)
    win_cols = ext_cols // WW
    ext_r = jnp.arange(ext_rows, dtype=jnp.int32)[:, None]
    ext_c = jnp.arange(ext_cols, dtype=jnp.int32)[None, :]
    key_grid = jnp.where(row_valid[:, None], (ext_r // WH) * win_cols + ext_c // WW, -1)
    query_win = key_grid[half_rows : half_rows + band_rows, half_cols : half_cols + band_cols]
    key_win = jnp.concatenate([query_win.reshape(-1), ring(key_grid)])
    latent = masked_window_attention(
        queries,
        keyval,
        query_win.reshape(-1, 1),
        key_win.reshape(1, -1),
        HEADS,
        patches.reshape(-1, width),
        output_proj,
    ).reshape(band_rows, band_cols, width)
    dataset_row = tile_dataset[0]
    dataset_ids = jnp.arange(level_counts.shape[0], dtype=jnp.int32)
    tile_levels = jnp.sum(
        jnp.where(dataset_row[:, None] == dataset_ids[None, :], level_counts[None, :], 0), axis=1
    )
    live_tiles = (slot_level[None, :] < tile_levels[:, None]).astype(jnp.float32)
    heads_full = lax.all_gather(head_weight, LAT, axis=1, tiled=True)
    tile_ids = jnp.arange(var_count, dtype=jnp.int32)
    gather = chip_ring_gather if var_count == 8 else chip_pair_gather
    tiles = gather(latent.reshape(band_rows * band_cols, width), "var", var_count, 1)
    piece = (
        tiles.reshape(var_count, band_rows, band_cols, width)
        .transpose(1, 0, 2, 3)
        .reshape(band_rows, var_count * band_cols, width)
    )
    piece_cols = piece.shape[1]
    column_tile = jnp.arange(piece_cols, dtype=jnp.int32) // band_cols
    onehot = (column_tile[:, None] == tile_ids[None, :]).astype(jnp.float32)
    column_live = jnp.dot(onehot, live_tiles)
    piece_grad, head_add = slot_terms(
        piece, targets, column_live.T, level_scale, level_shift, heads_full
    )
    latent_terms = piece_grad
    latent_terms, head_terms = (latent_terms, head_add)
    grad_latent = lax.psum_scatter(
        latent_terms.astype(jnp.bfloat16), "var", scatter_dimension=1, tiled=True
    )
    head_terms = head_terms * (1.0 / math.sqrt(lat_count * band_rows * var_count * band_cols))
    outer, inner = lax.axis_size(LAT[0]), lax.axis_size(LAT[1])
    slots, outs = head_terms.shape[0], head_terms.shape[2]
    share_rows = width // lat_count
    head_parts = head_terms.astype(jnp.bfloat16).reshape(slots, outer, inner, share_rows, outs)
    grad_head = grid_reduce_scatter(head_parts, LAT[0], LAT[1], 3)
    return (latent, grad_latent, grad_head)


def solution(mesh):
    in_specs = (
        P(LAT, "var", None),
        P(),
        P(),
        P(),
        P("var", None),
        P("var", None),
        P("var", LAT, None),
        P("var", LAT, None, None),
        P(),
        P(LAT, None),
        P("var"),
    )
    out_specs = (P(LAT, "var", None), P(LAT, "var", None), P("var", LAT, None))
    lat_size = mesh.shape["lat"]
    inner = 4 if lat_size % 4 == 0 else 1
    grid = Mesh(
        mesh.devices.reshape(lat_size // inner, inner, mesh.shape["var"]), LAT + ("var",)
    )
    return jax.shard_map(local, mesh=grid, in_specs=in_specs, out_specs=out_specs, check_vma=False)
```

```python
import math

import jax
import jax.numpy as jnp
from jax import lax
from jax.experimental import pallas as pl
from jax.experimental.pallas import tpu as pltpu
from jax.sharding import Mesh, PartitionSpec as P

MESH_ID = pl.DeviceIdType.MESH
LAT = ("lat_hi", "lat_lo")


def _greet(axis, n, me):
    barrier = pltpu.get_barrier_semaphore()
    for k in range(1, n):
        pl.semaphore_signal(barrier, inc=1, device_id={axis: lax.rem(me + k, n)},
                            device_id_type=MESH_ID)
    pl.semaphore_wait(barrier, n - 1)


def peer_gather(block, axis, n, cid):
    def kernel(x_ref, out_ref, send_sem, recv_sem):
        me = lax.axis_index(axis)
        _greet(axis, n, me)
        sends = []
        for k in range(1, n):
            copy = pltpu.make_async_remote_copy(
                src_ref=x_ref, dst_ref=out_ref.at[me], send_sem=send_sem.at[k],
                recv_sem=recv_sem.at[me], device_id={axis: lax.rem(me + k, n)},
                device_id_type=MESH_ID)
            copy.start()
            sends.append(copy)
        out_ref[me] = x_ref[...]
        for k in range(1, n):
            src = lax.rem(me + n - k, n)
            pltpu.make_async_remote_copy(
                src_ref=x_ref, dst_ref=out_ref.at[src], send_sem=send_sem.at[k],
                recv_sem=recv_sem.at[src], device_id={axis: src},
                device_id_type=MESH_ID).wait_recv()
        for copy in sends:
            copy.wait_send()

    return pl.pallas_call(
        kernel,
        out_shape=jax.ShapeDtypeStruct((n,) + block.shape, block.dtype),
        in_specs=[pl.BlockSpec(memory_space=pltpu.VMEM)],
        out_specs=pl.BlockSpec(memory_space=pltpu.VMEM),
        scratch_shapes=[pltpu.SemaphoreType.DMA((n,)), pltpu.SemaphoreType.DMA((n,))],
        compiler_params=pltpu.CompilerParams(collective_id=cid, has_side_effects=True),
    )(block)


def peer_reduce_scatter(parts, axis, n, cid, out_dtype):
    def kernel(x_ref, out_ref, held, send_sem, recv_sem):
        me = lax.axis_index(axis)
        _greet(axis, n, me)
        sends = []
        for k in range(1, n):
            dst = lax.rem(me + k, n)
            copy = pltpu.make_async_remote_copy(
                src_ref=x_ref.at[dst], dst_ref=held.at[me], send_sem=send_sem.at[k],
                recv_sem=recv_sem.at[me], device_id={axis: dst},
                device_id_type=MESH_ID)
            copy.start()
            sends.append(copy)
        total = x_ref[me].astype(jnp.float32)
        for k in range(1, n):
            src = lax.rem(me + n - k, n)
            pltpu.make_async_remote_copy(
                src_ref=x_ref.at[src], dst_ref=held.at[src], send_sem=send_sem.at[k],
                recv_sem=recv_sem.at[src], device_id={axis: src},
                device_id_type=MESH_ID).wait_recv()
            total = total + held[src].astype(jnp.float32)
        out_ref[...] = total.astype(out_ref.dtype)
        for copy in sends:
            copy.wait_send()

    return pl.pallas_call(
        kernel,
        out_shape=jax.ShapeDtypeStruct(parts.shape[1:], out_dtype),
        in_specs=[pl.BlockSpec(memory_space=pltpu.VMEM)],
        out_specs=pl.BlockSpec(memory_space=pltpu.VMEM),
        scratch_shapes=[pltpu.VMEM(parts.shape, parts.dtype),
                        pltpu.SemaphoreType.DMA((n,)), pltpu.SemaphoreType.DMA((n,))],
        compiler_params=pltpu.CompilerParams(collective_id=cid, has_side_effects=True),
    )(parts)


def masked_window_attention(queries, own_kv, halo_kv, query_win, key_win, heads, patches, output_proj):
    nq, width = queries.shape
    head_size = width // heads
    scale = 1.0 / float(head_size) ** 0.5

    n_own = own_kv.shape[0]

    def kernel(q_ref, own_ref, halo_ref, qw_ref, kw_ref, p_ref, w_ref, out_ref, attn_ref, kv_ref):
        kv_ref[pl.ds(0, n_own), :] = own_ref[...]
        kv_ref[pl.ds(n_own, halo_ref.shape[0]), :] = halo_ref[...]
        mask = qw_ref[...] == kw_ref[...]
        for h in range(heads):
            cols = slice(h * head_size, (h + 1) * head_size)
            q = q_ref[:, cols]
            k = kv_ref[:, h * head_size:(h + 1) * head_size]
            v = kv_ref[:, width + h * head_size:width + (h + 1) * head_size]
            s = lax.dot_general(q, k, (((1,), (1,)), ((), ())),
                                preferred_element_type=jnp.float32) * scale
            s = jnp.where(mask, s, -jnp.inf)
            w = jnp.exp(s - jnp.max(s, axis=1, keepdims=True))
            p = (w / jnp.sum(w, axis=1, keepdims=True)).astype(jnp.bfloat16)
            attn_ref[:, cols] = jnp.dot(p, v, preferred_element_type=jnp.float32).astype(attn_ref.dtype)
        update = jnp.dot(attn_ref[...], w_ref[...], preferred_element_type=jnp.float32)
        out_ref[...] = (p_ref[...].astype(jnp.float32) + update).astype(out_ref.dtype)

    return pl.pallas_call(
        kernel,
        out_shape=jax.ShapeDtypeStruct((nq, width), patches.dtype),
        in_specs=[pl.BlockSpec(memory_space=pltpu.VMEM)] * 7,
        out_specs=pl.BlockSpec(memory_space=pltpu.VMEM),
        scratch_shapes=[
            pltpu.VMEM((nq, width), jnp.bfloat16),
            pltpu.VMEM((n_own + halo_kv.shape[0], own_kv.shape[1]), own_kv.dtype),
        ],
    )(queries, own_kv, halo_kv, query_win, key_win, patches, output_proj)


def chip_pair_gather(block, axis, n, cid):
    nz = n // 2

    def kernel(x_ref, out_ref, send_sem, recv_sem):
        me = lax.axis_index(axis)
        partner = me + 1 - 2 * lax.rem(me, 2)
        peers = [lax.rem(me + 2 * k, n) for k in range(1, nz)]
        barrier = pltpu.get_barrier_semaphore()
        for dev in peers + [partner]:
            pl.semaphore_signal(barrier, inc=1, device_id={axis: dev}, device_id_type=MESH_ID)
        pl.semaphore_wait(barrier, nz)

        def send(src_ref, slot, dev, index):
            copy = pltpu.make_async_remote_copy(
                src_ref=src_ref, dst_ref=out_ref.at[slot], send_sem=send_sem.at[index],
                recv_sem=recv_sem.at[slot], device_id={axis: dev}, device_id_type=MESH_ID)
            copy.start()
            return copy

        def arrive(slot):
            pltpu.make_async_remote_copy(
                src_ref=x_ref, dst_ref=out_ref.at[slot], send_sem=send_sem.at[0],
                recv_sem=recv_sem.at[slot], device_id={axis: slot},
                device_id_type=MESH_ID).wait_recv()

        sends = [send(x_ref, me, dev, i) for i, dev in enumerate(peers)]
        sends.append(send(x_ref, me, partner, nz - 1))
        out_ref[me] = x_ref[...]
        for k in range(1, nz):
            src = lax.rem(me + n - 2 * k, n)
            arrive(src)
            sends.append(send(out_ref.at[src], src, partner, nz - 1 + k))
        for k in range(nz):
            arrive(lax.rem(partner + 2 * k, n))
        for copy in sends:
            copy.wait_send()

    return pl.pallas_call(
        kernel,
        out_shape=jax.ShapeDtypeStruct((n,) + block.shape, block.dtype),
        in_specs=[pl.BlockSpec(memory_space=pltpu.VMEM)],
        out_specs=pl.BlockSpec(memory_space=pltpu.VMEM),
        scratch_shapes=[pltpu.SemaphoreType.DMA((n,)), pltpu.SemaphoreType.DMA((n,))],
        compiler_params=pltpu.CompilerParams(collective_id=cid, has_side_effects=True),
    )(block)


def grid_reduce_scatter(parts, outer, inner, cid):
    slots, n_hi, n_lo, rows, outs = parts.shape
    half = rows // 2

    def kernel(x_ref, out_ref, r1a, r1b, s1a, s1b, r2a, r2b, send_sem, recv_sem):
        hi = lax.axis_index(outer)
        lo = lax.axis_index(inner)
        barrier = pltpu.get_barrier_semaphore()
        for k in range(1, n_lo):
            pl.semaphore_signal(barrier, inc=1, device_id={inner: lax.rem(lo + k, n_lo)},
                                device_id_type=MESH_ID)
        for k in range(1, n_hi):
            pl.semaphore_signal(barrier, inc=1, device_id={outer: lax.rem(hi + k, n_hi)},
                                device_id_type=MESH_ID)
        pl.semaphore_wait(barrier, n_lo + n_hi - 2)

        def send(src_ref, dst_ref, axis, dev, group, k, slot):
            copy = pltpu.make_async_remote_copy(
                src_ref=src_ref, dst_ref=dst_ref, send_sem=send_sem.at[group, k],
                recv_sem=recv_sem.at[group, slot], device_id={axis: dev},
                device_id_type=MESH_ID)
            copy.start()
            return copy

        def arrive(dst_ref, group, slot):
            pltpu.make_async_remote_copy(
                src_ref=dst_ref, dst_ref=dst_ref, send_sem=send_sem.at[group, 0],
                recv_sem=recv_sem.at[group, slot], device_id={inner: lo},
                device_id_type=MESH_ID).wait_recv()

        sends = []
        for k in range(1, n_lo):
            dev = lax.rem(lo + k, n_lo)
            sends.append(send(x_ref.at[:, :, dev, pl.ds(0, half), :], r1a.at[lo], inner, dev, 0, k, lo))
        for k in range(1, n_hi):
            dev = lax.rem(hi + k, n_hi)
            sends.append(send(x_ref.at[:, dev, :, pl.ds(half, half), :], r1b.at[hi], outer, dev, 1, k, hi))

        sources_lo = [lax.rem(lo + n_lo - k, n_lo) for k in range(1, n_lo)]
        sources_hi = [lax.rem(hi + n_hi - k, n_hi) for k in range(1, n_hi)]
        for src in sources_lo:
            arrive(r1a.at[src], 0, src)
        for h in range(n_hi):
            total = x_ref[:, h, lo, pl.ds(0, half), :].astype(jnp.float32)
            for src in sources_lo:
                total = total + r1a[src, :, h].astype(jnp.float32)
            s1a[h] = total.astype(s1a.dtype)
        for k in range(1, n_hi):
            dev = lax.rem(hi + k, n_hi)
            sends.append(send(s1a.at[dev], r2a.at[hi], outer, dev, 2, k, hi))
        for src in sources_hi:
            arrive(r1b.at[src], 1, src)
        for l in range(n_lo):
            total = x_ref[:, hi, l, pl.ds(half, half), :].astype(jnp.float32)
            for src in sources_hi:
                total = total + r1b[src, :, l].astype(jnp.float32)
            s1b[l] = total.astype(s1b.dtype)
        for k in range(1, n_lo):
            dev = lax.rem(lo + k, n_lo)
            sends.append(send(s1b.at[dev], r2b.at[lo], inner, dev, 3, k, lo))

        total = s1a[hi].astype(jnp.float32)
        for src in sources_hi:
            arrive(r2a.at[src], 2, src)
            total = total + r2a[src].astype(jnp.float32)
        out_ref[:, pl.ds(0, half), :] = total
        total = s1b[lo].astype(jnp.float32)
        for src in sources_lo:
            arrive(r2b.at[src], 3, src)
            total = total + r2b[src].astype(jnp.float32)
        out_ref[:, pl.ds(half, half), :] = total
        for copy in sends:
            copy.wait_send()

    most = max(n_hi, n_lo)
    return pl.pallas_call(
        kernel,
        out_shape=jax.ShapeDtypeStruct((slots, rows, outs), jnp.float32),
        in_specs=[pl.BlockSpec(memory_space=pltpu.VMEM)],
        out_specs=pl.BlockSpec(memory_space=pltpu.VMEM),
        scratch_shapes=[
            pltpu.VMEM((n_lo, slots, n_hi, half, outs), parts.dtype),
            pltpu.VMEM((n_hi, slots, n_lo, half, outs), parts.dtype),
            pltpu.VMEM((n_hi, slots, half, outs), parts.dtype),
            pltpu.VMEM((n_lo, slots, half, outs), parts.dtype),
            pltpu.VMEM((n_hi, slots, half, outs), parts.dtype),
            pltpu.VMEM((n_lo, slots, half, outs), parts.dtype),
            pltpu.SemaphoreType.DMA((4, most)),
            pltpu.SemaphoreType.DMA((4, most)),
        ],
        compiler_params=pltpu.CompilerParams(collective_id=cid, has_side_effects=True),
    )(parts)


def chip_ring_gather(block, axis, n, cid):
    rows = block.shape[0]
    cut = rows // 32 * 16

    def kernel(x_ref, out_ref, send_sem, recv_sem):
        me = lax.axis_index(axis)
        partner = me + 1 - 2 * lax.rem(me, 2)
        up, down, far = lax.rem(me + 2, n), lax.rem(me + n - 2, n), lax.rem(me + 4, n)
        barrier = pltpu.get_barrier_semaphore()
        for dev in (up, down, partner):
            pl.semaphore_signal(barrier, inc=1, device_id={axis: dev}, device_id_type=MESH_ID)
        pl.semaphore_wait(barrier, 3)
        head, tail = pl.ds(0, cut), pl.ds(cut, rows - cut)

        def send(src_ref, slot, part, dev, index, sem_col):
            copy = pltpu.make_async_remote_copy(
                src_ref=src_ref, dst_ref=out_ref.at[slot, part], send_sem=send_sem.at[index],
                recv_sem=recv_sem.at[slot, sem_col], device_id={axis: dev},
                device_id_type=MESH_ID)
            copy.start()
            return copy

        def arrive(slot, part, sem_col):
            pltpu.make_async_remote_copy(
                src_ref=out_ref.at[slot, part], dst_ref=out_ref.at[slot, part],
                send_sem=send_sem.at[0], recv_sem=recv_sem.at[slot, sem_col],
                device_id={axis: slot}, device_id_type=MESH_ID).wait_recv()

        whole = pl.ds(0, rows)
        sends = [send(x_ref, me, whole, up, 0, 0), send(x_ref, me, whole, down, 1, 0),
                 send(x_ref, me, whole, partner, 2, 0)]
        out_ref[me] = x_ref[...]
        arrive(down, whole, 0)
        sends.append(send(out_ref.at[down, head], down, head, up, 3, 0))
        sends.append(send(out_ref.at[down], down, whole, partner, 4, 0))
        arrive(up, whole, 0)
        sends.append(send(out_ref.at[up, tail], up, tail, down, 5, 1))
        sends.append(send(out_ref.at[up], up, whole, partner, 6, 0))
        arrive(far, head, 0)
        arrive(far, tail, 1)
        sends.append(send(out_ref.at[far], far, whole, partner, 7, 0))
        for k in range(4):
            arrive(lax.rem(partner + 2 * k, n), whole, 0)
        for copy in sends:
            copy.wait_send()

    return pl.pallas_call(
        kernel,
        out_shape=jax.ShapeDtypeStruct((n,) + block.shape, block.dtype),
        in_specs=[pl.BlockSpec(memory_space=pltpu.VMEM)],
        out_specs=pl.BlockSpec(memory_space=pltpu.VMEM),
        scratch_shapes=[pltpu.SemaphoreType.DMA((8,)), pltpu.SemaphoreType.DMA((n, 2))],
        compiler_params=pltpu.CompilerParams(collective_id=cid, has_side_effects=True),
    )(block)

HEADS = 16
WH = 6
WW = 12


EPS = 1e-05


def padded(array, sides, width, wrap):
    for axis, dim in sides:
        size, length = (lax.axis_size(axis), array.shape[dim])
        up = [(i, (i + 1) % size) for i in range(size if wrap else size - 1)]
        down = [(j, i) for i, j in up]
        last = lax.slice_in_dim(array, length - width, length, axis=dim)
        initial = lax.slice_in_dim(array, 0, width, axis=dim)
        before = lax.ppermute(last, axis, up)
        after = lax.ppermute(initial, axis, down)
        array = jnp.concatenate([before, array, after], axis=dim)
    return array


def layer_norm(values, gain):
    wide = values.astype(jnp.float32)
    average = jnp.mean(wide, axis=-1, keepdims=True)
    centred = wide - average
    variance = jnp.mean(centred * centred, axis=-1, keepdims=True)
    return (centred * lax.rsqrt(variance + EPS) * gain).astype(jnp.bfloat16)


def window_attention(query_ext, keyval, row_valid, heads):
    ext_rows, ext_cols, width = query_ext.shape
    head_size = width // heads
    win_rows = ext_rows // WH
    win_cols = ext_cols // WW

    def split(values, parts):
        shaped = values.reshape(win_rows, WH, win_cols, WW, parts, heads, head_size)
        return shaped.transpose(0, 2, 1, 3, 4, 5, 6).reshape(
            win_rows * win_cols, WH * WW, parts, heads, head_size
        )

    query_win = split(query_ext, 1)[:, :, 0]
    pairs = split(keyval, 2)
    key_win = pairs[:, :, 0]
    value_win = pairs[:, :, 1]
    key_mask = jnp.broadcast_to(
        row_valid.reshape(win_rows, 1, WH, 1), (win_rows, win_cols, WH, WW)
    ).reshape(win_rows * win_cols, WH * WW)
    scores = jnp.einsum(
        "wqhd,wkhd->whqk", query_win, key_win, preferred_element_type=jnp.float32
    ) / math.sqrt(head_size)
    scores = jnp.where(key_mask[:, None, None, :], scores, -jnp.inf)
    peak = jnp.max(scores, axis=-1, keepdims=True)
    weights = jnp.exp(scores - peak)
    probs = (weights / jnp.sum(weights, axis=-1, keepdims=True)).astype(jnp.bfloat16)
    mixed = jnp.einsum("whqk,wkhd->wqhd", probs, value_win, preferred_element_type=jnp.float32)
    return (
        mixed.reshape(win_rows, win_cols, WH, WW, width)
        .transpose(0, 2, 1, 3, 4)
        .reshape(ext_rows, ext_cols, width)
    )


def slot_terms(piece, target_rows, live_cols, level_scale, level_shift, heads_full):
    piece_wide = piece.astype(jnp.float32)
    rows = (
        piece_wide[None] * level_scale[:, None, None, :] + level_shift[:, None, None, :]
    ).astype(jnp.bfloat16)
    predicted = jnp.einsum("krnd,kdo->krno", rows, heads_full, preferred_element_type=jnp.float32)
    errors = ((predicted - target_rows.astype(jnp.float32)) * live_cols[:, None, :, None]).astype(
        jnp.bfloat16
    )
    back_grad = jnp.einsum("krno,kdo->krnd", errors, heads_full, preferred_element_type=jnp.float32)
    piece_grad = jnp.sum(back_grad * level_scale[:, None, None, :], axis=0)
    head_add = jnp.einsum("krnd,krno->kdo", rows, errors, preferred_element_type=jnp.float32)
    return (piece_grad, head_add)


def local(
    patches,
    norm_gain,
    input_proj,
    output_proj,
    level_scale,
    level_shift,
    head_weight,
    targets,
    level_counts,
    tile_dataset,
    slot_level,
):
    band_rows, band_cols, width = patches.shape
    half_rows = WH // 2
    half_cols = WW // 2
    lat_count = lax.axis_size(LAT)
    var_count = lax.axis_size("var")
    lat_place = lax.axis_index(LAT)
    ext_rows = band_rows + WH
    ext_cols = band_cols + WW
    own_normed = layer_norm(patches, norm_gain).reshape(-1, width)
    extended = padded(patches, ((LAT, 0),), half_rows, False)
    extended, own_normed = lax.optimization_barrier((extended, own_normed))
    queries = jnp.dot(own_normed, input_proj[:, :width], preferred_element_type=jnp.float32)
    queries = queries.astype(jnp.bfloat16)
    own_keyval = jnp.dot(own_normed, input_proj[:, width:], preferred_element_type=jnp.float32)
    extended = padded(extended, (("var", 1),), half_cols, True)

    def ring(grid):
        top, bottom = grid[:half_rows], grid[half_rows + band_rows :]
        middle = grid[half_rows : half_rows + band_rows]
        left, right = middle[:, :half_cols], middle[:, half_cols + band_cols :]
        return jnp.concatenate(
            [part.reshape((-1,) + grid.shape[2:]) for part in (top, bottom, left, right)]
        )

    halo_normed = layer_norm(ring(extended), norm_gain)
    halo_keyval = jnp.dot(halo_normed, input_proj[:, width:], preferred_element_type=jnp.float32)
    global_row = lat_place * band_rows - half_rows + jnp.arange(ext_rows, dtype=jnp.int32)
    row_valid = (global_row >= 0) & (global_row < lat_count * band_rows)
    win_cols = ext_cols // WW
    ext_r = jnp.arange(ext_rows, dtype=jnp.int32)[:, None]
    ext_c = jnp.arange(ext_cols, dtype=jnp.int32)[None, :]
    key_grid = jnp.where(row_valid[:, None], (ext_r // WH) * win_cols + ext_c // WW, -1)
    query_win = key_grid[half_rows : half_rows + band_rows, half_cols : half_cols + band_cols]
    key_win = jnp.concatenate([query_win.reshape(-1), ring(key_grid)])
    latent = masked_window_attention(
        queries,
        own_keyval.astype(jnp.bfloat16),
        halo_keyval.astype(jnp.bfloat16),
        query_win.reshape(-1, 1),
        key_win.reshape(1, -1),
        HEADS,
        patches.reshape(-1, width),
        output_proj,
    ).reshape(band_rows, band_cols, width)
    dataset_row = tile_dataset[0]
    dataset_ids = jnp.arange(level_counts.shape[0], dtype=jnp.int32)
    tile_levels = jnp.sum(
        jnp.where(dataset_row[:, None] == dataset_ids[None, :], level_counts[None, :], 0), axis=1
    )
    live_tiles = (slot_level[None, :] < tile_levels[:, None]).astype(jnp.float32)
    heads_full = lax.all_gather(head_weight, LAT, axis=1, tiled=True)
    tile_ids = jnp.arange(var_count, dtype=jnp.int32)
    gather = chip_ring_gather if var_count == 8 else chip_pair_gather
    tiles = gather(latent.reshape(band_rows * band_cols, width), "var", var_count, 1)
    piece = (
        tiles.reshape(var_count, band_rows, band_cols, width)
        .transpose(1, 0, 2, 3)
        .reshape(band_rows, var_count * band_cols, width)
    )
    piece_cols = piece.shape[1]
    column_tile = jnp.arange(piece_cols, dtype=jnp.int32) // band_cols
    onehot = (column_tile[:, None] == tile_ids[None, :]).astype(jnp.float32)
    column_live = jnp.dot(onehot, live_tiles)
    piece_grad, head_add = slot_terms(
        piece, targets, column_live.T, level_scale, level_shift, heads_full
    )
    latent_terms = piece_grad
    latent_terms, head_terms = (latent_terms, head_add)
    grad_latent = lax.psum_scatter(
        latent_terms.astype(jnp.bfloat16), "var", scatter_dimension=1, tiled=True
    )
    head_terms = head_terms * (1.0 / math.sqrt(lat_count * band_rows * var_count * band_cols))
    outer, inner = lax.axis_size(LAT[0]), lax.axis_size(LAT[1])
    slots, outs = head_terms.shape[0], head_terms.shape[2]
    share_rows = width // lat_count
    head_parts = head_terms.astype(jnp.bfloat16).reshape(slots, outer, inner, share_rows, outs)
    grad_head = grid_reduce_scatter(head_parts, LAT[0], LAT[1], 3)
    return (latent, grad_latent, grad_head)


def solution(mesh):
    in_specs = (
        P(LAT, "var", None),
        P(),
        P(),
        P(),
        P("var", None),
        P("var", None),
        P("var", LAT, None),
        P("var", LAT, None, None),
        P(),
        P(LAT, None),
        P("var"),
    )
    out_specs = (P(LAT, "var", None), P(LAT, "var", None), P("var", LAT, None))
    lat_size = mesh.shape["lat"]
    inner = 4 if lat_size % 4 == 0 else 1
    grid = Mesh(
        mesh.devices.reshape(lat_size // inner, inner, mesh.shape["var"]), LAT + ("var",)
    )
    return jax.shard_map(local, mesh=grid, in_specs=in_specs, out_specs=out_specs, check_vma=False)
```

```python
import math

import jax
import jax.numpy as jnp
from jax import lax
from jax.experimental import pallas as pl
from jax.experimental.pallas import tpu as pltpu
from jax.sharding import Mesh, PartitionSpec as P

MESH_ID = pl.DeviceIdType.MESH
LAT = ("lat_hi", "lat_lo")


def _greet(axis, n, me):
    barrier = pltpu.get_barrier_semaphore()
    for k in range(1, n):
        pl.semaphore_signal(barrier, inc=1, device_id={axis: lax.rem(me + k, n)},
                            device_id_type=MESH_ID)
    pl.semaphore_wait(barrier, n - 1)


def peer_gather(block, axis, n, cid):
    def kernel(x_ref, out_ref, send_sem, recv_sem):
        me = lax.axis_index(axis)
        _greet(axis, n, me)
        sends = []
        for k in range(1, n):
            copy = pltpu.make_async_remote_copy(
                src_ref=x_ref, dst_ref=out_ref.at[me], send_sem=send_sem.at[k],
                recv_sem=recv_sem.at[me], device_id={axis: lax.rem(me + k, n)},
                device_id_type=MESH_ID)
            copy.start()
            sends.append(copy)
        out_ref[me] = x_ref[...]
        for k in range(1, n):
            src = lax.rem(me + n - k, n)
            pltpu.make_async_remote_copy(
                src_ref=x_ref, dst_ref=out_ref.at[src], send_sem=send_sem.at[k],
                recv_sem=recv_sem.at[src], device_id={axis: src},
                device_id_type=MESH_ID).wait_recv()
        for copy in sends:
            copy.wait_send()

    return pl.pallas_call(
        kernel,
        out_shape=jax.ShapeDtypeStruct((n,) + block.shape, block.dtype),
        in_specs=[pl.BlockSpec(memory_space=pltpu.VMEM)],
        out_specs=pl.BlockSpec(memory_space=pltpu.VMEM),
        scratch_shapes=[pltpu.SemaphoreType.DMA((n,)), pltpu.SemaphoreType.DMA((n,))],
        compiler_params=pltpu.CompilerParams(collective_id=cid, has_side_effects=True),
    )(block)


def peer_reduce_scatter(parts, axis, n, cid, out_dtype):
    def kernel(x_ref, out_ref, held, send_sem, recv_sem):
        me = lax.axis_index(axis)
        _greet(axis, n, me)
        sends = []
        for k in range(1, n):
            dst = lax.rem(me + k, n)
            copy = pltpu.make_async_remote_copy(
                src_ref=x_ref.at[dst], dst_ref=held.at[me], send_sem=send_sem.at[k],
                recv_sem=recv_sem.at[me], device_id={axis: dst},
                device_id_type=MESH_ID)
            copy.start()
            sends.append(copy)
        total = x_ref[me].astype(jnp.float32)
        for k in range(1, n):
            src = lax.rem(me + n - k, n)
            pltpu.make_async_remote_copy(
                src_ref=x_ref.at[src], dst_ref=held.at[src], send_sem=send_sem.at[k],
                recv_sem=recv_sem.at[src], device_id={axis: src},
                device_id_type=MESH_ID).wait_recv()
            total = total + held[src].astype(jnp.float32)
        out_ref[...] = total.astype(out_ref.dtype)
        for copy in sends:
            copy.wait_send()

    return pl.pallas_call(
        kernel,
        out_shape=jax.ShapeDtypeStruct(parts.shape[1:], out_dtype),
        in_specs=[pl.BlockSpec(memory_space=pltpu.VMEM)],
        out_specs=pl.BlockSpec(memory_space=pltpu.VMEM),
        scratch_shapes=[pltpu.VMEM(parts.shape, parts.dtype),
                        pltpu.SemaphoreType.DMA((n,)), pltpu.SemaphoreType.DMA((n,))],
        compiler_params=pltpu.CompilerParams(collective_id=cid, has_side_effects=True),
    )(parts)


def masked_window_attention(queries, own_kv, halo, gain, kv_proj, query_win, key_win, heads, patches, output_proj):
    nq, width = queries.shape
    head_size = width // heads
    scale = 1.0 / float(head_size) ** 0.5

    n_own = own_kv.shape[0]

    def kernel(q_ref, own_ref, halo_ref, g_ref, kvw_ref, qw_ref, kw_ref, p_ref, w_ref, out_ref,
               attn_ref, kv_ref):
        wide = halo_ref[...].astype(jnp.float32)
        centred = wide - jnp.mean(wide, axis=1, keepdims=True)
        variance = jnp.mean(centred * centred, axis=1, keepdims=True)
        normed = (centred * lax.rsqrt(variance + EPS) * g_ref[...]).astype(jnp.bfloat16)
        kv_ref[pl.ds(n_own, halo_ref.shape[0]), :] = jnp.dot(
            normed, kvw_ref[...], preferred_element_type=jnp.float32).astype(kv_ref.dtype)
        kv_ref[pl.ds(0, n_own), :] = own_ref[...]
        mask = qw_ref[...] == kw_ref[...]
        for h in range(heads):
            cols = slice(h * head_size, (h + 1) * head_size)
            q = q_ref[:, cols]
            k = kv_ref[:, h * head_size:(h + 1) * head_size]
            v = kv_ref[:, width + h * head_size:width + (h + 1) * head_size]
            s = lax.dot_general(q, k, (((1,), (1,)), ((), ())),
                                preferred_element_type=jnp.float32) * scale
            s = jnp.where(mask, s, -jnp.inf)
            w = jnp.exp(s - jnp.max(s, axis=1, keepdims=True))
            p = (w / jnp.sum(w, axis=1, keepdims=True)).astype(jnp.bfloat16)
            attn_ref[:, cols] = jnp.dot(p, v, preferred_element_type=jnp.float32).astype(attn_ref.dtype)
        update = jnp.dot(attn_ref[...], w_ref[...], preferred_element_type=jnp.float32)
        out_ref[...] = (p_ref[...].astype(jnp.float32) + update).astype(out_ref.dtype)

    return pl.pallas_call(
        kernel,
        out_shape=jax.ShapeDtypeStruct((nq, width), patches.dtype),
        in_specs=[pl.BlockSpec(memory_space=pltpu.VMEM)] * 9,
        out_specs=pl.BlockSpec(memory_space=pltpu.VMEM),
        scratch_shapes=[
            pltpu.VMEM((nq, width), jnp.bfloat16),
            pltpu.VMEM((n_own + halo.shape[0], own_kv.shape[1]), own_kv.dtype),
        ],
    )(queries, own_kv, halo, gain, kv_proj, query_win, key_win, patches, output_proj)


def chip_pair_gather(block, axis, n, cid):
    nz = n // 2

    def kernel(x_ref, out_ref, send_sem, recv_sem):
        me = lax.axis_index(axis)
        partner = me + 1 - 2 * lax.rem(me, 2)
        peers = [lax.rem(me + 2 * k, n) for k in range(1, nz)]
        barrier = pltpu.get_barrier_semaphore()
        for dev in peers + [partner]:
            pl.semaphore_signal(barrier, inc=1, device_id={axis: dev}, device_id_type=MESH_ID)
        pl.semaphore_wait(barrier, nz)

        def send(src_ref, slot, dev, index):
            copy = pltpu.make_async_remote_copy(
                src_ref=src_ref, dst_ref=out_ref.at[slot], send_sem=send_sem.at[index],
                recv_sem=recv_sem.at[slot], device_id={axis: dev}, device_id_type=MESH_ID)
            copy.start()
            return copy

        def arrive(slot):
            pltpu.make_async_remote_copy(
                src_ref=x_ref, dst_ref=out_ref.at[slot], send_sem=send_sem.at[0],
                recv_sem=recv_sem.at[slot], device_id={axis: slot},
                device_id_type=MESH_ID).wait_recv()

        sends = [send(x_ref, me, dev, i) for i, dev in enumerate(peers)]
        sends.append(send(x_ref, me, partner, nz - 1))
        out_ref[me] = x_ref[...]
        for k in range(1, nz):
            src = lax.rem(me + n - 2 * k, n)
            arrive(src)
            sends.append(send(out_ref.at[src], src, partner, nz - 1 + k))
        for k in range(nz):
            arrive(lax.rem(partner + 2 * k, n))
        for copy in sends:
            copy.wait_send()

    return pl.pallas_call(
        kernel,
        out_shape=jax.ShapeDtypeStruct((n,) + block.shape, block.dtype),
        in_specs=[pl.BlockSpec(memory_space=pltpu.VMEM)],
        out_specs=pl.BlockSpec(memory_space=pltpu.VMEM),
        scratch_shapes=[pltpu.SemaphoreType.DMA((n,)), pltpu.SemaphoreType.DMA((n,))],
        compiler_params=pltpu.CompilerParams(collective_id=cid, has_side_effects=True),
    )(block)


def grid_reduce_scatter(parts, outer, inner, cid):
    slots, n_hi, n_lo, rows, outs = parts.shape
    half = rows // 2

    def kernel(x_ref, out_ref, r1a, r1b, s1a, s1b, r2a, r2b, send_sem, recv_sem):
        hi = lax.axis_index(outer)
        lo = lax.axis_index(inner)
        barrier = pltpu.get_barrier_semaphore()
        for k in range(1, n_lo):
            pl.semaphore_signal(barrier, inc=1, device_id={inner: lax.rem(lo + k, n_lo)},
                                device_id_type=MESH_ID)
        for k in range(1, n_hi):
            pl.semaphore_signal(barrier, inc=1, device_id={outer: lax.rem(hi + k, n_hi)},
                                device_id_type=MESH_ID)
        pl.semaphore_wait(barrier, n_lo + n_hi - 2)

        def send(src_ref, dst_ref, axis, dev, group, k, slot):
            copy = pltpu.make_async_remote_copy(
                src_ref=src_ref, dst_ref=dst_ref, send_sem=send_sem.at[group, k],
                recv_sem=recv_sem.at[group, slot], device_id={axis: dev},
                device_id_type=MESH_ID)
            copy.start()
            return copy

        def arrive(dst_ref, group, slot):
            pltpu.make_async_remote_copy(
                src_ref=dst_ref, dst_ref=dst_ref, send_sem=send_sem.at[group, 0],
                recv_sem=recv_sem.at[group, slot], device_id={inner: lo},
                device_id_type=MESH_ID).wait_recv()

        sends = []
        for k in range(1, n_lo):
            dev = lax.rem(lo + k, n_lo)
            sends.append(send(x_ref.at[:, :, dev, pl.ds(0, half), :], r1a.at[lo], inner, dev, 0, k, lo))
        for k in range(1, n_hi):
            dev = lax.rem(hi + k, n_hi)
            sends.append(send(x_ref.at[:, dev, :, pl.ds(half, half), :], r1b.at[hi], outer, dev, 1, k, hi))

        sources_lo = [lax.rem(lo + n_lo - k, n_lo) for k in range(1, n_lo)]
        sources_hi = [lax.rem(hi + n_hi - k, n_hi) for k in range(1, n_hi)]
        for src in sources_lo:
            arrive(r1a.at[src], 0, src)
        for h in range(n_hi):
            total = x_ref[:, h, lo, pl.ds(0, half), :].astype(jnp.float32)
            for src in sources_lo:
                total = total + r1a[src, :, h].astype(jnp.float32)
            s1a[h] = total.astype(s1a.dtype)
        for k in range(1, n_hi):
            dev = lax.rem(hi + k, n_hi)
            sends.append(send(s1a.at[dev], r2a.at[hi], outer, dev, 2, k, hi))
        for src in sources_hi:
            arrive(r1b.at[src], 1, src)
        for l in range(n_lo):
            total = x_ref[:, hi, l, pl.ds(half, half), :].astype(jnp.float32)
            for src in sources_hi:
                total = total + r1b[src, :, l].astype(jnp.float32)
            s1b[l] = total.astype(s1b.dtype)
        for k in range(1, n_lo):
            dev = lax.rem(lo + k, n_lo)
            sends.append(send(s1b.at[dev], r2b.at[lo], inner, dev, 3, k, lo))

        total = s1a[hi].astype(jnp.float32)
        for src in sources_hi:
            arrive(r2a.at[src], 2, src)
            total = total + r2a[src].astype(jnp.float32)
        out_ref[:, pl.ds(0, half), :] = total
        total = s1b[lo].astype(jnp.float32)
        for src in sources_lo:
            arrive(r2b.at[src], 3, src)
            total = total + r2b[src].astype(jnp.float32)
        out_ref[:, pl.ds(half, half), :] = total
        for copy in sends:
            copy.wait_send()

    most = max(n_hi, n_lo)
    return pl.pallas_call(
        kernel,
        out_shape=jax.ShapeDtypeStruct((slots, rows, outs), jnp.float32),
        in_specs=[pl.BlockSpec(memory_space=pltpu.VMEM)],
        out_specs=pl.BlockSpec(memory_space=pltpu.VMEM),
        scratch_shapes=[
            pltpu.VMEM((n_lo, slots, n_hi, half, outs), parts.dtype),
            pltpu.VMEM((n_hi, slots, n_lo, half, outs), parts.dtype),
            pltpu.VMEM((n_hi, slots, half, outs), parts.dtype),
            pltpu.VMEM((n_lo, slots, half, outs), parts.dtype),
            pltpu.VMEM((n_hi, slots, half, outs), parts.dtype),
            pltpu.VMEM((n_lo, slots, half, outs), parts.dtype),
            pltpu.SemaphoreType.DMA((4, most)),
            pltpu.SemaphoreType.DMA((4, most)),
        ],
        compiler_params=pltpu.CompilerParams(collective_id=cid, has_side_effects=True),
    )(parts)


def chip_ring_gather(block, axis, n, cid):
    rows = block.shape[0]
    cut = rows // 32 * 16

    def kernel(x_ref, out_ref, send_sem, recv_sem):
        me = lax.axis_index(axis)
        partner = me + 1 - 2 * lax.rem(me, 2)
        up, down, far = lax.rem(me + 2, n), lax.rem(me + n - 2, n), lax.rem(me + 4, n)
        barrier = pltpu.get_barrier_semaphore()
        for dev in (up, down, partner):
            pl.semaphore_signal(barrier, inc=1, device_id={axis: dev}, device_id_type=MESH_ID)
        pl.semaphore_wait(barrier, 3)
        head, tail = pl.ds(0, cut), pl.ds(cut, rows - cut)

        def send(src_ref, slot, part, dev, index, sem_col):
            copy = pltpu.make_async_remote_copy(
                src_ref=src_ref, dst_ref=out_ref.at[slot, part], send_sem=send_sem.at[index],
                recv_sem=recv_sem.at[slot, sem_col], device_id={axis: dev},
                device_id_type=MESH_ID)
            copy.start()
            return copy

        def arrive(slot, part, sem_col):
            pltpu.make_async_remote_copy(
                src_ref=out_ref.at[slot, part], dst_ref=out_ref.at[slot, part],
                send_sem=send_sem.at[0], recv_sem=recv_sem.at[slot, sem_col],
                device_id={axis: slot}, device_id_type=MESH_ID).wait_recv()

        whole = pl.ds(0, rows)
        sends = [send(x_ref, me, whole, up, 0, 0), send(x_ref, me, whole, down, 1, 0),
                 send(x_ref, me, whole, partner, 2, 0)]
        out_ref[me] = x_ref[...]
        arrive(down, whole, 0)
        sends.append(send(out_ref.at[down, head], down, head, up, 3, 0))
        sends.append(send(out_ref.at[down], down, whole, partner, 4, 0))
        arrive(up, whole, 0)
        sends.append(send(out_ref.at[up, tail], up, tail, down, 5, 1))
        sends.append(send(out_ref.at[up], up, whole, partner, 6, 0))
        arrive(far, head, 0)
        arrive(far, tail, 1)
        sends.append(send(out_ref.at[far], far, whole, partner, 7, 0))
        for k in range(4):
            arrive(lax.rem(partner + 2 * k, n), whole, 0)
        for copy in sends:
            copy.wait_send()

    return pl.pallas_call(
        kernel,
        out_shape=jax.ShapeDtypeStruct((n,) + block.shape, block.dtype),
        in_specs=[pl.BlockSpec(memory_space=pltpu.VMEM)],
        out_specs=pl.BlockSpec(memory_space=pltpu.VMEM),
        scratch_shapes=[pltpu.SemaphoreType.DMA((8,)), pltpu.SemaphoreType.DMA((n, 2))],
        compiler_params=pltpu.CompilerParams(collective_id=cid, has_side_effects=True),
    )(block)

HEADS = 16
WH = 6
WW = 12


EPS = 1e-05


def padded(array, sides, width, wrap):
    for axis, dim in sides:
        size, length = (lax.axis_size(axis), array.shape[dim])
        up = [(i, (i + 1) % size) for i in range(size if wrap else size - 1)]
        down = [(j, i) for i, j in up]
        last = lax.slice_in_dim(array, length - width, length, axis=dim)
        initial = lax.slice_in_dim(array, 0, width, axis=dim)
        before = lax.ppermute(last, axis, up)
        after = lax.ppermute(initial, axis, down)
        array = jnp.concatenate([before, array, after], axis=dim)
    return array


def layer_norm(values, gain):
    wide = values.astype(jnp.float32)
    average = jnp.mean(wide, axis=-1, keepdims=True)
    centred = wide - average
    variance = jnp.mean(centred * centred, axis=-1, keepdims=True)
    return (centred * lax.rsqrt(variance + EPS) * gain).astype(jnp.bfloat16)


def window_attention(query_ext, keyval, row_valid, heads):
    ext_rows, ext_cols, width = query_ext.shape
    head_size = width // heads
    win_rows = ext_rows // WH
    win_cols = ext_cols // WW

    def split(values, parts):
        shaped = values.reshape(win_rows, WH, win_cols, WW, parts, heads, head_size)
        return shaped.transpose(0, 2, 1, 3, 4, 5, 6).reshape(
            win_rows * win_cols, WH * WW, parts, heads, head_size
        )

    query_win = split(query_ext, 1)[:, :, 0]
    pairs = split(keyval, 2)
    key_win = pairs[:, :, 0]
    value_win = pairs[:, :, 1]
    key_mask = jnp.broadcast_to(
        row_valid.reshape(win_rows, 1, WH, 1), (win_rows, win_cols, WH, WW)
    ).reshape(win_rows * win_cols, WH * WW)
    scores = jnp.einsum(
        "wqhd,wkhd->whqk", query_win, key_win, preferred_element_type=jnp.float32
    ) / math.sqrt(head_size)
    scores = jnp.where(key_mask[:, None, None, :], scores, -jnp.inf)
    peak = jnp.max(scores, axis=-1, keepdims=True)
    weights = jnp.exp(scores - peak)
    probs = (weights / jnp.sum(weights, axis=-1, keepdims=True)).astype(jnp.bfloat16)
    mixed = jnp.einsum("whqk,wkhd->wqhd", probs, value_win, preferred_element_type=jnp.float32)
    return (
        mixed.reshape(win_rows, win_cols, WH, WW, width)
        .transpose(0, 2, 1, 3, 4)
        .reshape(ext_rows, ext_cols, width)
    )


def slot_terms(piece, target_rows, live_cols, level_scale, level_shift, heads_full):
    piece_wide = piece.astype(jnp.float32)
    rows = (
        piece_wide[None] * level_scale[:, None, None, :] + level_shift[:, None, None, :]
    ).astype(jnp.bfloat16)
    predicted = jnp.einsum("krnd,kdo->krno", rows, heads_full, preferred_element_type=jnp.float32)
    errors = ((predicted - target_rows.astype(jnp.float32)) * live_cols[:, None, :, None]).astype(
        jnp.bfloat16
    )
    back_grad = jnp.einsum("krno,kdo->krnd", errors, heads_full, preferred_element_type=jnp.float32)
    piece_grad = jnp.sum(back_grad * level_scale[:, None, None, :], axis=0)
    head_add = jnp.einsum("krnd,krno->kdo", rows, errors, preferred_element_type=jnp.float32)
    return (piece_grad, head_add)


def local(
    patches,
    norm_gain,
    input_proj,
    output_proj,
    level_scale,
    level_shift,
    head_weight,
    targets,
    level_counts,
    tile_dataset,
    slot_level,
):
    band_rows, band_cols, width = patches.shape
    half_rows = WH // 2
    half_cols = WW // 2
    lat_count = lax.axis_size(LAT)
    var_count = lax.axis_size("var")
    lat_place = lax.axis_index(LAT)
    ext_rows = band_rows + WH
    ext_cols = band_cols + WW
    own_normed = layer_norm(patches, norm_gain).reshape(-1, width)
    extended = padded(patches, ((LAT, 0),), half_rows, False)
    extended, own_normed = lax.optimization_barrier((extended, own_normed))
    queries = jnp.dot(own_normed, input_proj[:, :width], preferred_element_type=jnp.float32)
    queries = queries.astype(jnp.bfloat16)
    own_keyval = jnp.dot(own_normed, input_proj[:, width:], preferred_element_type=jnp.float32)
    extended = padded(extended, (("var", 1),), half_cols, True)

    def ring(grid):
        top, bottom = grid[:half_rows], grid[half_rows + band_rows :]
        middle = grid[half_rows : half_rows + band_rows]
        left, right = middle[:, :half_cols], middle[:, half_cols + band_cols :]
        return jnp.concatenate(
            [part.reshape((-1,) + grid.shape[2:]) for part in (top, bottom, left, right)]
        )

    global_row = lat_place * band_rows - half_rows + jnp.arange(ext_rows, dtype=jnp.int32)
    row_valid = (global_row >= 0) & (global_row < lat_count * band_rows)
    win_cols = ext_cols // WW
    ext_r = jnp.arange(ext_rows, dtype=jnp.int32)[:, None]
    ext_c = jnp.arange(ext_cols, dtype=jnp.int32)[None, :]
    key_grid = jnp.where(row_valid[:, None], (ext_r // WH) * win_cols + ext_c // WW, -1)
    query_win = key_grid[half_rows : half_rows + band_rows, half_cols : half_cols + band_cols]
    key_win = jnp.concatenate([query_win.reshape(-1), ring(key_grid)])
    latent = masked_window_attention(
        queries,
        own_keyval.astype(jnp.bfloat16),
        ring(extended),
        norm_gain.reshape(1, width),
        input_proj[:, width:],
        query_win.reshape(-1, 1),
        key_win.reshape(1, -1),
        HEADS,
        patches.reshape(-1, width),
        output_proj,
    ).reshape(band_rows, band_cols, width)
    dataset_row = tile_dataset[0]
    dataset_ids = jnp.arange(level_counts.shape[0], dtype=jnp.int32)
    tile_levels = jnp.sum(
        jnp.where(dataset_row[:, None] == dataset_ids[None, :], level_counts[None, :], 0), axis=1
    )
    live_tiles = (slot_level[None, :] < tile_levels[:, None]).astype(jnp.float32)
    heads_full = lax.all_gather(head_weight, LAT, axis=1, tiled=True)
    tile_ids = jnp.arange(var_count, dtype=jnp.int32)
    gather = chip_ring_gather if var_count == 8 else chip_pair_gather
    tiles = gather(latent.reshape(band_rows * band_cols, width), "var", var_count, 1)
    piece = (
        tiles.reshape(var_count, band_rows, band_cols, width)
        .transpose(1, 0, 2, 3)
        .reshape(band_rows, var_count * band_cols, width)
    )
    piece_cols = piece.shape[1]
    column_tile = jnp.arange(piece_cols, dtype=jnp.int32) // band_cols
    onehot = (column_tile[:, None] == tile_ids[None, :]).astype(jnp.float32)
    column_live = jnp.dot(onehot, live_tiles)
    piece_grad, head_add = slot_terms(
        piece, targets, column_live.T, level_scale, level_shift, heads_full
    )
    latent_terms = piece_grad
    latent_terms, head_terms = (latent_terms, head_add)
    grad_latent = lax.psum_scatter(
        latent_terms.astype(jnp.bfloat16), "var", scatter_dimension=1, tiled=True
    )
    head_terms = head_terms * (1.0 / math.sqrt(lat_count * band_rows * var_count * band_cols))
    outer, inner = lax.axis_size(LAT[0]), lax.axis_size(LAT[1])
    slots, outs = head_terms.shape[0], head_terms.shape[2]
    share_rows = width // lat_count
    head_parts = head_terms.astype(jnp.bfloat16).reshape(slots, outer, inner, share_rows, outs)
    grad_head = grid_reduce_scatter(head_parts, LAT[0], LAT[1], 3)
    return (latent, grad_latent, grad_head)


def solution(mesh):
    in_specs = (
        P(LAT, "var", None),
        P(),
        P(),
        P(),
        P("var", None),
        P("var", None),
        P("var", LAT, None),
        P("var", LAT, None, None),
        P(),
        P(LAT, None),
        P("var"),
    )
    out_specs = (P(LAT, "var", None), P(LAT, "var", None), P("var", LAT, None))
    lat_size = mesh.shape["lat"]
    inner = 4 if lat_size % 4 == 0 else 1
    grid = Mesh(
        mesh.devices.reshape(lat_size // inner, inner, mesh.shape["var"]), LAT + ("var",)
    )
    return jax.shard_map(local, mesh=grid, in_specs=in_specs, out_specs=out_specs, check_vma=False)
```
